32 devices in a mesh: rep: 4 (over z), shard: 8 (over y, x, core).
Axes of the slice: x: 2, y: 2, z: 4, core: 2. Of those that a mesh axis runs over, the one named last changes fastest.
Arguments:
- tokens: bfloat16 [16384, 1024], P(('rep', 'shard')), may hold values from -6 to 6
- cotangent: bfloat16 [16384, 1024], P(('rep', 'shard')), may hold values from -6 to 6
- seq_lengths: int32 [32, 4], P(('rep', 'shard')), may hold values from 1 to 256, 512 in all within a row
- pack_order: int32 [16384], P(('rep', 'shard')), may hold values from 0 to 511, as said below
- unpack_order: int32 [16384], P(('rep', 'shard')), may hold values from 0 to 511, as said below
- expert_ids: int32 [16384, 8], P(('rep', 'shard')), may hold values from 0 to 15, all different within a row; in each aligned block of 512 rows (0 to 511, 512 to 1023, ...) at most 384 rows name the same one
- gates: float32 [16384, 8], P(('rep', 'shard')), may hold values from 0.06 to 0.19
- first_gain: bfloat16 [1024], P('shard'), may hold values from 0.5 to 1.5
- query_weight: bfloat16 [1024, 1024], P('shard'), may hold values from -0.1875 to 0.1875
- key_matrix: bfloat16 [1024, 512], P('shard'), may hold values from -0.1875 to 0.1875
- value_matrix: bfloat16 [1024, 512], P('shard'), may hold values from -0.1875 to 0.1875
- output_weight: bfloat16 [1024, 1024], P('shard'), may hold values from -0.75 to 0.75
- second_gain: bfloat16 [1024], P('shard'), may hold values from 0.5 to 1.5
- gate_weight: bfloat16 [16, 1024, 512], P('shard'), may hold values from -0.1875 to 0.1875
- up_weight: bfloat16 [16, 1024, 512], P('shard'), may hold values from -0.1875 to 0.1875
- down_weight: bfloat16 [16, 512, 1024], P('shard'), may hold values from -1 to 1
Outputs:
- out_tokens: bfloat16 [16384, 1024], P(('rep', 'shard'))
- delta_tokens: bfloat16 [16384, 1024], P(('rep', 'shard'))
- delta_first: float32 [1024], P('shard')
- delta_query: float32 [1024, 1024], P('shard')
- delta_key: float32 [1024, 512], P('shard')
- delta_value: float32 [1024, 512], P('shard')
- delta_output: float32 [1024, 1024], P('shard')
- delta_second: float32 [1024], P('shard')
- delta_gate: float32 [16, 1024, 512], P('shard')
- delta_up: float32 [16, 1024, 512], P('shard')
- delta_down: float32 [16, 512, 1024], P('shard')
The draws below stay inside these ranges and needn't reach their ends.
Inputs may be any that keep to these rules, and one draw needn't show every extreme that they name: `seq_lengths`: each row sums to 512, and its longest entry is exactly 256. `pack_order`: the 512 entries of each pack form a permutation. `unpack_order`: the 512 entries of each pack form the inverse of that pack's permutation in pack_order. `expert_ids`: A row names 8 different experts; among the 512 rows of one pack no expert is named more than 384 times, and in some pack one expert is named exactly 384 times.
All inputs are finite; a program needn't handle non-finite values.
Results may differ from the reference program's by a relative error of at most 0.02.
Values may be sent and summed in bfloat16 or wider, within the bound.
A program may use at most 256 MiB of HBM per device.

```python
import math
import jax
import jax.numpy as jnp
import numpy as np
from jax import lax

MODEL_WIDTH = 1024
QUERY_HEADS = 16
KEY_VALUE_HEADS = 8
HEAD_SIZE = 64
F = 512
TOPK = 8
TOK_DEV = 512
SEQS = 4
EXPERTS = 16
MAXLEN = 256
BLK = 64
PACKS = 32
TOKENS = 16384
CAP = 384
N_REP = 4
N_SHARD = 8


def order_pair(key):
    packs = TOKENS // TOK_DEV
    key_rows = jax.random.split(jax.random.fold_in(key, 11), packs)
    perms = jax.vmap(lambda single: jax.random.permutation(single, TOK_DEV))(key_rows).astype(jnp.int32)
    inverse = jnp.argsort(perms, axis=1, stable=True).astype(jnp.int32)
    return (perms, inverse)


def draw_pack_order(key, part):
    return order_pair(key)[0].reshape(TOKENS)


def draw_unpack_order(key, part):
    return order_pair(key)[1].reshape(TOKENS)


def levels(own_key, shape, pieces, smallest, top_value):
    def one(axis_at, shards_of):
        steps = jax.random.uniform(jax.random.fold_in(jax.random.fold_in(own_key, 6), axis_at), (shards_of,), jnp.float32, smallest / len(pieces), top_value / len(pieces))
        return jnp.repeat(jnp.exp(steps), shape[axis_at] // shards_of).reshape((-1,) + (1,) * (len(shape) - axis_at - 1))

    gain = one(*pieces[0])
    for cut in pieces[1:]:
        gain = gain * one(*cut)
    return gain


def length_profile(count, total, bound, slope):
    portions = [(1 << 20) // math.isqrt(rank ** slope) + 1 for rank in range(2, count + 1)]
    surplus, given = total - bound - (count - 1), [1] * (count - 1)
    while surplus > 0:
        candidates = [i for i in range(count - 1) if given[i] < bound]
        pool, budget = sum([portions[i] for i in candidates]), surplus
        for i in candidates:
            addition = min(bound - given[i], max(1, budget * portions[i] // pool), surplus)
            given[i] = given[i] + addition
            surplus = surplus - addition
    return np.array([bound] + given)


def uneven_parts(key, number_of, total, bound, slope):
    if number_of == 2:
        one = jax.random.randint(key, (), max(1, total - bound), min(bound, total - 1) + 1)
        return jnp.stack([one, total - one])
    sizes = jnp.asarray(length_profile(number_of, total, bound, slope), jnp.int32)
    couples = (number_of - 1) // 2
    giver, sink = sizes[1:1 + 2 * couples:2], sizes[2:2 + 2 * couples:2]
    margin = jnp.minimum(giver - 1, bound - sink)
    shifted = jax.random.randint(jax.random.fold_in(key, 1), (couples,), 0, 1 << 20) % (margin + 1)
    sizes = sizes.at[1:1 + 2 * couples:2].set(giver - shifted).at[2:2 + 2 * couples:2].set(sink + shifted)
    return sizes[jax.random.permutation(jax.random.fold_in(key, 2), number_of)]


def shared_out(own_key, own, number, rows, amount, top, most, lean):
    order = jax.random.permutation(own_key, amount)
    crowded, ordinary = portions_of(amount, rows * top, most, lean, True), portions_of(amount, rows * top, most, lean, False)
    places = jnp.arange(amount)

    def named(sizes, turn):
        used = int((sizes > 0).sum())
        fixed = max(1, used // 4)
        shifted = fixed + (places - fixed + turn * (used - fixed)) % max(1, amount - fixed)
        return jnp.zeros((amount,), jnp.int32).at[order[jnp.where(places < fixed, places, shifted)]].set(jnp.asarray(sizes, jnp.int32))

    sizes = jnp.where(number % 4 == 0, named(crowded, number // 4), named(ordinary, number - number // 4 - 1))
    mixed = jax.random.permutation(jax.random.fold_in(own, 3), amount)
    donor, receiver = mixed[0:amount // 2 * 2:2], mixed[1:amount // 2 * 2:2]
    margin = jnp.minimum(sizes[donor] - 1, most - sizes[receiver]) // 2
    margin = jnp.where((donor == order[0]) | (receiver == order[0]) | (sizes[receiver] == 0), 0, jnp.maximum(margin, 0))
    shifted = jax.random.randint(jax.random.fold_in(own, 4), (amount // 2,), 0, 1 << 20) % (margin + 1)
    sizes = sizes.at[donor].add(-shifted).at[receiver].add(shifted)
    labels = jnp.searchsorted(jnp.cumsum(sizes), jnp.arange(rows * top), side="right").astype(jnp.int32)
    table = labels.reshape(top, rows).T
    table = table[jax.random.permutation(jax.random.fold_in(own, 1), rows)]
    turn = jax.random.randint(jax.random.fold_in(own, 2), (rows, 1), 0, top)
    return jnp.take_along_axis(table, (jnp.arange(top)[None, :] + turn) % top, axis=1)


def portions_of(amount, total, reach, slope, full):
    portions = [(1 << 20) // math.isqrt(standing ** slope) + 1 for standing in range(1, amount + 1)]
    largest = reach if full else min(reach, max(-(-total // amount), total * portions[0] // sum(portions)))
    least = 1 if total - largest >= amount - 1 else 0
    counts, spare = [largest] + [least] * (amount - 1), total - largest - least * (amount - 1)
    while spare > 0:
        movable = [i for i in range(1, amount) if counts[i] < largest] or [i for i in range(1, amount) if counts[i] < reach]
        pool, budget = sum([portions[i] for i in movable]), spare
        for i in movable:
            more = min(reach - counts[i], max(1, budget * portions[i] // pool), spare)
            counts[i] = counts[i] + more
            spare = spare - more
    return np.array(counts)


def bell_draw(rng, dims, scale, reach, cuts=(), kind=jnp.bfloat16):
    entries = jax.random.normal(rng, dims, jnp.float32) * scale
    if len(cuts) > 0:
        entries = levels(rng, dims, cuts, -0.22, 0.18) * entries
    return jnp.clip(entries, min=-reach, max=reach).astype(kind)


def setup_inputs(seed: int = 0) -> dict:
    seeds = jax.random.split(jax.random.key(seed), 17)
    tokens = bell_draw(seeds[0], (TOKENS, MODEL_WIDTH), 1.0, 6.0, ((0, 32),))
    cotangent = bell_draw(seeds[1], (TOKENS, MODEL_WIDTH), 1.0, 6.0, ((0, 32),))
    seq_lengths = jax.vmap(lambda own: uneven_parts(own, SEQS, TOK_DEV, MAXLEN, 2))(jax.random.split(seeds[2], PACKS)).reshape((PACKS, SEQS)).astype(jnp.int32)
    pack_order = draw_pack_order(jax.random.fold_in(seeds[16], 71), 0)
    unpack_order = draw_unpack_order(jax.random.fold_in(seeds[16], 71), 0)
    expert_ids_keys = jax.random.split(jax.random.fold_in(seeds[5], 1), TOKENS // TOK_DEV)
    expert_ids_turns = jax.random.permutation(jax.random.fold_in(seeds[5], 3), TOKENS // TOK_DEV)
    expert_ids = jax.vmap(lambda own, number: shared_out(jax.random.fold_in(seeds[5], 2), own, number, TOK_DEV, EXPERTS, TOPK, CAP, 1))(expert_ids_keys, expert_ids_turns).reshape((TOKENS, TOPK))
    gates = jnp.clip(0.06 + 0.13 * jax.random.uniform(seeds[6], (TOKENS, TOPK), jnp.float32) ** levels(seeds[6], (TOKENS, TOPK), ((0, 32),), -0.2, 0.2), 0.06, 0.19)
    first_gain = jnp.clip(1.0 + 0.1 * jax.random.normal(seeds[7], (MODEL_WIDTH,), jnp.float32), 0.5, 1.5).astype(jnp.bfloat16)
    query_weight = bell_draw(seeds[8], (MODEL_WIDTH, QUERY_HEADS * HEAD_SIZE), MODEL_WIDTH ** -0.5, 0.1875, ((0, 8),))
    key_matrix = bell_draw(seeds[9], (MODEL_WIDTH, KEY_VALUE_HEADS * HEAD_SIZE), MODEL_WIDTH ** -0.5, 0.1875, ((0, 8),))
    value_matrix = bell_draw(seeds[10], (MODEL_WIDTH, KEY_VALUE_HEADS * HEAD_SIZE), MODEL_WIDTH ** -0.5, 0.1875, ((0, 8),))
    output_weight = bell_draw(seeds[11], (QUERY_HEADS * HEAD_SIZE, MODEL_WIDTH), (QUERY_HEADS * HEAD_SIZE // 16) ** -0.5, 0.75, ((0, 8),))
    second_gain = jnp.clip(1.0 + 0.1 * jax.random.normal(seeds[12], (MODEL_WIDTH,), jnp.float32), 0.5, 1.5).astype(jnp.bfloat16)
    gate_weight = bell_draw(seeds[13], (EXPERTS, MODEL_WIDTH, F), MODEL_WIDTH ** -0.5, 0.1875, ((0, 8),))
    up_weight = bell_draw(seeds[14], (EXPERTS, MODEL_WIDTH, F), MODEL_WIDTH ** -0.5, 0.1875, ((0, 8),))
    down_weight = bell_draw(seeds[15], (EXPERTS, F, MODEL_WIDTH), (F // 16) ** -0.5, 1.0, ((0, 8),))
    return dict(tokens=tokens, cotangent=cotangent, seq_lengths=seq_lengths, pack_order=pack_order, unpack_order=unpack_order, expert_ids=expert_ids, gates=gates, first_gain=first_gain, query_weight=query_weight, key_matrix=key_matrix, value_matrix=value_matrix, output_weight=output_weight, second_gain=second_gain, gate_weight=gate_weight, up_weight=up_weight, down_weight=down_weight)


@jax.custom_vjp
def lower_precision(v):
    return lax.optimization_barrier(v.astype(jnp.bfloat16)).astype(jnp.float32)

@jax.custom_vjp
def low_back(v):
    return v

def low_keep(v):
    return (lower_precision(v), None)

def low_pass(kept, grad):
    return (grad,)

def back_keep(v):
    return (v, None)

def back_low(kept, grad):
    return (lower_precision(grad),)
lower_precision.defvjp(low_keep, low_pass)
low_back.defvjp(back_keep, back_low)
EPS = 1e-05
THETA = 10000.0
HIGH = lax.Precision.HIGHEST

def rope_tables(place, size):
    half = size // 2
    freq = THETA ** (-2.0 * jnp.arange(half, dtype=jnp.float32) / size)
    angle = place.astype(jnp.float32)[:, None] * freq[None, :]
    return (jnp.cos(angle), jnp.sin(angle))

def rotary_apply(heads, cosine_table, sine_table):
    half = heads.shape[-1] // 2
    first = heads[..., :half]
    second = heads[..., half:]
    along = cosine_table[:, None, :]
    across = sine_table[:, None, :]
    return jnp.concatenate([first * along - second * across, second * along + first * across], axis=-1)

def segment_info(lengths, group_count):
    lengths = lengths.astype(jnp.int32)
    ends = jnp.cumsum(lengths).astype(jnp.int32)
    starts = ends - lengths
    place = jnp.arange(group_count, dtype=jnp.int32)
    inside = ((place[:, None] >= starts[None, :]) & (place[:, None] < ends[None, :])).astype(jnp.int32)
    segment = lax.optimization_barrier(jnp.sum(inside * jnp.arange(lengths.shape[0], dtype=jnp.int32)[None, :], axis=1)).astype(jnp.int32)
    offset = lax.optimization_barrier(jnp.sum(inside * starts[None, :], axis=1)).astype(jnp.int32)
    return (segment, place - offset)

def pack_forward(weights, piece):
    first_gain, query_weight, key_matrix, value_matrix, output_weight, second_gain, gate_weight, up_weight, down_weight = weights
    inputs, lengths, routes, gate_rows = piece
    group_count = inputs.shape[0]
    segment, place = segment_info(lengths, group_count)
    cosine_table, sine_table = rope_tables(place, HEAD_SIZE)
    first_scale = lax.rsqrt(lax.optimization_barrier(jnp.mean(inputs * inputs, axis=1, keepdims=True)) + EPS)
    normed = lower_precision(inputs * first_scale * first_gain)
    query_projected = low_back(jnp.dot(normed, query_weight, precision=HIGH))
    key_projected = low_back(jnp.dot(normed, key_matrix, precision=HIGH))
    value_rows = lower_precision(low_back(jnp.dot(normed, value_matrix, precision=HIGH)))
    query_rows = lower_precision(rotary_apply(query_projected.reshape(group_count, QUERY_HEADS, HEAD_SIZE), cosine_table, sine_table)).reshape(group_count, KEY_VALUE_HEADS, QUERY_HEADS // KEY_VALUE_HEADS, HEAD_SIZE)
    key_rows = lower_precision(rotary_apply(key_projected.reshape(group_count, KEY_VALUE_HEADS, HEAD_SIZE), cosine_table, sine_table))
    value_rows = value_rows.reshape(group_count, KEY_VALUE_HEADS, HEAD_SIZE)
    scores = low_back(jnp.einsum('igzd,jgd->gzij', query_rows, key_rows, precision=HIGH) * HEAD_SIZE ** (-0.5))
    position = jnp.arange(group_count, dtype=jnp.int32)
    allowed = (segment[:, None] == segment[None, :]) & (position[None, :] <= position[:, None])
    probs = lower_precision(jax.nn.softmax(jnp.where(allowed, scores, -1e+30), axis=-1))
    mixed = jnp.einsum('gzij,jgd->igzd', probs, value_rows, precision=HIGH).reshape(group_count, QUERY_HEADS * HEAD_SIZE)
    mixed = lower_precision(low_back(mixed))
    hidden_one = inputs + low_back(jnp.dot(mixed, output_weight, precision=HIGH))
    second_scale = lax.rsqrt(lax.optimization_barrier(jnp.mean(hidden_one * hidden_one, axis=1, keepdims=True)) + EPS)
    normed_two = lower_precision(hidden_one * second_scale * second_gain)
    copies = low_back(jnp.broadcast_to(normed_two[None], (EXPERTS, group_count, MODEL_WIDTH)))
    gate_act = low_back(jnp.einsum('etd,edf->etf', copies, gate_weight, precision=HIGH))
    up_act = low_back(jnp.einsum('etd,edf->etf', copies, up_weight, precision=HIGH))
    inner = lower_precision(jax.nn.silu(gate_act) * up_act)
    result = lower_precision(low_back(jnp.einsum('etf,efd->etd', inner, down_weight, precision=HIGH)))
    named = (routes[:, :, None] == jnp.arange(EXPERTS, dtype=jnp.int32)[None, None, :]).astype(jnp.float32)
    mixing = lax.optimization_barrier(jnp.sum(named * gate_rows[:, :, None], axis=1))
    return hidden_one + jnp.einsum('te,etd->td', mixing, result, precision=HIGH)

def arrive(rows):
    shaped = rows.reshape(N_REP, N_SHARD, N_SHARD, BLK, rows.shape[-1])
    return jnp.swapaxes(shaped, 1, 2).reshape(PACKS, TOK_DEV, rows.shape[-1])

def depart(rows):
    shaped = rows.reshape(N_REP, N_SHARD, N_SHARD, BLK, rows.shape[-1])
    return jnp.swapaxes(shaped, 1, 2).reshape(PACKS * TOK_DEV, rows.shape[-1])

def reference(tokens, cotangent, seq_lengths, pack_order, unpack_order, expert_ids, gates, first_gain, query_weight, key_matrix, value_matrix, output_weight, second_gain, gate_weight, up_weight, down_weight):
    order = pack_order.reshape(PACKS, TOK_DEV, 1).astype(jnp.int32)
    reverse = unpack_order.reshape(PACKS, TOK_DEV, 1).astype(jnp.int32)
    inputs = jnp.take_along_axis(arrive(tokens), order, axis=1).astype(jnp.float32)
    slopes = jnp.take_along_axis(arrive(cotangent), order, axis=1).astype(jnp.float32)
    routes = expert_ids.reshape(PACKS, TOK_DEV, TOPK).astype(jnp.int32)
    gate_rows = gates.reshape(PACKS, TOK_DEV, TOPK).astype(jnp.float32)
    lengths = seq_lengths.astype(jnp.int32)
    weights = tuple((array.astype(jnp.float32) for array in (first_gain, query_weight, key_matrix, value_matrix, output_weight, second_gain, gate_weight, up_weight, down_weight)))

    def forward(packed, params):

        def step(carry, piece):
            return (carry, jax.checkpoint(pack_forward)(params, piece))
        _, outputs = lax.scan(step, jnp.zeros((), jnp.float32), (packed, lengths, routes, gate_rows))
        return outputs
    outputs, pullback = jax.vjp(forward, inputs, weights)
    delta_inputs, delta_weights = pullback(slopes)

    def restore(packed):
        return depart(jnp.take_along_axis(packed, reverse, axis=1))
    return (restore(outputs).astype(jnp.bfloat16), restore(delta_inputs).astype(jnp.bfloat16), delta_weights[0], delta_weights[1], delta_weights[2], delta_weights[3], delta_weights[4], delta_weights[5], delta_weights[6], delta_weights[7], delta_weights[8])
```

```python
import jax
import jax.numpy as jnp
from jax import lax
from jax.sharding import PartitionSpec as P

QUERY_HEADS = 16
KEY_VALUE_HEADS = 8
HEAD_SIZE = 64


EPS = 1e-05
THETA = 10000.0


def rope_tables(place, size):
    half = size // 2
    freq = THETA ** (-2.0 * jnp.arange(half, dtype=jnp.float32) / size)
    angle = place.astype(jnp.float32)[:, None] * freq[None, :]
    return (jnp.cos(angle), jnp.sin(angle))


def rotary_apply(heads, cosine_table, sine_table):
    half = heads.shape[-1] // 2
    first = heads[..., :half]
    second = heads[..., half:]
    along = cosine_table[:, None, :]
    across = sine_table[:, None, :]
    return jnp.concatenate(
        [first * along - second * across, second * along + first * across], axis=-1
    )


def rotary_inverse(heads, cosine_table, sine_table):
    half = heads.shape[-1] // 2
    first = heads[..., :half]
    second = heads[..., half:]
    along = cosine_table[:, None, :]
    across = sine_table[:, None, :]
    return jnp.concatenate(
        [first * along + second * across, second * along - first * across], axis=-1
    )


def segment_info(lengths, group_count):
    ends = jnp.cumsum(lengths)
    starts = ends - lengths
    place = jnp.arange(group_count, dtype=jnp.int32)
    inside = ((place[:, None] >= starts[None, :]) & (place[:, None] < ends[None, :])).astype(
        jnp.int32
    )
    segment = jnp.sum(inside * jnp.arange(lengths.shape[0], dtype=jnp.int32)[None, :], axis=1)
    offset = jnp.sum(inside * starts[None, :], axis=1)
    return (segment, place - offset)


def masked_scores(query_block, key_rows, start, segment, scale):
    width = query_block.shape[0]
    scores = (
        jnp.einsum("igzd,jgd->gzij", query_block, key_rows, preferred_element_type=jnp.float32)
        * scale
    )
    rows = start + jnp.arange(width, dtype=jnp.int32)
    columns = jnp.arange(key_rows.shape[0], dtype=jnp.int32)
    allowed = (segment[:, None] == segment[None, :]) & (columns[None, :] <= rows[:, None])
    return jnp.where(allowed, scores, -1e30)


def block_starts(group_count):
    width = min(512, group_count)
    blocks = group_count // width
    return (width, blocks, jnp.arange(blocks, dtype=jnp.int32) * width)


def attend(query_rows, key_rows, value_rows, segment, scale):
    group_count = query_rows.shape[0]
    width, blocks, starts = block_starts(group_count)
    grouped = query_rows.reshape((blocks, width) + query_rows.shape[1:])

    def one_block(piece):
        query_block, start = piece
        scores = masked_scores(query_block, key_rows, start, segment, scale)
        largest = jnp.max(scores, axis=-1, keepdims=True)
        powers = jnp.exp(scores - largest)
        totals = jnp.sum(powers, axis=-1, keepdims=True)
        weights = (powers / totals).astype(jnp.bfloat16)
        mixed = jnp.einsum(
            "gzij,jgd->igzd", weights, value_rows, preferred_element_type=jnp.float32
        )
        return (mixed.astype(jnp.bfloat16), (largest + jnp.log(totals))[..., 0])

    mixed, logsum = lax.map(one_block, (grouped, starts))
    return (mixed.reshape(group_count, -1), logsum)


def attend_back(query_rows, key_rows, value_rows, segment, scale, logsum, mixed_slope):
    group_count = query_rows.shape[0]
    width, blocks, starts = block_starts(group_count)
    grouped = query_rows.reshape((blocks, width) + query_rows.shape[1:])
    slope_blocks = mixed_slope.reshape(grouped.shape)

    def one_block(piece):
        query_block, slope_block, logsum_block, start = piece
        scores = masked_scores(query_block, key_rows, start, segment, scale)
        probs = jnp.exp(scores - logsum_block[..., None])
        prob_slope = jnp.einsum(
            "igzd,jgd->gzij", slope_block, value_rows, preferred_element_type=jnp.float32
        )
        inner = jnp.sum(probs * prob_slope, axis=-1, keepdims=True)
        score_slope = (probs * (prob_slope - inner)).astype(jnp.bfloat16)
        query_slope = (
            jnp.einsum("gzij,jgd->igzd", score_slope, key_rows, preferred_element_type=jnp.float32)
            * scale
        )
        key_gradient = (
            jnp.einsum(
                "gzij,igzd->jgd", score_slope, query_block, preferred_element_type=jnp.float32
            )
            * scale
        )
        value_gradient = jnp.einsum(
            "gzij,igzd->jgd",
            probs.astype(jnp.bfloat16),
            slope_block,
            preferred_element_type=jnp.float32,
        )
        return (query_slope, key_gradient, value_gradient)

    query_slope, key_gradient, value_gradient = lax.map(
        one_block, (grouped, slope_blocks, logsum, starts)
    )
    return (
        query_slope.reshape(group_count, -1, query_rows.shape[-1]),
        jnp.sum(key_gradient, axis=0),
        jnp.sum(value_gradient, axis=0),
    )


def norm_back(inputs, scale_rows, gain, slope):
    scaled = slope * gain
    gain_slope = jnp.sum(slope * inputs * scale_rows, axis=0)
    input_slope = scale_rows * scaled - inputs * scale_rows**3 * jnp.mean(
        inputs * scaled, axis=1, keepdims=True
    )
    return (input_slope, gain_slope)


def local(
    tokens,
    cotangent,
    seq_lengths,
    pack_order,
    unpack_order,
    expert_ids,
    gates,
    first_gain,
    query_weight,
    key_matrix,
    value_matrix,
    output_weight,
    second_gain,
    gate_weight,
    up_weight,
    down_weight,
):
    shards = lax.axis_size("shard")
    me = lax.axis_index("shard")
    group_count, width = tokens.shape
    block = group_count // shards
    low = jnp.bfloat16
    full = jnp.float32
    arrived = lax.all_to_all(tokens, "shard", split_axis=0, concat_axis=0, tiled=True)
    inputs_low = arrived[pack_order]
    inputs = inputs_low.astype(full)
    query_width = query_weight.shape[1]
    key_width = key_matrix.shape[1]
    joined = lax.all_gather(
        jnp.concatenate([query_weight, key_matrix, value_matrix, output_weight], axis=1),
        "shard",
        axis=0,
        tiled=True,
    )
    full_query = joined[:, :query_width]
    full_key = joined[:, query_width : query_width + key_width]
    full_value = joined[:, query_width + key_width : query_width + 2 * key_width]
    full_output = joined[:, query_width + 2 * key_width :]
    gains = lax.all_gather(jnp.stack([first_gain, second_gain]), "shard", axis=1, tiled=True)
    gain_one = gains[0].astype(full)
    gain_two = gains[1].astype(full)
    all_slopes = lax.all_gather(cotangent, "shard", axis=0, tiled=False)
    slope_arrived = lax.dynamic_slice_in_dim(all_slopes, me * block, block, axis=1).reshape(
        group_count, width
    )
    slope_low = slope_arrived[pack_order]
    slopes = slope_low.astype(full)
    segment, place = segment_info(seq_lengths[0], group_count)
    cosine_table, sine_table = rope_tables(place, HEAD_SIZE)
    scale = HEAD_SIZE ** (-0.5)
    head_groups = QUERY_HEADS // KEY_VALUE_HEADS
    first_scale = lax.rsqrt(jnp.mean(inputs * inputs, axis=1, keepdims=True) + EPS)
    normed = (inputs * first_scale * gain_one).astype(low)
    query_projected = jnp.dot(normed, full_query, preferred_element_type=full)
    key_projected = jnp.dot(normed, full_key, preferred_element_type=full)
    value_projected = jnp.dot(normed, full_value, preferred_element_type=full)
    query_rows = (
        rotary_apply(
            query_projected.reshape(group_count, QUERY_HEADS, HEAD_SIZE), cosine_table, sine_table
        )
        .astype(low)
        .reshape(group_count, KEY_VALUE_HEADS, head_groups, HEAD_SIZE)
    )
    key_rows = rotary_apply(
        key_projected.reshape(group_count, KEY_VALUE_HEADS, HEAD_SIZE), cosine_table, sine_table
    ).astype(low)
    value_rows = value_projected.astype(low).reshape(group_count, KEY_VALUE_HEADS, HEAD_SIZE)
    mixed, logsum = attend(query_rows, key_rows, value_rows, segment, scale)
    hidden_one = inputs + jnp.dot(mixed, full_output, preferred_element_type=full)
    second_scale = lax.rsqrt(jnp.mean(hidden_one * hidden_one, axis=1, keepdims=True) + EPS)
    normed_two = (hidden_one * second_scale * gain_two).astype(low)
    local_experts = gate_weight.shape[0]
    experts = local_experts * shards
    hidden_width = gate_weight.shape[2]
    hits = expert_ids[:, :, None] == jnp.arange(experts, dtype=jnp.int32)[None, None, :]
    mixing = jnp.sum(jnp.where(hits, gates[:, :, None], 0.0), axis=1)[unpack_order]
    mixing = lax.all_to_all(mixing.T, "shard", split_axis=0, concat_axis=0, tiled=True)
    mixing = mixing.reshape(shards, local_experts, shards, block)
    mixing = mixing.transpose(1, 2, 0, 3).reshape(local_experts, shards * group_count, 1)

    def swap(rows):
        return rows.reshape(shards, shards, block, width).swapaxes(0, 1).reshape(-1, width)

    rows = swap(lax.all_gather(normed_two[unpack_order], "shard", axis=0, tiled=True))
    slope_rows = all_slopes.reshape(-1, width)
    gate_act = jnp.einsum("td,edf->etf", rows, gate_weight, preferred_element_type=full)
    up_act = jnp.einsum("td,edf->etf", rows, up_weight, preferred_element_type=full)
    sigmoid_gate = jax.nn.sigmoid(gate_act)
    silu_gate = gate_act * sigmoid_gate
    inner = (mixing * (silu_gate * up_act)).astype(low)
    inner_slope = mixing * jnp.einsum(
        "td,efd->etf", slope_rows, down_weight, preferred_element_type=full
    )
    up_slope = (inner_slope * silu_gate).astype(low)
    gate_slope = (
        inner_slope * up_act * sigmoid_gate * (1.0 + gate_act * (1.0 - sigmoid_gate))
    ).astype(low)
    delta_down = jnp.einsum("etf,td->efd", inner, slope_rows, preferred_element_type=full)
    delta_gate = jnp.einsum("td,etf->edf", rows, gate_slope, preferred_element_type=full)
    delta_up = jnp.einsum("td,etf->edf", rows, up_slope, preferred_element_type=full)
    expert_deltas = lax.psum(
        (delta_gate.astype(low), delta_up.astype(low), delta_down.astype(low)), "rep"
    )
    row_slopes = jnp.einsum("etf,edf->td", gate_slope, gate_weight, preferred_element_type=full)
    row_slopes = row_slopes + jnp.einsum(
        "etf,edf->td", up_slope, up_weight, preferred_element_type=full
    )
    back = lax.psum_scatter(
        swap(row_slopes.astype(low)), "shard", scatter_dimension=0, tiled=True
    )
    normed_two_slope = back[pack_order].astype(full)
    result = jnp.einsum("etf,efd->td", inner, down_weight, preferred_element_type=full)
    shared = lax.dynamic_update_slice_in_dim(
        jnp.zeros((shards, shards, block, width), low),
        hidden_one.astype(low)[unpack_order].reshape(shards, 1, block, width),
        me,
        axis=1,
    ).reshape(-1, width)
    out_tokens = lax.psum_scatter(
        (result + shared.astype(full)).astype(low), "shard", scatter_dimension=0, tiled=True
    )
    hidden_slope, delta_second = norm_back(hidden_one, second_scale, gain_two, normed_two_slope)
    hidden_slope = slopes + hidden_slope
    attn_slope = hidden_slope.astype(low)
    delta_output = jnp.einsum("ta,td->ad", mixed, attn_slope, preferred_element_type=full)
    mixed_slope = jnp.einsum(
        "td,ad->ta", attn_slope, full_output, preferred_element_type=full
    ).astype(low)
    query_slope, key_gradient, value_gradient = attend_back(
        query_rows, key_rows, value_rows, segment, scale, logsum, mixed_slope
    )
    query_back = (
        rotary_inverse(query_slope, cosine_table, sine_table)
        .reshape(group_count, QUERY_HEADS * HEAD_SIZE)
        .astype(low)
    )
    key_back = (
        rotary_inverse(key_gradient, cosine_table, sine_table)
        .reshape(group_count, KEY_VALUE_HEADS * HEAD_SIZE)
        .astype(low)
    )
    value_back = value_gradient.reshape(group_count, KEY_VALUE_HEADS * HEAD_SIZE).astype(low)
    backs = jnp.concatenate([query_back, key_back, value_back], axis=1)
    inputs_width = backs.shape[1]
    deltas = jnp.einsum("td,ta->da", normed, backs, preferred_element_type=full)
    normed_slope = jnp.einsum(
        "ta,da->td", backs, joined[:, :inputs_width], preferred_element_type=full
    )
    input_slope, delta_first = norm_back(inputs, first_scale, gain_one, normed_slope)
    input_slope = (hidden_slope + input_slope).astype(low)
    delta_tokens = lax.all_to_all(
        input_slope[unpack_order], "shard", split_axis=0, concat_axis=0, tiled=True
    )
    attention_deltas = lax.psum_scatter(
        jnp.concatenate([deltas.astype(low), delta_output.astype(low)], axis=1),
        "shard",
        scatter_dimension=0,
        tiled=True,
    )
    attention_deltas = lax.psum(attention_deltas, "rep").astype(full)
    gain_deltas = lax.psum(jnp.stack([delta_first, delta_second]), ("rep", "shard"))
    gain_deltas = lax.dynamic_slice_in_dim(
        gain_deltas, me * first_gain.shape[0], first_gain.shape[0], axis=1
    )
    return (
        out_tokens,
        delta_tokens,
        gain_deltas[0],
        attention_deltas[:, :query_width],
        attention_deltas[:, query_width : query_width + key_width],
        attention_deltas[:, query_width + key_width : inputs_width],
        attention_deltas[:, inputs_width:],
        gain_deltas[1],
        expert_deltas[0].astype(full),
        expert_deltas[1].astype(full),
        expert_deltas[2].astype(full),
    )


def solution(mesh):
    placed = (
        P(("rep", "shard"), None),
        P(("rep", "shard"), None),
        P(("rep", "shard"), None),
        P(("rep", "shard")),
        P(("rep", "shard")),
        P(("rep", "shard"), None),
        P(("rep", "shard"), None),
        P("shard"),
        P("shard", None),
        P("shard", None),
        P("shard", None),
        P("shard", None),
        P("shard"),
        P("shard", None, None),
        P("shard", None, None),
        P("shard", None, None),
    )
    return jax.shard_map(
        local,
        mesh=mesh,
        in_specs=placed,
        out_specs=(
            P(("rep", "shard"), None),
            P(("rep", "shard"), None),
            P("shard"),
            P("shard", None),
            P("shard", None),
            P("shard", None),
            P("shard", None),
            P("shard"),
            P("shard", None, None),
            P("shard", None, None),
            P("shard", None, None),
        ),
        check_vma=False,
    )
```

```python
import functools

import jax
import jax.numpy as jnp
from jax import lax
from jax.experimental import pallas as pl
from jax.experimental.pallas import tpu as pltpu
from jax.sharding import PartitionSpec as P

QUERY_HEADS = 16
KEY_VALUE_HEADS = 8
HEAD_SIZE = 64


EPS = 1e-05
THETA = 10000.0


def rope_tables(place, size):
    half = size // 2
    freq = THETA ** (-2.0 * jnp.arange(half, dtype=jnp.float32) / size)
    angle = place.astype(jnp.float32)[:, None] * freq[None, :]
    return (jnp.cos(angle), jnp.sin(angle))


def rotary_apply(heads, cosine_table, sine_table):
    half = heads.shape[-1] // 2
    first = heads[..., :half]
    second = heads[..., half:]
    along = cosine_table[:, None, :]
    across = sine_table[:, None, :]
    return jnp.concatenate(
        [first * along - second * across, second * along + first * across], axis=-1
    )


def rotary_inverse(heads, cosine_table, sine_table):
    half = heads.shape[-1] // 2
    first = heads[..., :half]
    second = heads[..., half:]
    along = cosine_table[:, None, :]
    across = sine_table[:, None, :]
    return jnp.concatenate(
        [first * along + second * across, second * along - first * across], axis=-1
    )


def segment_info(lengths, group_count):
    ends = jnp.cumsum(lengths)
    starts = ends - lengths
    place = jnp.arange(group_count, dtype=jnp.int32)
    inside = ((place[:, None] >= starts[None, :]) & (place[:, None] < ends[None, :])).astype(
        jnp.int32
    )
    segment = jnp.sum(inside * jnp.arange(lengths.shape[0], dtype=jnp.int32)[None, :], axis=1)
    offset = jnp.sum(inside * starts[None, :], axis=1)
    return (segment, place - offset)


def masked_scores(query_block, key_rows, start, segment, scale):
    width = query_block.shape[0]
    scores = (
        jnp.einsum("igzd,jgd->gzij", query_block, key_rows, preferred_element_type=jnp.float32)
        * scale
    )
    rows = start + jnp.arange(width, dtype=jnp.int32)
    columns = jnp.arange(key_rows.shape[0], dtype=jnp.int32)
    allowed = (segment[:, None] == segment[None, :]) & (columns[None, :] <= rows[:, None])
    return jnp.where(allowed, scores, -1e30)


def block_starts(group_count):
    width = min(512, group_count)
    blocks = group_count // width
    return (width, blocks, jnp.arange(blocks, dtype=jnp.int32) * width)


def attend(query_rows, key_rows, value_rows, segment, scale):
    group_count = query_rows.shape[0]
    width, blocks, starts = block_starts(group_count)
    grouped = query_rows.reshape((blocks, width) + query_rows.shape[1:])

    def one_block(piece):
        query_block, start = piece
        scores = masked_scores(query_block, key_rows, start, segment, scale)
        largest = jnp.max(scores, axis=-1, keepdims=True)
        powers = jnp.exp(scores - largest)
        totals = jnp.sum(powers, axis=-1, keepdims=True)
        weights = (powers / totals).astype(jnp.bfloat16)
        mixed = jnp.einsum(
            "gzij,jgd->igzd", weights, value_rows, preferred_element_type=jnp.float32
        )
        return (mixed.astype(jnp.bfloat16), (largest + jnp.log(totals))[..., 0])

    mixed, logsum = lax.map(one_block, (grouped, starts))
    return (mixed.reshape(group_count, -1), logsum)


def attend_back(query_rows, key_rows, value_rows, segment, scale, logsum, mixed_slope):
    group_count = query_rows.shape[0]
    width, blocks, starts = block_starts(group_count)
    grouped = query_rows.reshape((blocks, width) + query_rows.shape[1:])
    slope_blocks = mixed_slope.reshape(grouped.shape)

    def one_block(piece):
        query_block, slope_block, logsum_block, start = piece
        scores = masked_scores(query_block, key_rows, start, segment, scale)
        probs = jnp.exp(scores - logsum_block[..., None])
        prob_slope = jnp.einsum(
            "igzd,jgd->gzij", slope_block, value_rows, preferred_element_type=jnp.float32
        )
        inner = jnp.sum(probs * prob_slope, axis=-1, keepdims=True)
        score_slope = (probs * (prob_slope - inner)).astype(jnp.bfloat16)
        query_slope = (
            jnp.einsum("gzij,jgd->igzd", score_slope, key_rows, preferred_element_type=jnp.float32)
            * scale
        )
        key_gradient = (
            jnp.einsum(
                "gzij,igzd->jgd", score_slope, query_block, preferred_element_type=jnp.float32
            )
            * scale
        )
        value_gradient = jnp.einsum(
            "gzij,igzd->jgd",
            probs.astype(jnp.bfloat16),
            slope_block,
            preferred_element_type=jnp.float32,
        )
        return (query_slope, key_gradient, value_gradient)

    query_slope, key_gradient, value_gradient = lax.map(
        one_block, (grouped, slope_blocks, logsum, starts)
    )
    return (
        query_slope.reshape(group_count, -1, query_rows.shape[-1]),
        jnp.sum(key_gradient, axis=0),
        jnp.sum(value_gradient, axis=0),
    )


def norm_back(inputs, scale_rows, gain, slope):
    scaled = slope * gain
    gain_slope = jnp.sum(slope * inputs * scale_rows, axis=0)
    input_slope = scale_rows * scaled - inputs * scale_rows**3 * jnp.mean(
        inputs * scaled, axis=1, keepdims=True
    )
    return (input_slope, gain_slope)

MESH = pl.DeviceIdType.MESH
NN = (((1,), (0,)), ((), ()))
NT = (((1,), (1,)), ((), ()))
TN = (((0,), (0,)), ((), ()))
TILE = 256
VMEM_MOST = 66_000_000


def matmul(left, right, dims):
    return lax.dot_general(left, right, dims, preferred_element_type=jnp.float32)


def flip(number, mask, count):
    out = 0
    bit = 1
    while bit < count:
        a = (number // bit) % 2
        b = (mask // bit) % 2
        out = out + (a + b - 2 * a * b) * bit
        bit *= 2
    return out


def greet(me, rep, count):
    barrier = pltpu.get_barrier_semaphore()
    for k in range(1, count):
        pl.semaphore_signal(
            barrier, inc=1, device_id=(rep, lax.rem(me + k, count)), device_id_type=MESH
        )
    pl.semaphore_wait(barrier, count - 1)


def expert_kernel(
    count,
    own_ref,
    slope_ref,
    mix_ref,
    gate_ref,
    up_ref,
    down_ref,
    hidden_out,
    grad_out,
    delta_gate_ref,
    delta_up_ref,
    delta_down_ref,
    rows,
    slope_buf,
    hidden_buf,
    grad_buf,
    acc_gate,
    acc_up,
    acc_down,
    send_sem,
    recv_sem,
    own_sem,
    slope_sem,
    hidden_sem,
    grad_sem,
):
    rep = lax.axis_index("rep")
    me = lax.axis_index("shard")
    experts, width, hidden = gate_ref.shape
    tokens = own_ref.shape[0]
    low = jnp.bfloat16

    def remote(source, slot, index, target):
        return pltpu.make_async_remote_copy(
            src_ref=source,
            dst_ref=rows.at[slot],
            send_sem=send_sem.at[index],
            recv_sem=recv_sem.at[index],
            device_id=(rep, target),
            device_id_type=MESH,
        )

    def slope_copy(k):
        return pltpu.make_async_copy(
            slope_ref.at[:, flip(me, k, count)], slope_buf.at[k % 2], slope_sem.at[k % 2]
        )

    def hidden_copy(k):
        return pltpu.make_async_copy(
            hidden_buf.at[k % 2], hidden_out.at[flip(me, k, count)], hidden_sem.at[k % 2]
        )

    def grad_copy(k):
        return pltpu.make_async_copy(
            grad_buf.at[k % 2], grad_out.at[flip(me, k, count)], grad_sem.at[k % 2]
        )

    slope_copy(0).start()
    own = pltpu.make_async_copy(own_ref, rows.at[me], own_sem)
    own.start()
    greet(me, rep, count)
    for k in [1] + list(range(2, count, 2)):
        remote(own_ref, me, k, flip(me, k, count)).start()
    own.wait()

    def step(k, carry):
        pack = flip(me, k, count)

        @pl.when(k >= 1)
        def _():
            remote(own_ref, pack, k, me).wait_recv()

        @pl.when((k >= 2) & (k % 2 == 0))
        def _():
            remote(rows.at[pack], pack, k + 1, flip(me, 1, count)).start()

        @pl.when(k + 1 < count)
        def _():
            slope_copy(k + 1).start()

        slope_copy(k).wait()

        @pl.when(k >= 2)
        def _():
            hidden_copy(k - 2).wait()
            grad_copy(k - 2).wait()

        slot = k % 2
        x = rows[pack]
        dy = slope_buf[slot].reshape(tokens, width)
        for e in range(experts):
            mix = mix_ref[pack, :, e : e + 1]
            for part in range(hidden // TILE):
                span = pl.ds(part * TILE, TILE)
                ga = matmul(x, gate_ref[e, :, span], NN)
                ua = matmul(x, up_ref[e, :, span], NN)
                dh = matmul(dy, down_ref[e, span, :], NT) * mix
                sig = jax.nn.sigmoid(ga)
                act = ga * sig
                out = pl.ds(e * hidden + part * TILE, TILE)
                hidden_buf[slot, :, out] = (mix * (act * ua)).astype(low)
                grad_buf[slot, :, out] = (dh * ua * sig * (1.0 + ga * (1.0 - sig))).astype(low)
                grad_buf[
                    slot, :, pl.ds(experts * hidden + e * hidden + part * TILE, TILE)
                ] = (dh * act).astype(low)
        hidden_copy(k).start()
        grad_copy(k).start()

        def add(acc, value):
            @pl.when(k == 0)
            def _():
                acc[...] = value

            @pl.when(k > 0)
            def _():
                acc[...] += value

        half = experts * hidden
        add(acc_gate, matmul(x, grad_buf[slot, :, :half], TN))
        add(acc_up, matmul(x, grad_buf[slot, :, half:], TN))
        add(acc_down, matmul(hidden_buf[slot], dy, TN))
        return carry

    lax.fori_loop(0, count, step, 0)
    for e in range(experts):
        span = pl.ds(e * hidden, hidden)
        delta_gate_ref[e] = acc_gate[:, span].astype(low)
        delta_up_ref[e] = acc_up[:, span].astype(low)
        delta_down_ref[e] = acc_down[span, :].astype(low)
    for k in (count - 2, count - 1):
        hidden_copy(k).wait()
        grad_copy(k).wait()
    for k in range(1, count):
        remote(own_ref, me, k, me).wait_send()


def expert_pass(normed, all_slopes, mixing, gate_weight, up_weight, down_weight, count):
    tokens, width = normed.shape
    experts, _, hidden = gate_weight.shape
    block = tokens // count
    low = jnp.bfloat16
    anywhere = pl.BlockSpec(memory_space=pl.ANY)
    inside = pl.BlockSpec(memory_space=pltpu.VMEM)
    flops = 2 * count * tokens * width * hidden * experts * 6
    return pl.pallas_call(
        functools.partial(expert_kernel, count),
        name="expert_pass",
        out_shape=(
            jax.ShapeDtypeStruct((count, tokens, experts * hidden), low),
            jax.ShapeDtypeStruct((count, tokens, 2 * experts * hidden), low),
            jax.ShapeDtypeStruct(gate_weight.shape, low),
            jax.ShapeDtypeStruct(up_weight.shape, low),
            jax.ShapeDtypeStruct(down_weight.shape, low),
        ),
        in_specs=[inside, anywhere, inside, inside, inside, inside],
        out_specs=(anywhere, anywhere, inside, inside, inside),
        scratch_shapes=[
            pltpu.VMEM((count, tokens, width), low),
            pltpu.VMEM((2, count, block, width), low),
            pltpu.VMEM((2, tokens, experts * hidden), low),
            pltpu.VMEM((2, tokens, 2 * experts * hidden), low),
            pltpu.VMEM((width, experts * hidden), jnp.float32),
            pltpu.VMEM((width, experts * hidden), jnp.float32),
            pltpu.VMEM((experts * hidden, width), jnp.float32),
            pltpu.SemaphoreType.DMA((count,)),
            pltpu.SemaphoreType.DMA((count,)),
            pltpu.SemaphoreType.DMA,
            pltpu.SemaphoreType.DMA((2,)),
            pltpu.SemaphoreType.DMA((2,)),
            pltpu.SemaphoreType.DMA((2,)),
        ],
        compiler_params=pltpu.CompilerParams(
            collective_id=1, has_side_effects=True, vmem_limit_bytes=VMEM_MOST
        ),
        cost_estimate=pl.CostEstimate(flops=flops, bytes_accessed=1 << 26, transcendentals=0),
    )(
        normed,
        all_slopes.reshape(count, count, block, width),
        mixing,
        gate_weight,
        up_weight,
        down_weight,
    )


def return_kernel(
    count,
    grad_ref,
    hidden_ref,
    gate_ref,
    up_ref,
    down_ref,
    own_ref,
    back_ref,
    out_ref,
    grad_buf,
    hidden_buf,
    pair_send,
    far_send,
    pair_recv,
    far_recv,
    total,
    load_sem,
    pair_send_sem,
    pair_recv_sem,
    far_send_sem,
    far_recv_sem,
):
    rep = lax.axis_index("rep")
    me = lax.axis_index("shard")
    experts, width, hidden = gate_ref.shape
    tokens = own_ref.shape[0]
    block = tokens // count
    low = jnp.bfloat16
    pairs = count // 2
    partner = flip(me, 1, count)
    greet(me, rep, count)

    def reduce(phase, load, part, base):
        def pair_copy(turn):
            return pltpu.make_async_remote_copy(
                src_ref=pair_send.at[turn % 2],
                dst_ref=pair_recv.at[base + turn],
                send_sem=pair_send_sem.at[turn % 2],
                recv_sem=pair_recv_sem.at[base + turn],
                device_id=(rep, partner),
                device_id_type=MESH,
            )

        def far_copy(turn, target):
            return pltpu.make_async_remote_copy(
                src_ref=far_send.at[turn % 2],
                dst_ref=far_recv.at[base + turn],
                send_sem=far_send_sem.at[turn % 2],
                recv_sem=far_recv_sem.at[base + turn],
                device_id=(rep, target),
                device_id_type=MESH,
            )

        load(0).start()

        def turn_step(turn, carry):
            mask = count - 2 - 2 * turn
            load(2 * turn + 1).start()
            load(2 * turn).wait()
            value = part(0, flip(me, mask + 1, count))

            @pl.when(turn >= 2)
            def _():
                pair_copy(turn - 2).wait_send()

            pair_send[turn % 2] = value.astype(low)
            pair_copy(turn).start()

            @pl.when(turn + 1 < pairs)
            def _():
                load(2 * turn + 2).start()

            load(2 * turn + 1).wait()
            total[...] = part(1, flip(me, mask, count))
            pair_copy(turn).wait_recv()

            @pl.when(turn + 1 < pairs)
            def _():
                @pl.when(turn >= 2)
                def _():
                    far_copy(turn - 2, me).wait_send()

                far_send[turn % 2] = (
                    total[...] + pair_recv[base + turn].astype(jnp.float32)
                ).astype(low)
                far_copy(turn, flip(me, mask, count)).start()

            return carry

        lax.fori_loop(0, pairs, turn_step, 0)
        total[...] += pair_recv[base + pairs - 1].astype(jnp.float32)

        def finish():
            def add(turn, carry):
                far_copy(turn, me).wait_recv()
                total[...] += far_recv[base + turn].astype(jnp.float32)
                return carry

            lax.fori_loop(0, pairs - 1, add, 0)
            for turn in range(max(0, pairs - 2), pairs):
                pair_copy(turn).wait_send()
            for turn in range(max(0, pairs - 3), pairs - 1):
                far_copy(turn, me).wait_send()

        finish()

    def target(item):
        turn = item // 2
        mask = count - 2 - 2 * turn + 1 - item % 2
        return flip(me, mask, count)

    def grad_load(item):
        return pltpu.make_async_copy(
            grad_ref.at[target(item)], grad_buf.at[item % 2], load_sem.at[item % 2]
        )

    def grad_part(slot, pack):
        value = None
        for e in range(experts):
            for at, weight in ((e, gate_ref), (experts + e, up_ref)):
                term = matmul(grad_buf[slot, :, pl.ds(at * hidden, hidden)], weight[e], NT)
                value = term if value is None else value + term
        return value

    def hidden_load(item):
        return pltpu.make_async_copy(
            hidden_ref.at[:, target(item)], hidden_buf.at[item % 2], load_sem.at[item % 2]
        )

    def hidden_part(slot, pack):
        value = None
        for e in range(experts):
            term = matmul(
                hidden_buf[slot, :, :, pl.ds(e * hidden, hidden)].reshape(tokens, hidden),
                down_ref[e],
                NN,
            )
            value = term if value is None else value + term
        total[...] = value
        mine = pl.ds(pl.multiple_of(me * block, block), block)
        theirs = pl.ds(pl.multiple_of(pack * block, block), block)
        total[mine, :] += own_ref[theirs, :]
        return total[...]

    reduce(0, grad_load, grad_part, 0)
    back_ref[...] = total[...]
    reduce(1, hidden_load, hidden_part, pairs)
    out_ref[...] = total[...].astype(low)


def return_pass(grads, hiddens, gate_weight, up_weight, down_weight, own, count):
    tokens, width = own.shape
    experts, _, hidden = gate_weight.shape
    block = tokens // count
    low = jnp.bfloat16
    pairs = count // 2
    anywhere = pl.BlockSpec(memory_space=pl.ANY)
    inside = pl.BlockSpec(memory_space=pltpu.VMEM)
    flops = 2 * count * tokens * width * hidden * experts * 3
    return pl.pallas_call(
        functools.partial(return_kernel, count),
        name="return_pass",
        out_shape=(
            jax.ShapeDtypeStruct((tokens, width), jnp.float32),
            jax.ShapeDtypeStruct((tokens, width), low),
        ),
        in_specs=[anywhere, anywhere, inside, inside, inside, inside],
        out_specs=(inside, inside),
        scratch_shapes=[
            pltpu.VMEM((2, tokens, 2 * experts * hidden), low),
            pltpu.VMEM((2, count, block, experts * hidden), low),
            pltpu.VMEM((2, tokens, width), low),
            pltpu.VMEM((2, tokens, width), low),
            pltpu.VMEM((2 * pairs, tokens, width), low),
            pltpu.VMEM((2 * pairs, tokens, width), low),
            pltpu.VMEM((tokens, width), jnp.float32),
            pltpu.SemaphoreType.DMA((2,)),
            pltpu.SemaphoreType.DMA((2,)),
            pltpu.SemaphoreType.DMA((2 * pairs,)),
            pltpu.SemaphoreType.DMA((2,)),
            pltpu.SemaphoreType.DMA((2 * pairs,)),
        ],
        compiler_params=pltpu.CompilerParams(
            collective_id=2, has_side_effects=True, vmem_limit_bytes=VMEM_MOST
        ),
        cost_estimate=pl.CostEstimate(flops=flops, bytes_accessed=1 << 26, transcendentals=0),
    )(
        grads,
        hiddens.reshape(count, count, block, experts * hidden),
        gate_weight,
        up_weight,
        down_weight,
        own,
    )


def settle_kernel(
    count,
    reps,
    delta_ref,
    gain_ref,
    slope_ref,
    delta_out,
    gain_out,
    slope_out,
    pair_recv,
    far_send,
    far_recv,
    piece,
    line_recv,
    line_send,
    gain_recv,
    gain_sum,
    gain_line,
    pair_send_sem,
    pair_recv_sem,
    far_send_sem,
    far_recv_sem,
    line_send_sem,
    line_recv_sem,
    gain_send_sem,
    gain_recv_sem,
    gain_line_send,
    gain_line_recv,
    slope_send_sem,
    slope_recv_sem,
    own_sem,
):
    rep = lax.axis_index("rep")
    me = lax.axis_index("shard")
    low = jnp.bfloat16
    full = jnp.float32
    rows = piece.shape[0]
    pairs = count // 2
    partner = flip(me, 1, count)
    barrier = pltpu.get_barrier_semaphore()
    for k in range(1, count):
        pl.semaphore_signal(
            barrier, inc=1, device_id=(rep, lax.rem(me + k, count)), device_id_type=MESH
        )
    for k in range(1, reps):
        pl.semaphore_signal(
            barrier, inc=1, device_id=(lax.rem(rep + k, reps), me), device_id_type=MESH
        )
    pl.semaphore_wait(barrier, count + reps - 2)

    def copy(source, target, sends, recvs, device):
        return pltpu.make_async_remote_copy(
            src_ref=source,
            dst_ref=target,
            send_sem=sends,
            recv_sem=recvs,
            device_id=device,
            device_id_type=MESH,
        )

    def block(owner):
        return pl.ds(pl.multiple_of(owner * rows, rows), rows)

    def pair_copy(turn):
        owner = flip(partner, 2 * turn, count)
        return copy(
            delta_ref.at[block(owner)],
            pair_recv.at[turn],
            pair_send_sem.at[turn],
            pair_recv_sem.at[turn],
            (rep, partner),
        )

    def far_copy(turn):
        return copy(
            far_send.at[turn],
            far_recv.at[turn],
            far_send_sem.at[turn],
            far_recv_sem.at[turn],
            (rep, flip(me, 2 * turn, count)),
        )

    def gain_copy(k):
        target = flip(me, k, count)
        return copy(
            gain_ref.at[target],
            gain_recv.at[k],
            gain_send_sem.at[k],
            gain_recv_sem.at[k],
            (rep, target),
        )

    def slope_copy(k):
        target = flip(me, k, count)
        return copy(
            slope_ref.at[target],
            slope_out.at[me],
            slope_send_sem.at[k],
            slope_recv_sem.at[k],
            (rep, target),
        )

    def gain_line_copy(k):
        return copy(
            gain_sum,
            gain_line.at[rep],
            gain_line_send.at[k],
            gain_line_recv.at[k],
            (lax.rem(rep + k, reps), me),
        )

    order = list(range(pairs - 1, 0, -1)) + [0]
    for turn in order:
        pair_copy(turn).start()
    for k in range(1, count):
        gain_copy(k).start()
    own = pltpu.make_async_copy(slope_ref.at[me], slope_out.at[me], own_sem)
    own.start()
    for turn in order[:-1]:
        pair_copy(turn).wait_recv()
        mine = delta_ref[block(flip(me, 2 * turn, count)), :].astype(full)
        far_send[turn] = (mine + pair_recv[turn].astype(full)).astype(low)
        far_copy(turn).start()
    for k in range(count - 1, 0, -1):
        slope_copy(k).start()
    total = gain_ref[me]
    for k in range(1, count):
        gain_copy(k).wait_recv()
        total = total + gain_recv[k]
    gain_sum[...] = total
    gain_line[rep] = total
    for k in range(1, reps):
        gain_line_copy(k).start()
    pair_copy(0).wait_recv()
    for turn in range(1, pairs):
        far_copy(turn).wait_recv()

    segments = 4
    size = rows // segments

    def span(i):
        return pl.ds(i * size, size)

    for i in range(segments):
        value = delta_ref[
            pl.ds(pl.multiple_of(me * rows + i * size, size), size), :
        ].astype(full)
        for turn in range(pairs):
            source = pair_recv if turn == 0 else far_recv
            value = value + source[turn, span(i), :].astype(full)
        piece[span(i), :] = value.astype(low)

    if reps == 4:
        outer = (rep == 0) | (rep == reps - 1)
        inside = jnp.where(rep == 0, 1, 2)
        outside = jnp.where(rep == 1, 0, 3)
        across = 3 - rep

        def up_copy(i):
            return copy(
                piece.at[span(i)],
                line_recv.at[0, span(i)],
                line_send_sem.at[0, i],
                line_recv_sem.at[0, i],
                (inside, me),
            )

        def across_copy(i):
            return copy(
                line_send.at[0, span(i)],
                line_recv.at[1, span(i)],
                line_send_sem.at[1, i],
                line_recv_sem.at[1, i],
                (across, me),
            )

        def down_copy(i):
            return copy(
                line_send.at[1, span(i)],
                line_recv.at[2, span(i)],
                line_send_sem.at[2, i],
                line_recv_sem.at[2, i],
                (outside, me),
            )

        @pl.when(outer)
        def _():
            for i in range(segments):
                up_copy(i).start()
            for i in range(segments):
                down_copy(i).wait_recv()
                delta_out[span(i), :] = line_recv[2, span(i), :].astype(full)
            for i in range(segments):
                up_copy(i).wait_send()

        @pl.when(jnp.logical_not(outer))
        def _():
            for i in range(segments + 1):
                if i < segments:
                    up_copy(i).wait_recv()
                    both = piece[span(i), :].astype(full) + line_recv[0, span(i), :].astype(full)
                    line_send[0, span(i), :] = both.astype(low)
                    across_copy(i).start()
                if i > 0:
                    j = i - 1
                    across_copy(j).wait_recv()
                    every = line_send[0, span(j), :].astype(full) + line_recv[
                        1, span(j), :
                    ].astype(full)
                    line_send[1, span(j), :] = every.astype(low)
                    down_copy(j).start()
                    delta_out[span(j), :] = every.astype(low).astype(full)
            for i in range(segments):
                across_copy(i).wait_send()
                down_copy(i).wait_send()
    else:

        def spread_copy(k):
            return copy(
                piece,
                line_recv.at[rep],
                line_send_sem.at[k],
                line_recv_sem.at[k],
                (lax.rem(rep + k, reps), me),
            )

        for k in range(1, reps):
            spread_copy(k).start()
        line_recv[rep] = piece[...]
        for k in range(1, reps):
            spread_copy(k).wait_recv()
        value = line_recv[0].astype(full)
        for k in range(1, reps):
            value = value + line_recv[k].astype(full)
        delta_out[...] = value
        for k in range(1, reps):
            spread_copy(k).wait_send()

    for k in range(1, reps):
        gain_line_copy(k).wait_recv()
    total = gain_line[0]
    for k in range(1, reps):
        total = total + gain_line[k]
    gain_out[...] = total
    own.wait()
    for k in range(1, count):
        slope_copy(k).wait_recv()
    for k in range(1, count):
        slope_copy(k).wait_send()
        gain_copy(k).wait_send()
    for turn in range(pairs):
        pair_copy(turn).wait_send()
    for turn in range(1, pairs):
        far_copy(turn).wait_send()
    for k in range(1, reps):
        gain_line_copy(k).wait_send()


def settle_pass(deltas, gains, slopes, count, reps):
    width, columns = deltas.shape
    rows = width // count
    tokens = slopes.shape[0]
    pairs = count // 2
    low = jnp.bfloat16
    full = jnp.float32
    dma = pltpu.SemaphoreType.DMA
    inside = pl.BlockSpec(memory_space=pltpu.VMEM)
    line = (3, 4) if reps == 4 else (reps,)
    return pl.pallas_call(
        functools.partial(settle_kernel, count, reps),
        name="settle_pass",
        out_shape=(
            jax.ShapeDtypeStruct((rows, columns), full),
            jax.ShapeDtypeStruct((8, rows), full),
            jax.ShapeDtypeStruct((count, tokens // count, width), low),
        ),
        in_specs=[inside, inside, inside],
        out_specs=(inside, inside, inside),
        scratch_shapes=[
            pltpu.VMEM((pairs, rows, columns), low),
            pltpu.VMEM((pairs, rows, columns), low),
            pltpu.VMEM((pairs, rows, columns), low),
            pltpu.VMEM((rows, columns), low),
            pltpu.VMEM((3 if reps == 4 else reps, rows, columns), low),
            pltpu.VMEM((2, rows, columns), low),
            pltpu.VMEM((count, 8, rows), full),
            pltpu.VMEM((8, rows), full),
            pltpu.VMEM((reps, 8, rows), full),
            dma((pairs,)),
            dma((pairs,)),
            dma((pairs,)),
            dma((pairs,)),
            dma(line),
            dma(line),
            dma((count,)),
            dma((count,)),
            dma((reps,)),
            dma((reps,)),
            dma((count,)),
            dma((count,)),
            dma,
        ],
        compiler_params=pltpu.CompilerParams(
            collective_id=3, has_side_effects=True, vmem_limit_bytes=VMEM_MOST
        ),
        cost_estimate=pl.CostEstimate(flops=1 << 24, bytes_accessed=1 << 26, transcendentals=0),
    )(deltas, gains, slopes.reshape(count, tokens // count, width))


def local(
    tokens,
    cotangent,
    seq_lengths,
    pack_order,
    unpack_order,
    expert_ids,
    gates,
    first_gain,
    query_weight,
    key_matrix,
    value_matrix,
    output_weight,
    second_gain,
    gate_weight,
    up_weight,
    down_weight,
):
    shards = lax.axis_size("shard")
    me = lax.axis_index("shard")
    group_count, width = tokens.shape
    block = group_count // shards
    low = jnp.bfloat16
    full = jnp.float32
    arrived = lax.all_to_all(tokens, "shard", split_axis=0, concat_axis=0, tiled=True)
    inputs_low = arrived[pack_order]
    inputs = inputs_low.astype(full)
    query_width = query_weight.shape[1]
    key_width = key_matrix.shape[1]
    joined = lax.all_gather(
        jnp.concatenate([query_weight, key_matrix, value_matrix, output_weight], axis=1),
        "shard",
        axis=0,
        tiled=True,
    )
    full_query = joined[:, :query_width]
    full_key = joined[:, query_width : query_width + key_width]
    full_value = joined[:, query_width + key_width : query_width + 2 * key_width]
    full_output = joined[:, query_width + 2 * key_width :]
    gains = lax.all_gather(jnp.stack([first_gain, second_gain]), "shard", axis=1, tiled=True)
    gain_one = gains[0].astype(full)
    gain_two = gains[1].astype(full)
    all_slopes = lax.all_gather(cotangent, "shard", axis=0, tiled=False)
    slope_arrived = lax.dynamic_slice_in_dim(all_slopes, me * block, block, axis=1).reshape(
        group_count, width
    )
    slope_low = slope_arrived[pack_order]
    slopes = slope_low.astype(full)
    segment, place = segment_info(seq_lengths[0], group_count)
    cosine_table, sine_table = rope_tables(place, HEAD_SIZE)
    scale = HEAD_SIZE ** (-0.5)
    head_groups = QUERY_HEADS // KEY_VALUE_HEADS
    first_scale = lax.rsqrt(jnp.mean(inputs * inputs, axis=1, keepdims=True) + EPS)
    normed = (inputs * first_scale * gain_one).astype(low)
    query_projected = jnp.dot(normed, full_query, preferred_element_type=full)
    key_projected = jnp.dot(normed, full_key, preferred_element_type=full)
    value_projected = jnp.dot(normed, full_value, preferred_element_type=full)
    query_rows = (
        rotary_apply(
            query_projected.reshape(group_count, QUERY_HEADS, HEAD_SIZE), cosine_table, sine_table
        )
        .astype(low)
        .reshape(group_count, KEY_VALUE_HEADS, head_groups, HEAD_SIZE)
    )
    key_rows = rotary_apply(
        key_projected.reshape(group_count, KEY_VALUE_HEADS, HEAD_SIZE), cosine_table, sine_table
    ).astype(low)
    value_rows = value_projected.astype(low).reshape(group_count, KEY_VALUE_HEADS, HEAD_SIZE)
    mixed, logsum = attend(query_rows, key_rows, value_rows, segment, scale)
    hidden_one = inputs + jnp.dot(mixed, full_output, preferred_element_type=full)
    second_scale = lax.rsqrt(jnp.mean(hidden_one * hidden_one, axis=1, keepdims=True) + EPS)
    normed_two = (hidden_one * second_scale * gain_two).astype(low)
    local_experts = gate_weight.shape[0]
    experts = local_experts * shards
    hits = expert_ids[:, :, None] == jnp.arange(experts, dtype=jnp.int32)[None, None, :]
    mixing = jnp.sum(jnp.where(hits, gates[:, :, None], 0.0), axis=1)[unpack_order]
    mixing = lax.all_to_all(mixing.T, "shard", split_axis=0, concat_axis=0, tiled=True)
    mixing = mixing.reshape(shards, local_experts, group_count).swapaxes(1, 2)
    inner, row_slopes, delta_gate, delta_up, delta_down = expert_pass(
        normed_two[unpack_order],
        all_slopes,
        mixing,
        gate_weight,
        up_weight,
        down_weight,
        shards,
    )
    expert_deltas = lax.psum((delta_gate, delta_up, delta_down), "rep")
    back, out_tokens = return_pass(
        row_slopes,
        inner,
        gate_weight,
        up_weight,
        down_weight,
        hidden_one[unpack_order],
        shards,
    )
    normed_two_slope = back[pack_order]
    hidden_slope, delta_second = norm_back(hidden_one, second_scale, gain_two, normed_two_slope)
    hidden_slope = slopes + hidden_slope
    attn_slope = hidden_slope.astype(low)
    delta_output = jnp.einsum("ta,td->ad", mixed, attn_slope, preferred_element_type=full)
    mixed_slope = jnp.einsum(
        "td,ad->ta", attn_slope, full_output, preferred_element_type=full
    ).astype(low)
    query_slope, key_gradient, value_gradient = attend_back(
        query_rows, key_rows, value_rows, segment, scale, logsum, mixed_slope
    )
    query_back = (
        rotary_inverse(query_slope, cosine_table, sine_table)
        .reshape(group_count, QUERY_HEADS * HEAD_SIZE)
        .astype(low)
    )
    key_back = (
        rotary_inverse(key_gradient, cosine_table, sine_table)
        .reshape(group_count, KEY_VALUE_HEADS * HEAD_SIZE)
        .astype(low)
    )
    value_back = value_gradient.reshape(group_count, KEY_VALUE_HEADS * HEAD_SIZE).astype(low)
    backs = jnp.concatenate([query_back, key_back, value_back], axis=1)
    inputs_width = backs.shape[1]
    deltas = jnp.einsum("td,ta->da", normed, backs, preferred_element_type=full)
    normed_slope = jnp.einsum(
        "ta,da->td", backs, joined[:, :inputs_width], preferred_element_type=full
    )
    input_slope, delta_first = norm_back(inputs, first_scale, gain_one, normed_slope)
    input_slope = (hidden_slope + input_slope).astype(low)
    gain_rows = jnp.stack([delta_first, delta_second] + [jnp.zeros_like(delta_first)] * 6)
    attention_deltas, gain_deltas, delta_tokens = settle_pass(
        jnp.concatenate([deltas.astype(low), delta_output.astype(low)], axis=1),
        gain_rows.reshape(8, shards, -1).swapaxes(0, 1),
        input_slope[unpack_order],
        shards,
        lax.axis_size("rep"),
    )
    return (
        out_tokens,
        delta_tokens.reshape(group_count, width),
        gain_deltas[0],
        attention_deltas[:, :query_width],
        attention_deltas[:, query_width : query_width + key_width],
        attention_deltas[:, query_width + key_width : inputs_width],
        attention_deltas[:, inputs_width:],
        gain_deltas[1],
        expert_deltas[0].astype(full),
        expert_deltas[1].astype(full),
        expert_deltas[2].astype(full),
    )


def solution(mesh):
    placed = (
        P(("rep", "shard"), None),
        P(("rep", "shard"), None),
        P(("rep", "shard"), None),
        P(("rep", "shard")),
        P(("rep", "shard")),
        P(("rep", "shard"), None),
        P(("rep", "shard"), None),
        P("shard"),
        P("shard", None),
        P("shard", None),
        P("shard", None),
        P("shard", None),
        P("shard"),
        P("shard", None, None),
        P("shard", None, None),
        P("shard", None, None),
    )
    return jax.shard_map(
        local,
        mesh=mesh,
        in_specs=placed,
        out_specs=(
            P(("rep", "shard"), None),
            P(("rep", "shard"), None),
            P("shard"),
            P("shard", None),
            P("shard", None),
            P("shard", None),
            P("shard", None),
            P("shard"),
            P("shard", None, None),
            P("shard", None, None),
            P("shard", None, None),
        ),
        check_vma=False,
    )
```

```python
import functools

import jax
import jax.numpy as jnp
from jax import lax
from jax.experimental import pallas as pl
from jax.experimental.pallas import tpu as pltpu
from jax.sharding import PartitionSpec as P

QUERY_HEADS = 16
KEY_VALUE_HEADS = 8
HEAD_SIZE = 64


EPS = 1e-05
THETA = 10000.0


def rope_tables(place, size):
    half = size // 2
    freq = THETA ** (-2.0 * jnp.arange(half, dtype=jnp.float32) / size)
    angle = place.astype(jnp.float32)[:, None] * freq[None, :]
    return (jnp.cos(angle), jnp.sin(angle))


def segment_info(lengths, group_count):
    ends = jnp.cumsum(lengths)
    starts = ends - lengths
    place = jnp.arange(group_count, dtype=jnp.int32)
    inside = ((place[:, None] >= starts[None, :]) & (place[:, None] < ends[None, :])).astype(
        jnp.int32
    )
    segment = jnp.sum(inside * jnp.arange(lengths.shape[0], dtype=jnp.int32)[None, :], axis=1)
    offset = jnp.sum(inside * starts[None, :], axis=1)
    return (segment, place - offset)


MESH = pl.DeviceIdType.MESH
NN = (((1,), (0,)), ((), ()))
NT = (((1,), (1,)), ((), ()))
TN = (((0,), (0,)), ((), ()))
TILE = 256
VMEM_MOST = 66_000_000


def matmul(left, right, dims):
    return lax.dot_general(left, right, dims, preferred_element_type=jnp.float32)


def flip(number, mask, count):
    out = 0
    bit = 1
    while bit < count:
        a = (number // bit) % 2
        b = (mask // bit) % 2
        out = out + (a + b - 2 * a * b) * bit
        bit *= 2
    return out


def greet(me, rep, count):
    barrier = pltpu.get_barrier_semaphore()
    for k in range(1, count):
        pl.semaphore_signal(
            barrier, inc=1, device_id=(rep, lax.rem(me + k, count)), device_id_type=MESH
        )
    pl.semaphore_wait(barrier, count - 1)


def expert_kernel(
    count,
    own_ref,
    slope_ref,
    mix_ref,
    gate_ref,
    up_ref,
    down_ref,
    hidden_out,
    grad_out,
    delta_gate_ref,
    delta_up_ref,
    delta_down_ref,
    rows,
    slope_buf,
    hidden_buf,
    grad_buf,
    acc_gate,
    acc_up,
    acc_down,
    send_sem,
    recv_sem,
    own_sem,
    slope_sem,
    hidden_sem,
    grad_sem,
):
    rep = lax.axis_index("rep")
    me = lax.axis_index("shard")
    experts, width, hidden = gate_ref.shape
    tokens = own_ref.shape[0]
    low = jnp.bfloat16

    def remote(source, slot, index, target):
        return pltpu.make_async_remote_copy(
            src_ref=source,
            dst_ref=rows.at[slot],
            send_sem=send_sem.at[index],
            recv_sem=recv_sem.at[index],
            device_id=(rep, target),
            device_id_type=MESH,
        )

    def slope_copy(k):
        return pltpu.make_async_copy(
            slope_ref.at[:, flip(me, k, count)], slope_buf.at[k % 2], slope_sem.at[k % 2]
        )

    def hidden_copy(k):
        return pltpu.make_async_copy(
            hidden_buf.at[k % 2], hidden_out.at[flip(me, k, count)], hidden_sem.at[k % 2]
        )

    def grad_copy(k):
        return pltpu.make_async_copy(
            grad_buf.at[k % 2], grad_out.at[flip(me, k, count)], grad_sem.at[k % 2]
        )

    slope_copy(0).start()
    own = pltpu.make_async_copy(own_ref, rows.at[me], own_sem)
    own.start()
    greet(me, rep, count)
    for k in [1] + list(range(2, count, 2)):
        remote(own_ref, me, k, flip(me, k, count)).start()
    own.wait()

    def step(k, carry):
        pack = flip(me, k, count)

        @pl.when(k >= 1)
        def _():
            remote(own_ref, pack, k, me).wait_recv()

        @pl.when((k >= 2) & (k % 2 == 0))
        def _():
            remote(rows.at[pack], pack, k + 1, flip(me, 1, count)).start()

        @pl.when(k + 1 < count)
        def _():
            slope_copy(k + 1).start()

        slope_copy(k).wait()

        @pl.when(k >= 2)
        def _():
            hidden_copy(k - 2).wait()
            grad_copy(k - 2).wait()

        slot = k % 2
        x = rows[pack]
        dy = slope_buf[slot].reshape(tokens, width)
        for e in range(experts):
            mix = mix_ref[pack, :, e : e + 1]
            for part in range(hidden // TILE):
                span = pl.ds(part * TILE, TILE)
                ga = matmul(x, gate_ref[e, :, span], NN)
                ua = matmul(x, up_ref[e, :, span], NN)
                dh = matmul(dy, down_ref[e, span, :], NT) * mix
                sig = jax.nn.sigmoid(ga)
                act = ga * sig
                out = pl.ds(e * hidden + part * TILE, TILE)
                hidden_buf[slot, :, out] = (mix * (act * ua)).astype(low)
                grad_buf[slot, :, out] = (dh * ua * sig * (1.0 + ga * (1.0 - sig))).astype(low)
                grad_buf[
                    slot, :, pl.ds(experts * hidden + e * hidden + part * TILE, TILE)
                ] = (dh * act).astype(low)
        hidden_copy(k).start()
        grad_copy(k).start()

        def add(acc, value):
            @pl.when(k == 0)
            def _():
                acc[...] = value

            @pl.when(k > 0)
            def _():
                acc[...] += value

        half = experts * hidden
        add(acc_gate, matmul(x, grad_buf[slot, :, :half], TN))
        add(acc_up, matmul(x, grad_buf[slot, :, half:], TN))
        add(acc_down, matmul(hidden_buf[slot], dy, TN))
        return carry

    lax.fori_loop(0, count, step, 0)
    for e in range(experts):
        span = pl.ds(e * hidden, hidden)
        delta_gate_ref[e] = acc_gate[:, span].astype(low)
        delta_up_ref[e] = acc_up[:, span].astype(low)
        delta_down_ref[e] = acc_down[span, :].astype(low)
    for k in (count - 2, count - 1):
        hidden_copy(k).wait()
        grad_copy(k).wait()
    for k in range(1, count):
        remote(own_ref, me, k, me).wait_send()


def expert_pass(normed, all_slopes, mixing, gate_weight, up_weight, down_weight, count):
    tokens, width = normed.shape
    experts, _, hidden = gate_weight.shape
    block = tokens // count
    low = jnp.bfloat16
    anywhere = pl.BlockSpec(memory_space=pl.ANY)
    inside = pl.BlockSpec(memory_space=pltpu.VMEM)
    flops = 2 * count * tokens * width * hidden * experts * 6
    return pl.pallas_call(
        functools.partial(expert_kernel, count),
        name="expert_pass",
        out_shape=(
            jax.ShapeDtypeStruct((count, tokens, experts * hidden), low),
            jax.ShapeDtypeStruct((count, tokens, 2 * experts * hidden), low),
            jax.ShapeDtypeStruct(gate_weight.shape, low),
            jax.ShapeDtypeStruct(up_weight.shape, low),
            jax.ShapeDtypeStruct(down_weight.shape, low),
        ),
        in_specs=[inside, anywhere, inside, inside, inside, inside],
        out_specs=(anywhere, anywhere, inside, inside, inside),
        scratch_shapes=[
            pltpu.VMEM((count, tokens, width), low),
            pltpu.VMEM((2, count, block, width), low),
            pltpu.VMEM((2, tokens, experts * hidden), low),
            pltpu.VMEM((2, tokens, 2 * experts * hidden), low),
            pltpu.VMEM((width, experts * hidden), jnp.float32),
            pltpu.VMEM((width, experts * hidden), jnp.float32),
            pltpu.VMEM((experts * hidden, width), jnp.float32),
            pltpu.SemaphoreType.DMA((count,)),
            pltpu.SemaphoreType.DMA((count,)),
            pltpu.SemaphoreType.DMA,
            pltpu.SemaphoreType.DMA((2,)),
            pltpu.SemaphoreType.DMA((2,)),
            pltpu.SemaphoreType.DMA((2,)),
        ],
        compiler_params=pltpu.CompilerParams(
            collective_id=1, has_side_effects=True, vmem_limit_bytes=VMEM_MOST
        ),
        cost_estimate=pl.CostEstimate(flops=flops, bytes_accessed=1 << 26, transcendentals=0),
    )(
        normed,
        all_slopes.reshape(count, count, block, width),
        mixing,
        gate_weight,
        up_weight,
        down_weight,
    )


def return_kernel(
    count,
    grad_ref,
    hidden_ref,
    gate_ref,
    up_ref,
    down_ref,
    own_ref,
    back_ref,
    out_ref,
    grad_buf,
    hidden_buf,
    pair_send,
    far_send,
    pair_recv,
    far_recv,
    total,
    load_sem,
    pair_send_sem,
    pair_recv_sem,
    far_send_sem,
    far_recv_sem,
):
    rep = lax.axis_index("rep")
    me = lax.axis_index("shard")
    experts, width, hidden = gate_ref.shape
    tokens = own_ref.shape[0]
    block = tokens // count
    low = jnp.bfloat16
    pairs = count // 2
    partner = flip(me, 1, count)
    greet(me, rep, count)

    def reduce(phase, load, part, base):
        def pair_copy(turn):
            return pltpu.make_async_remote_copy(
                src_ref=pair_send.at[turn % 2],
                dst_ref=pair_recv.at[base + turn],
                send_sem=pair_send_sem.at[turn % 2],
                recv_sem=pair_recv_sem.at[base + turn],
                device_id=(rep, partner),
                device_id_type=MESH,
            )

        def far_copy(turn, target):
            return pltpu.make_async_remote_copy(
                src_ref=far_send.at[turn % 2],
                dst_ref=far_recv.at[base + turn],
                send_sem=far_send_sem.at[turn % 2],
                recv_sem=far_recv_sem.at[base + turn],
                device_id=(rep, target),
                device_id_type=MESH,
            )

        load(0).start()

        def turn_step(turn, carry):
            mask = count - 2 - 2 * turn
            load(2 * turn + 1).start()
            load(2 * turn).wait()
            value = part(0, flip(me, mask + 1, count))

            @pl.when(turn >= 2)
            def _():
                pair_copy(turn - 2).wait_send()

            pair_send[turn % 2] = value.astype(low)
            pair_copy(turn).start()

            @pl.when(turn + 1 < pairs)
            def _():
                load(2 * turn + 2).start()

            load(2 * turn + 1).wait()
            total[...] = part(1, flip(me, mask, count))
            pair_copy(turn).wait_recv()

            @pl.when(turn + 1 < pairs)
            def _():
                @pl.when(turn >= 2)
                def _():
                    far_copy(turn - 2, me).wait_send()

                far_send[turn % 2] = (
                    total[...] + pair_recv[base + turn].astype(jnp.float32)
                ).astype(low)
                far_copy(turn, flip(me, mask, count)).start()

            return carry

        lax.fori_loop(0, pairs, turn_step, 0)
        total[...] += pair_recv[base + pairs - 1].astype(jnp.float32)

        def finish():
            def add(turn, carry):
                far_copy(turn, me).wait_recv()
                total[...] += far_recv[base + turn].astype(jnp.float32)
                return carry

            lax.fori_loop(0, pairs - 1, add, 0)
            for turn in range(max(0, pairs - 2), pairs):
                pair_copy(turn).wait_send()
            for turn in range(max(0, pairs - 3), pairs - 1):
                far_copy(turn, me).wait_send()

        finish()

    def target(item):
        turn = item // 2
        mask = count - 2 - 2 * turn + 1 - item % 2
        return flip(me, mask, count)

    def grad_load(item):
        return pltpu.make_async_copy(
            grad_ref.at[target(item)], grad_buf.at[item % 2], load_sem.at[item % 2]
        )

    def grad_part(slot, pack):
        value = None
        for e in range(experts):
            for at, weight in ((e, gate_ref), (experts + e, up_ref)):
                term = matmul(grad_buf[slot, :, pl.ds(at * hidden, hidden)], weight[e], NT)
                value = term if value is None else value + term
        return value

    def hidden_load(item):
        return pltpu.make_async_copy(
            hidden_ref.at[:, target(item)], hidden_buf.at[item % 2], load_sem.at[item % 2]
        )

    def hidden_part(slot, pack):
        value = None
        for e in range(experts):
            term = matmul(
                hidden_buf[slot, :, :, pl.ds(e * hidden, hidden)].reshape(tokens, hidden),
                down_ref[e],
                NN,
            )
            value = term if value is None else value + term
        total[...] = value
        mine = pl.ds(pl.multiple_of(me * block, block), block)
        theirs = pl.ds(pl.multiple_of(pack * block, block), block)
        total[mine, :] += own_ref[theirs, :].astype(jnp.float32)
        return total[...]

    reduce(0, grad_load, grad_part, 0)
    back_ref[...] = total[...]
    reduce(1, hidden_load, hidden_part, pairs)
    out_ref[...] = total[...].astype(low)


def return_pass(grads, hiddens, gate_weight, up_weight, down_weight, own, count):
    tokens, width = own.shape
    experts, _, hidden = gate_weight.shape
    block = tokens // count
    low = jnp.bfloat16
    pairs = count // 2
    anywhere = pl.BlockSpec(memory_space=pl.ANY)
    inside = pl.BlockSpec(memory_space=pltpu.VMEM)
    flops = 2 * count * tokens * width * hidden * experts * 3
    return pl.pallas_call(
        functools.partial(return_kernel, count),
        name="return_pass",
        out_shape=(
            jax.ShapeDtypeStruct((tokens, width), jnp.float32),
            jax.ShapeDtypeStruct((tokens, width), low),
        ),
        in_specs=[anywhere, anywhere, inside, inside, inside, inside],
        out_specs=(inside, inside),
        scratch_shapes=[
            pltpu.VMEM((2, tokens, 2 * experts * hidden), low),
            pltpu.VMEM((2, count, block, experts * hidden), low),
            pltpu.VMEM((2, tokens, width), low),
            pltpu.VMEM((2, tokens, width), low),
            pltpu.VMEM((2 * pairs, tokens, width), low),
            pltpu.VMEM((2 * pairs, tokens, width), low),
            pltpu.VMEM((tokens, width), jnp.float32),
            pltpu.SemaphoreType.DMA((2,)),
            pltpu.SemaphoreType.DMA((2,)),
            pltpu.SemaphoreType.DMA((2 * pairs,)),
            pltpu.SemaphoreType.DMA((2,)),
            pltpu.SemaphoreType.DMA((2 * pairs,)),
        ],
        compiler_params=pltpu.CompilerParams(
            collective_id=2, has_side_effects=True, vmem_limit_bytes=VMEM_MOST
        ),
        cost_estimate=pl.CostEstimate(flops=flops, bytes_accessed=1 << 26, transcendentals=0),
    )(
        grads,
        hiddens.reshape(count, count, block, experts * hidden),
        gate_weight,
        up_weight,
        down_weight,
        own,
    )


def settle_kernel(
    count,
    reps,
    delta_ref,
    gain_ref,
    slope_ref,
    delta_out,
    gain_out,
    slope_out,
    pair_recv,
    far_send,
    far_recv,
    piece,
    line_recv,
    line_send,
    gain_recv,
    gain_sum,
    gain_line,
    pair_send_sem,
    pair_recv_sem,
    far_send_sem,
    far_recv_sem,
    line_send_sem,
    line_recv_sem,
    gain_send_sem,
    gain_recv_sem,
    gain_line_send,
    gain_line_recv,
    slope_send_sem,
    slope_recv_sem,
    own_sem,
):
    rep = lax.axis_index("rep")
    me = lax.axis_index("shard")
    low = jnp.bfloat16
    full = jnp.float32
    rows = piece.shape[0]
    pairs = count // 2
    partner = flip(me, 1, count)
    barrier = pltpu.get_barrier_semaphore()
    for k in range(1, count):
        pl.semaphore_signal(
            barrier, inc=1, device_id=(rep, lax.rem(me + k, count)), device_id_type=MESH
        )
    for k in range(1, reps):
        pl.semaphore_signal(
            barrier, inc=1, device_id=(lax.rem(rep + k, reps), me), device_id_type=MESH
        )
    pl.semaphore_wait(barrier, count + reps - 2)

    def copy(source, target, sends, recvs, device):
        return pltpu.make_async_remote_copy(
            src_ref=source,
            dst_ref=target,
            send_sem=sends,
            recv_sem=recvs,
            device_id=device,
            device_id_type=MESH,
        )

    def block(owner):
        return pl.ds(pl.multiple_of(owner * rows, rows), rows)

    def pair_copy(turn):
        owner = flip(partner, 2 * turn, count)
        return copy(
            delta_ref.at[block(owner)],
            pair_recv.at[turn],
            pair_send_sem.at[turn],
            pair_recv_sem.at[turn],
            (rep, partner),
        )

    def far_copy(turn):
        return copy(
            far_send.at[turn],
            far_recv.at[turn],
            far_send_sem.at[turn],
            far_recv_sem.at[turn],
            (rep, flip(me, 2 * turn, count)),
        )

    def gain_copy(k):
        target = flip(me, k, count)
        return copy(
            gain_ref.at[target],
            gain_recv.at[k],
            gain_send_sem.at[k],
            gain_recv_sem.at[k],
            (rep, target),
        )

    def slope_copy(k):
        target = flip(me, k, count)
        return copy(
            slope_ref.at[target],
            slope_out.at[me],
            slope_send_sem.at[k],
            slope_recv_sem.at[k],
            (rep, target),
        )

    def gain_line_copy(k):
        return copy(
            gain_sum,
            gain_line.at[rep],
            gain_line_send.at[k],
            gain_line_recv.at[k],
            (lax.rem(rep + k, reps), me),
        )

    order = list(range(pairs - 1, 0, -1)) + [0]
    for turn in order:
        pair_copy(turn).start()
    for k in range(1, count):
        gain_copy(k).start()
    own = pltpu.make_async_copy(slope_ref.at[me], slope_out.at[me], own_sem)
    own.start()
    for turn in order[:-1]:
        pair_copy(turn).wait_recv()
        mine = delta_ref[block(flip(me, 2 * turn, count)), :].astype(full)
        far_send[turn] = (mine + pair_recv[turn].astype(full)).astype(low)
        far_copy(turn).start()
    for k in range(count - 1, 0, -1):
        slope_copy(k).start()
    total = gain_ref[me]
    for k in range(1, count):
        gain_copy(k).wait_recv()
        total = total + gain_recv[k]
    gain_sum[...] = total
    gain_line[rep] = total
    for k in range(1, reps):
        gain_line_copy(k).start()
    pair_copy(0).wait_recv()
    for turn in range(1, pairs):
        far_copy(turn).wait_recv()

    segments = 4
    size = rows // segments

    def span(i):
        return pl.ds(i * size, size)

    for i in range(segments):
        value = delta_ref[
            pl.ds(pl.multiple_of(me * rows + i * size, size), size), :
        ].astype(full)
        for turn in range(pairs):
            source = pair_recv if turn == 0 else far_recv
            value = value + source[turn, span(i), :].astype(full)
        piece[span(i), :] = value.astype(low)

    if reps == 4:
        outer = (rep == 0) | (rep == reps - 1)
        inside = jnp.where(rep == 0, 1, 2)
        outside = jnp.where(rep == 1, 0, 3)
        across = 3 - rep

        def up_copy(i):
            return copy(
                piece.at[span(i)],
                line_recv.at[0, span(i)],
                line_send_sem.at[0, i],
                line_recv_sem.at[0, i],
                (inside, me),
            )

        def across_copy(i):
            return copy(
                line_send.at[0, span(i)],
                line_recv.at[1, span(i)],
                line_send_sem.at[1, i],
                line_recv_sem.at[1, i],
                (across, me),
            )

        def down_copy(i):
            return copy(
                line_send.at[1, span(i)],
                line_recv.at[2, span(i)],
                line_send_sem.at[2, i],
                line_recv_sem.at[2, i],
                (outside, me),
            )

        @pl.when(outer)
        def _():
            for i in range(segments):
                up_copy(i).start()
            for i in range(segments):
                down_copy(i).wait_recv()
                delta_out[span(i), :] = line_recv[2, span(i), :].astype(full)
            for i in range(segments):
                up_copy(i).wait_send()

        @pl.when(jnp.logical_not(outer))
        def _():
            for i in range(segments + 1):
                if i < segments:
                    up_copy(i).wait_recv()
                    both = piece[span(i), :].astype(full) + line_recv[0, span(i), :].astype(full)
                    line_send[0, span(i), :] = both.astype(low)
                    across_copy(i).start()
                if i > 0:
                    j = i - 1
                    across_copy(j).wait_recv()
                    every = line_send[0, span(j), :].astype(full) + line_recv[
                        1, span(j), :
                    ].astype(full)
                    line_send[1, span(j), :] = every.astype(low)
                    down_copy(j).start()
                    delta_out[span(j), :] = every.astype(low).astype(full)
            for i in range(segments):
                across_copy(i).wait_send()
                down_copy(i).wait_send()
    else:

        def spread_copy(k):
            return copy(
                piece,
                line_recv.at[rep],
                line_send_sem.at[k],
                line_recv_sem.at[k],
                (lax.rem(rep + k, reps), me),
            )

        for k in range(1, reps):
            spread_copy(k).start()
        line_recv[rep] = piece[...]
        for k in range(1, reps):
            spread_copy(k).wait_recv()
        value = line_recv[0].astype(full)
        for k in range(1, reps):
            value = value + line_recv[k].astype(full)
        delta_out[...] = value
        for k in range(1, reps):
            spread_copy(k).wait_send()

    for k in range(1, reps):
        gain_line_copy(k).wait_recv()
    total = gain_line[0]
    for k in range(1, reps):
        total = total + gain_line[k]
    gain_out[...] = total
    own.wait()
    for k in range(1, count):
        slope_copy(k).wait_recv()
    for k in range(1, count):
        slope_copy(k).wait_send()
        gain_copy(k).wait_send()
    for turn in range(pairs):
        pair_copy(turn).wait_send()
    for turn in range(1, pairs):
        far_copy(turn).wait_send()
    for k in range(1, reps):
        gain_line_copy(k).wait_send()


def settle_pass(deltas, gains, slopes, count, reps):
    width, columns = deltas.shape
    rows = width // count
    tokens = slopes.shape[0]
    pairs = count // 2
    low = jnp.bfloat16
    full = jnp.float32
    dma = pltpu.SemaphoreType.DMA
    inside = pl.BlockSpec(memory_space=pltpu.VMEM)
    line = (3, 4) if reps == 4 else (reps,)
    return pl.pallas_call(
        functools.partial(settle_kernel, count, reps),
        name="settle_pass",
        out_shape=(
            jax.ShapeDtypeStruct((rows, columns), full),
            jax.ShapeDtypeStruct((8, rows), full),
            jax.ShapeDtypeStruct((count, tokens // count, width), low),
        ),
        in_specs=[inside, inside, inside],
        out_specs=(inside, inside, inside),
        scratch_shapes=[
            pltpu.VMEM((pairs, rows, columns), low),
            pltpu.VMEM((pairs, rows, columns), low),
            pltpu.VMEM((pairs, rows, columns), low),
            pltpu.VMEM((rows, columns), low),
            pltpu.VMEM((3 if reps == 4 else reps, rows, columns), low),
            pltpu.VMEM((2, rows, columns), low),
            pltpu.VMEM((count, 8, rows), full),
            pltpu.VMEM((8, rows), full),
            pltpu.VMEM((reps, 8, rows), full),
            dma((pairs,)),
            dma((pairs,)),
            dma((pairs,)),
            dma((pairs,)),
            dma(line),
            dma(line),
            dma((count,)),
            dma((count,)),
            dma((reps,)),
            dma((reps,)),
            dma((count,)),
            dma((count,)),
            dma,
        ],
        compiler_params=pltpu.CompilerParams(
            collective_id=3, has_side_effects=True, vmem_limit_bytes=VMEM_MOST
        ),
        cost_estimate=pl.CostEstimate(flops=1 << 24, bytes_accessed=1 << 26, transcendentals=0),
    )(deltas, gains, slopes.reshape(count, tokens // count, width))


def turn_pairs(rows, along, across, sign):
    lane = lax.broadcasted_iota(jnp.int32, (rows.shape[0], 128), 1)
    early = (lane % HEAD_SIZE) < HEAD_SIZE // 2
    pieces = []
    for at in range(0, rows.shape[1], 128):
        part = rows[:, at : at + 128]
        other = jnp.where(
            early,
            pltpu.roll(part, 128 - HEAD_SIZE // 2, 1),
            pltpu.roll(part, HEAD_SIZE // 2, 1),
        )
        pieces.append(part * along + sign * (other * across))
    return pieces[0] if len(pieces) == 1 else jnp.concatenate(pieces, axis=1)


def permutation(order_ref):
    tokens = order_ref.shape[0]
    columns = lax.broadcasted_iota(jnp.int32, (tokens, tokens), 1)
    return jnp.where(order_ref[...] == columns, 1.0, 0.0).astype(jnp.bfloat16)


def fill_bias(bias, row_ref, column_ref):
    tokens = bias.shape[0]
    keys = lax.broadcasted_iota(jnp.int32, (tokens, tokens), 0)
    queries = lax.broadcasted_iota(jnp.int32, (tokens, tokens), 1)
    allowed = (column_ref[...] == row_ref[...]) & (keys <= queries)
    bias[...] = jnp.where(allowed, 0.0, -1e30)


def query_spans(tokens):
    half = tokens // 2
    return ((0, half, half), (half, half, tokens))


def attention_kernel(
    arrived_ref,
    order_ref,
    row_ref,
    column_ref,
    along_ref,
    across_ref,
    weight_ref,
    gain_ref,
    input_out,
    query_out,
    key_out,
    value_out,
    mixed_out,
    logsum_out,
    hidden_out,
    normed_out,
    shared_out,
    place,
    bias,
    normed,
):
    low = jnp.bfloat16
    full = jnp.float32
    tokens, width = arrived_ref.shape
    key_width = key_out.shape[1]
    place[...] = permutation(order_ref)
    inputs = matmul(place[...], arrived_ref[...], NN)
    input_out[...] = inputs.astype(low)
    scale = lax.rsqrt(jnp.mean(inputs * inputs, axis=1, keepdims=True) + EPS)
    normed[...] = (inputs * scale * gain_ref[0:1, :]).astype(low)
    fill_bias(bias, row_ref, column_ref)
    along = along_ref[...]
    across = across_ref[...]
    for at in range(0, width, 512):
        part = matmul(normed[...], weight_ref[:, at : at + 512], NN)
        query_out[:, at : at + 512] = turn_pairs(part, along, across, 1.0).astype(low)
    part = matmul(normed[...], weight_ref[:, width : width + key_width], NN)
    key_out[...] = turn_pairs(part, along, across, 1.0).astype(low)
    part = matmul(normed[...], weight_ref[:, width + key_width : width + 2 * key_width], NN)
    value_out[...] = part.astype(low)

    def heads(g, carry):
        kv = pl.ds(pl.multiple_of(g * 128, 128), 128)
        qs = pl.ds(pl.multiple_of(g * 256, 256), 256)
        keys = key_out[:, kv]
        values = value_out[:, kv]
        queries = query_out[:, qs] * jnp.bfloat16(HEAD_SIZE**-0.5)
        for start, size, reach in query_spans(tokens):
            pieces = []
            for h in range(4):
                a = (h // 2) * HEAD_SIZE
                score = matmul(
                    keys[:reach, a : a + HEAD_SIZE],
                    queries[start : start + size, h * HEAD_SIZE : (h + 1) * HEAD_SIZE],
                    NT,
                )
                score = score + bias[:reach, start : start + size]
                largest = jnp.max(score, axis=0, keepdims=True)
                powers = jnp.exp(score - largest)
                totals = jnp.sum(powers, axis=0, keepdims=True)
                weights = (powers * (1.0 / totals)).astype(low)
                pieces.append(matmul(weights, values[:reach, a : a + HEAD_SIZE], TN))
                logsum_out[g, h : h + 1, start : start + size] = largest + jnp.log(totals)
            mixed_out[start : start + size, qs] = jnp.concatenate(pieces, axis=1).astype(low)
        return carry

    lax.fori_loop(0, key_width // 128, heads, 0)
    hidden = input_out[...].astype(full) + matmul(
        mixed_out[...], weight_ref[:, width + 2 * key_width :], NN
    )
    hidden_out[...] = hidden
    scale = lax.rsqrt(jnp.mean(hidden * hidden, axis=1, keepdims=True) + EPS)
    normed[...] = (hidden * scale * gain_ref[1:2, :]).astype(low)
    normed_out[...] = matmul(place[...], normed[...], TN).astype(low)
    shared_out[...] = matmul(place[...], hidden_out[...].astype(low), TN).astype(low)


def attention_pass(arrived, order, row, column, along, across, weights, gains):
    tokens, width = arrived.shape
    key_width = (weights.shape[1] - 2 * width) // 2
    low = jnp.bfloat16
    full = jnp.float32
    inside = pl.BlockSpec(memory_space=pltpu.VMEM)
    shape = jax.ShapeDtypeStruct
    return pl.pallas_call(
        attention_kernel,
        name="attention_pass",
        out_shape=(
            shape((tokens, width), low),
            shape((tokens, width), low),
            shape((tokens, key_width), low),
            shape((tokens, key_width), low),
            shape((tokens, width), low),
            shape((key_width // 128, 4, tokens), full),
            shape((tokens, width), full),
            shape((tokens, width), low),
            shape((tokens, width), low),
        ),
        in_specs=[inside] * 8,
        out_specs=(inside,) * 9,
        scratch_shapes=[
            pltpu.VMEM((tokens, tokens), low),
            pltpu.VMEM((tokens, tokens), full),
            pltpu.VMEM((tokens, width), low),
        ],
        compiler_params=pltpu.CompilerParams(vmem_limit_bytes=VMEM_MOST),
        cost_estimate=pl.CostEstimate(
            flops=12 << 30, bytes_accessed=1 << 24, transcendentals=1 << 22
        ),
    )(arrived, order, row, column, along, across, weights, gains)


def slope_kernel(
    back_ref,
    arrived_ref,
    order_ref,
    row_ref,
    column_ref,
    along_ref,
    across_ref,
    weight_ref,
    gain_ref,
    input_ref,
    query_ref,
    key_ref,
    value_ref,
    mixed_ref,
    logsum_ref,
    hidden_ref,
    delta_out,
    gain_out,
    slope_out,
    place,
    bias,
    normed,
    steep,
    mixed_slope,
    backs,
):
    low = jnp.bfloat16
    full = jnp.float32
    tokens, width = back_ref.shape
    key_width = key_ref.shape[1]
    place[...] = permutation(order_ref)
    fill_bias(bias, row_ref, column_ref)
    high = back_ref[...].astype(low)
    rest = (back_ref[...] - high.astype(full)).astype(low)
    slope = matmul(place[...], high, NN) + matmul(place[...], rest, NN)
    hidden = hidden_ref[...]
    scale = lax.rsqrt(jnp.mean(hidden * hidden, axis=1, keepdims=True) + EPS)
    scaled = slope * gain_ref[1:2, :]
    gain_out[1:2, :] = jnp.sum(slope * hidden * scale, axis=0, keepdims=True)
    steep[...] = (
        matmul(place[...], arrived_ref[...], NN)
        + scale * scaled
        - hidden * (scale * scale * scale) * jnp.mean(hidden * scaled, axis=1, keepdims=True)
    )
    sharp = steep[...].astype(low)
    joined = width + 2 * key_width
    for at in range(0, width, 512):
        delta_out[:, joined + at : joined + at + 512] = matmul(
            mixed_ref[...], sharp[:, at : at + 512], TN
        ).astype(low)
    mixed_slope[...] = matmul(sharp, weight_ref[:, joined:], NT).astype(low)
    along = along_ref[...]
    across = across_ref[...]

    def heads(g, carry):
        kv = pl.ds(pl.multiple_of(g * 128, 128), 128)
        qs = pl.ds(pl.multiple_of(g * 256, 256), 256)
        keys = key_ref[:, kv]
        values = value_ref[:, kv]
        queries = query_ref[:, qs] * jnp.bfloat16(HEAD_SIZE**-0.5)
        slopes = mixed_slope[:, qs]
        key_parts = []
        value_parts = []
        query_parts = [[], []]
        for a in range(2):
            key_h = keys[:, a * HEAD_SIZE : (a + 1) * HEAD_SIZE]
            value_h = values[:, a * HEAD_SIZE : (a + 1) * HEAD_SIZE]
            key_slope = [None, None]
            value_slope = [None, None]
            for b in range(2):
                h = 2 * a + b
                columns = slice(h * HEAD_SIZE, (h + 1) * HEAD_SIZE)
                for i, (start, size, reach) in enumerate(query_spans(tokens)):
                    q = queries[start : start + size, columns]
                    d = slopes[start : start + size, columns]
                    score = matmul(key_h[:reach], q, NT) + bias[:reach, start : start + size]
                    probs = jnp.exp(score - logsum_ref[g, h : h + 1, start : start + size])
                    prob_slope = matmul(value_h[:reach], d, NT)
                    inner = jnp.sum(probs * prob_slope, axis=0, keepdims=True)
                    score_slope = (probs * (prob_slope - inner)).astype(low)
                    term = matmul(probs.astype(low), d, NN)
                    value_slope[i] = term if b == 0 else value_slope[i] + term
                    term = matmul(score_slope, q, NN)
                    key_slope[i] = term if b == 0 else key_slope[i] + term
                    query_parts[i].append(matmul(score_slope, key_h[:reach], TN))
            half = tokens // 2
            key_parts.append(
                jnp.concatenate([key_slope[0] + key_slope[1][:half], key_slope[1][half:]], axis=0)
            )
            value_parts.append(
                jnp.concatenate(
                    [value_slope[0] + value_slope[1][:half], value_slope[1][half:]], axis=0
                )
            )
        for i, (start, size, reach) in enumerate(query_spans(tokens)):
            rows = slice(start, start + size)
            part = jnp.concatenate(query_parts[i], axis=1) * HEAD_SIZE**-0.5
            backs[rows, qs] = turn_pairs(part, along[rows], across[rows], -1.0).astype(low)
        part = jnp.concatenate(key_parts, axis=1)
        spot = pl.ds(pl.multiple_of(width + g * 128, 128), 128)
        backs[:, spot] = turn_pairs(part, along, across, -1.0).astype(low)
        part = jnp.concatenate(value_parts, axis=1)
        spot = pl.ds(pl.multiple_of(width + key_width + g * 128, 128), 128)
        backs[:, spot] = part.astype(low)
        return carry

    lax.fori_loop(0, key_width // 128, heads, 0)
    inputs = input_ref[...].astype(full)
    scale = lax.rsqrt(jnp.mean(inputs * inputs, axis=1, keepdims=True) + EPS)
    normed[...] = (inputs * scale * gain_ref[0:1, :]).astype(low)
    for at in range(0, joined, 512):
        delta_out[:, at : at + 512] = matmul(normed[...], backs[:, at : at + 512], TN).astype(low)
    slope = matmul(backs[...], weight_ref[:, :joined], NT)
    scaled = slope * gain_ref[0:1, :]
    gain_out[0:1, :] = jnp.sum(slope * inputs * scale, axis=0, keepdims=True)
    result = (
        steep[...]
        + scale * scaled
        - inputs * (scale * scale * scale) * jnp.mean(inputs * scaled, axis=1, keepdims=True)
    )
    slope_out[...] = matmul(place[...], result.astype(low), TN).astype(low)
    gain_out[2:8, :] = jnp.zeros((6, width), full)


def slope_pass(
    back,
    arrived,
    order,
    row,
    column,
    along,
    across,
    weights,
    gains,
    inputs,
    queries,
    keys,
    values,
    mixed,
    logsum,
    hidden,
):
    tokens, width = back.shape
    key_width = keys.shape[1]
    low = jnp.bfloat16
    full = jnp.float32
    inside = pl.BlockSpec(memory_space=pltpu.VMEM)
    shape = jax.ShapeDtypeStruct
    return pl.pallas_call(
        slope_kernel,
        name="slope_pass",
        out_shape=(
            shape(weights.shape, low),
            shape((8, width), full),
            shape((tokens, width), low),
        ),
        in_specs=[inside] * 16,
        out_specs=(inside,) * 3,
        scratch_shapes=[
            pltpu.VMEM((tokens, tokens), low),
            pltpu.VMEM((tokens, tokens), full),
            pltpu.VMEM((tokens, width), low),
            pltpu.VMEM((tokens, width), full),
            pltpu.VMEM((tokens, width), low),
            pltpu.VMEM((tokens, width + 2 * key_width), low),
        ],
        compiler_params=pltpu.CompilerParams(vmem_limit_bytes=VMEM_MOST),
        cost_estimate=pl.CostEstimate(
            flops=24 << 30, bytes_accessed=1 << 24, transcendentals=1 << 22
        ),
    )(
        back,
        arrived,
        order,
        row,
        column,
        along,
        across,
        weights,
        gains,
        inputs,
        queries,
        keys,
        values,
        mixed,
        logsum,
        hidden,
    )


def local(
    tokens,
    cotangent,
    seq_lengths,
    pack_order,
    unpack_order,
    expert_ids,
    gates,
    first_gain,
    query_weight,
    key_matrix,
    value_matrix,
    output_weight,
    second_gain,
    gate_weight,
    up_weight,
    down_weight,
):
    shards = lax.axis_size("shard")
    me = lax.axis_index("shard")
    group_count, width = tokens.shape
    block = group_count // shards
    full = jnp.float32
    arrived = lax.all_to_all(tokens, "shard", split_axis=0, concat_axis=0, tiled=True)
    query_width = query_weight.shape[1]
    key_width = key_matrix.shape[1]
    inputs_width = query_width + 2 * key_width
    joined = lax.all_gather(
        jnp.concatenate([query_weight, key_matrix, value_matrix, output_weight], axis=1),
        "shard",
        axis=0,
        tiled=True,
    )
    gains = lax.all_gather(jnp.stack([first_gain, second_gain]), "shard", axis=1, tiled=True)
    gains = gains.astype(full)
    all_slopes = lax.all_gather(cotangent, "shard", axis=0, tiled=False)
    slope_arrived = lax.dynamic_slice_in_dim(all_slopes, me * block, block, axis=1).reshape(
        group_count, width
    )
    segment, place = segment_info(seq_lengths[0], group_count)
    cosine_table, sine_table = rope_tables(place, HEAD_SIZE)
    along = jnp.concatenate([cosine_table] * 4, axis=1)
    across = jnp.concatenate([-sine_table, sine_table] * 2, axis=1)
    order = pack_order[:, None]
    local_experts = gate_weight.shape[0]
    experts = local_experts * shards
    hits = expert_ids[:, :, None] == jnp.arange(experts, dtype=jnp.int32)[None, None, :]
    mixing = jnp.sum(jnp.where(hits, gates[:, :, None], 0.0), axis=1)[unpack_order]
    mixing = lax.all_to_all(mixing.T, "shard", split_axis=0, concat_axis=0, tiled=True)
    mixing = mixing.reshape(shards, local_experts, group_count).swapaxes(1, 2)
    tables = (order, segment[None, :], segment[:, None], along, across, joined, gains)
    inputs, queries, keys, values, mixed, logsum, hidden, normed, shared = attention_pass(
        arrived, *tables
    )
    inner, row_slopes, delta_gate, delta_up, delta_down = expert_pass(
        normed, all_slopes, mixing, gate_weight, up_weight, down_weight, shards
    )
    expert_deltas = lax.psum((delta_gate, delta_up, delta_down), "rep")
    back, out_tokens = return_pass(
        row_slopes, inner, gate_weight, up_weight, down_weight, shared, shards
    )
    deltas, gain_rows, slope_rows = slope_pass(
        back, slope_arrived, *tables, inputs, queries, keys, values, mixed, logsum, hidden
    )
    attention_deltas, gain_deltas, delta_tokens = settle_pass(
        deltas,
        gain_rows.reshape(8, shards, -1).swapaxes(0, 1),
        slope_rows,
        shards,
        lax.axis_size("rep"),
    )
    return (
        out_tokens,
        delta_tokens.reshape(group_count, width),
        gain_deltas[0],
        attention_deltas[:, :query_width],
        attention_deltas[:, query_width : query_width + key_width],
        attention_deltas[:, query_width + key_width : inputs_width],
        attention_deltas[:, inputs_width:],
        gain_deltas[1],
        expert_deltas[0].astype(full),
        expert_deltas[1].astype(full),
        expert_deltas[2].astype(full),
    )


def solution(mesh):
    placed = (
        P(("rep", "shard"), None),
        P(("rep", "shard"), None),
        P(("rep", "shard"), None),
        P(("rep", "shard")),
        P(("rep", "shard")),
        P(("rep", "shard"), None),
        P(("rep", "shard"), None),
        P("shard"),
        P("shard", None),
        P("shard", None),
        P("shard", None),
        P("shard", None),
        P("shard"),
        P("shard", None, None),
        P("shard", None, None),
        P("shard", None, None),
    )
    return jax.shard_map(
        local,
        mesh=mesh,
        in_specs=placed,
        out_specs=(
            P(("rep", "shard"), None),
            P(("rep", "shard"), None),
            P("shard"),
            P("shard", None),
            P("shard", None),
            P("shard", None),
            P("shard", None),
            P("shard"),
            P("shard", None, None),
            P("shard", None, None),
            P("shard", None, None),
        ),
        check_vma=False,
    )
```

```python
import functools

import jax
import jax.numpy as jnp
from jax import lax
from jax.experimental import pallas as pl
from jax.experimental.pallas import tpu as pltpu
from jax.sharding import PartitionSpec as P

QUERY_HEADS = 16
KEY_VALUE_HEADS = 8
HEAD_SIZE = 64


EPS = 1e-05
THETA = 10000.0


def rope_tables(place, size):
    half = size // 2
    freq = THETA ** (-2.0 * jnp.arange(half, dtype=jnp.float32) / size)
    angle = place.astype(jnp.float32)[:, None] * freq[None, :]
    return (jnp.cos(angle), jnp.sin(angle))


def segment_info(lengths, group_count):
    ends = jnp.cumsum(lengths)
    starts = ends - lengths
    place = jnp.arange(group_count, dtype=jnp.int32)
    inside = ((place[:, None] >= starts[None, :]) & (place[:, None] < ends[None, :])).astype(
        jnp.int32
    )
    segment = jnp.sum(inside * jnp.arange(lengths.shape[0], dtype=jnp.int32)[None, :], axis=1)
    offset = jnp.sum(inside * starts[None, :], axis=1)
    return (segment, place - offset)


MESH = pl.DeviceIdType.MESH
NN = (((1,), (0,)), ((), ()))
NT = (((1,), (1,)), ((), ()))
TN = (((0,), (0,)), ((), ()))
TILE = 256
VMEM_MOST = 66_000_000


def matmul(left, right, dims):
    return lax.dot_general(left, right, dims, preferred_element_type=jnp.float32)


def flip(number, mask, count):
    out = 0
    bit = 1
    while bit < count:
        a = (number // bit) % 2
        b = (mask // bit) % 2
        out = out + (a + b - 2 * a * b) * bit
        bit *= 2
    return out


def greet(me, rep, count, reps=1):
    barrier = pltpu.get_barrier_semaphore()
    for k in range(1, count):
        pl.semaphore_signal(
            barrier, inc=1, device_id=(rep, lax.rem(me + k, count)), device_id_type=MESH
        )
    for k in range(1, reps):
        pl.semaphore_signal(
            barrier, inc=1, device_id=(lax.rem(rep + k, reps), me), device_id_type=MESH
        )
    pl.semaphore_wait(barrier, count + reps - 2)


LINE = 4
LAG = 3


class Line:
    def __init__(self, rep, me, source, out, first, second, both, sends, recvs):
        self.rep, self.me = rep, me
        self.source, self.out = source, out
        self.first, self.second, self.both = first, second, both
        self.sends, self.recvs = sends, recvs
        self.count = source.shape[0]
        self.outer = (rep == 0) | (rep == LINE - 1)
        self.inner = jnp.logical_not(self.outer)
        self.inside = jnp.where(rep == 0, 1, 2)
        self.outside = jnp.where(rep == 1, 0, 3)
        self.across = LINE - 1 - rep

    def copy(self, stage, i):
        source = (self.source, self.both, self.first)[stage].at[i]
        target = (self.first, self.second, self.first)[stage].at[i]
        device = (self.inside, self.across, self.outside)[stage]
        return pltpu.make_async_remote_copy(
            src_ref=source,
            dst_ref=target,
            send_sem=self.sends.at[stage, i],
            recv_sem=self.recvs.at[stage, i],
            device_id=(device, self.me),
            device_id_type=MESH,
        )

    def loop(self, body):
        def step(i, carry):
            body(i)
            return carry

        lax.fori_loop(0, self.count, step, 0)

    def start(self):
        @pl.when(self.outer)
        def _():
            self.loop(lambda i: self.copy(0, i).start())

    def tick(self, j):
        full = jnp.float32

        @pl.when(self.inner & (j >= 0) & (j < self.count))
        def _():
            self.copy(0, j).wait_recv()
            both = self.source[j].astype(full) + self.first[j].astype(full)
            self.both[j] = both.astype(jnp.bfloat16)
            self.copy(1, j).start()

        i = j - LAG

        @pl.when(self.inner & (i >= 0) & (i < self.count))
        def _():
            self.copy(1, i).wait_recv()
            every = self.both[i].astype(full) + self.second[i].astype(full)
            every = every.astype(jnp.bfloat16)
            self.first[i] = every
            self.copy(2, i).start()
            self.out[i] = every.astype(full)

    def ticks(self, begin, end):
        def step(j, carry):
            self.tick(j)
            return carry

        lax.fori_loop(begin, end, step, 0)

    def finish(self):
        @pl.when(self.outer)
        def _():
            def receive(i):
                self.copy(2, i).wait_recv()
                self.out[i] = self.first[i].astype(jnp.float32)

            self.loop(receive)
            self.loop(lambda i: self.copy(0, i).wait_send())

        @pl.when(self.inner)
        def _():
            self.loop(lambda i: self.copy(1, i).wait_send())
            self.loop(lambda i: self.copy(2, i).wait_send())


def line_scratch(shape):
    low = jnp.bfloat16
    dma = pltpu.SemaphoreType.DMA
    return [
        pltpu.VMEM(shape, low),
        pltpu.VMEM(shape, low),
        pltpu.VMEM(shape, low),
        dma((3, shape[0])),
        dma((3, shape[0])),
    ]


SEGMENTS = 16


def expert_kernel(
    count,
    own_ref,
    slope_ref,
    mix_ref,
    gate_ref,
    up_ref,
    down_ref,
    hidden_out,
    grad_out,
    delta_gate_ref,
    delta_up_ref,
    delta_down_ref,
    rows,
    slope_buf,
    hidden_buf,
    grad_buf,
    acc_gate,
    acc_up,
    acc_down,
    send_sem,
    recv_sem,
    own_sem,
    slope_sem,
    hidden_sem,
    grad_sem,
):
    rep = lax.axis_index("rep")
    me = lax.axis_index("shard")
    experts, width, hidden = gate_ref.shape
    tokens = own_ref.shape[0]
    low = jnp.bfloat16

    def row_copy(source, slot, index, target):
        return pltpu.make_async_remote_copy(
            src_ref=source,
            dst_ref=rows.at[slot],
            send_sem=send_sem.at[index],
            recv_sem=recv_sem.at[index],
            device_id=(rep, target),
            device_id_type=MESH,
        )

    def slope_copy(k):
        return pltpu.make_async_copy(
            slope_ref.at[:, flip(me, k, count)], slope_buf.at[k % 2], slope_sem.at[k % 2]
        )

    def hidden_copy(k):
        return pltpu.make_async_copy(
            hidden_buf.at[k % 2], hidden_out.at[flip(me, k, count)], hidden_sem.at[k % 2]
        )

    def grad_copy(k):
        return pltpu.make_async_copy(
            grad_buf.at[k % 2], grad_out.at[flip(me, k, count)], grad_sem.at[k % 2]
        )

    slope_copy(0).start()
    own = pltpu.make_async_copy(own_ref, rows.at[me], own_sem)
    own.start()
    greet(me, rep, count)
    for k in [1] + list(range(2, count, 2)):
        row_copy(own_ref, me, k, flip(me, k, count)).start()
    own.wait()

    def step(k, carry):
        pack = flip(me, k, count)

        @pl.when(k >= 1)
        def _():
            row_copy(own_ref, pack, k, me).wait_recv()

        @pl.when((k >= 2) & (k % 2 == 0))
        def _():
            row_copy(rows.at[pack], pack, k + 1, flip(me, 1, count)).start()

        @pl.when(k + 1 < count)
        def _():
            slope_copy(k + 1).start()

        slope_copy(k).wait()

        @pl.when(k >= 2)
        def _():
            hidden_copy(k - 2).wait()
            grad_copy(k - 2).wait()

        slot = k % 2
        x = rows[pack]
        dy = slope_buf[slot].reshape(tokens, width)
        mixes = jnp.transpose(mix_ref[pack])
        for e in range(experts):
            mix = mixes[:, e : e + 1]
            for part in range(hidden // TILE):
                span = pl.ds(part * TILE, TILE)
                ga = matmul(x, gate_ref[e, :, span], NN)
                ua = matmul(x, up_ref[e, :, span], NN)
                dh = matmul(dy, down_ref[e, span, :], NT) * mix
                sig = jax.nn.sigmoid(ga)
                act = ga * sig
                out = pl.ds(e * hidden + part * TILE, TILE)
                hidden_buf[slot, :, out] = (mix * (act * ua)).astype(low)
                grad_buf[slot, :, out] = (dh * ua * sig * (1.0 + ga * (1.0 - sig))).astype(low)
                grad_buf[
                    slot, :, pl.ds(experts * hidden + e * hidden + part * TILE, TILE)
                ] = (dh * act).astype(low)
        hidden_copy(k).start()
        grad_copy(k).start()

        def add(acc, value):
            @pl.when(k == 0)
            def _():
                acc[...] = value

            @pl.when(k > 0)
            def _():
                acc[...] += value

        half = experts * hidden
        add(acc_gate, matmul(x, grad_buf[slot, :, :half], TN))
        add(acc_up, matmul(x, grad_buf[slot, :, half:], TN))
        add(acc_down, matmul(hidden_buf[slot], dy, TN))
        return carry

    lax.fori_loop(0, count, step, 0)
    for e in range(experts):
        span = pl.ds(e * hidden, hidden)
        delta_gate_ref[e] = acc_gate[:, span].astype(low)
        delta_up_ref[e] = acc_up[:, span].astype(low)
        delta_down_ref[e] = acc_down[span, :].astype(low)
    for k in (count - 2, count - 1):
        hidden_copy(k).wait()
        grad_copy(k).wait()
    for k in range(1, count):
        row_copy(own_ref, me, k, me).wait_send()


def expert_pass(normed, all_slopes, mixing, gate_weight, up_weight, down_weight, count):
    tokens, width = normed.shape
    experts, _, hidden = gate_weight.shape
    block = tokens // count
    low = jnp.bfloat16
    anywhere = pl.BlockSpec(memory_space=pl.ANY)
    inside = pl.BlockSpec(memory_space=pltpu.VMEM)
    flops = 2 * count * tokens * width * hidden * experts * 6
    return pl.pallas_call(
        functools.partial(expert_kernel, count),
        name="expert_pass",
        out_shape=(
            jax.ShapeDtypeStruct((count, tokens, experts * hidden), low),
            jax.ShapeDtypeStruct((count, tokens, 2 * experts * hidden), low),
            jax.ShapeDtypeStruct(gate_weight.shape, low),
            jax.ShapeDtypeStruct(up_weight.shape, low),
            jax.ShapeDtypeStruct(down_weight.shape, low),
        ),
        in_specs=[inside, anywhere, inside, inside, inside, inside],
        out_specs=(anywhere, anywhere, inside, inside, inside),
        scratch_shapes=[
            pltpu.VMEM((count, tokens, width), low),
            pltpu.VMEM((2, count, block, width), low),
            pltpu.VMEM((2, tokens, experts * hidden), low),
            pltpu.VMEM((2, tokens, 2 * experts * hidden), low),
            pltpu.VMEM((width, experts * hidden), jnp.float32),
            pltpu.VMEM((width, experts * hidden), jnp.float32),
            pltpu.VMEM((experts * hidden, width), jnp.float32),
            pltpu.SemaphoreType.DMA((count,)),
            pltpu.SemaphoreType.DMA((count,)),
            pltpu.SemaphoreType.DMA,
            pltpu.SemaphoreType.DMA((2,)),
            pltpu.SemaphoreType.DMA((2,)),
            pltpu.SemaphoreType.DMA((2,)),
        ],
        compiler_params=pltpu.CompilerParams(
            collective_id=1, has_side_effects=True, vmem_limit_bytes=VMEM_MOST
        ),
        cost_estimate=pl.CostEstimate(flops=flops, bytes_accessed=1 << 26, transcendentals=0),
    )(
        normed,
        all_slopes.reshape(count, count, block, width),
        mixing,
        gate_weight,
        up_weight,
        down_weight,
    )


def return_kernel(count, reps, *refs):
    (
        grad_ref,
        hidden_ref,
        gate_ref,
        up_ref,
        down_ref,
        own_ref,
    ) = refs[:6]
    lined = reps == LINE
    refs = refs[6:]
    if lined:
        line_ref, back_ref, piece_out, line_out = refs[:4]
        refs = refs[4:]
    else:
        back_ref, piece_out = refs[:2]
        refs = refs[2:]
    (
        grad_buf,
        hidden_buf,
        pair_send,
        far_send,
        pair_recv,
        far_recv,
        total,
        piece,
        load_sem,
        pair_send_sem,
        pair_recv_sem,
        far_send_sem,
        far_recv_sem,
        piece_sem,
    ) = refs[:14]
    rep = lax.axis_index("rep")
    me = lax.axis_index("shard")
    experts, width, hidden = gate_ref.shape
    tokens = own_ref.shape[0]
    block = tokens // count
    low = jnp.bfloat16
    full = jnp.float32
    pairs = count // 2
    partner = flip(me, 1, count)
    line = Line(rep, me, line_ref, line_out, *refs[14:]) if lined else None

    def target(item):
        turn = item // 2
        mask = count - 2 - 2 * turn + 1 - item % 2
        return flip(me, mask, count)

    def grad_load(item):
        return pltpu.make_async_copy(
            grad_ref.at[target(item)], grad_buf.at[item % 2], load_sem.at[item % 2]
        )

    def grad_part(slot, pack):
        value = None
        for e in range(experts):
            for at, weight in ((e, gate_ref), (experts + e, up_ref)):
                term = matmul(grad_buf[slot, :, pl.ds(at * hidden, hidden)], weight[e], NT)
                value = term if value is None else value + term
        return value

    def hidden_load(item):
        return pltpu.make_async_copy(
            hidden_ref.at[:, target(item)], hidden_buf.at[item % 2], load_sem.at[item % 2]
        )

    def hidden_part(slot, pack):
        value = None
        for e in range(experts):
            term = matmul(
                hidden_buf[slot, :, :, pl.ds(e * hidden, hidden)].reshape(tokens, hidden),
                down_ref[e],
                NN,
            )
            value = term if value is None else value + term
        total[...] = value
        mine = pl.ds(pl.multiple_of(me * block, block), block)
        theirs = pl.ds(pl.multiple_of(pack * block, block), block)
        total[mine, :] += own_ref[theirs, :].astype(full)
        return total[...]

    def pair_copy(base, turn):
        return remote(
            pair_send.at[turn % 2],
            pair_recv.at[base + turn],
            pair_send_sem,
            pair_recv_sem,
            base + turn,
            (rep, partner),
        )

    def far_copy(turn, device):
        return remote(
            far_send.at[turn % 2], far_recv.at[turn], far_send_sem, far_recv_sem, turn, (rep, device)
        )

    def piece_copy(turn):
        return pltpu.make_async_copy(
            piece.at[turn % 2], piece_out.at[turn], piece_sem.at[turn % 2]
        )

    grad_load(0).start()
    greet(me, rep, count, reps if lined else 1)
    if lined:
        line.start()

    def sweep(base, load, part, combine, tick):
        def turn_step(turn, carry):
            mask = count - 2 - 2 * turn
            load(2 * turn + 1).start()
            load(2 * turn).wait()
            value = part(0, flip(me, mask + 1, count))

            @pl.when(turn >= 2)
            def _():
                pair_copy(base, turn - 2).wait_send()

            pair_send[turn % 2] = value.astype(low)
            pair_copy(base, turn).start()

            @pl.when(turn + 1 < pairs)
            def _():
                load(2 * turn + 2).start()

            tick(2 * turn)
            load(2 * turn + 1).wait()
            total[...] = part(1, flip(me, mask, count))
            pair_copy(base, turn).wait_recv()
            combine(turn, mask)
            tick(2 * turn + 1)
            return carry

        lax.fori_loop(0, pairs, turn_step, 0)
        for turn in range(max(0, pairs - 2), pairs):
            pair_copy(base, turn).wait_send()

    def grad_combine(turn, mask):
        @pl.when(turn + 1 < pairs)
        def _():
            @pl.when(turn >= 2)
            def _():
                far_copy(turn - 2, me).wait_send()

            far_send[turn % 2] = (total[...] + pair_recv[turn].astype(full)).astype(low)
            far_copy(turn, flip(me, mask, count)).start()

    def hidden_combine(turn, mask):
        @pl.when(turn >= 2)
        def _():
            piece_copy(turn - 2).wait()

        piece[turn % 2] = (total[...] + pair_recv[pairs + turn].astype(full)).astype(low)
        piece_copy(turn).start()

    def early(j):
        if lined:
            line.tick(j - 1)

    def late(j):
        if lined:
            line.tick(2 * pairs + j - 1)

    sweep(0, grad_load, grad_part, grad_combine, early)
    back_ref[...] = total[...] + pair_recv[pairs - 1].astype(full)
    hidden_load(0).start()
    sweep(pairs, hidden_load, hidden_part, hidden_combine, late)
    if lined:
        line.ticks(4 * pairs - 1, SEGMENTS + LAG)

    def add(turn, carry):
        far_copy(turn, me).wait_recv()
        back_ref[...] += far_recv[turn].astype(full)
        return carry

    lax.fori_loop(0, pairs - 1, add, 0)
    for turn in range(max(0, pairs - 3), pairs - 1):
        far_copy(turn, me).wait_send()
    for turn in range(max(0, pairs - 2), pairs):
        piece_copy(turn).wait()
    if lined:
        line.finish()


def return_pass(grads, hiddens, gate_weight, up_weight, down_weight, own, deltas, count, reps):
    tokens, width = own.shape
    experts, _, hidden = gate_weight.shape
    block = tokens // count
    low = jnp.bfloat16
    full = jnp.float32
    pairs = count // 2
    dma = pltpu.SemaphoreType.DMA
    shape = jax.ShapeDtypeStruct
    anywhere = pl.BlockSpec(memory_space=pl.ANY)
    inside = pl.BlockSpec(memory_space=pltpu.VMEM)
    flops = 2 * count * tokens * width * hidden * experts * 3
    lined = reps == LINE
    extra = [deltas] if lined else []
    return pl.pallas_call(
        functools.partial(return_kernel, count, reps),
        name="return_pass",
        out_shape=(
            shape((tokens, width), full),
            shape((pairs, tokens, width), low),
        )
        + tuple(shape(d.shape, full) for d in extra),
        in_specs=[anywhere, anywhere] + [inside] * (4 + len(extra)),
        out_specs=(inside, anywhere) + (inside,) * len(extra),
        scratch_shapes=[
            pltpu.VMEM((2, tokens, 2 * experts * hidden), low),
            pltpu.VMEM((2, count, block, experts * hidden), low),
            pltpu.VMEM((2, tokens, width), low),
            pltpu.VMEM((2, tokens, width), low),
            pltpu.VMEM((2 * pairs, tokens, width), low),
            pltpu.VMEM((pairs, tokens, width), low),
            pltpu.VMEM((tokens, width), full),
            pltpu.VMEM((2, tokens, width), low),
            dma((2,)),
            dma((2 * pairs,)),
            dma((2 * pairs,)),
            dma((pairs,)),
            dma((pairs,)),
            dma((2,)),
        ]
        + (line_scratch(deltas.shape) if lined else []),
        compiler_params=pltpu.CompilerParams(
            collective_id=2, has_side_effects=True, vmem_limit_bytes=VMEM_MOST
        ),
        cost_estimate=pl.CostEstimate(flops=flops, bytes_accessed=1 << 26, transcendentals=0),
    )(
        grads,
        hiddens.reshape(count, count, block, experts * hidden),
        gate_weight,
        up_weight,
        down_weight,
        own,
        *extra,
    )


def settle_kernel(count, reps, *refs):
    lined = reps == LINE
    delta_ref, gain_ref, slope_ref = refs[:3]
    refs = refs[3:]
    if lined:
        line_ref = refs[0]
        refs = refs[1:]
    delta_out, gain_out, slope_out = refs[:3]
    refs = refs[3:]
    if lined:
        line_out = refs[0]
        refs = refs[1:]
    (
        pair_recv,
        far_send,
        far_recv,
        piece,
        line_recv,
        line_send,
        gain_recv,
        gain_sum,
        gain_line,
        pair_send_sem,
        pair_recv_sem,
        far_send_sem,
        far_recv_sem,
        line_send_sem,
        line_recv_sem,
        gain_send_sem,
        gain_recv_sem,
        gain_line_send,
        gain_line_recv,
        slope_send_sem,
        slope_recv_sem,
        own_sem,
    ) = refs[:22]
    rep = lax.axis_index("rep")
    me = lax.axis_index("shard")
    low = jnp.bfloat16
    full = jnp.float32
    rows = piece.shape[0]
    pairs = count // 2
    partner = flip(me, 1, count)
    greet(me, rep, count, reps)
    line = Line(rep, me, line_ref, line_out, *refs[22:]) if lined else None
    if lined:
        line.start()

    def copy(source, target, sends, recvs, device):
        return pltpu.make_async_remote_copy(
            src_ref=source,
            dst_ref=target,
            send_sem=sends,
            recv_sem=recvs,
            device_id=device,
            device_id_type=MESH,
        )

    def block(owner):
        return pl.ds(pl.multiple_of(owner * rows, rows), rows)

    def pair_copy(turn):
        owner = flip(partner, 2 * turn, count)
        return copy(
            delta_ref.at[block(owner)],
            pair_recv.at[turn],
            pair_send_sem.at[turn],
            pair_recv_sem.at[turn],
            (rep, partner),
        )

    def far_copy(turn):
        return copy(
            far_send.at[turn],
            far_recv.at[turn],
            far_send_sem.at[turn],
            far_recv_sem.at[turn],
            (rep, flip(me, 2 * turn, count)),
        )

    def gain_copy(k):
        target = flip(me, k, count)
        return copy(
            gain_ref.at[target],
            gain_recv.at[k],
            gain_send_sem.at[k],
            gain_recv_sem.at[k],
            (rep, target),
        )

    def slope_copy(k):
        target = flip(me, k, count)
        return copy(
            slope_ref.at[target],
            slope_out.at[me],
            slope_send_sem.at[k],
            slope_recv_sem.at[k],
            (rep, target),
        )

    def gain_line_copy(k):
        return copy(
            gain_sum,
            gain_line.at[rep],
            gain_line_send.at[k],
            gain_line_recv.at[k],
            (lax.rem(rep + k, reps), me),
        )

    order = list(range(pairs - 1, 0, -1)) + [0]
    for turn in order:
        pair_copy(turn).start()
    for k in range(1, count):
        gain_copy(k).start()
    own = pltpu.make_async_copy(slope_ref.at[me], slope_out.at[me], own_sem)
    own.start()
    for step, turn in enumerate(order[:-1]):
        if lined:
            line.ticks(2 * step, 2 * step + 2)
        pair_copy(turn).wait_recv()
        mine = delta_ref[block(flip(me, 2 * turn, count)), :].astype(full)
        far_send[turn] = (mine + pair_recv[turn].astype(full)).astype(low)
        far_copy(turn).start()
    for k in range(count - 1, 0, -1):
        slope_copy(k).start()
    total = gain_ref[me]
    for k in range(1, count):
        gain_copy(k).wait_recv()
        total = total + gain_recv[k]
    gain_sum[...] = total
    gain_line[rep] = total
    for k in range(1, reps):
        gain_line_copy(k).start()
    pair_copy(0).wait_recv()
    if lined:
        line.ticks(2 * pairs - 2, SEGMENTS + LAG)
    for turn in range(1, pairs):
        far_copy(turn).wait_recv()

    segments = 4
    size = rows // segments

    def span(i):
        return pl.ds(i * size, size)

    for i in range(segments):
        value = delta_ref[
            pl.ds(pl.multiple_of(me * rows + i * size, size), size), :
        ].astype(full)
        for turn in range(pairs):
            source = pair_recv if turn == 0 else far_recv
            value = value + source[turn, span(i), :].astype(full)
        piece[span(i), :] = value.astype(low)

    if reps == 4:
        outer = (rep == 0) | (rep == reps - 1)
        inside = jnp.where(rep == 0, 1, 2)
        outside = jnp.where(rep == 1, 0, 3)
        across = 3 - rep

        def up_copy(i):
            return copy(
                piece.at[span(i)],
                line_recv.at[0, span(i)],
                line_send_sem.at[0, i],
                line_recv_sem.at[0, i],
                (inside, me),
            )

        def across_copy(i):
            return copy(
                line_send.at[0, span(i)],
                line_recv.at[1, span(i)],
                line_send_sem.at[1, i],
                line_recv_sem.at[1, i],
                (across, me),
            )

        def down_copy(i):
            return copy(
                line_send.at[1, span(i)],
                line_recv.at[2, span(i)],
                line_send_sem.at[2, i],
                line_recv_sem.at[2, i],
                (outside, me),
            )

        @pl.when(outer)
        def _():
            for i in range(segments):
                up_copy(i).start()
            for i in range(segments):
                down_copy(i).wait_recv()
                delta_out[span(i), :] = line_recv[2, span(i), :].astype(full)
            for i in range(segments):
                up_copy(i).wait_send()

        @pl.when(jnp.logical_not(outer))
        def _():
            for i in range(segments + 1):
                if i < segments:
                    up_copy(i).wait_recv()
                    both = piece[span(i), :].astype(full) + line_recv[0, span(i), :].astype(full)
                    line_send[0, span(i), :] = both.astype(low)
                    across_copy(i).start()
                if i > 0:
                    j = i - 1
                    across_copy(j).wait_recv()
                    every = line_send[0, span(j), :].astype(full) + line_recv[
                        1, span(j), :
                    ].astype(full)
                    line_send[1, span(j), :] = every.astype(low)
                    down_copy(j).start()
                    delta_out[span(j), :] = every.astype(low).astype(full)
            for i in range(segments):
                across_copy(i).wait_send()
                down_copy(i).wait_send()
    else:

        def spread_copy(k):
            return copy(
                piece,
                line_recv.at[rep],
                line_send_sem.at[k],
                line_recv_sem.at[k],
                (lax.rem(rep + k, reps), me),
            )

        for k in range(1, reps):
            spread_copy(k).start()
        line_recv[rep] = piece[...]
        for k in range(1, reps):
            spread_copy(k).wait_recv()
        value = line_recv[0].astype(full)
        for k in range(1, reps):
            value = value + line_recv[k].astype(full)
        delta_out[...] = value
        for k in range(1, reps):
            spread_copy(k).wait_send()

    for k in range(1, reps):
        gain_line_copy(k).wait_recv()
    total = gain_line[0]
    for k in range(1, reps):
        total = total + gain_line[k]
    gain_out[...] = total
    own.wait()
    for k in range(1, count):
        slope_copy(k).wait_recv()
    for k in range(1, count):
        slope_copy(k).wait_send()
        gain_copy(k).wait_send()
    for turn in range(pairs):
        pair_copy(turn).wait_send()
    for turn in range(1, pairs):
        far_copy(turn).wait_send()
    for k in range(1, reps):
        gain_line_copy(k).wait_send()
    if lined:
        line.finish()


def settle_pass(deltas, gains, slopes, extra, count, reps):
    width, columns = deltas.shape
    rows = width // count
    tokens = slopes.shape[0]
    pairs = count // 2
    low = jnp.bfloat16
    full = jnp.float32
    dma = pltpu.SemaphoreType.DMA
    inside = pl.BlockSpec(memory_space=pltpu.VMEM)
    line = (3, 4) if reps == 4 else (reps,)
    extra = [extra] if reps == LINE else []
    return pl.pallas_call(
        functools.partial(settle_kernel, count, reps),
        name="settle_pass",
        out_shape=(
            jax.ShapeDtypeStruct((rows, columns), full),
            jax.ShapeDtypeStruct((8, rows), full),
            jax.ShapeDtypeStruct((count, tokens // count, width), low),
        )
        + tuple(jax.ShapeDtypeStruct(d.shape, full) for d in extra),
        in_specs=[inside] * (3 + len(extra)),
        out_specs=(inside,) * (3 + len(extra)),
        scratch_shapes=[
            pltpu.VMEM((pairs, rows, columns), low),
            pltpu.VMEM((pairs, rows, columns), low),
            pltpu.VMEM((pairs, rows, columns), low),
            pltpu.VMEM((rows, columns), low),
            pltpu.VMEM((3 if reps == 4 else reps, rows, columns), low),
            pltpu.VMEM((2, rows, columns), low),
            pltpu.VMEM((count, 8, rows), full),
            pltpu.VMEM((8, rows), full),
            pltpu.VMEM((reps, 8, rows), full),
            dma((pairs,)),
            dma((pairs,)),
            dma((pairs,)),
            dma((pairs,)),
            dma(line),
            dma(line),
            dma((count,)),
            dma((count,)),
            dma((reps,)),
            dma((reps,)),
            dma((count,)),
            dma((count,)),
            dma,
        ]
        + (line_scratch(extra[0].shape) if extra else []),
        compiler_params=pltpu.CompilerParams(
            collective_id=3, has_side_effects=True, vmem_limit_bytes=VMEM_MOST
        ),
        cost_estimate=pl.CostEstimate(flops=1 << 24, bytes_accessed=1 << 26, transcendentals=0),
    )(deltas, gains, slopes.reshape(count, tokens // count, width), *extra)


def turn_pairs(rows, along, across, sign):
    lane = lax.broadcasted_iota(jnp.int32, (rows.shape[0], 128), 1)
    early = (lane % HEAD_SIZE) < HEAD_SIZE // 2
    pieces = []
    for at in range(0, rows.shape[1], 128):
        part = rows[:, at : at + 128]
        other = jnp.where(
            early,
            pltpu.roll(part, 128 - HEAD_SIZE // 2, 1),
            pltpu.roll(part, HEAD_SIZE // 2, 1),
        )
        pieces.append(part * along + sign * (other * across))
    return pieces[0] if len(pieces) == 1 else jnp.concatenate(pieces, axis=1)


def permutation(order_ref):
    tokens = order_ref.shape[0]
    columns = lax.broadcasted_iota(jnp.int32, (tokens, tokens), 1)
    return jnp.where(order_ref[...] == columns, 1.0, 0.0).astype(jnp.bfloat16)


def fill_bias(bias, row_ref, column_ref):
    tokens = bias.shape[0]
    keys = lax.broadcasted_iota(jnp.int32, (tokens, tokens), 0)
    queries = lax.broadcasted_iota(jnp.int32, (tokens, tokens), 1)
    allowed = (column_ref[...] == row_ref[...]) & (keys <= queries)
    bias[...] = jnp.where(allowed, 0.0, -1e30)


def query_spans(tokens):
    half = tokens // 2
    return ((0, half, half), (half, half, tokens))


def remote(source, target, sends, recvs, index, device):
    return pltpu.make_async_remote_copy(
        src_ref=source,
        dst_ref=target,
        send_sem=sends.at[index],
        recv_sem=recvs.at[index],
        device_id=device,
        device_id_type=MESH,
    )


class Gather:
    def __init__(self, count, rep, me, own, slot, sends, recvs):
        self.count, self.rep, self.me = count, rep, me
        self.own, self.slot, self.sends, self.recvs = own, slot, sends, recvs
        self.waiting = []

    def near(self, mask):
        return flip(self.me, mask, self.count)

    def send(self, source, owner, part, mask, index):
        copy = remote(
            source,
            self.slot(owner, part),
            self.sends,
            self.recvs,
            index,
            (self.rep, self.near(mask)),
        )
        copy.start()
        self.waiting.append(copy)

    def arrived(self, owner, part, index):
        remote(
            self.slot(owner, part),
            self.slot(owner, part),
            self.sends,
            self.recvs,
            index,
            (self.rep, self.me),
        ).wait_recv()

    def pass_on(self, mask, part, index, new, onward):
        owner = self.near(mask)
        if index is not None:
            self.arrived(owner, part, index)
        self.send(self.slot(owner, part), owner, part, onward, new)

    def start(self):
        if self.count == 8:
            plan = ((2, 0, 0), (4, 1, 1), (2, 1, 2), (4, 0, 3), (1, 0, 4), (1, 1, 5))
            for mask, part, index in plan:
                self.send(self.own(part), self.me, part, mask, index)
        else:
            for mask in [1] + list(range(2, self.count, 2)):
                for part in range(2):
                    self.send(self.own(part), self.me, part, mask, 2 * mask + part)

    def relay(self, stage):
        if self.count == 8:
            if stage == 0:
                self.pass_on(2, 0, 0, 6, 4)
                self.pass_on(4, 1, 1, 8, 2)
                self.pass_on(2, 0, None, 7, 1)
                self.pass_on(4, 1, None, 9, 1)
            elif stage == 1:
                self.pass_on(2, 1, 2, 10, 1)
                self.pass_on(4, 0, 3, 11, 1)
            else:
                self.pass_on(6, 0, 6, 12, 1)
                self.pass_on(6, 1, 8, 13, 1)
        elif stage == 2:
            for mask in range(2, self.count, 2):
                for part in range(2):
                    self.pass_on(mask, part, 2 * mask + part, 2 * mask + 2 + part, 1)

    def finish(self):
        if self.count == 8:
            last = ((1, 0, 4), (1, 1, 5), (3, 0, 7), (5, 1, 9), (3, 1, 10), (5, 0, 11))
            last += ((7, 0, 12), (7, 1, 13))
        else:
            last = [(m, p, 2 * m + p) for m in range(1, self.count, 2) for p in range(2)]
        for mask, part, index in last:
            self.arrived(self.near(mask), part, index)
        for copy in self.waiting:
            copy.wait_send()


def first_kernel(
    count,
    token_ref,
    query_ref,
    key_ref,
    value_ref,
    output_ref,
    gain_ref,
    order_ref,
    id_ref,
    gate_ref,
    arrived_out,
    joined_out,
    gain_out,
    mix_out,
    mix_buf,
    gain_buf,
    token_send,
    token_recv,
    gain_send,
    gain_recv,
    mix_send,
    mix_recv,
    weight_send,
    weight_recv,
    local_sem,
):
    rep = lax.axis_index("rep")
    me = lax.axis_index("shard")
    full = jnp.float32
    low = jnp.bfloat16
    rows = query_ref.shape[0]
    experts = mix_out.shape[0] * 2
    mine = pl.multiple_of(me * rows, rows)
    locals_ = [pltpu.make_async_copy(token_ref.at[me], arrived_out.at[me], local_sem.at[0])]
    at = 0
    for i, ref in enumerate((query_ref, key_ref, value_ref, output_ref)):
        size = ref.shape[1]
        target = joined_out.at[pl.ds(mine, rows), pl.ds(at, size)]
        locals_.append(pltpu.make_async_copy(ref, target, local_sem.at[1 + i]))
        at += size
    for copy in locals_:
        copy.start()
    greet(me, rep, count)

    def token_copy(k):
        target = flip(me, k, count)
        return remote(
            token_ref.at[target], arrived_out.at[me], token_send, token_recv, k, (rep, target)
        )

    def gain_copy(k):
        return remote(
            gain_ref, gain_buf.at[me], gain_send, gain_recv, k, (rep, flip(me, k, count))
        )

    def mix_copy(k):
        target = flip(me, k, count)
        return remote(mix_buf.at[target], mix_out.at[me], mix_send, mix_recv, k, (rep, target))

    for k in range(count - 1, 0, -1):
        token_copy(k).start()
    for copy in locals_[1:]:
        copy.wait()
    half = rows // 2

    def block(owner, part):
        return joined_out.at[pl.ds(pl.multiple_of(owner * rows + part * half, half), half)]

    weights = Gather(count, rep, me, lambda p: block(me, p), block, weight_send, weight_recv)
    weights.start()
    for k in range(1, count):
        gain_copy(k).start()
    gain_buf[me] = gain_ref[...]
    tokens = order_ref.shape[0]
    lane = lax.broadcasted_iota(jnp.int32, (tokens, experts), 1)
    mixing = jnp.zeros((tokens, experts), full)
    for k in range(id_ref.shape[1]):
        mixing = mixing + jnp.where(id_ref[:, k : k + 1] == lane, gate_ref[:, k : k + 1], 0.0)
    place = permutation(order_ref)
    moved = jnp.zeros((experts, tokens), full)
    for _ in range(3):
        high = mixing.astype(low)
        moved = moved + matmul(high, place, TN)
        mixing = mixing - high.astype(full)
    for owner in range(count):
        mix_buf[owner, 0:2, :] = moved[2 * owner : 2 * owner + 2, :]
        mix_buf[owner, 2:8, :] = jnp.zeros((6, tokens), full)
    weights.relay(0)
    for k in range(1, count):
        mix_copy(k).start()
    mix_out[me] = mix_buf[me]
    weights.relay(1)
    weights.relay(2)
    locals_[0].wait()
    for k in range(1, count):
        gain_copy(k).wait_recv()
    for owner in range(count):
        gain_out[:, owner * rows : (owner + 1) * rows] = gain_buf[owner]
    for k in range(1, count):
        token_copy(k).wait_recv()
        mix_copy(k).wait_recv()
    weights.finish()
    for k in range(1, count):
        token_copy(k).wait_send()
        gain_copy(k).wait_send()
        mix_copy(k).wait_send()


def first_pass(tokens, weights, gains, order, expert_ids, gates, count):
    rows = weights[0].shape[0]
    number, width = tokens.shape
    block = number // count
    low = jnp.bfloat16
    full = jnp.float32
    dma = pltpu.SemaphoreType.DMA
    inside = pl.BlockSpec(memory_space=pltpu.VMEM)
    columns = sum(w.shape[1] for w in weights)
    shape = jax.ShapeDtypeStruct
    return pl.pallas_call(
        functools.partial(first_kernel, count),
        name="first_pass",
        out_shape=(
            shape((count, block, width), low),
            shape((rows * count, columns), low),
            shape((8, rows * count), full),
            shape((count, 8, number), full),
        ),
        in_specs=[inside] * 9,
        out_specs=(inside,) * 4,
        scratch_shapes=[
            pltpu.VMEM((count, 8, number), full),
            pltpu.VMEM((count, 8, rows), full),
            dma((count,)),
            dma((count,)),
            dma((count,)),
            dma((count,)),
            dma((count,)),
            dma((count,)),
            dma((2 * count + 2,)),
            dma((2 * count + 2,)),
            dma((5,)),
        ],
        compiler_params=pltpu.CompilerParams(
            collective_id=4, has_side_effects=True, vmem_limit_bytes=VMEM_MOST
        ),
        cost_estimate=pl.CostEstimate(flops=1 << 24, bytes_accessed=1 << 26, transcendentals=0),
    )(tokens.reshape(count, block, width), *weights, gains, order, expert_ids, gates)


def attention_kernel(
    count,
    arrived_ref,
    order_ref,
    row_ref,
    column_ref,
    along_ref,
    across_ref,
    weight_ref,
    gain_ref,
    cotangent_ref,
    input_out,
    query_out,
    key_out,
    value_out,
    mixed_out,
    logsum_out,
    hidden_out,
    normed_out,
    shared_out,
    slopes_out,
    place,
    bias,
    normed,
    sends,
    recvs,
    local_sem,
):
    rep = lax.axis_index("rep")
    me = lax.axis_index("shard")
    half = cotangent_ref.shape[0] // 2
    own = pltpu.make_async_copy(cotangent_ref, slopes_out.at[me], local_sem)
    own.start()
    greet(me, rep, count)
    slopes = Gather(
        count,
        rep,
        me,
        lambda p: cotangent_ref.at[pl.ds(p * half, half)],
        lambda owner, p: slopes_out.at[owner, pl.ds(p * half, half)],
        sends,
        recvs,
    )
    slopes.start()
    low = jnp.bfloat16
    full = jnp.float32
    tokens, width = arrived_ref.shape
    key_width = key_out.shape[1]
    place[...] = permutation(order_ref)
    inputs = matmul(place[...], arrived_ref[...], NN)
    input_out[...] = inputs.astype(low)
    scale = lax.rsqrt(jnp.mean(inputs * inputs, axis=1, keepdims=True) + EPS)
    normed[...] = (inputs * scale * gain_ref[0:1, :]).astype(low)
    fill_bias(bias, row_ref, column_ref)
    along = along_ref[...]
    across = across_ref[...]
    for at in range(0, width, 512):
        part = matmul(normed[...], weight_ref[:, at : at + 512], NN)
        query_out[:, at : at + 512] = turn_pairs(part, along, across, 1.0).astype(low)
    part = matmul(normed[...], weight_ref[:, width : width + key_width], NN)
    key_out[...] = turn_pairs(part, along, across, 1.0).astype(low)
    part = matmul(normed[...], weight_ref[:, width + key_width : width + 2 * key_width], NN)
    value_out[...] = part.astype(low)

    def heads(g, carry):
        kv = pl.ds(pl.multiple_of(g * 128, 128), 128)
        qs = pl.ds(pl.multiple_of(g * 256, 256), 256)
        keys = key_out[:, kv]
        values = value_out[:, kv]
        queries = query_out[:, qs] * jnp.bfloat16(HEAD_SIZE**-0.5)
        for start, size, reach in query_spans(tokens):
            pieces = []
            for h in range(4):
                a = (h // 2) * HEAD_SIZE
                score = matmul(
                    keys[:reach, a : a + HEAD_SIZE],
                    queries[start : start + size, h * HEAD_SIZE : (h + 1) * HEAD_SIZE],
                    NT,
                )
                score = score + bias[:reach, start : start + size]
                largest = jnp.max(score, axis=0, keepdims=True)
                powers = jnp.exp(score - largest)
                totals = jnp.sum(powers, axis=0, keepdims=True)
                weights = (powers * (1.0 / totals)).astype(low)
                pieces.append(matmul(weights, values[:reach, a : a + HEAD_SIZE], TN))
                logsum_out[g, h : h + 1, start : start + size] = largest + jnp.log(totals)
            mixed_out[start : start + size, qs] = jnp.concatenate(pieces, axis=1).astype(low)
        return carry

    lax.fori_loop(0, key_width // 256, heads, 0)
    slopes.relay(0)
    lax.fori_loop(key_width // 256, key_width // 128, heads, 0)
    hidden = input_out[...].astype(full) + matmul(
        mixed_out[...], weight_ref[:, width + 2 * key_width :], NN
    )
    hidden_out[...] = hidden
    scale = lax.rsqrt(jnp.mean(hidden * hidden, axis=1, keepdims=True) + EPS)
    normed[...] = (hidden * scale * gain_ref[1:2, :]).astype(low)
    normed_out[...] = matmul(place[...], normed[...], TN).astype(low)
    shared_out[...] = matmul(place[...], hidden_out[...].astype(low), TN).astype(low)
    slopes.relay(1)
    slopes.relay(2)
    own.wait()
    slopes.finish()


def attention_pass(
    count, arrived, order, row, column, along, across, weights, gains, cotangent
):
    tokens, width = arrived.shape
    key_width = (weights.shape[1] - 2 * width) // 2
    low = jnp.bfloat16
    full = jnp.float32
    inside = pl.BlockSpec(memory_space=pltpu.VMEM)
    shape = jax.ShapeDtypeStruct
    return pl.pallas_call(
        functools.partial(attention_kernel, count),
        name="attention_pass",
        out_shape=(
            shape((tokens, width), low),
            shape((tokens, width), low),
            shape((tokens, key_width), low),
            shape((tokens, key_width), low),
            shape((tokens, width), low),
            shape((key_width // 128, 4, tokens), full),
            shape((tokens, width), full),
            shape((tokens, width), low),
            shape((tokens, width), low),
            shape((count, tokens, width), low),
        ),
        in_specs=[inside] * 9,
        out_specs=(inside,) * 9 + (pl.BlockSpec(memory_space=pl.ANY),),
        scratch_shapes=[
            pltpu.VMEM((tokens, tokens), low),
            pltpu.VMEM((tokens, tokens), full),
            pltpu.VMEM((tokens, width), low),
            pltpu.SemaphoreType.DMA((2 * count + 2,)),
            pltpu.SemaphoreType.DMA((2 * count + 2,)),
            pltpu.SemaphoreType.DMA,
        ],
        compiler_params=pltpu.CompilerParams(
            collective_id=5, has_side_effects=True, vmem_limit_bytes=VMEM_MOST
        ),
        cost_estimate=pl.CostEstimate(
            flops=12 << 30, bytes_accessed=1 << 24, transcendentals=1 << 22
        ),
    )(arrived, order, row, column, along, across, weights, gains, cotangent)


def slope_kernel(count, reps, *refs):
    lined = reps == LINE
    (
        back_ref,
        slopes_ref,
        order_ref,
        row_ref,
        column_ref,
        along_ref,
        across_ref,
        weight_ref,
        gain_ref,
        input_ref,
        query_ref,
        key_ref,
        value_ref,
        mixed_ref,
        logsum_ref,
        hidden_ref,
        piece_ref,
    ) = refs[:17]
    refs = refs[17:]
    if lined:
        line_ref = refs[0]
        refs = refs[1:]
    delta_out, gain_out, slope_out, out_ref = refs[:4]
    refs = refs[4:]
    if lined:
        line_out = refs[0]
        refs = refs[1:]
    (
        place,
        bias,
        normed,
        steep,
        mixed_slope,
        backs,
        arrived,
        final,
        far_recv,
        far_send_sem,
        far_recv_sem,
        local_sem,
    ) = refs[:12]
    rep = lax.axis_index("rep")
    me = lax.axis_index("shard")
    pairs = count // 2
    block = slopes_ref.shape[1] // count
    own_slopes = pltpu.make_async_copy(
        slopes_ref.at[:, pl.ds(pl.multiple_of(me * block, block), block)],
        arrived,
        local_sem.at[0],
    )
    own_slopes.start()
    own_piece = pltpu.make_async_copy(piece_ref.at[pairs - 1], final, local_sem.at[1])
    own_piece.start()
    greet(me, rep, count, reps if lined else 1)
    line = Line(rep, me, line_ref, line_out, *refs[12:]) if lined else None
    if lined:
        line.start()

    def far_copy(turn):
        return remote(
            piece_ref.at[turn],
            far_recv.at[turn],
            far_send_sem,
            far_recv_sem,
            turn,
            (rep, flip(me, count - 2 - 2 * turn, count)),
        )

    for turn in range(pairs - 1):
        far_copy(turn).start()
    low = jnp.bfloat16
    full = jnp.float32
    tokens, width = back_ref.shape
    key_width = key_ref.shape[1]
    place[...] = permutation(order_ref)
    fill_bias(bias, row_ref, column_ref)
    own_slopes.wait()
    high = back_ref[...].astype(low)
    rest = (back_ref[...] - high.astype(full)).astype(low)
    slope = matmul(place[...], high, NN) + matmul(place[...], rest, NN)
    hidden = hidden_ref[...]
    scale = lax.rsqrt(jnp.mean(hidden * hidden, axis=1, keepdims=True) + EPS)
    scaled = slope * gain_ref[1:2, :]
    gain_out[1:2, :] = jnp.sum(slope * hidden * scale, axis=0, keepdims=True)
    steep[...] = (
        matmul(place[...], arrived[...].reshape(tokens, width), NN)
        + scale * scaled
        - hidden * (scale * scale * scale) * jnp.mean(hidden * scaled, axis=1, keepdims=True)
    )
    sharp = steep[...].astype(low)
    joined = width + 2 * key_width
    for at in range(0, width, 512):
        delta_out[:, joined + at : joined + at + 512] = matmul(
            mixed_ref[...], sharp[:, at : at + 512], TN
        ).astype(low)
    mixed_slope[...] = matmul(sharp, weight_ref[:, joined:], NT).astype(low)
    along = along_ref[...]
    across = across_ref[...]
    if lined:
        line.ticks(0, 3)

    def heads(g, carry):
        if lined:
            line.ticks(3 + 2 * g, 5 + 2 * g)
        kv = pl.ds(pl.multiple_of(g * 128, 128), 128)
        qs = pl.ds(pl.multiple_of(g * 256, 256), 256)
        keys = key_ref[:, kv]
        values = value_ref[:, kv]
        queries = query_ref[:, qs] * jnp.bfloat16(HEAD_SIZE**-0.5)
        slopes = mixed_slope[:, qs]
        key_parts = []
        value_parts = []
        query_parts = [[], []]
        for a in range(2):
            key_h = keys[:, a * HEAD_SIZE : (a + 1) * HEAD_SIZE]
            value_h = values[:, a * HEAD_SIZE : (a + 1) * HEAD_SIZE]
            key_slope = [None, None]
            value_slope = [None, None]
            for b in range(2):
                h = 2 * a + b
                columns = slice(h * HEAD_SIZE, (h + 1) * HEAD_SIZE)
                for i, (start, size, reach) in enumerate(query_spans(tokens)):
                    q = queries[start : start + size, columns]
                    d = slopes[start : start + size, columns]
                    score = matmul(key_h[:reach], q, NT) + bias[:reach, start : start + size]
                    probs = jnp.exp(score - logsum_ref[g, h : h + 1, start : start + size])
                    prob_slope = matmul(value_h[:reach], d, NT)
                    inner = jnp.sum(probs * prob_slope, axis=0, keepdims=True)
                    score_slope = (probs * (prob_slope - inner)).astype(low)
                    term = matmul(probs.astype(low), d, NN)
                    value_slope[i] = term if b == 0 else value_slope[i] + term
                    term = matmul(score_slope, q, NN)
                    key_slope[i] = term if b == 0 else key_slope[i] + term
                    query_parts[i].append(matmul(score_slope, key_h[:reach], TN))
            half = tokens // 2
            key_parts.append(
                jnp.concatenate([key_slope[0] + key_slope[1][:half], key_slope[1][half:]], axis=0)
            )
            value_parts.append(
                jnp.concatenate(
                    [value_slope[0] + value_slope[1][:half], value_slope[1][half:]], axis=0
                )
            )
        for i, (start, size, reach) in enumerate(query_spans(tokens)):
            rows = slice(start, start + size)
            part = jnp.concatenate(query_parts[i], axis=1) * HEAD_SIZE**-0.5
            backs[rows, qs] = turn_pairs(part, along[rows], across[rows], -1.0).astype(low)
        part = jnp.concatenate(key_parts, axis=1)
        spot = pl.ds(pl.multiple_of(width + g * 128, 128), 128)
        backs[:, spot] = turn_pairs(part, along, across, -1.0).astype(low)
        part = jnp.concatenate(value_parts, axis=1)
        spot = pl.ds(pl.multiple_of(width + key_width + g * 128, 128), 128)
        backs[:, spot] = part.astype(low)
        return carry

    lax.fori_loop(0, key_width // 128, heads, 0)
    inputs = input_ref[...].astype(full)
    scale = lax.rsqrt(jnp.mean(inputs * inputs, axis=1, keepdims=True) + EPS)
    normed[...] = (inputs * scale * gain_ref[0:1, :]).astype(low)
    for at in range(0, joined, 512):
        if lined:
            j = 3 + key_width // 64 + at // 512
            line.ticks(j, j + 1)
        delta_out[:, at : at + 512] = matmul(normed[...], backs[:, at : at + 512], TN).astype(low)
    slope = matmul(backs[...], weight_ref[:, :joined], NT)
    scaled = slope * gain_ref[0:1, :]
    gain_out[0:1, :] = jnp.sum(slope * inputs * scale, axis=0, keepdims=True)
    result = (
        steep[...]
        + scale * scaled
        - inputs * (scale * scale * scale) * jnp.mean(inputs * scaled, axis=1, keepdims=True)
    )
    slope_out[...] = matmul(place[...], result.astype(low), TN).astype(low)
    gain_out[2:8, :] = jnp.zeros((6, width), full)
    if lined:
        line.ticks(3 + key_width // 64 + joined // 512, SEGMENTS + LAG)
    own_piece.wait()
    result = final[...].astype(full)
    for turn in range(pairs - 1):
        far_copy(turn).wait_recv()
        result = result + far_recv[turn].astype(full)
    out_ref[...] = result.astype(low)
    for turn in range(pairs - 1):
        far_copy(turn).wait_send()
    if lined:
        line.finish()


def slope_pass(
    count,
    reps,
    back,
    slopes,
    order,
    row,
    column,
    along,
    across,
    weights,
    gains,
    inputs,
    queries,
    keys,
    values,
    mixed,
    logsum,
    hidden,
    pieces,
    extra,
):
    tokens, width = back.shape
    pairs = count // 2
    dma = pltpu.SemaphoreType.DMA
    extra = [extra] if reps == LINE else []
    key_width = keys.shape[1]
    low = jnp.bfloat16
    full = jnp.float32
    anywhere = pl.BlockSpec(memory_space=pl.ANY)
    inside = pl.BlockSpec(memory_space=pltpu.VMEM)
    shape = jax.ShapeDtypeStruct
    return pl.pallas_call(
        functools.partial(slope_kernel, count, reps),
        name="slope_pass",
        out_shape=(
            shape(weights.shape, low),
            shape((8, width), full),
            shape((tokens, width), low),
            shape((tokens, width), low),
        )
        + tuple(shape(d.shape, full) for d in extra),
        in_specs=[inside, anywhere] + [inside] * 14 + [anywhere] + [inside] * len(extra),
        out_specs=(inside,) * (4 + len(extra)),
        scratch_shapes=[
            pltpu.VMEM((tokens, tokens), low),
            pltpu.VMEM((tokens, tokens), full),
            pltpu.VMEM((tokens, width), low),
            pltpu.VMEM((tokens, width), full),
            pltpu.VMEM((tokens, width), low),
            pltpu.VMEM((tokens, width + 2 * key_width), low),
            pltpu.VMEM((count, tokens // count, width), low),
            pltpu.VMEM((tokens, width), low),
            pltpu.VMEM((pairs - 1, tokens, width), low),
            dma((pairs,)),
            dma((pairs,)),
            dma((2,)),
        ]
        + (line_scratch(extra[0].shape) if extra else []),
        compiler_params=pltpu.CompilerParams(
            collective_id=6, has_side_effects=True, vmem_limit_bytes=VMEM_MOST
        ),
        cost_estimate=pl.CostEstimate(
            flops=24 << 30, bytes_accessed=1 << 24, transcendentals=1 << 22
        ),
    )(
        back,
        slopes,
        order,
        row,
        column,
        along,
        across,
        weights,
        gains,
        inputs,
        queries,
        keys,
        values,
        mixed,
        logsum,
        hidden,
        pieces,
        *extra,
    )


def local(
    tokens,
    cotangent,
    seq_lengths,
    pack_order,
    unpack_order,
    expert_ids,
    gates,
    first_gain,
    query_weight,
    key_matrix,
    value_matrix,
    output_weight,
    second_gain,
    gate_weight,
    up_weight,
    down_weight,
):
    shards = lax.axis_size("shard")
    group_count, width = tokens.shape
    full = jnp.float32
    query_width = query_weight.shape[1]
    key_width = key_matrix.shape[1]
    inputs_width = query_width + 2 * key_width
    order = pack_order[:, None]
    gain_block = jnp.stack([first_gain, second_gain] + [jnp.zeros_like(first_gain)] * 6)
    arrived, joined, gains, mixing = first_pass(
        tokens,
        (query_weight, key_matrix, value_matrix, output_weight),
        gain_block.astype(full),
        order,
        expert_ids,
        gates,
        shards,
    )
    arrived = arrived.reshape(group_count, width)
    segment, place = segment_info(seq_lengths[0], group_count)
    cosine_table, sine_table = rope_tables(place, HEAD_SIZE)
    along = jnp.concatenate([cosine_table] * 4, axis=1)
    across = jnp.concatenate([-sine_table, sine_table] * 2, axis=1)
    tables = (order, segment[None, :], segment[:, None], along, across, joined, gains)
    (
        inputs,
        queries,
        keys,
        values,
        mixed,
        logsum,
        hidden,
        normed,
        shared,
        all_slopes,
    ) = attention_pass(shards, arrived, *tables, cotangent)
    inner, row_slopes, *expert_deltas = expert_pass(
        normed, all_slopes, mixing, gate_weight, up_weight, down_weight, shards
    )
    reps = lax.axis_size("rep")
    shapes = [d.shape for d in expert_deltas]
    if reps == LINE:
        cut = [d.reshape(SEGMENTS, -1, d.shape[2]) for d in expert_deltas]
    else:
        cut = [None] * 3
    back, pieces, *down_sum = return_pass(
        row_slopes, inner, gate_weight, up_weight, down_weight, shared, cut[2], shards, reps
    )
    deltas, gain_rows, slope_rows, out_tokens, *gate_sum = slope_pass(
        shards,
        reps,
        back,
        all_slopes,
        *tables,
        inputs,
        queries,
        keys,
        values,
        mixed,
        logsum,
        hidden,
        pieces,
        cut[0],
    )
    attention_deltas, gain_deltas, delta_tokens, *up_sum = settle_pass(
        deltas,
        gain_rows.reshape(8, shards, -1).swapaxes(0, 1),
        slope_rows,
        cut[1],
        shards,
        reps,
    )
    if reps == LINE:
        expert_deltas = [
            part[0].reshape(shape)
            for part, shape in zip((gate_sum, up_sum, down_sum), shapes, strict=True)
        ]
    else:
        expert_deltas = lax.psum(expert_deltas, "rep")
    return (
        out_tokens,
        delta_tokens.reshape(group_count, width),
        gain_deltas[0],
        attention_deltas[:, :query_width],
        attention_deltas[:, query_width : query_width + key_width],
        attention_deltas[:, query_width + key_width : inputs_width],
        attention_deltas[:, inputs_width:],
        gain_deltas[1],
        expert_deltas[0].astype(full),
        expert_deltas[1].astype(full),
        expert_deltas[2].astype(full),
    )


def solution(mesh):
    placed = (
        P(("rep", "shard"), None),
        P(("rep", "shard"), None),
        P(("rep", "shard"), None),
        P(("rep", "shard")),
        P(("rep", "shard")),
        P(("rep", "shard"), None),
        P(("rep", "shard"), None),
        P("shard"),
        P("shard", None),
        P("shard", None),
        P("shard", None),
        P("shard", None),
        P("shard"),
        P("shard", None, None),
        P("shard", None, None),
        P("shard", None, None),
    )
    return jax.shard_map(
        local,
        mesh=mesh,
        in_specs=placed,
        out_specs=(
            P(("rep", "shard"), None),
            P(("rep", "shard"), None),
            P("shard"),
            P("shard", None),
            P("shard", None),
            P("shard", None),
            P("shard", None),
            P("shard"),
            P("shard", None, None),
            P("shard", None, None),
            P("shard", None, None),
        ),
        check_vma=False,
    )
```

```python
import functools

import jax
import jax.numpy as jnp
from jax import lax
from jax.experimental import pallas as pl
from jax.experimental.pallas import tpu as pltpu
from jax.sharding import PartitionSpec as P

QUERY_HEADS = 16
KEY_VALUE_HEADS = 8
HEAD_SIZE = 64


EPS = 1e-05
THETA = 10000.0


def rope_tables(place, size):
    half = size // 2
    freq = THETA ** (-2.0 * jnp.arange(half, dtype=jnp.float32) / size)
    angle = place.astype(jnp.float32)[:, None] * freq[None, :]
    return (jnp.cos(angle), jnp.sin(angle))


def segment_info(lengths, group_count):
    ends = jnp.cumsum(lengths)
    starts = ends - lengths
    place = jnp.arange(group_count, dtype=jnp.int32)
    inside = ((place[:, None] >= starts[None, :]) & (place[:, None] < ends[None, :])).astype(
        jnp.int32
    )
    segment = jnp.sum(inside * jnp.arange(lengths.shape[0], dtype=jnp.int32)[None, :], axis=1)
    offset = jnp.sum(inside * starts[None, :], axis=1)
    return (segment, place - offset)


MESH = pl.DeviceIdType.MESH
NN = (((1,), (0,)), ((), ()))
NT = (((1,), (1,)), ((), ()))
TN = (((0,), (0,)), ((), ()))
TILE = 256
VMEM_MOST = 66_000_000


def matmul(left, right, dims):
    return lax.dot_general(left, right, dims, preferred_element_type=jnp.float32)


def flip(number, mask, count):
    out = 0
    bit = 1
    while bit < count:
        a = (number // bit) % 2
        b = (mask // bit) % 2
        out = out + (a + b - 2 * a * b) * bit
        bit *= 2
    return out


def greet(me, rep, count, reps=1):
    barrier = pltpu.get_barrier_semaphore()
    for k in range(1, count):
        pl.semaphore_signal(
            barrier, inc=1, device_id=(rep, lax.rem(me + k, count)), device_id_type=MESH
        )
    for k in range(1, reps):
        pl.semaphore_signal(
            barrier, inc=1, device_id=(lax.rem(rep + k, reps), me), device_id_type=MESH
        )
    pl.semaphore_wait(barrier, count + reps - 2)


LINE = 4
LAG = 2
RING = 4


class Line:
    def __init__(
        self,
        rep,
        me,
        source,
        out,
        first,
        second,
        both,
        sends,
        recvs,
        held=None,
        sems=None,
        base=0,
        count=None,
    ):
        self.rep, self.me = rep, me
        self.source, self.out = source, out
        self.first, self.second, self.both = first, second, both
        self.sends, self.recvs = sends, recvs
        self.held, self.sems = held, sems
        self.base = base
        self.count = source.shape[0] if count is None else count
        self.outer = (rep == 0) | (rep == LINE - 1)
        self.inner = jnp.logical_not(self.outer)
        self.inside = jnp.where(rep == 0, 1, 2)
        self.outside = jnp.where(rep == 1, 0, 3)
        self.across = LINE - 1 - rep

    def copy(self, stage, i):
        ring = self.both.at[i % RING]
        if stage == 0:
            source = self.source.at[self.base + i]
        else:
            source = ring if stage == 1 else self.first.at[i]
        target = (self.first, self.second, self.first)[stage].at[i]
        device = (self.inside, self.across, self.outside)[stage]
        return pltpu.make_async_remote_copy(
            src_ref=source,
            dst_ref=target,
            send_sem=self.sends.at[stage, i],
            recv_sem=self.recvs.at[stage, i],
            device_id=(device, self.me),
            device_id_type=MESH,
        )

    def load(self, i):
        return pltpu.make_async_copy(
            self.source.at[self.base + i], self.held.at[i % 2], self.sems.at[self.count + i % 2]
        )

    def put(self, i):
        return pltpu.make_async_copy(self.first.at[i], self.out.at[i], self.sems.at[i])

    def loop(self, body, begin=0):
        def step(i, carry):
            body(i)
            return carry

        lax.fori_loop(begin, self.count, step, 0)

    def start(self, begin=0, end=None):
        end = self.count if end is None else end

        @pl.when(self.outer)
        def _():
            def step(i, carry):
                self.copy(0, i).start()
                return carry

            lax.fori_loop(begin, end, step, 0)

        if self.held is not None:

            @pl.when(self.inner)
            def _():
                self.load(0).start()

    def tick(self, j):
        full = jnp.float32
        low = jnp.bfloat16

        @pl.when(self.inner & (j >= 0) & (j < self.count))
        def _():
            if self.held is None:
                own = self.source[self.base + j]
            else:

                @pl.when(j + 1 < self.count)
                def _():
                    self.load(j + 1).start()

                self.load(j).wait()
                own = self.held[j % 2]
            self.copy(0, j).wait_recv()

            @pl.when(j >= RING)
            def _():
                self.copy(1, j - RING).wait_send()

            self.both[j % RING] = (own.astype(full) + self.first[j].astype(full)).astype(low)
            self.copy(1, j).start()

        i = j - LAG

        @pl.when(self.inner & (i >= 0) & (i < self.count))
        def _():
            self.copy(1, i).wait_recv()
            every = self.both[i % RING].astype(full) + self.second[i].astype(full)
            self.first[i] = every.astype(low)
            self.copy(2, i).start()
            if self.held is None:
                self.out[i] = every.astype(low)
            else:
                self.put(i).start()

    def ticks(self, begin, end):
        def step(j, carry):
            self.tick(j)
            return carry

        lax.fori_loop(begin, end, step, 0)

    def finish(self):
        @pl.when(self.outer)
        def _():
            def receive(i):
                self.copy(2, i).wait_recv()
                if self.held is None:
                    self.out[i] = self.first[i]
                else:
                    self.put(i).start()

            self.loop(receive)
            self.loop(lambda i: self.copy(0, i).wait_send())

        @pl.when(self.inner)
        def _():
            self.loop(lambda i: self.copy(1, i).wait_send(), self.count - RING)
            self.loop(lambda i: self.copy(2, i).wait_send())

        if self.held is not None:
            self.loop(lambda i: self.put(i).wait())


def line_scratch(shape, streamed=True):
    low = jnp.bfloat16
    dma = pltpu.SemaphoreType.DMA
    scratch = [
        pltpu.VMEM(shape, low),
        pltpu.VMEM(shape, low),
        pltpu.VMEM((RING,) + shape[1:], low),
        dma((3, shape[0])),
        dma((3, shape[0])),
    ]
    if streamed:
        scratch += [pltpu.VMEM((2,) + shape[1:], low), dma((shape[0] + 2,))]
    return scratch


def remote(source, target, sends, recvs, index, device):
    return pltpu.make_async_remote_copy(
        src_ref=source,
        dst_ref=target,
        send_sem=sends.at[index],
        recv_sem=recvs.at[index],
        device_id=device,
        device_id_type=MESH,
    )


class Gather:
    def __init__(self, count, rep, me, own, slot, sends, recvs):
        self.count, self.rep, self.me = count, rep, me
        self.own, self.slot, self.sends, self.recvs = own, slot, sends, recvs
        self.waiting = []

    def near(self, mask):
        return flip(self.me, mask, self.count)

    def send(self, source, owner, part, mask, index):
        remote(
            source,
            self.slot(owner, part),
            self.sends,
            self.recvs,
            index,
            (self.rep, self.near(mask)),
        ).start()
        self.waiting.append(index)

    def arrived(self, owner, part, index):
        remote(
            self.slot(owner, part),
            self.slot(owner, part),
            self.sends,
            self.recvs,
            index,
            (self.rep, self.me),
        ).wait_recv()

    def pass_on(self, mask, part, index, new, onward):
        owner = self.near(mask)
        if index is not None:
            self.arrived(owner, part, index)
        self.send(self.slot(owner, part), owner, part, onward, new)

    def start(self):
        if self.count == 8:
            plan = ((2, 0, 0), (4, 1, 1), (2, 1, 2), (4, 0, 3), (1, 0, 4), (1, 1, 5))
            for mask, part, index in plan:
                self.send(self.own(part), self.me, part, mask, index)
        else:
            for mask in [1] + list(range(2, self.count, 2)):
                for part in range(2):
                    self.send(self.own(part), self.me, part, mask, 2 * mask + part)

    def relay(self, stage):
        if self.count == 8:
            if stage == 0:
                self.pass_on(2, 0, 0, 6, 4)
                self.pass_on(4, 1, 1, 8, 2)
                self.pass_on(2, 0, None, 7, 1)
                self.pass_on(4, 1, None, 9, 1)
            elif stage == 1:
                self.pass_on(2, 1, 2, 10, 1)
                self.pass_on(4, 0, 3, 11, 1)
            else:
                self.pass_on(6, 0, 6, 12, 1)
                self.pass_on(6, 1, 8, 13, 1)
        elif stage == 2:
            for mask in range(2, self.count, 2):
                for part in range(2):
                    self.pass_on(mask, part, 2 * mask + part, 2 * mask + 2 + part, 1)

    def ready(self, masks):
        if self.count == 8:
            last = ((1, 0, 4), (1, 1, 5), (3, 0, 7), (5, 1, 9), (3, 1, 10), (5, 0, 11))
            last += ((7, 0, 12), (7, 1, 13))
        else:
            last = [(m, p, 2 * m + p) for m in range(1, self.count, 2) for p in range(2)]
        for mask, part, index in last:
            if mask in masks:
                self.arrived(self.near(mask), part, index)

    def finish(self, masks=None):
        self.ready(range(self.count) if masks is None else masks)
        for index in self.waiting:
            spot = self.slot(self.me, 0)
            remote(
                spot, spot, self.sends, self.recvs, index, (self.rep, self.me)
            ).wait_send()


PARTS = 8


def expert_kernel(count, reps, *refs):
    lined = reps == LINE
    own_ref, slope_ref, mix_ref, gate_ref, up_ref, down_ref = refs[:6]
    hidden_out, grad_out, delta_out = refs[6:9]
    refs = refs[9:]
    if lined:
        line_out = refs[0]
        refs = refs[1:]
    (
        rows,
        slope_buf,
        hidden_buf,
        grad_buf,
        acc_both,
        acc_down,
        stage,
        send_sem,
        recv_sem,
        own_sem,
        slope_sem,
        hidden_sem,
        grad_sem,
        stage_sem,
    ) = refs[:14]
    rep = lax.axis_index("rep")
    me = lax.axis_index("shard")
    experts, width, hidden = gate_ref.shape
    tokens = own_ref.shape[0]
    half = tokens // 2
    low = jnp.bfloat16
    turns = experts * count
    swap = 2 + count

    def pair(t):
        late = jnp.where(t < swap, t - 2, t - count)
        return (
            jnp.where(t < 4, t // 2, late),
            jnp.where(t < 4, t % 2, jnp.where(t < swap, 0, 1)),
        )

    def pack_of(t):
        return flip(me, pair(t)[0], count)

    def slope_copy(t):
        return pltpu.make_async_copy(
            slope_ref.at[:, pack_of(t)], slope_buf.at[t % 2], slope_sem.at[t % 2]
        )

    def hidden_copy(t):
        spot = pl.ds(pl.multiple_of(pair(t)[1] * hidden, hidden), hidden)
        return pltpu.make_async_copy(
            hidden_buf.at[t % 2], hidden_out.at[pack_of(t), :, spot], hidden_sem.at[t % 2]
        )

    def grad_copy(t):
        spot = pl.ds(pl.multiple_of(pair(t)[1] * 2 * hidden, 2 * hidden), 2 * hidden)
        return pltpu.make_async_copy(
            grad_buf.at[t % 2], grad_out.at[pack_of(t), :, spot], grad_sem.at[t % 2]
        )

    def stage_copy(e):
        span = pl.ds(e * 3 * PARTS, 3 * PARTS)
        return pltpu.make_async_copy(stage.at[span], delta_out.at[span], stage_sem.at[e])

    slope_copy(0).start()
    own = pltpu.make_async_copy(own_ref, rows.at[me], own_sem)
    own.start()
    greet(me, rep, count, reps if lined else 1)
    gather = Gather(
        count,
        rep,
        me,
        lambda p: own_ref.at[pl.ds(p * half, half)],
        lambda owner, p: rows.at[owner, pl.ds(p * half, half)],
        send_sem,
        recv_sem,
    )
    gather.start()
    own.wait()
    if lined:
        line = Line(rep, me, stage, line_out, *refs[14:], count=PARTS)

    def wrap_up(e):
        size = acc_down.shape[1] // PARTS
        side = acc_both.shape[1] // (2 * PARTS)
        base = e * 3 * PARTS
        for i in range(PARTS):
            down = base + (0 if e == 0 else 2 * PARTS) + i
            stage[down] = acc_down[e, i * size : (i + 1) * size, :].astype(low)
            for which in range(2):
                at = base + (PARTS if e == 0 else 0) + which * PARTS + i
                for piece in range(2):
                    span = slice((2 * i + piece) * side, (2 * i + piece + 1) * side)
                    stage[at, :, piece * hidden : (piece + 1) * hidden] = acc_both[
                        e, span, which * hidden : (which + 1) * hidden
                    ].astype(low)
        stage_copy(e).start()

    if count == 8:
        plan = {2: ((1,), 0), 4: ((), 1), 5: ((3,), None), 7: ((5,), 2), 9: ((7,), None)}
    else:
        plan = {2: ((1,), None), 4: ((), 2), 5: (tuple(range(3, count, 2)), None)}

    def step(t, carry):
        k, e = pair(t)
        pack = flip(me, k, count)
        for at, (masks, stage_at) in plan.items():

            @pl.when(t == at)
            def _():
                gather.ready(masks)
                if stage_at is not None:
                    gather.relay(stage_at)

        @pl.when(t + 1 < turns)
        def _():
            slope_copy(t + 1).start()

        if lined:
            line.ticks(2 * (t - swap - 1), 2 * (t - swap))
        slope_copy(t).wait()

        @pl.when(t >= 2)
        def _():
            hidden_copy(t - 2).wait()
            grad_copy(t - 2).wait()

        slot = t % 2
        x = rows[pack]
        dy = slope_buf[slot].reshape(tokens, width)
        mixes = jnp.transpose(mix_ref[pack])
        mix = jnp.where(e == 0, mixes[:, 0:1], mixes[:, 1:2])
        for part in range(hidden // TILE):
            span = pl.ds(part * TILE, TILE)
            ga = matmul(x, gate_ref[e, :, span], NN)
            ua = matmul(x, up_ref[e, :, span], NN)
            dh = matmul(dy, down_ref[e, span, :], NT) * mix
            sig = jax.nn.sigmoid(ga)
            act = ga * sig
            hidden_buf[slot, :, span] = (mix * (act * ua)).astype(low)
            grad_buf[slot, :, span] = (dh * ua * sig * (1.0 + ga * (1.0 - sig))).astype(low)
            grad_buf[slot, :, pl.ds(hidden + part * TILE, TILE)] = (dh * act).astype(low)
        hidden_copy(t).start()
        grad_copy(t).start()

        def add(acc, value):
            @pl.when(k == 0)
            def _():
                acc[e] = value

            @pl.when(k > 0)
            def _():
                acc[e] += value

        add(acc_both, matmul(x, grad_buf[slot], TN))
        add(acc_down, matmul(hidden_buf[slot], dy, TN))

        @pl.when(t == swap - 1)
        def _():
            wrap_up(0)
            if lined:
                line.start()

        return carry

    lax.fori_loop(0, turns, step, 0)
    wrap_up(1)
    if lined:
        line.ticks(2 * (turns - swap - 1), PARTS + LAG)
    for t in (turns - 2, turns - 1):
        hidden_copy(t).wait()
        grad_copy(t).wait()
    gather.finish(())
    stage_copy(0).wait()
    if lined:
        line.finish()
    stage_copy(1).wait()


def expert_pass(normed, all_slopes, mixing, gate_weight, up_weight, down_weight, count, reps):
    tokens, width = normed.shape
    experts, _, hidden = gate_weight.shape
    block = tokens // count
    low = jnp.bfloat16
    full = jnp.float32
    dma = pltpu.SemaphoreType.DMA
    vmem = pltpu.VMEM
    shape = jax.ShapeDtypeStruct
    anywhere = pl.BlockSpec(memory_space=pl.ANY)
    inside = pl.BlockSpec(memory_space=pltpu.VMEM)
    flops = 2 * count * tokens * width * hidden * experts * 6
    lined = reps == LINE
    segment = (hidden // PARTS, width)
    summed = (PARTS,) + segment
    return pl.pallas_call(
        functools.partial(expert_kernel, count, reps),
        name="expert_pass",
        out_shape=(
            shape((count, tokens, experts * hidden), low),
            shape((count, tokens, 2 * experts * hidden), low),
            shape((6 * PARTS,) + segment, low),
        )
        + ((shape(summed, low),) if lined else ()),
        in_specs=[inside, anywhere, inside, inside, inside, inside],
        out_specs=(anywhere,) * 3 + ((inside,) if lined else ()),
        scratch_shapes=[
            vmem((count, tokens, width), low),
            vmem((2, count, block, width), low),
            vmem((2, tokens, hidden), low),
            vmem((2, tokens, 2 * hidden), low),
            vmem((experts, width, 2 * hidden), full),
            vmem((experts, hidden, width), full),
            vmem((6 * PARTS,) + segment, low),
            dma((2 * count + 2,)),
            dma((2 * count + 2,)),
            dma,
            dma((2,)),
            dma((2,)),
            dma((2,)),
            dma((2,)),
        ]
        + (line_scratch(summed, False) if lined else []),
        compiler_params=pltpu.CompilerParams(
            collective_id=1, has_side_effects=True, vmem_limit_bytes=VMEM_MOST
        ),
        cost_estimate=pl.CostEstimate(flops=flops, bytes_accessed=1 << 26, transcendentals=0),
    )(
        normed,
        all_slopes.reshape(count, count, block, width),
        mixing,
        gate_weight,
        up_weight,
        down_weight,
    )


def return_kernel(count, reps, *refs):
    (
        grad_ref,
        hidden_ref,
        gate_ref,
        up_ref,
        down_ref,
        own_ref,
    ) = refs[:6]
    lined = reps == LINE
    refs = refs[6:]
    if lined:
        line_ref, back_ref, piece_out, line_out = refs[:4]
        refs = refs[4:]
    else:
        back_ref, piece_out = refs[:2]
        refs = refs[2:]
    (
        grad_buf,
        hidden_buf,
        pair_send,
        far_send,
        pair_recv,
        far_recv,
        total,
        piece,
        last_recv,
        relay_recv,
        load_sem,
        pair_send_sem,
        pair_recv_sem,
        far_send_sem,
        far_recv_sem,
        piece_sem,
        last_sem,
        relay_send_sem,
        relay_recv_sem,
    ) = refs[:19]
    rep = lax.axis_index("rep")
    me = lax.axis_index("shard")
    experts, width, hidden = gate_ref.shape
    tokens = own_ref.shape[0]
    block = tokens // count
    low = jnp.bfloat16
    full = jnp.float32
    pairs = count // 2
    partner = flip(me, 1, count)
    line = Line(rep, me, line_ref, line_out, *refs[19:], base=PARTS, count=2 * PARTS) if lined else None

    relayed = count == 8
    half = tokens // 2

    def mask_of(turn):
        rest = jnp.where(turn == 1, 0, count - 2 * turn)
        return jnp.where(turn == 0, count - 2, rest)

    def target(item):
        return flip(me, mask_of(item // 2) + 1 - item % 2, count)

    def grad_load(item):
        return pltpu.make_async_copy(
            grad_ref.at[target(item)], grad_buf.at[item % 2], load_sem.at[item % 2]
        )

    def grad_part(slot, pack):
        value = None
        for e in range(experts):
            for at, weight in ((2 * e, gate_ref), (2 * e + 1, up_ref)):
                term = matmul(grad_buf[slot, :, pl.ds(at * hidden, hidden)], weight[e], NT)
                value = term if value is None else value + term
        return value

    def hidden_load(item):
        return pltpu.make_async_copy(
            hidden_ref.at[:, target(item)], hidden_buf.at[item % 2], load_sem.at[item % 2]
        )

    def hidden_part(slot, pack):
        value = None
        for e in range(experts):
            term = matmul(
                hidden_buf[slot, :, :, pl.ds(e * hidden, hidden)].reshape(tokens, hidden),
                down_ref[e],
                NN,
            )
            value = term if value is None else value + term
        total[...] = value
        mine = pl.ds(pl.multiple_of(me * block, block), block)
        theirs = pl.ds(pl.multiple_of(pack * block, block), block)
        total[mine, :] += own_ref[theirs, :].astype(full)
        return total[...]

    def pair_copy(base, turn):
        return remote(
            pair_send.at[turn % 2],
            pair_recv.at[base + turn],
            pair_send_sem,
            pair_recv_sem,
            base + turn,
            (rep, partner),
        )

    def far_copy(turn, device):
        return remote(
            far_send.at[turn % 2], far_recv.at[turn], far_send_sem, far_recv_sem, turn, (rep, device)
        )

    grad_load(0).start()
    greet(me, rep, count, reps if lined else 1)
    if lined:
        line.start()

    def sweep(base, load, part, combine, tick):
        def turn_step(turn, carry):
            mask = mask_of(turn)
            load(2 * turn + 1).start()
            load(2 * turn).wait()
            value = part(0, flip(me, mask + 1, count))

            @pl.when(turn >= 2)
            def _():
                pair_copy(base, turn - 2).wait_send()

            pair_send[turn % 2] = value.astype(low)
            pair_copy(base, turn).start()

            @pl.when(turn + 1 < pairs)
            def _():
                load(2 * turn + 2).start()

            tick(2 * turn)
            load(2 * turn + 1).wait()
            total[...] = part(1, flip(me, mask, count))
            pair_copy(base, turn).wait_recv()
            combine(turn, mask)
            tick(2 * turn + 1)
            return carry

        lax.fori_loop(0, pairs, turn_step, 0)
        for turn in range(max(0, pairs - 2), pairs):
            pair_copy(base, turn).wait_send()

    def relay_copy(phase, side, source):
        return remote(
            source.at[pl.ds(side * half, half)],
            relay_recv.at[2 * phase + side],
            relay_send_sem,
            relay_recv_sem,
            2 * phase + side,
            (rep, flip(me, 2 + 2 * side, count)),
        )

    def grad_combine(turn, mask):
        @pl.when(turn == 1)
        def _():
            back_ref[...] = total[...] + pair_recv[1].astype(full)

        @pl.when(turn != 1)
        def _():
            if relayed:
                for side in range(2):

                    @pl.when(turn == 2 + side)
                    def _():
                        relay_copy(0, side, far_send.at[0]).wait_recv()
                        total[pl.ds(side * half, half), :] += relay_recv[side].astype(full)

            @pl.when(turn == 2)
            def _():
                if relayed:
                    for side in range(2):
                        relay_copy(0, side, far_send.at[0]).wait_send()
                else:
                    far_copy(0, me).wait_send()

            @pl.when(turn >= 4)
            def _():
                far_copy(turn - 2, me).wait_send()

            far_send[turn % 2] = (total[...] + pair_recv[turn].astype(full)).astype(low)

            @pl.when(turn == 0)
            def _():
                if relayed:
                    for side in range(2):
                        relay_copy(0, side, far_send.at[0]).start()
                else:
                    far_copy(0, flip(me, mask, count)).start()

            @pl.when(turn >= 2)
            def _():
                far_copy(turn, flip(me, mask, count)).start()

    def last_copy(device):
        return pltpu.make_async_remote_copy(
            src_ref=piece.at[0],
            dst_ref=last_recv,
            send_sem=last_sem.at[0],
            recv_sem=last_sem.at[1],
            device_id=(rep, device),
            device_id_type=MESH,
        )

    def slot(turn):
        return jnp.where(turn < 2, turn, 2 + turn % 2)

    def piece_copy(turn):
        return pltpu.make_async_copy(
            piece.at[slot(turn)], piece_out.at[turn], piece_sem.at[turn % 2]
        )

    def hidden_combine(turn, mask):
        if not relayed:

            @pl.when(turn >= 4)
            def _():
                piece_copy(turn - 2).wait()

        piece[slot(turn)] = (total[...] + pair_recv[pairs + turn].astype(full)).astype(low)

        @pl.when(turn == 0)
        def _():
            if relayed:
                for side in range(2):
                    relay_copy(1, side, piece.at[0]).start()
            else:
                last_copy(flip(me, mask, count)).start()

        if not relayed:

            @pl.when(turn >= 2)
            def _():
                piece_copy(turn).start()

    def early(j):
        if lined:
            line.tick(j - 2)

    def late(j):
        if lined:
            line.tick(2 * pairs + j - 2)

    sweep(0, grad_load, grad_part, grad_combine, early)
    hidden_load(0).start()
    sweep(pairs, hidden_load, hidden_part, hidden_combine, late)
    if lined:
        line.ticks(4 * pairs - 2, 2 * PARTS - 1)

    def add(turn, carry):
        far_copy(turn, me).wait_recv()
        back_ref[...] += far_recv[turn].astype(full)
        return carry

    if not relayed:
        add(0, 0)
    lax.fori_loop(2, pairs, add, 0)
    for turn in (pairs - 2, pairs - 1):
        far_copy(turn, me).wait_send()
    if lined:
        line.ticks(2 * PARTS - 1, 2 * PARTS + LAG)
    if relayed:
        for side in range(2):
            relay_copy(1, side, piece.at[0]).wait_recv()
            rows = pl.ds(side * half, half)
            value = piece[2 + side, rows, :].astype(full) + relay_recv[2 + side].astype(full)
            piece[2 + side, rows, :] = value.astype(low)
            piece_copy(2 + side).start()
            relay_copy(1, side, piece.at[0]).wait_send()
    else:
        last_copy(me).wait_recv()
        value = piece[1].astype(full) + last_recv[...].astype(full)
        piece[1] = value.astype(low)
        last_copy(me).wait_send()
    for turn in (pairs - 2, pairs - 1):
        piece_copy(turn).wait()
    piece_copy(1).start()
    if lined:
        line.finish()
    piece_copy(1).wait()


def return_pass(grads, hiddens, gate_weight, up_weight, down_weight, own, deltas, count, reps):
    tokens, width = own.shape
    experts, _, hidden = gate_weight.shape
    block = tokens // count
    low = jnp.bfloat16
    full = jnp.float32
    pairs = count // 2
    dma = pltpu.SemaphoreType.DMA
    shape = jax.ShapeDtypeStruct
    anywhere = pl.BlockSpec(memory_space=pl.ANY)
    inside = pl.BlockSpec(memory_space=pltpu.VMEM)
    flops = 2 * count * tokens * width * hidden * experts * 3
    lined = reps == LINE
    extra = [deltas] if lined else []
    return pl.pallas_call(
        functools.partial(return_kernel, count, reps),
        name="return_pass",
        out_shape=(
            shape((tokens, width), full),
            shape((pairs, tokens, width), low),
        )
        + tuple(shape((2 * PARTS,) + d.shape[1:], low) for d in extra),
        in_specs=[anywhere, anywhere] + [inside] * 4 + [anywhere] * len(extra),
        out_specs=(inside, anywhere) + (anywhere,) * len(extra),
        scratch_shapes=[
            pltpu.VMEM((2, tokens, 2 * experts * hidden), low),
            pltpu.VMEM((2, count, block, experts * hidden), low),
            pltpu.VMEM((2, tokens, width), low),
            pltpu.VMEM((2, tokens, width), low),
            pltpu.VMEM((2 * pairs, tokens, width), low),
            pltpu.VMEM((pairs, tokens, width), low),
            pltpu.VMEM((tokens, width), full),
            pltpu.VMEM((4, tokens, width), low),
            pltpu.VMEM((8, 128) if count == 8 else (tokens, width), low),
            pltpu.VMEM((4, tokens // 2, width), low),
            dma((2,)),
            dma((2 * pairs,)),
            dma((2 * pairs,)),
            dma((pairs,)),
            dma((pairs,)),
            dma((2,)),
            dma((3,)),
            dma((4,)),
            dma((4,)),
        ]
        + (line_scratch((2 * PARTS,) + deltas.shape[1:]) if lined else []),
        compiler_params=pltpu.CompilerParams(
            collective_id=2, has_side_effects=True, vmem_limit_bytes=VMEM_MOST
        ),
        cost_estimate=pl.CostEstimate(flops=flops, bytes_accessed=1 << 26, transcendentals=0),
    )(
        grads,
        hiddens.reshape(count, count, block, experts * hidden),
        gate_weight,
        up_weight,
        down_weight,
        own,
        *extra,
    )


def turn_pairs(rows, along, across, sign):
    lane = lax.broadcasted_iota(jnp.int32, (rows.shape[0], 128), 1)
    early = (lane % HEAD_SIZE) < HEAD_SIZE // 2
    pieces = []
    for at in range(0, rows.shape[1], 128):
        part = rows[:, at : at + 128]
        other = jnp.where(
            early,
            pltpu.roll(part, 128 - HEAD_SIZE // 2, 1),
            pltpu.roll(part, HEAD_SIZE // 2, 1),
        )
        pieces.append(part * along + sign * (other * across))
    return pieces[0] if len(pieces) == 1 else jnp.concatenate(pieces, axis=1)


def permutation(order_ref):
    tokens = order_ref.shape[0]
    columns = lax.broadcasted_iota(jnp.int32, (tokens, tokens), 1)
    return jnp.where(order_ref[...] == columns, 1.0, 0.0).astype(jnp.bfloat16)


def fill_bias(bias, row_ref, column_ref):
    tokens = bias.shape[0]
    keys = lax.broadcasted_iota(jnp.int32, (tokens, tokens), 0)
    queries = lax.broadcasted_iota(jnp.int32, (tokens, tokens), 1)
    allowed = (column_ref[...] == row_ref[...]) & (keys <= queries)
    bias[...] = jnp.where(allowed, 0.0, -1e30)


def query_spans(tokens):
    half = tokens // 2
    return ((0, half, half), (half, half, tokens))


def first_kernel(
    count,
    token_ref,
    query_ref,
    key_ref,
    value_ref,
    output_ref,
    gain_ref,
    order_ref,
    id_ref,
    gate_ref,
    arrived_out,
    joined_out,
    gain_out,
    mix_out,
    mix_buf,
    gain_buf,
    token_send,
    token_recv,
    gain_send,
    gain_recv,
    mix_send,
    mix_recv,
    weight_send,
    weight_recv,
    local_sem,
):
    rep = lax.axis_index("rep")
    me = lax.axis_index("shard")
    full = jnp.float32
    low = jnp.bfloat16
    rows = query_ref.shape[0]
    experts = mix_out.shape[0] * 2
    mine = pl.multiple_of(me * rows, rows)
    locals_ = [pltpu.make_async_copy(token_ref.at[me], arrived_out.at[me], local_sem.at[0])]
    at = 0
    for i, ref in enumerate((query_ref, key_ref, value_ref, output_ref)):
        size = ref.shape[1]
        target = joined_out.at[pl.ds(mine, rows), pl.ds(at, size)]
        locals_.append(pltpu.make_async_copy(ref, target, local_sem.at[1 + i]))
        at += size
    for copy in locals_:
        copy.start()
    greet(me, rep, count)

    def token_copy(k):
        target = flip(me, k, count)
        return remote(
            token_ref.at[target], arrived_out.at[me], token_send, token_recv, k, (rep, target)
        )

    def gain_copy(k):
        return remote(
            gain_ref, gain_buf.at[me], gain_send, gain_recv, k, (rep, flip(me, k, count))
        )

    def mix_copy(k):
        target = flip(me, k, count)
        return remote(mix_buf.at[target], mix_out.at[me], mix_send, mix_recv, k, (rep, target))

    for k in range(count - 1, 0, -1):
        token_copy(k).start()
    for copy in locals_[1:]:
        copy.wait()
    half = rows // 2

    def block(owner, part):
        return joined_out.at[pl.ds(pl.multiple_of(owner * rows + part * half, half), half)]

    weights = Gather(count, rep, me, lambda p: block(me, p), block, weight_send, weight_recv)
    weights.start()
    for k in range(1, count):
        gain_copy(k).start()
    gain_buf[me] = gain_ref[...]
    tokens = order_ref.shape[0]
    lane = lax.broadcasted_iota(jnp.int32, (tokens, experts), 1)
    mixing = jnp.zeros((tokens, experts), full)
    for k in range(id_ref.shape[1]):
        mixing = mixing + jnp.where(id_ref[:, k : k + 1] == lane, gate_ref[:, k : k + 1], 0.0)
    place = permutation(order_ref)
    moved = jnp.zeros((experts, tokens), full)
    for _ in range(3):
        high = mixing.astype(low)
        moved = moved + matmul(high, place, TN)
        mixing = mixing - high.astype(full)
    for owner in range(count):
        mix_buf[owner, 0:2, :] = moved[2 * owner : 2 * owner + 2, :]
        mix_buf[owner, 2:8, :] = jnp.zeros((6, tokens), full)
    weights.relay(0)
    for k in range(1, count):
        mix_copy(k).start()
    mix_out[me] = mix_buf[me]
    weights.relay(1)
    weights.relay(2)
    locals_[0].wait()
    for k in range(1, count):
        gain_copy(k).wait_recv()
    for owner in range(count):
        gain_out[:, owner * rows : (owner + 1) * rows] = gain_buf[owner]
    for k in range(1, count):
        token_copy(k).wait_recv()
        mix_copy(k).wait_recv()
    weights.finish()
    for k in range(1, count):
        token_copy(k).wait_send()
        gain_copy(k).wait_send()
        mix_copy(k).wait_send()


def first_pass(tokens, weights, gains, order, expert_ids, gates, count):
    rows = weights[0].shape[0]
    number, width = tokens.shape
    block = number // count
    low = jnp.bfloat16
    full = jnp.float32
    dma = pltpu.SemaphoreType.DMA
    inside = pl.BlockSpec(memory_space=pltpu.VMEM)
    columns = sum(w.shape[1] for w in weights)
    shape = jax.ShapeDtypeStruct
    return pl.pallas_call(
        functools.partial(first_kernel, count),
        name="first_pass",
        out_shape=(
            shape((count, block, width), low),
            shape((rows * count, columns), low),
            shape((8, rows * count), full),
            shape((count, 8, number), full),
        ),
        in_specs=[inside] * 9,
        out_specs=(inside,) * 4,
        scratch_shapes=[
            pltpu.VMEM((count, 8, number), full),
            pltpu.VMEM((count, 8, rows), full),
            dma((count,)),
            dma((count,)),
            dma((count,)),
            dma((count,)),
            dma((count,)),
            dma((count,)),
            dma((2 * count + 2,)),
            dma((2 * count + 2,)),
            dma((5,)),
        ],
        compiler_params=pltpu.CompilerParams(
            collective_id=4, has_side_effects=True, vmem_limit_bytes=VMEM_MOST
        ),
        cost_estimate=pl.CostEstimate(flops=1 << 24, bytes_accessed=1 << 26, transcendentals=0),
    )(tokens.reshape(count, block, width), *weights, gains, order, expert_ids, gates)


def attention_kernel(
    count,
    arrived_ref,
    order_ref,
    row_ref,
    column_ref,
    along_ref,
    across_ref,
    weight_ref,
    gain_ref,
    cotangent_ref,
    input_out,
    query_out,
    key_out,
    value_out,
    mixed_out,
    logsum_out,
    hidden_out,
    normed_out,
    shared_out,
    slopes_out,
    place,
    bias,
    normed,
    sends,
    recvs,
    local_sem,
):
    rep = lax.axis_index("rep")
    me = lax.axis_index("shard")
    half = cotangent_ref.shape[0] // 2
    own = pltpu.make_async_copy(cotangent_ref, slopes_out.at[me], local_sem)
    own.start()
    greet(me, rep, count)
    slopes = Gather(
        count,
        rep,
        me,
        lambda p: cotangent_ref.at[pl.ds(p * half, half)],
        lambda owner, p: slopes_out.at[owner, pl.ds(p * half, half)],
        sends,
        recvs,
    )
    slopes.start()
    low = jnp.bfloat16
    full = jnp.float32
    tokens, width = arrived_ref.shape
    key_width = key_out.shape[1]
    place[...] = permutation(order_ref)
    inputs = matmul(place[...], arrived_ref[...], NN)
    input_out[...] = inputs.astype(low)
    scale = lax.rsqrt(jnp.mean(inputs * inputs, axis=1, keepdims=True) + EPS)
    normed[...] = (inputs * scale * gain_ref[0:1, :]).astype(low)
    fill_bias(bias, row_ref, column_ref)
    along = along_ref[...]
    across = across_ref[...]
    for at in range(0, width, 512):
        part = matmul(normed[...], weight_ref[:, at : at + 512], NN)
        query_out[:, at : at + 512] = turn_pairs(part, along, across, 1.0).astype(low)
    part = matmul(normed[...], weight_ref[:, width : width + key_width], NN)
    key_out[...] = turn_pairs(part, along, across, 1.0).astype(low)
    part = matmul(normed[...], weight_ref[:, width + key_width : width + 2 * key_width], NN)
    value_out[...] = part.astype(low)

    def heads(g, carry):
        kv = pl.ds(pl.multiple_of(g * 128, 128), 128)
        qs = pl.ds(pl.multiple_of(g * 256, 256), 256)
        keys = key_out[:, kv]
        values = value_out[:, kv]
        queries = query_out[:, qs] * jnp.bfloat16(HEAD_SIZE**-0.5)
        for start, size, reach in query_spans(tokens):
            pieces = []
            for h in range(4):
                a = (h // 2) * HEAD_SIZE
                score = matmul(
                    keys[:reach, a : a + HEAD_SIZE],
                    queries[start : start + size, h * HEAD_SIZE : (h + 1) * HEAD_SIZE],
                    NT,
                )
                score = score + bias[:reach, start : start + size]
                largest = jnp.max(score, axis=0, keepdims=True)
                powers = jnp.exp(score - largest)
                totals = jnp.sum(powers, axis=0, keepdims=True)
                weights = (powers * (1.0 / totals)).astype(low)
                pieces.append(matmul(weights, values[:reach, a : a + HEAD_SIZE], TN))
                logsum_out[g, h : h + 1, start : start + size] = largest + jnp.log(totals)
            mixed_out[start : start + size, qs] = jnp.concatenate(pieces, axis=1).astype(low)
        return carry

    lax.fori_loop(0, key_width // 256, heads, 0)
    slopes.relay(0)
    lax.fori_loop(key_width // 256, key_width // 128, heads, 0)
    hidden = input_out[...].astype(full) + matmul(
        mixed_out[...], weight_ref[:, width + 2 * key_width :], NN
    )
    hidden_out[...] = hidden
    scale = lax.rsqrt(jnp.mean(hidden * hidden, axis=1, keepdims=True) + EPS)
    normed[...] = (hidden * scale * gain_ref[1:2, :]).astype(low)
    normed_out[...] = matmul(place[...], normed[...], TN).astype(low)
    shared_out[...] = matmul(place[...], hidden_out[...].astype(low), TN).astype(low)
    slopes.relay(1)
    slopes.relay(2)
    own.wait()
    slopes.finish()


def attention_pass(
    count, arrived, order, row, column, along, across, weights, gains, cotangent
):
    tokens, width = arrived.shape
    key_width = (weights.shape[1] - 2 * width) // 2
    low = jnp.bfloat16
    full = jnp.float32
    inside = pl.BlockSpec(memory_space=pltpu.VMEM)
    shape = jax.ShapeDtypeStruct
    return pl.pallas_call(
        functools.partial(attention_kernel, count),
        name="attention_pass",
        out_shape=(
            shape((tokens, width), low),
            shape((tokens, width), low),
            shape((tokens, key_width), low),
            shape((tokens, key_width), low),
            shape((tokens, width), low),
            shape((key_width // 128, 4, tokens), full),
            shape((tokens, width), full),
            shape((tokens, width), low),
            shape((tokens, width), low),
            shape((count, tokens, width), low),
        ),
        in_specs=[inside] * 9,
        out_specs=(inside,) * 9 + (pl.BlockSpec(memory_space=pl.ANY),),
        scratch_shapes=[
            pltpu.VMEM((tokens, tokens), low),
            pltpu.VMEM((tokens, tokens), full),
            pltpu.VMEM((tokens, width), low),
            pltpu.SemaphoreType.DMA((2 * count + 2,)),
            pltpu.SemaphoreType.DMA((2 * count + 2,)),
            pltpu.SemaphoreType.DMA,
        ],
        compiler_params=pltpu.CompilerParams(
            collective_id=5, has_side_effects=True, vmem_limit_bytes=VMEM_MOST
        ),
        cost_estimate=pl.CostEstimate(
            flops=12 << 30, bytes_accessed=1 << 24, transcendentals=1 << 22
        ),
    )(arrived, order, row, column, along, across, weights, gains, cotangent)


def finish_kernel(count, reps, *refs):
    lined = reps == LINE
    (
        back_ref,
        slopes_ref,
        order_ref,
        row_ref,
        column_ref,
        along_ref,
        across_ref,
        weight_ref,
        gain_ref,
        input_ref,
        query_ref,
        key_ref,
        value_ref,
        mixed_ref,
        logsum_ref,
        hidden_ref,
        piece_ref,
    ) = refs[:17]
    refs = refs[17:]
    if lined:
        line_ref = refs[0]
        refs = refs[1:]
    delta_out, gain_out, slope_out, out_ref = refs[:4]
    refs = refs[4:]
    if lined:
        line_out = refs[0]
        refs = refs[1:]
    (
        place,
        bias,
        normed,
        steep,
        mixed_slope,
        backs,
        arrived,
        far_piece,
        far_piece_send,
        far_piece_recv,
        local_sem,
        delta,
        pair_recv,
        far_send,
        far_recv,
        pair_send_sem,
        pair_recv_sem,
        far_send_sem,
        far_recv_sem,
        slope_send_sem,
        slope_recv_sem,
        gain_buf,
        gain_recv,
        gain_sum,
        gain_line,
        gain_send_sem,
        gain_recv_sem,
        gain_line_send,
        gain_line_recv,
        owned,
    ) = refs[:30]
    refs = refs[30:]
    low = jnp.bfloat16
    full = jnp.float32
    rep = lax.axis_index("rep")
    me = lax.axis_index("shard")
    pairs = count // 2
    partner = flip(me, 1, count)
    tokens, width = back_ref.shape
    key_width = key_ref.shape[1]
    joined = width + 2 * key_width
    rows = width // count
    block = tokens // count
    own_slopes = pltpu.make_async_copy(
        slopes_ref.at[:, pl.ds(pl.multiple_of(me * block, block), block)],
        arrived,
        local_sem.at[0],
    )
    own_slopes.start()
    own_piece = pltpu.make_async_copy(piece_ref.at[1], mixed_slope, local_sem.at[1])
    greet(me, rep, count, reps)
    if lined:
        line = Line(rep, me, line_ref, line_out, *refs[:7], base=3 * PARTS, count=3 * PARTS)
        sums = Line(rep, me, owned, delta_out, *refs[7:12])
        line.start()
    else:
        spread, spread_send, spread_recv = refs

    def tick(begin, end):
        if lined:
            line.ticks(begin, end)

    def piece_copy(turn):
        return remote(
            piece_ref.at[turn],
            far_piece.at[turn - 2],
            far_piece_send,
            far_piece_recv,
            turn,
            (rep, flip(me, count - 2 * turn, count)),
        )

    def rows_of(owner):
        return pl.ds(pl.multiple_of(owner * rows, rows), rows)

    columns = (slice(joined, joined + width), slice(0, joined))

    def pair_copy(part, turn):
        return remote(
            delta.at[rows_of(flip(partner, 2 * turn, count)), columns[part]],
            pair_recv.at[turn, :, columns[part]],
            pair_send_sem,
            pair_recv_sem,
            part * pairs + turn,
            (rep, partner),
        )

    def far_copy(part, turn):
        return remote(
            far_send.at[turn - 1, :, columns[part]],
            far_recv.at[turn - 1, :, columns[part]],
            far_send_sem,
            far_recv_sem,
            part * pairs + turn,
            (rep, flip(me, 2 * turn, count)),
        )

    def exchange(part):
        for turn in range(pairs - 1, -1, -1):
            pair_copy(part, turn).start()

    def combine(part):
        for turn in range(pairs - 1, 0, -1):
            pair_copy(part, turn).wait_recv()
            mine = delta[rows_of(flip(me, 2 * turn, count)), columns[part]].astype(full)
            far_send[turn - 1, :, columns[part]] = (
                mine + pair_recv[turn, :, columns[part]].astype(full)
            ).astype(low)
            far_copy(part, turn).start()

    def collect(part, first, number):
        pair_copy(part, 0).wait_recv()
        for turn in range(1, pairs):
            far_copy(part, turn).wait_recv()
        half = rows // 2
        for i in range(number):
            at = columns[part].start + (i // 2) * width
            span = slice((i % 2) * half, (i % 2 + 1) * half)
            value = delta[
                pl.ds(pl.multiple_of(me * rows + (i % 2) * half, half), half), at : at + width
            ].astype(full)
            value = value + pair_recv[0, span, at : at + width].astype(full)
            for turn in range(1, pairs):
                value = value + far_recv[turn - 1, span, at : at + width].astype(full)
            owned[first + i] = value.astype(low)

    def slope_copy(k):
        target = flip(me, k, count)
        return remote(
            arrived.at[target],
            slope_out.at[me],
            slope_send_sem,
            slope_recv_sem,
            k,
            (rep, target),
        )

    def gain_copy(k):
        target = flip(me, k, count)
        return remote(
            gain_buf.at[target], gain_recv.at[k], gain_send_sem, gain_recv_sem, k, (rep, target)
        )

    def gain_line_copy(k):
        return remote(
            gain_sum,
            gain_line.at[rep],
            gain_line_send,
            gain_line_recv,
            k,
            (lax.rem(rep + k, reps), me),
        )

    for turn in range(2, pairs):
        piece_copy(turn).start()
    place[...] = permutation(order_ref)
    fill_bias(bias, row_ref, column_ref)
    own_slopes.wait()
    high = back_ref[...].astype(low)
    rest = (back_ref[...] - high.astype(full)).astype(low)
    slope = matmul(place[...], high, NN) + matmul(place[...], rest, NN)
    tick(0, 1)
    hidden = hidden_ref[...]
    scale = lax.rsqrt(jnp.mean(hidden * hidden, axis=1, keepdims=True) + EPS)
    scaled = slope * gain_ref[1:2, :]
    second = jnp.sum(slope * hidden * scale, axis=0, keepdims=True)
    for owner in range(count):
        gain_buf[owner, 1:2, :] = second[:, owner * rows : (owner + 1) * rows]
    steep[...] = (
        matmul(place[...], arrived[...].reshape(tokens, width), NN)
        + scale * scaled
        - hidden * (scale * scale * scale) * jnp.mean(hidden * scaled, axis=1, keepdims=True)
    )
    tick(1, 2)
    sharp = steep[...].astype(low)
    for at in range(0, width, 512):
        delta[:, joined + at : joined + at + 512] = matmul(
            mixed_ref[...], sharp[:, at : at + 512], TN
        ).astype(low)
    exchange(0)
    tick(2, 3)
    mixed_slope[...] = matmul(sharp, weight_ref[:, joined:], NT).astype(low)
    tick(3, 4)
    along = along_ref[...]
    across = across_ref[...]

    def heads(g, carry):
        kv = pl.ds(pl.multiple_of(g * 128, 128), 128)
        qs = pl.ds(pl.multiple_of(g * 256, 256), 256)
        keys = key_ref[:, kv]
        values = value_ref[:, kv]
        queries = query_ref[:, qs] * jnp.bfloat16(HEAD_SIZE**-0.5)
        slopes = mixed_slope[:, qs]
        key_parts = []
        value_parts = []
        query_parts = [[], []]
        for a in range(2):
            tick(4 + 2 * g + a, 5 + 2 * g + a)
            key_h = keys[:, a * HEAD_SIZE : (a + 1) * HEAD_SIZE]
            value_h = values[:, a * HEAD_SIZE : (a + 1) * HEAD_SIZE]
            key_slope = [None, None]
            value_slope = [None, None]
            for b in range(2):
                h = 2 * a + b
                spot = slice(h * HEAD_SIZE, (h + 1) * HEAD_SIZE)
                for i, (start, size, reach) in enumerate(query_spans(tokens)):
                    q = queries[start : start + size, spot]
                    d = slopes[start : start + size, spot]
                    score = matmul(key_h[:reach], q, NT) + bias[:reach, start : start + size]
                    probs = jnp.exp(score - logsum_ref[g, h : h + 1, start : start + size])
                    prob_slope = matmul(value_h[:reach], d, NT)
                    inner = jnp.sum(probs * prob_slope, axis=0, keepdims=True)
                    score_slope = (probs * (prob_slope - inner)).astype(low)
                    term = matmul(probs.astype(low), d, NN)
                    value_slope[i] = term if b == 0 else value_slope[i] + term
                    term = matmul(score_slope, q, NN)
                    key_slope[i] = term if b == 0 else key_slope[i] + term
                    query_parts[i].append(matmul(score_slope, key_h[:reach], TN))
            half = tokens // 2
            key_parts.append(
                jnp.concatenate([key_slope[0] + key_slope[1][:half], key_slope[1][half:]], axis=0)
            )
            value_parts.append(
                jnp.concatenate(
                    [value_slope[0] + value_slope[1][:half], value_slope[1][half:]], axis=0
                )
            )
        for i, (start, size, reach) in enumerate(query_spans(tokens)):
            span = slice(start, start + size)
            part = jnp.concatenate(query_parts[i], axis=1) * HEAD_SIZE**-0.5
            backs[span, qs] = turn_pairs(part, along[span], across[span], -1.0).astype(low)
        part = jnp.concatenate(key_parts, axis=1)
        spot = pl.ds(pl.multiple_of(width + g * 128, 128), 128)
        backs[:, spot] = turn_pairs(part, along, across, -1.0).astype(low)
        part = jnp.concatenate(value_parts, axis=1)
        spot = pl.ds(pl.multiple_of(width + key_width + g * 128, 128), 128)
        backs[:, spot] = part.astype(low)

        @pl.when(g == 1)
        def _():
            combine(0)

        return carry

    loops = key_width // 128
    lax.fori_loop(0, loops, heads, 0)
    done = 4 + 2 * loops
    own_piece.start()
    inputs = input_ref[...].astype(full)
    scale = lax.rsqrt(jnp.mean(inputs * inputs, axis=1, keepdims=True) + EPS)
    normed[...] = (inputs * scale * gain_ref[0:1, :]).astype(low)
    for at in range(0, joined, 512):
        delta[:, at : at + 512] = matmul(normed[...], backs[:, at : at + 512], TN).astype(low)
    exchange(1)
    tick(done, done + 1)
    slope = matmul(backs[...], weight_ref[:, :joined], NT)
    combine(1)
    tick(done + 1, done + 2)
    scaled = slope * gain_ref[0:1, :]
    first = jnp.sum(slope * inputs * scale, axis=0, keepdims=True)
    for owner in range(count):
        gain_buf[owner, 0:1, :] = first[:, owner * rows : (owner + 1) * rows]
        gain_buf[owner, 2:8, :] = jnp.zeros((6, rows), full)
    for k in range(1, count):
        gain_copy(k).start()
    result = (
        steep[...]
        + scale * scaled
        - inputs * (scale * scale * scale) * jnp.mean(inputs * scaled, axis=1, keepdims=True)
    )
    moved = matmul(place[...], result.astype(low), TN).astype(low)
    arrived[...] = moved.reshape(arrived.shape)
    for k in range(count - 1, 0, -1):
        slope_copy(k).start()
    slope_out[me] = arrived[me]
    tick(done + 2, done + 5)
    own_piece.wait()
    result = mixed_slope[...].astype(full)
    for turn in range(2, pairs):
        piece_copy(turn).wait_recv()
        result = result + far_piece[turn - 2].astype(full)
    out_ref[...] = result.astype(low)
    collect(0, 0, 2)
    if lined:
        sums.start(0, 2)
    total = gain_buf[me]
    for k in range(1, count):
        gain_copy(k).wait_recv()
        total = total + gain_recv[k]
    gain_sum[...] = total
    gain_line[rep] = total
    for k in range(1, reps):
        gain_line_copy(k).start()
    tick(done + 5, done + 9)
    collect(1, 2, 4)
    if lined:
        sums.start(2, 6)
        tick(done + 9, 3 * PARTS + LAG)
        sums.ticks(0, 6 + LAG)
        sums.finish()
    else:

        def spread_copy(k):
            return remote(
                owned, spread.at[rep], spread_send, spread_recv, k, (lax.rem(rep + k, reps), me)
            )

        for k in range(1, reps):
            spread_copy(k).start()
        spread[rep] = owned[...]
        for k in range(1, reps):
            spread_copy(k).wait_recv()
        value = spread[0].astype(full)
        for k in range(1, reps):
            value = value + spread[k].astype(full)
        delta_out[...] = value.astype(low)
        for k in range(1, reps):
            spread_copy(k).wait_send()
    for k in range(1, reps):
        gain_line_copy(k).wait_recv()
    total = gain_line[0]
    for k in range(1, reps):
        total = total + gain_line[k]
    gain_out[...] = total
    for k in range(1, count):
        slope_copy(k).wait_recv()
    for k in range(1, count):
        slope_copy(k).wait_send()
        gain_copy(k).wait_send()
    for turn in range(2, pairs):
        piece_copy(turn).wait_send()
    for part in range(2):
        for turn in range(pairs):
            pair_copy(part, turn).wait_send()
        for turn in range(1, pairs):
            far_copy(part, turn).wait_send()
    for k in range(1, reps):
        gain_line_copy(k).wait_send()
    if lined:
        line.finish()


def finish_pass(count, reps, back, slopes, *rest):
    *rest, pieces, extra = rest
    tokens, width = back.shape
    weights = rest[5]
    key_width = (weights.shape[1] - 2 * width) // 2
    pairs = count // 2
    rows = width // count
    block = tokens // count
    columns = weights.shape[1]
    low = jnp.bfloat16
    full = jnp.float32
    dma = pltpu.SemaphoreType.DMA
    vmem = pltpu.VMEM
    shape = jax.ShapeDtypeStruct
    lined = reps == LINE
    extra = [extra] if lined else []
    owned = (2 * columns // width, rows // 2, width)
    anywhere = pl.BlockSpec(memory_space=pl.ANY)
    inside = pl.BlockSpec(memory_space=pltpu.VMEM)
    if lined:
        last = line_scratch((3 * PARTS,) + extra[0].shape[1:]) + line_scratch(owned, False)
    else:
        last = [vmem((reps,) + owned, low), dma((reps,)), dma((reps,))]
    return pl.pallas_call(
        functools.partial(finish_kernel, count, reps),
        name="finish_pass",
        out_shape=(
            shape(owned, low),
            shape((8, rows), full),
            shape((count, block, width), low),
            shape((tokens, width), low),
        )
        + tuple(shape((3 * PARTS,) + d.shape[1:], low) for d in extra),
        in_specs=[inside, anywhere] + [inside] * len(rest) + [anywhere] * (1 + len(extra)),
        out_specs=(inside,) * 4 + (anywhere,) * len(extra),
        scratch_shapes=[
            vmem((tokens, tokens), low),
            vmem((tokens, tokens), full),
            vmem((tokens, width), low),
            vmem((tokens, width), full),
            vmem((tokens, width), low),
            vmem((tokens, width + 2 * key_width), low),
            vmem((count, block, width), low),
            vmem((pairs - 2, tokens, width), low),
            dma((pairs,)),
            dma((pairs,)),
            dma((2,)),
            vmem((width, columns), low),
            vmem((pairs, rows, columns), low),
            vmem((pairs - 1, rows, columns), low),
            vmem((pairs - 1, rows, columns), low),
            dma((2 * pairs,)),
            dma((2 * pairs,)),
            dma((2 * pairs,)),
            dma((2 * pairs,)),
            dma((count,)),
            dma((count,)),
            vmem((count, 8, rows), full),
            vmem((count, 8, rows), full),
            vmem((8, rows), full),
            vmem((reps, 8, rows), full),
            dma((count,)),
            dma((count,)),
            dma((reps,)),
            dma((reps,)),
            vmem(owned, low),
        ]
        + last,
        compiler_params=pltpu.CompilerParams(
            collective_id=6, has_side_effects=True, vmem_limit_bytes=VMEM_MOST
        ),
        cost_estimate=pl.CostEstimate(
            flops=24 << 30, bytes_accessed=1 << 24, transcendentals=1 << 22
        ),
    )(back, slopes, *rest, pieces, *extra)


def emit_kernel(
    tokens_ref,
    slopes_ref,
    gain_ref,
    delta_ref,
    early_ref,
    middle_ref,
    late_ref,
    tokens_out,
    slopes_out,
    first_out,
    query_out,
    key_out,
    value_out,
    output_out,
    second_out,
    gate_out,
    up_out,
    down_out,
):
    full = jnp.float32
    tokens_out[...] = tokens_ref[...]
    slopes_out[...] = slopes_ref[...]
    rows = early_ref.shape[1]
    hidden = gate_out.shape[3]
    for piece in range(2):
        to = slice(piece * rows, (piece + 1) * rows)
        spot = slice(piece * hidden, (piece + 1) * hidden)
        gate_out[0, 0, to, :] = middle_ref[0, 0, :, spot].astype(full)
        up_out[0, 0, to, :] = middle_ref[1, 0, :, spot].astype(full)
        gate_out[1, 0, to, :] = late_ref[0, 0, :, spot].astype(full)
        up_out[1, 0, to, :] = late_ref[1, 0, :, spot].astype(full)
    down_out[0, 0] = early_ref[0].astype(full)
    down_out[1, 0] = late_ref[2, 0].astype(full)

    @pl.when(pl.program_id(0) == 0)
    def _():
        first_out[...] = gain_ref[0:1, :]
        second_out[...] = gain_ref[1:2, :]
        half = delta_ref.shape[1]
        key_width = key_out.shape[1]
        for i in range(2):
            span = slice(i * half, (i + 1) * half)
            output_out[span, :] = delta_ref[i].astype(full)
            query_out[span, :] = delta_ref[2 + i].astype(full)
            key_out[span, :] = delta_ref[4 + i, :, :key_width].astype(full)
            value_out[span, :] = delta_ref[4 + i, :, key_width:].astype(full)


def emit_pass(tokens, slopes, gains, deltas, early, middle, late):
    full = jnp.float32
    shape = jax.ShapeDtypeStruct
    number, width = tokens.shape
    rows = gains.shape[1]
    _, high, wide = early.shape
    hidden = high * PARTS

    def moving(*block):
        return pl.BlockSpec(block, lambda i: (i,) + (0,) * (len(block) - 1))

    def fixed(*block):
        return pl.BlockSpec(block, lambda i: (0,) * len(block))

    def inner(*block):
        return pl.BlockSpec(block, lambda i: (0, i, 0, 0))

    return pl.pallas_call(
        emit_kernel,
        name="emit_pass",
        grid=(PARTS,),
        out_shape=(
            shape(tokens.shape, tokens.dtype),
            shape(slopes.shape, slopes.dtype),
            shape((1, rows), full),
            shape((rows, width), full),
            shape((rows, width // 2), full),
            shape((rows, width // 2), full),
            shape((rows, width), full),
            shape((1, rows), full),
            shape((2, PARTS, 2 * high, hidden), full),
            shape((2, PARTS, 2 * high, hidden), full),
            shape((2, PARTS, high, wide), full),
        ),
        in_specs=[
            moving(number // PARTS, width),
            moving(number // PARTS, width),
            fixed(*gains.shape),
            fixed(*deltas.shape),
            moving(1, high, wide),
            inner(2, 1, high, wide),
            inner(3, 1, high, wide),
        ],
        out_specs=(
            moving(number // PARTS, width),
            moving(number // PARTS, width),
            fixed(1, rows),
            fixed(rows, width),
            fixed(rows, width // 2),
            fixed(rows, width // 2),
            fixed(rows, width),
            fixed(1, rows),
            inner(2, 1, 2 * high, hidden),
            inner(2, 1, 2 * high, hidden),
            inner(2, 1, high, wide),
        ),
        compiler_params=pltpu.CompilerParams(vmem_limit_bytes=VMEM_MOST),
        cost_estimate=pl.CostEstimate(flops=1 << 20, bytes_accessed=1 << 24, transcendentals=0),
    )(
        tokens,
        slopes,
        gains,
        deltas,
        early,
        middle.reshape(2, PARTS, high, wide),
        late.reshape(3, PARTS, high, wide),
    )


def local(
    tokens,
    cotangent,
    seq_lengths,
    pack_order,
    unpack_order,
    expert_ids,
    gates,
    first_gain,
    query_weight,
    key_matrix,
    value_matrix,
    output_weight,
    second_gain,
    gate_weight,
    up_weight,
    down_weight,
):
    shards = lax.axis_size("shard")
    group_count, width = tokens.shape
    full = jnp.float32
    order = pack_order[:, None]
    gain_block = jnp.stack([first_gain, second_gain] + [jnp.zeros_like(first_gain)] * 6)
    arrived, joined, gains, mixing = first_pass(
        tokens,
        (query_weight, key_matrix, value_matrix, output_weight),
        gain_block.astype(full),
        order,
        expert_ids,
        gates,
        shards,
    )
    arrived = arrived.reshape(group_count, width)
    segment, place = segment_info(seq_lengths[0], group_count)
    cosine_table, sine_table = rope_tables(place, HEAD_SIZE)
    along = jnp.concatenate([cosine_table] * 4, axis=1)
    across = jnp.concatenate([-sine_table, sine_table] * 2, axis=1)
    tables = (order, segment[None, :], segment[:, None], along, across, joined, gains)
    (
        inputs,
        queries,
        keys,
        values,
        mixed,
        logsum,
        hidden,
        normed,
        shared,
        all_slopes,
    ) = attention_pass(shards, arrived, *tables, cotangent)
    reps = lax.axis_size("rep")
    inner, row_slopes, partial, *early = expert_pass(
        normed, all_slopes, mixing, gate_weight, up_weight, down_weight, shards, reps
    )
    back, pieces, *middle = return_pass(
        row_slopes, inner, gate_weight, up_weight, down_weight, shared, partial, shards, reps
    )
    deltas, gain_deltas, delta_tokens, out_tokens, *late = finish_pass(
        shards,
        reps,
        back,
        all_slopes,
        *tables,
        inputs,
        queries,
        keys,
        values,
        mixed,
        logsum,
        hidden,
        pieces,
        partial,
    )
    if reps == LINE:
        early, middle, late = early[0], middle[0], late[0]
    else:
        summed = lax.psum(partial, "rep")
        early, middle, late = summed[:PARTS], summed[PARTS : 3 * PARTS], summed[3 * PARTS :]
    (
        out_tokens,
        delta_tokens,
        delta_first,
        delta_query,
        delta_key,
        delta_value,
        delta_output,
        delta_second,
        delta_gate,
        delta_up,
        delta_down,
    ) = emit_pass(
        out_tokens, delta_tokens.reshape(group_count, width), gain_deltas, deltas, early, middle, late
    )
    return (
        out_tokens,
        delta_tokens,
        delta_first.reshape(first_gain.shape),
        delta_query,
        delta_key,
        delta_value,
        delta_output,
        delta_second.reshape(second_gain.shape),
        delta_gate.reshape(gate_weight.shape),
        delta_up.reshape(up_weight.shape),
        delta_down.reshape(down_weight.shape),
    )


def solution(mesh):
    placed = (
        P(("rep", "shard"), None),
        P(("rep", "shard"), None),
        P(("rep", "shard"), None),
        P(("rep", "shard")),
        P(("rep", "shard")),
        P(("rep", "shard"), None),
        P(("rep", "shard"), None),
        P("shard"),
        P("shard", None),
        P("shard", None),
        P("shard", None),
        P("shard", None),
        P("shard"),
        P("shard", None, None),
        P("shard", None, None),
        P("shard", None, None),
    )
    return jax.shard_map(
        local,
        mesh=mesh,
        in_specs=placed,
        out_specs=(
            P(("rep", "shard"), None),
            P(("rep", "shard"), None),
            P("shard"),
            P("shard", None),
            P("shard", None),
            P("shard", None),
            P("shard", None),
            P("shard"),
            P("shard", None, None),
            P("shard", None, None),
            P("shard", None, None),
        ),
        check_vma=False,
    )
```

```python
import functools

import jax
import jax.numpy as jnp
import numpy as np
from jax import lax
from jax.experimental import pallas as pl
from jax.experimental.pallas import tpu as pltpu
from jax.sharding import PartitionSpec as P

QUERY_HEADS = 16
KEY_VALUE_HEADS = 8
HEAD_SIZE = 64


EPS = 1e-05
THETA = 10000.0


MESH = pl.DeviceIdType.MESH
NN = (((1,), (0,)), ((), ()))
NT = (((1,), (1,)), ((), ()))
TN = (((0,), (0,)), ((), ()))
TILE = 256
VMEM_MOST = 66_000_000


def matmul(left, right, dims):
    return lax.dot_general(left, right, dims, preferred_element_type=jnp.float32)


def flip(number, mask, count):
    out = 0
    bit = 1
    while bit < count:
        a = (number // bit) % 2
        b = (mask // bit) % 2
        out = out + (a + b - 2 * a * b) * bit
        bit *= 2
    return out


def greet(me, rep, count, reps=1):
    barrier = pltpu.get_barrier_semaphore()
    for k in range(1, count):
        pl.semaphore_signal(
            barrier, inc=1, device_id=(rep, lax.rem(me + k, count)), device_id_type=MESH
        )
    for k in range(1, reps):
        pl.semaphore_signal(
            barrier, inc=1, device_id=(lax.rem(rep + k, reps), me), device_id_type=MESH
        )
    pl.semaphore_wait(barrier, count + reps - 2)


LINE = 4
LAG = 2
RING = 4


class Line:
    def __init__(
        self,
        rep,
        me,
        source,
        out,
        first,
        second,
        both,
        sends,
        recvs,
        held=None,
        sems=None,
        base=0,
        count=None,
    ):
        self.rep, self.me = rep, me
        self.source, self.out = source, out
        self.first, self.second, self.both = first, second, both
        self.sends, self.recvs = sends, recvs
        self.held, self.sems = held, sems
        self.base = base
        self.count = source.shape[0] if count is None else count
        self.outer = (rep == 0) | (rep == LINE - 1)
        self.inner = jnp.logical_not(self.outer)
        self.inside = jnp.where(rep == 0, 1, 2)
        self.outside = jnp.where(rep == 1, 0, 3)
        self.across = LINE - 1 - rep

    def copy(self, stage, i):
        ring = self.both.at[i % RING]
        if stage == 0:
            source = self.source.at[self.base + i]
        else:
            source = ring if stage == 1 else self.first.at[i]
        target = (self.first, self.second, self.first)[stage].at[i]
        device = (self.inside, self.across, self.outside)[stage]
        return pltpu.make_async_remote_copy(
            src_ref=source,
            dst_ref=target,
            send_sem=self.sends.at[stage, i],
            recv_sem=self.recvs.at[stage, i],
            device_id=(device, self.me),
            device_id_type=MESH,
        )

    def load(self, i):
        return pltpu.make_async_copy(
            self.source.at[self.base + i], self.held.at[i % 2], self.sems.at[self.count + i % 2]
        )

    def put(self, i):
        return pltpu.make_async_copy(self.first.at[i], self.out.at[i], self.sems.at[i])

    def loop(self, body, begin=0):
        def step(i, carry):
            body(i)
            return carry

        lax.fori_loop(begin, self.count, step, 0)

    def start(self, begin=0, end=None):
        end = self.count if end is None else end

        @pl.when(self.outer)
        def _():
            def step(i, carry):
                self.copy(0, i).start()
                return carry

            lax.fori_loop(begin, end, step, 0)

        if self.held is not None:

            @pl.when(self.inner)
            def _():
                self.load(0).start()

    def tick(self, j):
        full = jnp.float32
        low = jnp.bfloat16

        @pl.when(self.inner & (j >= 0) & (j < self.count))
        def _():
            if self.held is None:
                own = self.source[self.base + j]
            else:

                @pl.when(j + 1 < self.count)
                def _():
                    self.load(j + 1).start()

                self.load(j).wait()
                own = self.held[j % 2]
            self.copy(0, j).wait_recv()

            @pl.when(j >= RING)
            def _():
                self.copy(1, j - RING).wait_send()

            self.both[j % RING] = (own.astype(full) + self.first[j].astype(full)).astype(low)
            self.copy(1, j).start()

        i = j - LAG

        @pl.when(self.inner & (i >= 0) & (i < self.count))
        def _():
            self.copy(1, i).wait_recv()
            every = self.both[i % RING].astype(full) + self.second[i].astype(full)
            self.first[i] = every.astype(low)
            self.copy(2, i).start()
            if self.held is None:
                self.out[i] = every.astype(low)
            else:
                self.put(i).start()

    def ticks(self, begin, end):
        def step(j, carry):
            self.tick(j)
            return carry

        lax.fori_loop(begin, end, step, 0)

    def finish(self):
        @pl.when(self.outer)
        def _():
            def receive(i):
                self.copy(2, i).wait_recv()
                if self.held is None:
                    self.out[i] = self.first[i]
                else:
                    self.put(i).start()

            self.loop(receive)
            self.loop(lambda i: self.copy(0, i).wait_send())

        @pl.when(self.inner)
        def _():
            self.loop(lambda i: self.copy(1, i).wait_send(), self.count - RING)
            self.loop(lambda i: self.copy(2, i).wait_send())

        if self.held is not None:
            self.loop(lambda i: self.put(i).wait())


def line_scratch(shape, streamed=True):
    low = jnp.bfloat16
    dma = pltpu.SemaphoreType.DMA
    scratch = [
        pltpu.VMEM(shape, low),
        pltpu.VMEM(shape, low),
        pltpu.VMEM((RING,) + shape[1:], low),
        dma((3, shape[0])),
        dma((3, shape[0])),
    ]
    if streamed:
        scratch += [pltpu.VMEM((2,) + shape[1:], low), dma((shape[0] + 2,))]
    return scratch


def remote(source, target, sends, recvs, index, device):
    return pltpu.make_async_remote_copy(
        src_ref=source,
        dst_ref=target,
        send_sem=sends.at[index],
        recv_sem=recvs.at[index],
        device_id=device,
        device_id_type=MESH,
    )


class Gather:
    def __init__(self, count, rep, me, own, slot, sends, recvs):
        self.count, self.rep, self.me = count, rep, me
        self.own, self.slot, self.sends, self.recvs = own, slot, sends, recvs
        self.waiting = []

    def near(self, mask):
        return flip(self.me, mask, self.count)

    def send(self, source, owner, part, mask, index):
        remote(
            source,
            self.slot(owner, part),
            self.sends,
            self.recvs,
            index,
            (self.rep, self.near(mask)),
        ).start()
        self.waiting.append(index)

    def arrived(self, owner, part, index):
        remote(
            self.slot(owner, part),
            self.slot(owner, part),
            self.sends,
            self.recvs,
            index,
            (self.rep, self.me),
        ).wait_recv()

    def pass_on(self, mask, part, index, new, onward):
        owner = self.near(mask)
        if index is not None:
            self.arrived(owner, part, index)
        self.send(self.slot(owner, part), owner, part, onward, new)

    def start(self):
        if self.count == 8:
            plan = ((2, 0, 0), (4, 1, 1), (2, 1, 2), (4, 0, 3), (1, 0, 4), (1, 1, 5))
            for mask, part, index in plan:
                self.send(self.own(part), self.me, part, mask, index)
        else:
            for mask in [1] + list(range(2, self.count, 2)):
                for part in range(2):
                    self.send(self.own(part), self.me, part, mask, 2 * mask + part)

    def relay(self, stage):
        if self.count == 8:
            if stage == 0:
                self.pass_on(2, 0, 0, 6, 4)
                self.pass_on(4, 1, 1, 8, 2)
                self.pass_on(2, 0, None, 7, 1)
                self.pass_on(4, 1, None, 9, 1)
            elif stage == 1:
                self.pass_on(2, 1, 2, 10, 1)
                self.pass_on(4, 0, 3, 11, 1)
            else:
                self.pass_on(6, 0, 6, 12, 1)
                self.pass_on(6, 1, 8, 13, 1)
        elif stage == 2:
            for mask in range(2, self.count, 2):
                for part in range(2):
                    self.pass_on(mask, part, 2 * mask + part, 2 * mask + 2 + part, 1)

    def ready(self, masks):
        if self.count == 8:
            last = ((1, 0, 4), (1, 1, 5), (3, 0, 7), (5, 1, 9), (3, 1, 10), (5, 0, 11))
            last += ((7, 0, 12), (7, 1, 13))
        else:
            last = [(m, p, 2 * m + p) for m in range(1, self.count, 2) for p in range(2)]
        for mask, part, index in last:
            if mask in masks:
                self.arrived(self.near(mask), part, index)

    def finish(self, masks=None):
        self.ready(range(self.count) if masks is None else masks)
        for index in self.waiting:
            spot = self.slot(self.me, 0)
            remote(
                spot, spot, self.sends, self.recvs, index, (self.rep, self.me)
            ).wait_send()


PARTS = 8


def expert_kernel(count, reps, *refs):
    lined = reps == LINE
    own_ref, slope_ref, mix_ref, gate_ref, up_ref, down_ref = refs[:6]
    hidden_out, grad_out, delta_out = refs[6:9]
    refs = refs[9:]
    if lined:
        line_out = refs[0]
        refs = refs[1:]
    (
        rows,
        slope_buf,
        hidden_buf,
        grad_buf,
        acc_both,
        acc_down,
        stage,
        send_sem,
        recv_sem,
        own_sem,
        slope_sem,
        hidden_sem,
        grad_sem,
        stage_sem,
    ) = refs[:14]
    rep = lax.axis_index("rep")
    me = lax.axis_index("shard")
    experts, width, hidden = gate_ref.shape
    tokens = own_ref.shape[0]
    half = tokens // 2
    low = jnp.bfloat16
    turns = experts * count
    swap = 2 + count

    def pair(t):
        late = jnp.where(t < swap, t - 2, t - count)
        return (
            jnp.where(t < 4, t // 2, late),
            jnp.where(t < 4, t % 2, jnp.where(t < swap, 0, 1)),
        )

    def pack_of(t):
        return flip(me, pair(t)[0], count)

    def slope_copy(t):
        return pltpu.make_async_copy(
            slope_ref.at[:, pack_of(t)], slope_buf.at[t % 2], slope_sem.at[t % 2]
        )

    def hidden_copy(t):
        spot = pl.ds(pl.multiple_of(pair(t)[1] * hidden, hidden), hidden)
        return pltpu.make_async_copy(
            hidden_buf.at[t % 2], hidden_out.at[pack_of(t), :, spot], hidden_sem.at[t % 2]
        )

    def grad_copy(t):
        spot = pl.ds(pl.multiple_of(pair(t)[1] * 2 * hidden, 2 * hidden), 2 * hidden)
        return pltpu.make_async_copy(
            grad_buf.at[t % 2], grad_out.at[pack_of(t), :, spot], grad_sem.at[t % 2]
        )

    def stage_copy(e):
        span = pl.ds(e * 3 * PARTS, 3 * PARTS)
        return pltpu.make_async_copy(stage.at[span], delta_out.at[span], stage_sem.at[e])

    slope_copy(0).start()
    own = pltpu.make_async_copy(own_ref, rows.at[me], own_sem)
    own.start()
    greet(me, rep, count, reps if lined else 1)
    gather = Gather(
        count,
        rep,
        me,
        lambda p: own_ref.at[pl.ds(p * half, half)],
        lambda owner, p: rows.at[owner, pl.ds(p * half, half)],
        send_sem,
        recv_sem,
    )
    gather.start()
    own.wait()
    if lined:
        line = Line(rep, me, stage, line_out, *refs[14:], count=PARTS)

    def wrap_up(e):
        size = acc_down.shape[1] // PARTS
        side = acc_both.shape[1] // (2 * PARTS)
        base = e * 3 * PARTS
        for i in range(PARTS):
            down = base + (0 if e == 0 else 2 * PARTS) + i
            stage[down] = acc_down[e, i * size : (i + 1) * size, :].astype(low)
            for which in range(2):
                at = base + (PARTS if e == 0 else 0) + which * PARTS + i
                for piece in range(2):
                    span = slice((2 * i + piece) * side, (2 * i + piece + 1) * side)
                    stage[at, :, piece * hidden : (piece + 1) * hidden] = acc_both[
                        e, span, which * hidden : (which + 1) * hidden
                    ].astype(low)
        stage_copy(e).start()

    if count == 8:
        plan = {2: ((1,), 0), 4: ((), 1), 5: ((3,), None), 7: ((5,), 2), 9: ((7,), None)}
    else:
        plan = {2: ((1,), None), 4: ((), 2), 5: (tuple(range(3, count, 2)), None)}

    def step(t, carry):
        k, e = pair(t)
        pack = flip(me, k, count)
        for at, (masks, stage_at) in plan.items():

            @pl.when(t == at)
            def _():
                gather.ready(masks)
                if stage_at is not None:
                    gather.relay(stage_at)

        @pl.when(t + 1 < turns)
        def _():
            slope_copy(t + 1).start()

        if lined:
            line.ticks(2 * (t - swap - 1), 2 * (t - swap))
        slope_copy(t).wait()

        @pl.when(t >= 2)
        def _():
            hidden_copy(t - 2).wait()
            grad_copy(t - 2).wait()

        slot = t % 2
        x = rows[pack]
        dy = slope_buf[slot].reshape(tokens, width)
        mixes = jnp.transpose(mix_ref[pack])
        mix = jnp.where(e == 0, mixes[:, 0:1], mixes[:, 1:2])
        for part in range(hidden // TILE):
            span = pl.ds(part * TILE, TILE)
            ga = matmul(x, gate_ref[e, :, span], NN)
            ua = matmul(x, up_ref[e, :, span], NN)
            dh = matmul(dy, down_ref[e, span, :], NT) * mix
            sig = jax.nn.sigmoid(ga)
            act = ga * sig
            hidden_buf[slot, :, span] = (mix * (act * ua)).astype(low)
            grad_buf[slot, :, span] = (dh * ua * sig * (1.0 + ga * (1.0 - sig))).astype(low)
            grad_buf[slot, :, pl.ds(hidden + part * TILE, TILE)] = (dh * act).astype(low)
        hidden_copy(t).start()
        grad_copy(t).start()

        def add(acc, value):
            @pl.when(k == 0)
            def _():
                acc[e] = value

            @pl.when(k > 0)
            def _():
                acc[e] += value

        add(acc_both, matmul(x, grad_buf[slot], TN))
        add(acc_down, matmul(hidden_buf[slot], dy, TN))

        @pl.when(t == swap - 1)
        def _():
            wrap_up(0)
            if lined:
                line.start()

        return carry

    lax.fori_loop(0, turns, step, 0)
    wrap_up(1)
    if lined:
        line.ticks(2 * (turns - swap - 1), PARTS + LAG)
    for t in (turns - 2, turns - 1):
        hidden_copy(t).wait()
        grad_copy(t).wait()
    gather.finish(())
    stage_copy(0).wait()
    if lined:
        line.finish()
    stage_copy(1).wait()


def expert_pass(normed, all_slopes, mixing, gate_weight, up_weight, down_weight, count, reps):
    tokens, width = normed.shape
    experts, _, hidden = gate_weight.shape
    block = tokens // count
    low = jnp.bfloat16
    full = jnp.float32
    dma = pltpu.SemaphoreType.DMA
    vmem = pltpu.VMEM
    shape = jax.ShapeDtypeStruct
    anywhere = pl.BlockSpec(memory_space=pl.ANY)
    inside = pl.BlockSpec(memory_space=pltpu.VMEM)
    flops = 2 * count * tokens * width * hidden * experts * 6
    lined = reps == LINE
    segment = (hidden // PARTS, width)
    summed = (PARTS,) + segment
    return pl.pallas_call(
        functools.partial(expert_kernel, count, reps),
        name="expert_pass",
        out_shape=(
            shape((count, tokens, experts * hidden), low),
            shape((count, tokens, 2 * experts * hidden), low),
            shape((6 * PARTS,) + segment, low),
        )
        + ((shape(summed, low),) if lined else ()),
        in_specs=[inside, anywhere, inside, inside, inside, inside],
        out_specs=(anywhere,) * 3 + ((inside,) if lined else ()),
        scratch_shapes=[
            vmem((count, tokens, width), low),
            vmem((2, count, block, width), low),
            vmem((2, tokens, hidden), low),
            vmem((2, tokens, 2 * hidden), low),
            vmem((experts, width, 2 * hidden), full),
            vmem((experts, hidden, width), full),
            vmem((6 * PARTS,) + segment, low),
            dma((2 * count + 2,)),
            dma((2 * count + 2,)),
            dma,
            dma((2,)),
            dma((2,)),
            dma((2,)),
            dma((2,)),
        ]
        + (line_scratch(summed, False) if lined else []),
        compiler_params=pltpu.CompilerParams(
            collective_id=1, has_side_effects=True, vmem_limit_bytes=VMEM_MOST
        ),
        cost_estimate=pl.CostEstimate(flops=flops, bytes_accessed=1 << 26, transcendentals=0),
    )(
        normed,
        all_slopes.reshape(count, count, block, width),
        mixing,
        gate_weight,
        up_weight,
        down_weight,
    )


def return_kernel(count, reps, *refs):
    (
        grad_ref,
        hidden_ref,
        gate_ref,
        up_ref,
        down_ref,
        own_ref,
    ) = refs[:6]
    lined = reps == LINE
    refs = refs[6:]
    if lined:
        line_ref, back_ref, piece_out, line_out = refs[:4]
        refs = refs[4:]
    else:
        back_ref, piece_out = refs[:2]
        refs = refs[2:]
    (
        grad_buf,
        hidden_buf,
        pair_send,
        far_send,
        pair_recv,
        far_recv,
        total,
        piece,
        last_recv,
        relay_recv,
        load_sem,
        pair_send_sem,
        pair_recv_sem,
        far_send_sem,
        far_recv_sem,
        piece_sem,
        last_sem,
        relay_send_sem,
        relay_recv_sem,
    ) = refs[:19]
    rep = lax.axis_index("rep")
    me = lax.axis_index("shard")
    experts, width, hidden = gate_ref.shape
    tokens = own_ref.shape[0]
    block = tokens // count
    low = jnp.bfloat16
    full = jnp.float32
    pairs = count // 2
    partner = flip(me, 1, count)
    line = Line(rep, me, line_ref, line_out, *refs[19:], base=PARTS, count=2 * PARTS) if lined else None

    relayed = count == 8
    half = tokens // 2

    def mask_of(turn):
        rest = jnp.where(turn == 1, 0, count - 2 * turn)
        return jnp.where(turn == 0, count - 2, rest)

    def target(item):
        return flip(me, mask_of(item // 2) + 1 - item % 2, count)

    def grad_load(item):
        return pltpu.make_async_copy(
            grad_ref.at[target(item)], grad_buf.at[item % 2], load_sem.at[item % 2]
        )

    def grad_part(slot, pack):
        value = None
        for e in range(experts):
            for at, weight in ((2 * e, gate_ref), (2 * e + 1, up_ref)):
                term = matmul(grad_buf[slot, :, pl.ds(at * hidden, hidden)], weight[e], NT)
                value = term if value is None else value + term
        return value

    def hidden_load(item):
        return pltpu.make_async_copy(
            hidden_ref.at[:, target(item)], hidden_buf.at[item % 2], load_sem.at[item % 2]
        )

    def hidden_part(slot, pack):
        value = None
        for e in range(experts):
            term = matmul(
                hidden_buf[slot, :, :, pl.ds(e * hidden, hidden)].reshape(tokens, hidden),
                down_ref[e],
                NN,
            )
            value = term if value is None else value + term
        total[...] = value
        mine = pl.ds(pl.multiple_of(me * block, block), block)
        theirs = pl.ds(pl.multiple_of(pack * block, block), block)
        total[mine, :] += own_ref[theirs, :].astype(full)
        return total[...]

    def pair_copy(base, turn):
        return remote(
            pair_send.at[turn % 2],
            pair_recv.at[base + turn],
            pair_send_sem,
            pair_recv_sem,
            base + turn,
            (rep, partner),
        )

    def far_copy(turn, device):
        return remote(
            far_send.at[turn % 2], far_recv.at[turn], far_send_sem, far_recv_sem, turn, (rep, device)
        )

    grad_load(0).start()
    greet(me, rep, count, reps if lined else 1)
    if lined:
        line.start()

    def sweep(base, load, part, combine, tick):
        def turn_step(turn, carry):
            mask = mask_of(turn)
            load(2 * turn + 1).start()
            load(2 * turn).wait()
            value = part(0, flip(me, mask + 1, count))

            @pl.when(turn >= 2)
            def _():
                pair_copy(base, turn - 2).wait_send()

            pair_send[turn % 2] = value.astype(low)
            pair_copy(base, turn).start()

            @pl.when(turn + 1 < pairs)
            def _():
                load(2 * turn + 2).start()

            tick(2 * turn)
            load(2 * turn + 1).wait()
            total[...] = part(1, flip(me, mask, count))
            pair_copy(base, turn).wait_recv()
            combine(turn, mask)
            tick(2 * turn + 1)
            return carry

        lax.fori_loop(0, pairs, turn_step, 0)
        for turn in range(max(0, pairs - 2), pairs):
            pair_copy(base, turn).wait_send()

    def relay_copy(phase, side, source):
        return remote(
            source.at[pl.ds(side * half, half)],
            relay_recv.at[2 * phase + side],
            relay_send_sem,
            relay_recv_sem,
            2 * phase + side,
            (rep, flip(me, 2 + 2 * side, count)),
        )

    def grad_combine(turn, mask):
        @pl.when(turn == 1)
        def _():
            back_ref[...] = total[...] + pair_recv[1].astype(full)

        @pl.when(turn != 1)
        def _():
            if relayed:
                for side in range(2):

                    @pl.when(turn == 2 + side)
                    def _():
                        relay_copy(0, side, far_send.at[0]).wait_recv()
                        total[pl.ds(side * half, half), :] += relay_recv[side].astype(full)

            @pl.when(turn == 2)
            def _():
                if relayed:
                    for side in range(2):
                        relay_copy(0, side, far_send.at[0]).wait_send()
                else:
                    far_copy(0, me).wait_send()

            @pl.when(turn >= 4)
            def _():
                far_copy(turn - 2, me).wait_send()

            far_send[turn % 2] = (total[...] + pair_recv[turn].astype(full)).astype(low)

            @pl.when(turn == 0)
            def _():
                if relayed:
                    for side in range(2):
                        relay_copy(0, side, far_send.at[0]).start()
                else:
                    far_copy(0, flip(me, mask, count)).start()

            @pl.when(turn >= 2)
            def _():
                far_copy(turn, flip(me, mask, count)).start()

    def last_copy(device):
        return pltpu.make_async_remote_copy(
            src_ref=piece.at[0],
            dst_ref=last_recv,
            send_sem=last_sem.at[0],
            recv_sem=last_sem.at[1],
            device_id=(rep, device),
            device_id_type=MESH,
        )

    def slot(turn):
        return jnp.where(turn < 2, turn, 2 + turn % 2)

    def piece_copy(turn):
        return pltpu.make_async_copy(
            piece.at[slot(turn)], piece_out.at[turn], piece_sem.at[turn % 2]
        )

    def hidden_combine(turn, mask):
        if not relayed:

            @pl.when(turn >= 4)
            def _():
                piece_copy(turn - 2).wait()

        piece[slot(turn)] = (total[...] + pair_recv[pairs + turn].astype(full)).astype(low)

        @pl.when(turn == 0)
        def _():
            if relayed:
                for side in range(2):
                    relay_copy(1, side, piece.at[0]).start()
            else:
                last_copy(flip(me, mask, count)).start()

        if not relayed:

            @pl.when(turn >= 2)
            def _():
                piece_copy(turn).start()

    def early(j):
        if lined:
            line.tick(j - 2)

    def late(j):
        if lined:
            line.tick(2 * pairs + j - 2)

    sweep(0, grad_load, grad_part, grad_combine, early)
    hidden_load(0).start()
    sweep(pairs, hidden_load, hidden_part, hidden_combine, late)
    if lined:
        line.ticks(4 * pairs - 2, 2 * PARTS - 1)

    def add(turn, carry):
        far_copy(turn, me).wait_recv()
        back_ref[...] += far_recv[turn].astype(full)
        return carry

    if not relayed:
        add(0, 0)
    lax.fori_loop(2, pairs, add, 0)
    for turn in (pairs - 2, pairs - 1):
        far_copy(turn, me).wait_send()
    if lined:
        line.ticks(2 * PARTS - 1, 2 * PARTS + LAG)
    if relayed:
        for side in range(2):
            relay_copy(1, side, piece.at[0]).wait_recv()
            rows = pl.ds(side * half, half)
            value = piece[2 + side, rows, :].astype(full) + relay_recv[2 + side].astype(full)
            piece[2 + side, rows, :] = value.astype(low)
            piece_copy(2 + side).start()
            relay_copy(1, side, piece.at[0]).wait_send()
    else:
        last_copy(me).wait_recv()
        value = piece[1].astype(full) + last_recv[...].astype(full)
        piece[1] = value.astype(low)
        last_copy(me).wait_send()
    for turn in (pairs - 2, pairs - 1):
        piece_copy(turn).wait()
    piece_copy(1).start()
    if lined:
        line.finish()
    piece_copy(1).wait()


def return_pass(grads, hiddens, gate_weight, up_weight, down_weight, own, deltas, count, reps):
    tokens, width = own.shape
    experts, _, hidden = gate_weight.shape
    block = tokens // count
    low = jnp.bfloat16
    full = jnp.float32
    pairs = count // 2
    dma = pltpu.SemaphoreType.DMA
    shape = jax.ShapeDtypeStruct
    anywhere = pl.BlockSpec(memory_space=pl.ANY)
    inside = pl.BlockSpec(memory_space=pltpu.VMEM)
    flops = 2 * count * tokens * width * hidden * experts * 3
    lined = reps == LINE
    extra = [deltas] if lined else []
    return pl.pallas_call(
        functools.partial(return_kernel, count, reps),
        name="return_pass",
        out_shape=(
            shape((tokens, width), full),
            shape((pairs, tokens, width), low),
        )
        + tuple(shape((2 * PARTS,) + d.shape[1:], low) for d in extra),
        in_specs=[anywhere, anywhere] + [inside] * 4 + [anywhere] * len(extra),
        out_specs=(inside, anywhere) + (anywhere,) * len(extra),
        scratch_shapes=[
            pltpu.VMEM((2, tokens, 2 * experts * hidden), low),
            pltpu.VMEM((2, count, block, experts * hidden), low),
            pltpu.VMEM((2, tokens, width), low),
            pltpu.VMEM((2, tokens, width), low),
            pltpu.VMEM((2 * pairs, tokens, width), low),
            pltpu.VMEM((pairs, tokens, width), low),
            pltpu.VMEM((tokens, width), full),
            pltpu.VMEM((4, tokens, width), low),
            pltpu.VMEM((8, 128) if count == 8 else (tokens, width), low),
            pltpu.VMEM((4, tokens // 2, width), low),
            dma((2,)),
            dma((2 * pairs,)),
            dma((2 * pairs,)),
            dma((pairs,)),
            dma((pairs,)),
            dma((2,)),
            dma((3,)),
            dma((4,)),
            dma((4,)),
        ]
        + (line_scratch((2 * PARTS,) + deltas.shape[1:]) if lined else []),
        compiler_params=pltpu.CompilerParams(
            collective_id=2, has_side_effects=True, vmem_limit_bytes=VMEM_MOST
        ),
        cost_estimate=pl.CostEstimate(flops=flops, bytes_accessed=1 << 26, transcendentals=0),
    )(
        grads,
        hiddens.reshape(count, count, block, experts * hidden),
        gate_weight,
        up_weight,
        down_weight,
        own,
        *extra,
    )


def turn_pairs(rows, along, across, sign):
    lane = lax.broadcasted_iota(jnp.int32, (rows.shape[0], 128), 1)
    early = (lane % HEAD_SIZE) < HEAD_SIZE // 2
    pieces = []
    for at in range(0, rows.shape[1], 128):
        part = rows[:, at : at + 128]
        other = jnp.where(
            early,
            pltpu.roll(part, 128 - HEAD_SIZE // 2, 1),
            pltpu.roll(part, HEAD_SIZE // 2, 1),
        )
        pieces.append(part * along + sign * (other * across))
    return pieces[0] if len(pieces) == 1 else jnp.concatenate(pieces, axis=1)


def permutation(order_ref):
    tokens = order_ref.shape[1]
    rows = lax.broadcasted_iota(jnp.int32, (tokens, tokens), 0)
    return jnp.where(order_ref[...] == rows, 1.0, 0.0).astype(jnp.bfloat16)


def starts_of(position, length_ref):
    start = jnp.zeros_like(position)
    end = jnp.zeros((1, 1), jnp.int32)
    for k in range(length_ref.shape[1] - 1):
        end = end + length_ref[0:1, k : k + 1]
        start = jnp.where(position >= end, end, start)
    return start


def fill_bias(bias, length_ref):
    tokens = bias.shape[0]
    keys = lax.broadcasted_iota(jnp.int32, (tokens, tokens), 0)
    queries = lax.broadcasted_iota(jnp.int32, (tokens, tokens), 1)
    start = starts_of(lax.broadcasted_iota(jnp.int32, (1, tokens), 1), length_ref)
    bias[...] = jnp.where((keys >= start) & (keys <= queries), 0.0, -1e30)


def query_spans(tokens):
    half = tokens // 2
    return ((0, half, half), (half, half, tokens))


PARTS = 8


def expert_kernel(count, reps, *refs):
    lined = reps == LINE
    own_ref, slope_ref, mix_ref, gate_ref, up_ref, down_ref = refs[:6]
    hidden_out, grad_out, delta_out = refs[6:9]
    refs = refs[9:]
    if lined:
        line_out = refs[0]
        refs = refs[1:]
    (
        rows,
        slope_buf,
        hidden_buf,
        grad_buf,
        acc_both,
        acc_down,
        stage,
        send_sem,
        recv_sem,
        own_sem,
        slope_sem,
        hidden_sem,
        grad_sem,
        stage_sem,
    ) = refs[:14]
    rep = lax.axis_index("rep")
    me = lax.axis_index("shard")
    experts, width, hidden = gate_ref.shape
    tokens = own_ref.shape[0]
    half = tokens // 2
    low = jnp.bfloat16
    turns = experts * count
    swap = 2 + count

    def pair(t):
        late = jnp.where(t < swap, t - 2, t - count)
        return (
            jnp.where(t < 4, t // 2, late),
            jnp.where(t < 4, t % 2, jnp.where(t < swap, 0, 1)),
        )

    def pack_of(t):
        return flip(me, pair(t)[0], count)

    def slope_copy(t):
        return pltpu.make_async_copy(
            slope_ref.at[:, pack_of(t)], slope_buf.at[t % 2], slope_sem.at[t % 2]
        )

    def hidden_copy(t):
        spot = pl.ds(pl.multiple_of(pair(t)[1] * hidden, hidden), hidden)
        return pltpu.make_async_copy(
            hidden_buf.at[t % 2], hidden_out.at[pack_of(t), :, spot], hidden_sem.at[t % 2]
        )

    def grad_copy(t):
        spot = pl.ds(pl.multiple_of(pair(t)[1] * 2 * hidden, 2 * hidden), 2 * hidden)
        return pltpu.make_async_copy(
            grad_buf.at[t % 2], grad_out.at[pack_of(t), :, spot], grad_sem.at[t % 2]
        )

    def stage_copy(e):
        span = pl.ds(e * 3 * PARTS, 3 * PARTS)
        return pltpu.make_async_copy(stage.at[span], delta_out.at[span], stage_sem.at[e])

    slope_copy(0).start()
    own = pltpu.make_async_copy(own_ref, rows.at[me], own_sem)
    own.start()
    greet(me, rep, count, reps if lined else 1)
    gather = Gather(
        count,
        rep,
        me,
        lambda p: own_ref.at[pl.ds(p * half, half)],
        lambda owner, p: rows.at[owner, pl.ds(p * half, half)],
        send_sem,
        recv_sem,
    )
    gather.start()
    own.wait()
    if lined:
        line = Line(rep, me, stage, line_out, *refs[14:], count=PARTS)

    def wrap_up(e):
        size = acc_down.shape[1] // PARTS
        side = acc_both.shape[1] // (2 * PARTS)
        base = e * 3 * PARTS
        for i in range(PARTS):
            down = base + (0 if e == 0 else 2 * PARTS) + i
            stage[down] = acc_down[e, i * size : (i + 1) * size, :].astype(low)
            for which in range(2):
                at = base + (PARTS if e == 0 else 0) + which * PARTS + i
                for piece in range(2):
                    span = slice((2 * i + piece) * side, (2 * i + piece + 1) * side)
                    stage[at, :, piece * hidden : (piece + 1) * hidden] = acc_both[
                        e, span, which * hidden : (which + 1) * hidden
                    ].astype(low)
        stage_copy(e).start()

    if count == 8:
        plan = {2: ((1,), 0), 4: ((), 1), 5: ((3,), None), 7: ((5,), 2), 9: ((7,), None)}
    else:
        plan = {2: ((1,), None), 4: ((), 2), 5: (tuple(range(3, count, 2)), None)}

    def step(t, carry):
        k, e = pair(t)
        pack = flip(me, k, count)
        for at, (masks, stage_at) in plan.items():

            @pl.when(t == at)
            def _():
                gather.ready(masks)
                if stage_at is not None:
                    gather.relay(stage_at)

        @pl.when(t + 1 < turns)
        def _():
            slope_copy(t + 1).start()

        if lined:
            line.ticks(2 * (t - swap - 1), 2 * (t - swap))
        slope_copy(t).wait()

        @pl.when(t >= 2)
        def _():
            hidden_copy(t - 2).wait()
            grad_copy(t - 2).wait()

        slot = t % 2
        x = rows[pack]
        dy = slope_buf[slot].reshape(tokens, width)
        mixes = jnp.transpose(mix_ref[pack])
        mix = jnp.where(e == 0, mixes[:, 0:1], mixes[:, 1:2])
        for part in range(hidden // TILE):
            span = pl.ds(part * TILE, TILE)
            ga = matmul(x, gate_ref[e, :, span], NN)
            ua = matmul(x, up_ref[e, :, span], NN)
            dh = matmul(dy, down_ref[e, span, :], NT) * mix
            sig = jax.nn.sigmoid(ga)
            act = ga * sig
            hidden_buf[slot, :, span] = (mix * (act * ua)).astype(low)
            grad_buf[slot, :, span] = (dh * ua * sig * (1.0 + ga * (1.0 - sig))).astype(low)
            grad_buf[slot, :, pl.ds(hidden + part * TILE, TILE)] = (dh * act).astype(low)
        hidden_copy(t).start()
        grad_copy(t).start()

        def add(acc, value):
            @pl.when(k == 0)
            def _():
                acc[e] = value

            @pl.when(k > 0)
            def _():
                acc[e] += value

        add(acc_both, matmul(x, grad_buf[slot], TN))
        add(acc_down, matmul(hidden_buf[slot], dy, TN))

        @pl.when(t == swap - 1)
        def _():
            wrap_up(0)
            if lined:
                line.start()

        return carry

    lax.fori_loop(0, turns, step, 0)
    wrap_up(1)
    if lined:
        line.ticks(2 * (turns - swap - 1), PARTS + LAG)
    for t in (turns - 2, turns - 1):
        hidden_copy(t).wait()
        grad_copy(t).wait()
    gather.finish(())
    stage_copy(0).wait()
    if lined:
        line.finish()
    stage_copy(1).wait()


def expert_pass(normed, all_slopes, mixing, gate_weight, up_weight, down_weight, count, reps):
    tokens, width = normed.shape
    experts, _, hidden = gate_weight.shape
    block = tokens // count
    low = jnp.bfloat16
    full = jnp.float32
    dma = pltpu.SemaphoreType.DMA
    vmem = pltpu.VMEM
    shape = jax.ShapeDtypeStruct
    anywhere = pl.BlockSpec(memory_space=pl.ANY)
    inside = pl.BlockSpec(memory_space=pltpu.VMEM)
    flops = 2 * count * tokens * width * hidden * experts * 6
    lined = reps == LINE
    segment = (hidden // PARTS, width)
    summed = (PARTS,) + segment
    return pl.pallas_call(
        functools.partial(expert_kernel, count, reps),
        name="expert_pass",
        out_shape=(
            shape((count, tokens, experts * hidden), low),
            shape((count, tokens, 2 * experts * hidden), low),
            shape((6 * PARTS,) + segment, low),
        )
        + ((shape(summed, low),) if lined else ()),
        in_specs=[inside, anywhere, inside, inside, inside, inside],
        out_specs=(anywhere,) * 3 + ((inside,) if lined else ()),
        scratch_shapes=[
            vmem((count, tokens, width), low),
            vmem((2, count, block, width), low),
            vmem((2, tokens, hidden), low),
            vmem((2, tokens, 2 * hidden), low),
            vmem((experts, width, 2 * hidden), full),
            vmem((experts, hidden, width), full),
            vmem((6 * PARTS,) + segment, low),
            dma((2 * count + 2,)),
            dma((2 * count + 2,)),
            dma,
            dma((2,)),
            dma((2,)),
            dma((2,)),
            dma((2,)),
        ]
        + (line_scratch(summed, False) if lined else []),
        compiler_params=pltpu.CompilerParams(
            collective_id=1, has_side_effects=True, vmem_limit_bytes=VMEM_MOST
        ),
        cost_estimate=pl.CostEstimate(flops=flops, bytes_accessed=1 << 26, transcendentals=0),
    )(
        normed,
        all_slopes.reshape(count, count, block, width),
        mixing,
        gate_weight,
        up_weight,
        down_weight,
    )


def return_kernel(count, reps, *refs):
    (
        grad_ref,
        hidden_ref,
        gate_ref,
        up_ref,
        down_ref,
        own_ref,
    ) = refs[:6]
    lined = reps == LINE
    refs = refs[6:]
    if lined:
        line_ref, back_ref, piece_out, line_out = refs[:4]
        refs = refs[4:]
    else:
        back_ref, piece_out = refs[:2]
        refs = refs[2:]
    (
        grad_buf,
        hidden_buf,
        pair_send,
        far_send,
        pair_recv,
        far_recv,
        total,
        piece,
        last_recv,
        relay_recv,
        load_sem,
        pair_send_sem,
        pair_recv_sem,
        far_send_sem,
        far_recv_sem,
        piece_sem,
        last_sem,
        relay_send_sem,
        relay_recv_sem,
    ) = refs[:19]
    rep = lax.axis_index("rep")
    me = lax.axis_index("shard")
    experts, width, hidden = gate_ref.shape
    tokens = own_ref.shape[0]
    block = tokens // count
    low = jnp.bfloat16
    full = jnp.float32
    pairs = count // 2
    partner = flip(me, 1, count)
    line = Line(rep, me, line_ref, line_out, *refs[19:], base=PARTS, count=2 * PARTS) if lined else None

    relayed = count == 8
    half = tokens // 2

    def mask_of(turn):
        rest = jnp.where(turn == 1, 0, count - 2 * turn)
        return jnp.where(turn == 0, count - 2, rest)

    def target(item):
        return flip(me, mask_of(item // 2) + 1 - item % 2, count)

    def grad_load(item):
        return pltpu.make_async_copy(
            grad_ref.at[target(item)], grad_buf.at[item % 2], load_sem.at[item % 2]
        )

    def grad_part(slot, pack):
        value = None
        for e in range(experts):
            for at, weight in ((2 * e, gate_ref), (2 * e + 1, up_ref)):
                term = matmul(grad_buf[slot, :, pl.ds(at * hidden, hidden)], weight[e], NT)
                value = term if value is None else value + term
        return value

    def hidden_load(item):
        return pltpu.make_async_copy(
            hidden_ref.at[:, target(item)], hidden_buf.at[item % 2], load_sem.at[item % 2]
        )

    def hidden_part(slot, pack):
        value = None
        for e in range(experts):
            term = matmul(
                hidden_buf[slot, :, :, pl.ds(e * hidden, hidden)].reshape(tokens, hidden),
                down_ref[e],
                NN,
            )
            value = term if value is None else value + term
        total[...] = value
        mine = pl.ds(pl.multiple_of(me * block, block), block)
        theirs = pl.ds(pl.multiple_of(pack * block, block), block)
        total[mine, :] += own_ref[theirs, :].astype(full)
        return total[...]

    def pair_copy(base, turn):
        return remote(
            pair_send.at[turn % 2],
            pair_recv.at[base + turn],
            pair_send_sem,
            pair_recv_sem,
            base + turn,
            (rep, partner),
        )

    def far_copy(turn, device):
        return remote(
            far_send.at[turn % 2], far_recv.at[turn], far_send_sem, far_recv_sem, turn, (rep, device)
        )

    grad_load(0).start()
    greet(me, rep, count, reps if lined else 1)
    if lined:
        line.start()

    def sweep(base, load, part, combine, tick):
        def turn_step(turn, carry):
            mask = mask_of(turn)
            load(2 * turn + 1).start()
            load(2 * turn).wait()
            value = part(0, flip(me, mask + 1, count))

            @pl.when(turn >= 2)
            def _():
                pair_copy(base, turn - 2).wait_send()

            pair_send[turn % 2] = value.astype(low)
            pair_copy(base, turn).start()

            @pl.when(turn + 1 < pairs)
            def _():
                load(2 * turn + 2).start()

            tick(2 * turn)
            load(2 * turn + 1).wait()
            total[...] = part(1, flip(me, mask, count))
            pair_copy(base, turn).wait_recv()
            combine(turn, mask)
            tick(2 * turn + 1)
            return carry

        lax.fori_loop(0, pairs, turn_step, 0)
        for turn in range(max(0, pairs - 2), pairs):
            pair_copy(base, turn).wait_send()

    def relay_copy(phase, side, source):
        return remote(
            source.at[pl.ds(side * half, half)],
            relay_recv.at[2 * phase + side],
            relay_send_sem,
            relay_recv_sem,
            2 * phase + side,
            (rep, flip(me, 2 + 2 * side, count)),
        )

    def grad_combine(turn, mask):
        @pl.when(turn == 1)
        def _():
            back_ref[...] = total[...] + pair_recv[1].astype(full)

        @pl.when(turn != 1)
        def _():
            if relayed:
                for side in range(2):

                    @pl.when(turn == 2 + side)
                    def _():
                        relay_copy(0, side, far_send.at[0]).wait_recv()
                        total[pl.ds(side * half, half), :] += relay_recv[side].astype(full)

            @pl.when(turn == 2)
            def _():
                if relayed:
                    for side in range(2):
                        relay_copy(0, side, far_send.at[0]).wait_send()
                else:
                    far_copy(0, me).wait_send()

            @pl.when(turn >= 4)
            def _():
                far_copy(turn - 2, me).wait_send()

            far_send[turn % 2] = (total[...] + pair_recv[turn].astype(full)).astype(low)

            @pl.when(turn == 0)
            def _():
                if relayed:
                    for side in range(2):
                        relay_copy(0, side, far_send.at[0]).start()
                else:
                    far_copy(0, flip(me, mask, count)).start()

            @pl.when(turn >= 2)
            def _():
                far_copy(turn, flip(me, mask, count)).start()

    def last_copy(device):
        return pltpu.make_async_remote_copy(
            src_ref=piece.at[0],
            dst_ref=last_recv,
            send_sem=last_sem.at[0],
            recv_sem=last_sem.at[1],
            device_id=(rep, device),
            device_id_type=MESH,
        )

    def slot(turn):
        return jnp.where(turn < 2, turn, 2 + turn % 2)

    def piece_copy(turn):
        return pltpu.make_async_copy(
            piece.at[slot(turn)], piece_out.at[turn], piece_sem.at[turn % 2]
        )

    def hidden_combine(turn, mask):
        if not relayed:

            @pl.when(turn >= 4)
            def _():
                piece_copy(turn - 2).wait()

        piece[slot(turn)] = (total[...] + pair_recv[pairs + turn].astype(full)).astype(low)

        @pl.when(turn == 0)
        def _():
            if relayed:
                for side in range(2):
                    relay_copy(1, side, piece.at[0]).start()
            else:
                last_copy(flip(me, mask, count)).start()

        if not relayed:

            @pl.when(turn >= 2)
            def _():
                piece_copy(turn).start()

    def early(j):
        if lined:
            line.tick(j - 2)

    def late(j):
        if lined:
            line.tick(2 * pairs + j - 2)

    sweep(0, grad_load, grad_part, grad_combine, early)
    hidden_load(0).start()
    sweep(pairs, hidden_load, hidden_part, hidden_combine, late)
    if lined:
        line.ticks(4 * pairs - 2, 2 * PARTS - 1)

    def add(turn, carry):
        far_copy(turn, me).wait_recv()
        back_ref[...] += far_recv[turn].astype(full)
        return carry

    if not relayed:
        add(0, 0)
    lax.fori_loop(2, pairs, add, 0)
    for turn in (pairs - 2, pairs - 1):
        far_copy(turn, me).wait_send()
    if lined:
        line.ticks(2 * PARTS - 1, 2 * PARTS + LAG)
    if relayed:
        for side in range(2):
            relay_copy(1, side, piece.at[0]).wait_recv()
            rows = pl.ds(side * half, half)
            value = piece[2 + side, rows, :].astype(full) + relay_recv[2 + side].astype(full)
            piece[2 + side, rows, :] = value.astype(low)
            piece_copy(2 + side).start()
            relay_copy(1, side, piece.at[0]).wait_send()
    else:
        last_copy(me).wait_recv()
        value = piece[1].astype(full) + last_recv[...].astype(full)
        piece[1] = value.astype(low)
        last_copy(me).wait_send()
    for turn in (pairs - 2, pairs - 1):
        piece_copy(turn).wait()
    piece_copy(1).start()
    if lined:
        line.finish()
    piece_copy(1).wait()


def return_pass(grads, hiddens, gate_weight, up_weight, down_weight, own, deltas, count, reps):
    tokens, width = own.shape
    experts, _, hidden = gate_weight.shape
    block = tokens // count
    low = jnp.bfloat16
    full = jnp.float32
    pairs = count // 2
    dma = pltpu.SemaphoreType.DMA
    shape = jax.ShapeDtypeStruct
    anywhere = pl.BlockSpec(memory_space=pl.ANY)
    inside = pl.BlockSpec(memory_space=pltpu.VMEM)
    flops = 2 * count * tokens * width * hidden * experts * 3
    lined = reps == LINE
    extra = [deltas] if lined else []
    return pl.pallas_call(
        functools.partial(return_kernel, count, reps),
        name="return_pass",
        out_shape=(
            shape((tokens, width), full),
            shape((pairs, tokens, width), low),
        )
        + tuple(shape((2 * PARTS,) + d.shape[1:], low) for d in extra),
        in_specs=[anywhere, anywhere] + [inside] * 4 + [anywhere] * len(extra),
        out_specs=(inside, anywhere) + (anywhere,) * len(extra),
        scratch_shapes=[
            pltpu.VMEM((2, tokens, 2 * experts * hidden), low),
            pltpu.VMEM((2, count, block, experts * hidden), low),
            pltpu.VMEM((2, tokens, width), low),
            pltpu.VMEM((2, tokens, width), low),
            pltpu.VMEM((2 * pairs, tokens, width), low),
            pltpu.VMEM((pairs, tokens, width), low),
            pltpu.VMEM((tokens, width), full),
            pltpu.VMEM((4, tokens, width), low),
            pltpu.VMEM((8, 128) if count == 8 else (tokens, width), low),
            pltpu.VMEM((4, tokens // 2, width), low),
            dma((2,)),
            dma((2 * pairs,)),
            dma((2 * pairs,)),
            dma((pairs,)),
            dma((pairs,)),
            dma((2,)),
            dma((3,)),
            dma((4,)),
            dma((4,)),
        ]
        + (line_scratch((2 * PARTS,) + deltas.shape[1:]) if lined else []),
        compiler_params=pltpu.CompilerParams(
            collective_id=2, has_side_effects=True, vmem_limit_bytes=VMEM_MOST
        ),
        cost_estimate=pl.CostEstimate(flops=flops, bytes_accessed=1 << 26, transcendentals=0),
    )(
        grads,
        hiddens.reshape(count, count, block, experts * hidden),
        gate_weight,
        up_weight,
        down_weight,
        own,
        *extra,
    )


def turn_pairs(rows, along, across, sign):
    lane = lax.broadcasted_iota(jnp.int32, (rows.shape[0], 128), 1)
    early = (lane % HEAD_SIZE) < HEAD_SIZE // 2
    pieces = []
    for at in range(0, rows.shape[1], 128):
        part = rows[:, at : at + 128]
        other = jnp.where(
            early,
            pltpu.roll(part, 128 - HEAD_SIZE // 2, 1),
            pltpu.roll(part, HEAD_SIZE // 2, 1),
        )
        pieces.append(part * along + sign * (other * across))
    return pieces[0] if len(pieces) == 1 else jnp.concatenate(pieces, axis=1)


def permutation(order_ref):
    tokens = order_ref.shape[1]
    rows = lax.broadcasted_iota(jnp.int32, (tokens, tokens), 0)
    return jnp.where(order_ref[...] == rows, 1.0, 0.0).astype(jnp.bfloat16)


def starts_of(position, length_ref):
    start = jnp.zeros_like(position)
    end = jnp.zeros((1, 1), jnp.int32)
    for k in range(length_ref.shape[1] - 1):
        end = end + length_ref[0:1, k : k + 1]
        start = jnp.where(position >= end, end, start)
    return start


def fill_bias(bias, length_ref):
    tokens = bias.shape[0]
    keys = lax.broadcasted_iota(jnp.int32, (tokens, tokens), 0)
    queries = lax.broadcasted_iota(jnp.int32, (tokens, tokens), 1)
    start = starts_of(lax.broadcasted_iota(jnp.int32, (1, tokens), 1), length_ref)
    bias[...] = jnp.where((keys >= start) & (keys <= queries), 0.0, -1e30)


def query_spans(tokens):
    half = tokens // 2
    return ((0, half, half), (half, half, tokens))


def first_kernel(
    count,
    token_ref,
    query_ref,
    key_ref,
    value_ref,
    output_ref,
    gain_ref,
    order_ref,
    id_ref,
    gate_ref,
    arrived_out,
    joined_out,
    gain_out,
    mix_out,
    mix_buf,
    gain_buf,
    token_send,
    token_recv,
    gain_send,
    gain_recv,
    mix_send,
    mix_recv,
    weight_send,
    weight_recv,
    local_sem,
):
    rep = lax.axis_index("rep")
    me = lax.axis_index("shard")
    full = jnp.float32
    low = jnp.bfloat16
    rows = query_ref.shape[0]
    experts = mix_out.shape[0] * 2
    mine = pl.multiple_of(me * rows, rows)
    locals_ = [pltpu.make_async_copy(token_ref.at[me], arrived_out.at[me], local_sem.at[0])]
    at = 0
    for i, ref in enumerate((query_ref, key_ref, value_ref, output_ref)):
        size = ref.shape[1]
        target = joined_out.at[pl.ds(mine, rows), pl.ds(at, size)]
        locals_.append(pltpu.make_async_copy(ref, target, local_sem.at[1 + i]))
        at += size
    for copy in locals_:
        copy.start()
    greet(me, rep, count)

    def token_copy(k):
        target = flip(me, k, count)
        return remote(
            token_ref.at[target], arrived_out.at[me], token_send, token_recv, k, (rep, target)
        )

    def gain_copy(k):
        return remote(
            gain_ref, gain_buf.at[me], gain_send, gain_recv, k, (rep, flip(me, k, count))
        )

    def mix_copy(k):
        target = flip(me, k, count)
        return remote(mix_buf.at[target], mix_out.at[me], mix_send, mix_recv, k, (rep, target))

    for k in range(count - 1, 0, -1):
        token_copy(k).start()
    for copy in locals_[1:]:
        copy.wait()
    half = rows // 2

    def block(owner, part):
        return joined_out.at[pl.ds(pl.multiple_of(owner * rows + part * half, half), half)]

    weights = Gather(count, rep, me, lambda p: block(me, p), block, weight_send, weight_recv)
    weights.start()
    for k in range(1, count):
        gain_copy(k).start()
    gain_buf[me] = gain_ref[...]
    tokens = order_ref.shape[0]
    lane = lax.broadcasted_iota(jnp.int32, (tokens, experts), 1)
    mixing = jnp.zeros((tokens, experts), full)
    for k in range(id_ref.shape[1]):
        mixing = mixing + jnp.where(id_ref[:, k : k + 1] == lane, gate_ref[:, k : k + 1], 0.0)
    place = permutation(order_ref)
    moved = jnp.zeros((experts, tokens), full)
    for _ in range(3):
        high = mixing.astype(low)
        moved = moved + matmul(high, place, TN)
        mixing = mixing - high.astype(full)
    for owner in range(count):
        mix_buf[owner, 0:2, :] = moved[2 * owner : 2 * owner + 2, :]
        mix_buf[owner, 2:8, :] = jnp.zeros((6, tokens), full)
    weights.relay(0)
    for k in range(1, count):
        mix_copy(k).start()
    mix_out[me] = mix_buf[me]
    weights.relay(1)
    weights.relay(2)
    locals_[0].wait()
    for k in range(1, count):
        gain_copy(k).wait_recv()
    for owner in range(count):
        gain_out[:, owner * rows : (owner + 1) * rows] = gain_buf[owner]
    for k in range(1, count):
        token_copy(k).wait_recv()
        mix_copy(k).wait_recv()
    weights.finish()
    for k in range(1, count):
        token_copy(k).wait_send()
        gain_copy(k).wait_send()
        mix_copy(k).wait_send()


def first_pass(tokens, weights, gains, order, expert_ids, gates, count):
    rows = weights[0].shape[0]
    number, width = tokens.shape
    block = number // count
    low = jnp.bfloat16
    full = jnp.float32
    dma = pltpu.SemaphoreType.DMA
    inside = pl.BlockSpec(memory_space=pltpu.VMEM)
    columns = sum(w.shape[1] for w in weights)
    shape = jax.ShapeDtypeStruct
    return pl.pallas_call(
        functools.partial(first_kernel, count),
        name="first_pass",
        out_shape=(
            shape((count, block, width), low),
            shape((rows * count, columns), low),
            shape((8, rows * count), full),
            shape((count, 8, number), full),
        ),
        in_specs=[inside] * 9,
        out_specs=(inside,) * 4,
        scratch_shapes=[
            pltpu.VMEM((count, 8, number), full),
            pltpu.VMEM((count, 8, rows), full),
            dma((count,)),
            dma((count,)),
            dma((count,)),
            dma((count,)),
            dma((count,)),
            dma((count,)),
            dma((2 * count + 2,)),
            dma((2 * count + 2,)),
            dma((5,)),
        ],
        compiler_params=pltpu.CompilerParams(
            collective_id=4, has_side_effects=True, vmem_limit_bytes=VMEM_MOST
        ),
        cost_estimate=pl.CostEstimate(flops=1 << 24, bytes_accessed=1 << 26, transcendentals=0),
    )(tokens.reshape(count, block, width), *weights, gains, order, expert_ids, gates)


def front_kernel(
    count,
    token_ref,
    query_ref,
    key_ref,
    value_ref,
    output_ref,
    first_ref,
    second_ref,
    order_ref,
    id_ref,
    gate_ref,
    length_ref,
    speed_ref,
    cotangent_ref,
    joined_out,
    gain_out,
    mix_out,
    along_out,
    across_out,
    input_out,
    query_out,
    key_out,
    value_out,
    mixed_out,
    logsum_out,
    hidden_out,
    normed_out,
    shared_out,
    slopes_out,
    arrived,
    joined,
    mix_buf,
    gain_src,
    gain_buf,
    place,
    bias,
    normed,
    inputs,
    queries_all,
    keys_all,
    values_all,
    mixed,
    hidden,
    moved,
    shared,
    token_send,
    token_recv,
    gain_send,
    gain_recv,
    mix_send,
    mix_recv,
    weight_send,
    weight_recv,
    slope_send,
    slope_recv,
    local_sem,
    out_sem,
):
    rep = lax.axis_index("rep")
    me = lax.axis_index("shard")
    low = jnp.bfloat16
    full = jnp.float32
    rows = query_ref.shape[0]
    tokens, width = cotangent_ref.shape
    key_width = key_ref.shape[1]
    experts = mix_out.shape[0] * 2
    mine = pl.multiple_of(me * rows, rows)
    own = [pltpu.make_async_copy(token_ref.at[me], arrived.at[me], local_sem.at[0])]
    at = 0
    for i, ref in enumerate((query_ref, key_ref, value_ref, output_ref)):
        size = ref.shape[1]
        spot = joined.at[pl.ds(mine, rows), pl.ds(at, size)]
        own.append(pltpu.make_async_copy(ref, spot, local_sem.at[1 + i]))
        at += size
    own.append(pltpu.make_async_copy(cotangent_ref, slopes_out.at[me], local_sem.at[5]))
    for copy in own:
        copy.start()
    gain_src[...] = jnp.zeros(gain_src.shape, full)
    gain_src[0:1, :] = first_ref[...].astype(full)
    gain_src[1:2, :] = second_ref[...].astype(full)
    greet(me, rep, count)

    def token_copy(k):
        target = flip(me, k, count)
        return remote(
            token_ref.at[target], arrived.at[me], token_send, token_recv, k, (rep, target)
        )

    def gain_copy(k):
        return remote(
            gain_src, gain_buf.at[me], gain_send, gain_recv, k, (rep, flip(me, k, count))
        )

    def mix_copy(k):
        target = flip(me, k, count)
        return remote(mix_buf.at[target], mix_out.at[me], mix_send, mix_recv, k, (rep, target))

    for k in range(count - 1, 0, -1):
        token_copy(k).start()
    for copy in own[1:5]:
        copy.wait()
    half = rows // 2

    def block(owner, part):
        return joined.at[pl.ds(pl.multiple_of(owner * rows + part * half, half), half)]

    weights = Gather(count, rep, me, lambda p: block(me, p), block, weight_send, weight_recv)
    weights.start()
    for k in range(1, count):
        gain_copy(k).start()
    gain_buf[me] = gain_src[...]
    some = tokens // 2
    slopes = Gather(
        count,
        rep,
        me,
        lambda p: cotangent_ref.at[pl.ds(p * some, some)],
        lambda owner, p: slopes_out.at[owner, pl.ds(p * some, some)],
        slope_send,
        slope_recv,
    )
    kinds = lax.broadcasted_iota(jnp.int32, (experts, tokens), 0)
    mixing = jnp.zeros((experts, tokens), full)
    for k in range(id_ref.shape[0]):
        mixing = mixing + jnp.where(id_ref[k : k + 1, :] == kinds, gate_ref[k : k + 1, :], 0.0)
    place[...] = permutation(order_ref)
    dealt = jnp.zeros((experts, tokens), full)
    for _ in range(3):
        high = mixing.astype(low)
        dealt = dealt + matmul(high, place[...], NT)
        mixing = mixing - high.astype(full)
    for owner in range(count):
        mix_buf[owner, 0:2, :] = dealt[2 * owner : 2 * owner + 2, :]
        mix_buf[owner, 2:8, :] = jnp.zeros((6, tokens), full)
    weights.relay(0)
    for k in range(1, count):
        mix_copy(k).start()
    mix_out[me] = mix_buf[me]
    slopes.start()
    fill_bias(bias, length_ref)
    position = lax.broadcasted_iota(jnp.int32, along_out.shape, 0)
    angle = (position - starts_of(position, length_ref)).astype(full) * speed_ref[0:1, :]
    along_out[...] = jnp.cos(angle)
    across_out[...] = jnp.sin(angle) * speed_ref[1:2, :]
    own[0].wait()
    for k in range(1, count):
        token_copy(k).wait_recv()
        gain_copy(k).wait_recv()
    for owner in range(count):
        gain_out[:, owner * rows : (owner + 1) * rows] = gain_buf[owner]
    outs = (
        (inputs, input_out),
        (queries_all, query_out),
        (keys_all, key_out),
        (values_all, value_out),
        (mixed, mixed_out),
        (hidden, hidden_out),
        (moved, normed_out),
        (shared, shared_out),
        (joined, joined_out),
    )
    puts = [pltpu.make_async_copy(a, b, out_sem.at[k]) for k, (a, b) in enumerate(outs)]
    rows_in = matmul(place[...], arrived[...].reshape(tokens, width), TN)
    inputs[...] = rows_in.astype(low)
    scale = lax.rsqrt(jnp.mean(rows_in * rows_in, axis=1, keepdims=True) + EPS)
    normed[...] = (rows_in * scale * gain_out[0:1, :]).astype(low)
    puts[0].start()
    weights.relay(1)
    weights.relay(2)
    weights.ready(range(count))
    puts[8].start()
    along = along_out[...]
    across = across_out[...]
    for at in range(0, width, 512):
        part = matmul(normed[...], joined[:, at : at + 512], NN)
        queries_all[:, at : at + 512] = turn_pairs(part, along, across, 1.0).astype(low)
    part = matmul(normed[...], joined[:, width : width + key_width], NN)
    keys_all[...] = turn_pairs(part, along, across, 1.0).astype(low)
    part = matmul(normed[...], joined[:, width + key_width : width + 2 * key_width], NN)
    values_all[...] = part.astype(low)
    for copy in puts[1:4]:
        copy.start()

    def heads(g, carry):
        kv = pl.ds(pl.multiple_of(g * 128, 128), 128)
        qs = pl.ds(pl.multiple_of(g * 256, 256), 256)
        keys = keys_all[:, kv]
        values = values_all[:, kv]
        queries = queries_all[:, qs] * jnp.bfloat16(HEAD_SIZE**-0.5)
        for start, size, reach in query_spans(tokens):
            pieces = []
            for h in range(4):
                a = (h // 2) * HEAD_SIZE
                score = matmul(
                    keys[:reach, a : a + HEAD_SIZE],
                    queries[start : start + size, h * HEAD_SIZE : (h + 1) * HEAD_SIZE],
                    NT,
                )
                score = score + bias[:reach, start : start + size]
                largest = jnp.max(score, axis=0, keepdims=True)
                powers = jnp.exp(score - largest)
                totals = jnp.sum(powers, axis=0, keepdims=True)
                shares = (powers * (1.0 / totals)).astype(low)
                pieces.append(matmul(shares, values[:reach, a : a + HEAD_SIZE], TN))
                logsum_out[g, h : h + 1, start : start + size] = largest + jnp.log(totals)
            mixed[start : start + size, qs] = jnp.concatenate(pieces, axis=1).astype(low)

        @pl.when(g == 1)
        def _():
            slopes.relay(0)

        return carry

    lax.fori_loop(0, key_width // 128, heads, 0)
    puts[4].start()
    total = inputs[...].astype(full) + matmul(mixed[...], joined[:, width + 2 * key_width :], NN)
    hidden[...] = total
    scale = lax.rsqrt(jnp.mean(total * total, axis=1, keepdims=True) + EPS)
    normed[...] = (total * scale * gain_out[1:2, :]).astype(low)
    puts[5].start()
    moved[...] = matmul(place[...], normed[...], NN).astype(low)
    puts[6].start()
    shared[...] = matmul(place[...], hidden[...].astype(low), NN).astype(low)
    puts[7].start()
    slopes.relay(1)
    for k in range(1, count):
        mix_copy(k).wait_recv()
    for copy in puts:
        copy.wait()
    slopes.relay(2)
    own[5].wait()
    slopes.finish()
    weights.finish(())
    for k in range(1, count):
        token_copy(k).wait_send()
        gain_copy(k).wait_send()
        mix_copy(k).wait_send()


def front_pass(tokens, weights, gains, order, expert_ids, gates, lengths, cotangent, count):
    rows = weights[0].shape[0]
    number, width = tokens.shape
    key_width = weights[1].shape[1]
    block = number // count
    low = jnp.bfloat16
    full = jnp.float32
    dma = pltpu.SemaphoreType.DMA
    vmem = pltpu.VMEM
    anywhere = pl.BlockSpec(memory_space=pl.ANY)
    inside = pl.BlockSpec(memory_space=pltpu.VMEM)
    columns = sum(w.shape[1] for w in weights)
    shape = jax.ShapeDtypeStruct
    half = HEAD_SIZE // 2
    speed = np.tile(THETA ** (-2.0 * np.arange(half) / HEAD_SIZE), 128 // half)
    side = np.tile(np.repeat([-1.0, 1.0], half), 128 // HEAD_SIZE)
    speeds = jnp.asarray(np.stack([speed, side]).astype(np.float32))
    return pl.pallas_call(
        functools.partial(front_kernel, count),
        name="front_pass",
        out_shape=(
            shape((rows * count, columns), low),
            shape((8, rows * count), full),
            shape((count, 8, number), full),
            shape((number, 128), full),
            shape((number, 128), full),
            shape((number, width), low),
            shape((number, width), low),
            shape((number, key_width), low),
            shape((number, key_width), low),
            shape((number, width), low),
            shape((key_width // 128, 4, number), full),
            shape((number, width), full),
            shape((number, width), low),
            shape((number, width), low),
            shape((count, number, width), low),
        ),
        in_specs=[anywhere] * 5 + [inside] * 7 + [anywhere],
        out_specs=(anywhere,)
        + (inside,) * 4
        + (anywhere,) * 5
        + (inside,)
        + (anywhere,) * 4,
        scratch_shapes=[
            vmem((count, block, width), low),
            vmem((rows * count, columns), low),
            vmem((count, 8, number), full),
            vmem((8, rows), full),
            vmem((count, 8, rows), full),
            vmem((number, number), low),
            vmem((number, number), full),
            vmem((number, width), low),
            vmem((number, width), low),
            vmem((number, width), low),
            vmem((number, key_width), low),
            vmem((number, key_width), low),
            vmem((number, width), low),
            vmem((number, width), full),
            vmem((number, width), low),
            vmem((number, width), low),
            dma((count,)),
            dma((count,)),
            dma((count,)),
            dma((count,)),
            dma((count,)),
            dma((count,)),
            dma((2 * count + 2,)),
            dma((2 * count + 2,)),
            dma((2 * count + 2,)),
            dma((2 * count + 2,)),
            dma((6,)),
            dma((9,)),
        ],
        compiler_params=pltpu.CompilerParams(
            collective_id=4, has_side_effects=True, vmem_limit_bytes=VMEM_MOST
        ),
        cost_estimate=pl.CostEstimate(
            flops=12 << 30, bytes_accessed=1 << 26, transcendentals=1 << 22
        ),
    )(
        tokens.reshape(count, block, width),
        *weights,
        *(gain.reshape(1, rows) for gain in gains),
        order,
        expert_ids.T,
        gates.T,
        lengths,
        speeds,
        cotangent,
    )


def finish_kernel(count, reps, *refs):
    lined = reps == LINE
    (
        back_ref,
        slopes_ref,
        order_ref,
        length_ref,
        along_ref,
        across_ref,
        weight_ref,
        gain_ref,
        input_ref,
        query_ref,
        key_ref,
        value_ref,
        mixed_ref,
        logsum_ref,
        hidden_ref,
        piece_ref,
    ) = refs[:16]
    refs = refs[16:]
    staged = (
        back_ref,
        hidden_ref,
        mixed_ref,
        weight_ref,
        query_ref,
        key_ref,
        value_ref,
        input_ref,
    )
    held = refs[-len(staged) - 1 : -1]
    staging = [
        pltpu.make_async_copy(ref, buf, refs[-1].at[k])
        for k, (ref, buf) in enumerate(zip(staged, held, strict=True))
    ]
    refs = refs[: -len(staged) - 1]
    (
        back_ref,
        hidden_ref,
        mixed_ref,
        weight_ref,
        query_ref,
        key_ref,
        value_ref,
        input_ref,
    ) = held
    if lined:
        line_ref = refs[0]
        refs = refs[1:]
    delta_out, gain_out, slope_out, out_ref = refs[:4]
    refs = refs[4:]
    if lined:
        line_out = refs[0]
        refs = refs[1:]
    (
        place,
        bias,
        normed,
        steep,
        mixed_slope,
        backs,
        arrived,
        far_piece,
        far_piece_send,
        far_piece_recv,
        local_sem,
        delta,
        pair_recv,
        far_send,
        far_recv,
        pair_send_sem,
        pair_recv_sem,
        far_send_sem,
        far_recv_sem,
        slope_send_sem,
        slope_recv_sem,
        gain_buf,
        gain_recv,
        gain_sum,
        gain_line,
        gain_send_sem,
        gain_recv_sem,
        gain_line_send,
        gain_line_recv,
        owned,
    ) = refs[:30]
    refs = refs[30:]
    low = jnp.bfloat16
    full = jnp.float32
    rep = lax.axis_index("rep")
    me = lax.axis_index("shard")
    pairs = count // 2
    partner = flip(me, 1, count)
    tokens, width = back_ref.shape
    key_width = key_ref.shape[1]
    joined = width + 2 * key_width
    rows = width // count
    block = tokens // count
    own_slopes = pltpu.make_async_copy(
        slopes_ref.at[:, pl.ds(pl.multiple_of(me * block, block), block)],
        arrived,
        local_sem.at[0],
    )
    staging[0].start()
    own_slopes.start()
    for copy in staging[1:]:
        copy.start()
    own_piece = pltpu.make_async_copy(piece_ref.at[1], mixed_slope, local_sem.at[1])
    greet(me, rep, count, reps)
    if lined:
        line = Line(rep, me, line_ref, line_out, *refs[:7], base=3 * PARTS, count=3 * PARTS)
        sums = Line(rep, me, owned, delta_out, *refs[7:12])
        line.start()
    else:
        spread, spread_send, spread_recv = refs

    def tick(begin, end):
        if lined:
            line.ticks(begin, end)

    def piece_copy(turn):
        return remote(
            piece_ref.at[turn],
            far_piece.at[turn - 2],
            far_piece_send,
            far_piece_recv,
            turn,
            (rep, flip(me, count - 2 * turn, count)),
        )

    def rows_of(owner):
        return pl.ds(pl.multiple_of(owner * rows, rows), rows)

    columns = (slice(joined, joined + width), slice(0, joined))

    def pair_copy(part, turn):
        return remote(
            delta.at[rows_of(flip(partner, 2 * turn, count)), columns[part]],
            pair_recv.at[turn, :, columns[part]],
            pair_send_sem,
            pair_recv_sem,
            part * pairs + turn,
            (rep, partner),
        )

    def far_copy(part, turn):
        return remote(
            far_send.at[turn - 1, :, columns[part]],
            far_recv.at[turn - 1, :, columns[part]],
            far_send_sem,
            far_recv_sem,
            part * pairs + turn,
            (rep, flip(me, 2 * turn, count)),
        )

    def exchange(part):
        for turn in range(pairs - 1, -1, -1):
            pair_copy(part, turn).start()

    def combine(part):
        for turn in range(pairs - 1, 0, -1):
            pair_copy(part, turn).wait_recv()
            mine = delta[rows_of(flip(me, 2 * turn, count)), columns[part]].astype(full)
            far_send[turn - 1, :, columns[part]] = (
                mine + pair_recv[turn, :, columns[part]].astype(full)
            ).astype(low)
            far_copy(part, turn).start()

    def collect(part, first, number):
        pair_copy(part, 0).wait_recv()
        for turn in range(1, pairs):
            far_copy(part, turn).wait_recv()
        half = rows // 2
        for i in range(number):
            at = columns[part].start + (i // 2) * width
            span = slice((i % 2) * half, (i % 2 + 1) * half)
            value = delta[
                pl.ds(pl.multiple_of(me * rows + (i % 2) * half, half), half), at : at + width
            ].astype(full)
            value = value + pair_recv[0, span, at : at + width].astype(full)
            for turn in range(1, pairs):
                value = value + far_recv[turn - 1, span, at : at + width].astype(full)
            owned[first + i] = value.astype(low)

    def slope_copy(k):
        target = flip(me, k, count)
        return remote(
            arrived.at[target],
            slope_out.at[me],
            slope_send_sem,
            slope_recv_sem,
            k,
            (rep, target),
        )

    def gain_copy(k):
        target = flip(me, k, count)
        return remote(
            gain_buf.at[target], gain_recv.at[k], gain_send_sem, gain_recv_sem, k, (rep, target)
        )

    def gain_line_copy(k):
        return remote(
            gain_sum,
            gain_line.at[rep],
            gain_line_send,
            gain_line_recv,
            k,
            (lax.rem(rep + k, reps), me),
        )

    for turn in range(2, pairs):
        piece_copy(turn).start()
    place[...] = permutation(order_ref)
    fill_bias(bias, length_ref)
    own_slopes.wait()
    staging[0].wait()
    high = back_ref[...].astype(low)
    rest = (back_ref[...] - high.astype(full)).astype(low)
    slope = matmul(place[...], high, TN) + matmul(place[...], rest, TN)
    tick(0, 1)
    staging[1].wait()
    hidden = hidden_ref[...]
    scale = lax.rsqrt(jnp.mean(hidden * hidden, axis=1, keepdims=True) + EPS)
    scaled = slope * gain_ref[1:2, :]
    second = jnp.sum(slope * hidden * scale, axis=0, keepdims=True)
    for owner in range(count):
        gain_buf[owner, 1:2, :] = second[:, owner * rows : (owner + 1) * rows]
    steep[...] = (
        matmul(place[...], arrived[...].reshape(tokens, width), TN)
        + scale * scaled
        - hidden * (scale * scale * scale) * jnp.mean(hidden * scaled, axis=1, keepdims=True)
    )
    tick(1, 2)
    sharp = steep[...].astype(low)
    staging[2].wait()
    for at in range(0, width, 512):
        delta[:, joined + at : joined + at + 512] = matmul(
            mixed_ref[...], sharp[:, at : at + 512], TN
        ).astype(low)
    exchange(0)
    tick(2, 3)
    staging[3].wait()
    mixed_slope[...] = matmul(sharp, weight_ref[:, joined:], NT).astype(low)
    tick(3, 4)
    along = along_ref[...]
    across = across_ref[...]

    def heads(g, carry):
        kv = pl.ds(pl.multiple_of(g * 128, 128), 128)
        qs = pl.ds(pl.multiple_of(g * 256, 256), 256)
        keys = key_ref[:, kv]
        values = value_ref[:, kv]
        queries = query_ref[:, qs] * jnp.bfloat16(HEAD_SIZE**-0.5)
        slopes = mixed_slope[:, qs]
        key_parts = []
        value_parts = []
        query_parts = [[], []]
        for a in range(2):
            tick(4 + 2 * g + a, 5 + 2 * g + a)
            key_h = keys[:, a * HEAD_SIZE : (a + 1) * HEAD_SIZE]
            value_h = values[:, a * HEAD_SIZE : (a + 1) * HEAD_SIZE]
            key_slope = [None, None]
            value_slope = [None, None]
            for b in range(2):
                h = 2 * a + b
                spot = slice(h * HEAD_SIZE, (h + 1) * HEAD_SIZE)
                for i, (start, size, reach) in enumerate(query_spans(tokens)):
                    q = queries[start : start + size, spot]
                    d = slopes[start : start + size, spot]
                    score = matmul(key_h[:reach], q, NT) + bias[:reach, start : start + size]
                    probs = jnp.exp(score - logsum_ref[g, h : h + 1, start : start + size])
                    prob_slope = matmul(value_h[:reach], d, NT)
                    inner = jnp.sum(probs * prob_slope, axis=0, keepdims=True)
                    score_slope = (probs * (prob_slope - inner)).astype(low)
                    term = matmul(probs.astype(low), d, NN)
                    value_slope[i] = term if b == 0 else value_slope[i] + term
                    term = matmul(score_slope, q, NN)
                    key_slope[i] = term if b == 0 else key_slope[i] + term
                    query_parts[i].append(matmul(score_slope, key_h[:reach], TN))
            half = tokens // 2
            key_parts.append(
                jnp.concatenate([key_slope[0] + key_slope[1][:half], key_slope[1][half:]], axis=0)
            )
            value_parts.append(
                jnp.concatenate(
                    [value_slope[0] + value_slope[1][:half], value_slope[1][half:]], axis=0
                )
            )
        for i, (start, size, reach) in enumerate(query_spans(tokens)):
            span = slice(start, start + size)
            part = jnp.concatenate(query_parts[i], axis=1) * HEAD_SIZE**-0.5
            backs[span, qs] = turn_pairs(part, along[span], across[span], -1.0).astype(low)
        part = jnp.concatenate(key_parts, axis=1)
        spot = pl.ds(pl.multiple_of(width + g * 128, 128), 128)
        backs[:, spot] = turn_pairs(part, along, across, -1.0).astype(low)
        part = jnp.concatenate(value_parts, axis=1)
        spot = pl.ds(pl.multiple_of(width + key_width + g * 128, 128), 128)
        backs[:, spot] = part.astype(low)

        @pl.when(g == 1)
        def _():
            combine(0)

        return carry

    for copy in staging[4:]:
        copy.wait()
    loops = key_width // 128
    lax.fori_loop(0, loops, heads, 0)
    done = 4 + 2 * loops
    own_piece.start()
    inputs = input_ref[...].astype(full)
    scale = lax.rsqrt(jnp.mean(inputs * inputs, axis=1, keepdims=True) + EPS)
    normed[...] = (inputs * scale * gain_ref[0:1, :]).astype(low)
    for at in range(0, joined, 512):
        delta[:, at : at + 512] = matmul(normed[...], backs[:, at : at + 512], TN).astype(low)
    exchange(1)
    tick(done, done + 1)
    slope = matmul(backs[...], weight_ref[:, :joined], NT)
    combine(1)
    tick(done + 1, done + 2)
    scaled = slope * gain_ref[0:1, :]
    first = jnp.sum(slope * inputs * scale, axis=0, keepdims=True)
    for owner in range(count):
        gain_buf[owner, 0:1, :] = first[:, owner * rows : (owner + 1) * rows]
        gain_buf[owner, 2:8, :] = jnp.zeros((6, rows), full)
    for k in range(1, count):
        gain_copy(k).start()
    result = (
        steep[...]
        + scale * scaled
        - inputs * (scale * scale * scale) * jnp.mean(inputs * scaled, axis=1, keepdims=True)
    )
    moved = matmul(place[...], result.astype(low), NN).astype(low)
    arrived[...] = moved.reshape(arrived.shape)
    for k in range(count - 1, 0, -1):
        slope_copy(k).start()
    slope_out[me] = arrived[me]
    tick(done + 2, done + 5)
    own_piece.wait()
    result = mixed_slope[...].astype(full)
    for turn in range(2, pairs):
        piece_copy(turn).wait_recv()
        result = result + far_piece[turn - 2].astype(full)
    out_ref[...] = result.astype(low)
    collect(0, 0, 2)
    if lined:
        sums.start(0, 2)
    total = gain_buf[me]
    for k in range(1, count):
        gain_copy(k).wait_recv()
        total = total + gain_recv[k]
    gain_sum[...] = total
    gain_line[rep] = total
    for k in range(1, reps):
        gain_line_copy(k).start()
    tick(done + 5, done + 9)
    collect(1, 2, 4)
    if lined:
        sums.start(2, 6)
        tick(done + 9, 3 * PARTS + LAG)
        sums.ticks(0, 6 + LAG)
        sums.finish()
    else:

        def spread_copy(k):
            return remote(
                owned, spread.at[rep], spread_send, spread_recv, k, (lax.rem(rep + k, reps), me)
            )

        for k in range(1, reps):
            spread_copy(k).start()
        spread[rep] = owned[...]
        for k in range(1, reps):
            spread_copy(k).wait_recv()
        value = spread[0].astype(full)
        for k in range(1, reps):
            value = value + spread[k].astype(full)
        delta_out[...] = value.astype(low)
        for k in range(1, reps):
            spread_copy(k).wait_send()
    for k in range(1, reps):
        gain_line_copy(k).wait_recv()
    total = gain_line[0]
    for k in range(1, reps):
        total = total + gain_line[k]
    gain_out[...] = total
    for k in range(1, count):
        slope_copy(k).wait_recv()
    for k in range(1, count):
        slope_copy(k).wait_send()
        gain_copy(k).wait_send()
    for turn in range(2, pairs):
        piece_copy(turn).wait_send()
    for part in range(2):
        for turn in range(pairs):
            pair_copy(part, turn).wait_send()
        for turn in range(1, pairs):
            far_copy(part, turn).wait_send()
    for k in range(1, reps):
        gain_line_copy(k).wait_send()
    if lined:
        line.finish()


def finish_pass(count, reps, back, slopes, *rest):
    *rest, pieces, extra = rest
    tokens, width = back.shape
    weights = rest[4]
    key_width = (weights.shape[1] - 2 * width) // 2
    pairs = count // 2
    rows = width // count
    block = tokens // count
    columns = weights.shape[1]
    low = jnp.bfloat16
    full = jnp.float32
    dma = pltpu.SemaphoreType.DMA
    vmem = pltpu.VMEM
    shape = jax.ShapeDtypeStruct
    lined = reps == LINE
    extra = [extra] if lined else []
    owned = (2 * columns // width, rows // 2, width)
    anywhere = pl.BlockSpec(memory_space=pl.ANY)
    inside = pl.BlockSpec(memory_space=pltpu.VMEM)
    if lined:
        last = line_scratch((3 * PARTS,) + extra[0].shape[1:]) + line_scratch(owned, False)
    else:
        last = [vmem((reps,) + owned, low), dma((reps,)), dma((reps,))]
    return pl.pallas_call(
        functools.partial(finish_kernel, count, reps),
        name="finish_pass",
        out_shape=(
            shape(owned, low),
            shape((8, rows), full),
            shape((count, block, width), low),
            shape((tokens, width), low),
        )
        + tuple(shape((3 * PARTS,) + d.shape[1:], low) for d in extra),
        in_specs=[anywhere, anywhere]
        + [inside] * 4
        + [anywhere, inside]
        + [anywhere] * 5
        + [inside]
        + [anywhere] * (2 + len(extra)),
        out_specs=(inside,) * 4 + (anywhere,) * len(extra),
        scratch_shapes=[
            vmem((tokens, tokens), low),
            vmem((tokens, tokens), full),
            vmem((tokens, width), low),
            vmem((tokens, width), full),
            vmem((tokens, width), low),
            vmem((tokens, width + 2 * key_width), low),
            vmem((count, block, width), low),
            vmem((pairs - 2, tokens, width), low),
            dma((pairs,)),
            dma((pairs,)),
            dma((2,)),
            vmem((width, columns), low),
            vmem((pairs, rows, columns), low),
            vmem((pairs - 1, rows, columns), low),
            vmem((pairs - 1, rows, columns), low),
            dma((2 * pairs,)),
            dma((2 * pairs,)),
            dma((2 * pairs,)),
            dma((2 * pairs,)),
            dma((count,)),
            dma((count,)),
            vmem((count, 8, rows), full),
            vmem((count, 8, rows), full),
            vmem((8, rows), full),
            vmem((reps, 8, rows), full),
            dma((count,)),
            dma((count,)),
            dma((reps,)),
            dma((reps,)),
            vmem(owned, low),
        ]
        + last
        + [
            vmem(a.shape, a.dtype)
            for a in (back, rest[12], rest[10], weights, rest[7], rest[8], rest[9], rest[6])
        ]
        + [dma((8,))],
        compiler_params=pltpu.CompilerParams(
            collective_id=6, has_side_effects=True, vmem_limit_bytes=VMEM_MOST
        ),
        cost_estimate=pl.CostEstimate(
            flops=24 << 30, bytes_accessed=1 << 24, transcendentals=1 << 22
        ),
    )(back, slopes, *rest, pieces, *extra)


def emit_kernel(
    tokens_ref,
    slopes_ref,
    gain_ref,
    delta_ref,
    early_ref,
    middle_ref,
    late_ref,
    tokens_out,
    slopes_out,
    first_out,
    query_out,
    key_out,
    value_out,
    output_out,
    second_out,
    gate_out,
    up_out,
    down_out,
):
    full = jnp.float32
    tokens_out[...] = tokens_ref[...]
    slopes_out[...] = slopes_ref[...]
    rows = early_ref.shape[1]
    hidden = gate_out.shape[3]
    for piece in range(2):
        to = slice(piece * rows, (piece + 1) * rows)
        spot = slice(piece * hidden, (piece + 1) * hidden)
        gate_out[0, 0, to, :] = middle_ref[0, 0, :, spot].astype(full)
        up_out[0, 0, to, :] = middle_ref[1, 0, :, spot].astype(full)
        gate_out[1, 0, to, :] = late_ref[0, 0, :, spot].astype(full)
        up_out[1, 0, to, :] = late_ref[1, 0, :, spot].astype(full)
    down_out[0, 0] = early_ref[0].astype(full)
    down_out[1, 0] = late_ref[2, 0].astype(full)

    @pl.when(pl.program_id(0) == 0)
    def _():
        first_out[...] = gain_ref[0:1, :]
        second_out[...] = gain_ref[1:2, :]
        half = delta_ref.shape[1]
        key_width = key_out.shape[1]
        for i in range(2):
            span = slice(i * half, (i + 1) * half)
            output_out[span, :] = delta_ref[i].astype(full)
            query_out[span, :] = delta_ref[2 + i].astype(full)
            key_out[span, :] = delta_ref[4 + i, :, :key_width].astype(full)
            value_out[span, :] = delta_ref[4 + i, :, key_width:].astype(full)


def emit_pass(tokens, slopes, gains, deltas, early, middle, late):
    full = jnp.float32
    shape = jax.ShapeDtypeStruct
    number, width = tokens.shape
    rows = gains.shape[1]
    _, high, wide = early.shape
    hidden = high * PARTS

    def moving(*block):
        return pl.BlockSpec(block, lambda i: (i,) + (0,) * (len(block) - 1))

    def fixed(*block):
        return pl.BlockSpec(block, lambda i: (0,) * len(block))

    def inner(*block):
        return pl.BlockSpec(block, lambda i: (0, i, 0, 0))

    return pl.pallas_call(
        emit_kernel,
        name="emit_pass",
        grid=(PARTS,),
        out_shape=(
            shape(tokens.shape, tokens.dtype),
            shape(slopes.shape, slopes.dtype),
            shape((1, rows), full),
            shape((rows, width), full),
            shape((rows, width // 2), full),
            shape((rows, width // 2), full),
            shape((rows, width), full),
            shape((1, rows), full),
            shape((2, PARTS, 2 * high, hidden), full),
            shape((2, PARTS, 2 * high, hidden), full),
            shape((2, PARTS, high, wide), full),
        ),
        in_specs=[
            moving(number // PARTS, width),
            moving(number // PARTS, width),
            fixed(*gains.shape),
            fixed(*deltas.shape),
            moving(1, high, wide),
            inner(2, 1, high, wide),
            inner(3, 1, high, wide),
        ],
        out_specs=(
            moving(number // PARTS, width),
            moving(number // PARTS, width),
            fixed(1, rows),
            fixed(rows, width),
            fixed(rows, width // 2),
            fixed(rows, width // 2),
            fixed(rows, width),
            fixed(1, rows),
            inner(2, 1, 2 * high, hidden),
            inner(2, 1, 2 * high, hidden),
            inner(2, 1, high, wide),
        ),
        compiler_params=pltpu.CompilerParams(vmem_limit_bytes=VMEM_MOST),
        cost_estimate=pl.CostEstimate(flops=1 << 20, bytes_accessed=1 << 24, transcendentals=0),
    )(
        tokens,
        slopes,
        gains,
        deltas,
        early,
        middle.reshape(2, PARTS, high, wide),
        late.reshape(3, PARTS, high, wide),
    )


def local(
    tokens,
    cotangent,
    seq_lengths,
    pack_order,
    unpack_order,
    expert_ids,
    gates,
    first_gain,
    query_weight,
    key_matrix,
    value_matrix,
    output_weight,
    second_gain,
    gate_weight,
    up_weight,
    down_weight,
):
    shards = lax.axis_size("shard")
    group_count, width = tokens.shape
    order = pack_order.reshape(1, group_count)
    (
        joined,
        gains,
        mixing,
        along,
        across,
        inputs,
        queries,
        keys,
        values,
        mixed,
        logsum,
        hidden,
        normed,
        shared,
        all_slopes,
    ) = front_pass(
        tokens,
        (query_weight, key_matrix, value_matrix, output_weight),
        (first_gain, second_gain),
        order,
        expert_ids,
        gates,
        seq_lengths,
        cotangent,
        shards,
    )
    tables = (order, seq_lengths, along, across, joined, gains)
    reps = lax.axis_size("rep")
    inner, row_slopes, partial, *early = expert_pass(
        normed, all_slopes, mixing, gate_weight, up_weight, down_weight, shards, reps
    )
    back, pieces, *middle = return_pass(
        row_slopes, inner, gate_weight, up_weight, down_weight, shared, partial, shards, reps
    )
    deltas, gain_deltas, delta_tokens, out_tokens, *late = finish_pass(
        shards,
        reps,
        back,
        all_slopes,
        *tables,
        inputs,
        queries,
        keys,
        values,
        mixed,
        logsum,
        hidden,
        pieces,
        partial,
    )
    if reps == LINE:
        early, middle, late = early[0], middle[0], late[0]
    else:
        summed = lax.psum(partial, "rep")
        early, middle, late = summed[:PARTS], summed[PARTS : 3 * PARTS], summed[3 * PARTS :]
    (
        out_tokens,
        delta_tokens,
        delta_first,
        delta_query,
        delta_key,
        delta_value,
        delta_output,
        delta_second,
        delta_gate,
        delta_up,
        delta_down,
    ) = emit_pass(
        out_tokens, delta_tokens.reshape(group_count, width), gain_deltas, deltas, early, middle, late
    )
    return (
        out_tokens,
        delta_tokens,
        delta_first.reshape(first_gain.shape),
        delta_query,
        delta_key,
        delta_value,
        delta_output,
        delta_second.reshape(second_gain.shape),
        delta_gate.reshape(gate_weight.shape),
        delta_up.reshape(up_weight.shape),
        delta_down.reshape(down_weight.shape),
    )


def solution(mesh):
    placed = (
        P(("rep", "shard"), None),
        P(("rep", "shard"), None),
        P(("rep", "shard"), None),
        P(("rep", "shard")),
        P(("rep", "shard")),
        P(("rep", "shard"), None),
        P(("rep", "shard"), None),
        P("shard"),
        P("shard", None),
        P("shard", None),
        P("shard", None),
        P("shard", None),
        P("shard"),
        P("shard", None, None),
        P("shard", None, None),
        P("shard", None, None),
    )
    return jax.shard_map(
        local,
        mesh=mesh,
        in_specs=placed,
        out_specs=(
            P(("rep", "shard"), None),
            P(("rep", "shard"), None),
            P("shard"),
            P("shard", None),
            P("shard", None),
            P("shard", None),
            P("shard", None),
            P("shard"),
            P("shard", None, None),
            P("shard", None, None),
            P("shard", None, None),
        ),
        check_vma=False,
    )
```

```python
import functools

import jax
import jax.numpy as jnp
import numpy as np
from jax import lax
from jax.experimental import pallas as pl
from jax.experimental.pallas import tpu as pltpu
from jax.sharding import PartitionSpec as P

QUERY_HEADS = 16
KEY_VALUE_HEADS = 8
HEAD_SIZE = 64


EPS = 1e-05
THETA = 10000.0


MESH = pl.DeviceIdType.MESH
NN = (((1,), (0,)), ((), ()))
NT = (((1,), (1,)), ((), ()))
TN = (((0,), (0,)), ((), ()))
TILE = 256
VMEM_MOST = 66_000_000


def matmul(left, right, dims):
    return lax.dot_general(left, right, dims, preferred_element_type=jnp.float32)


def stage_in(refs, count, start=0):
    held = refs[-count - 1 : -1]
    copies = [
        pltpu.make_async_copy(refs[start + k], held[k], refs[-1].at[k]) for k in range(count)
    ]
    return held, copies, refs[: -count - 1]


def flip(number, mask, count):
    out = 0
    bit = 1
    while bit < count:
        a = (number // bit) % 2
        b = (mask // bit) % 2
        out = out + (a + b - 2 * a * b) * bit
        bit *= 2
    return out


def greet(me, rep, count, reps=1):
    barrier = pltpu.get_barrier_semaphore()
    for k in range(1, count):
        pl.semaphore_signal(
            barrier, inc=1, device_id=(rep, lax.rem(me + k, count)), device_id_type=MESH
        )
    for k in range(1, reps):
        pl.semaphore_signal(
            barrier, inc=1, device_id=(lax.rem(rep + k, reps), me), device_id_type=MESH
        )
    pl.semaphore_wait(barrier, count + reps - 2)


LINE = 4
LAG = 2
RING = 4


class Line:
    def __init__(
        self,
        rep,
        me,
        source,
        out,
        first,
        second,
        both,
        sends,
        recvs,
        held=None,
        sems=None,
        base=0,
        count=None,
    ):
        self.rep, self.me = rep, me
        self.source, self.out = source, out
        self.first, self.second, self.both = first, second, both
        self.sends, self.recvs = sends, recvs
        self.held, self.sems = held, sems
        self.base = base
        self.count = source.shape[0] if count is None else count
        self.outer = (rep == 0) | (rep == LINE - 1)
        self.inner = jnp.logical_not(self.outer)
        self.inside = jnp.where(rep == 0, 1, 2)
        self.outside = jnp.where(rep == 1, 0, 3)
        self.across = LINE - 1 - rep

    def copy(self, stage, i):
        ring = self.both.at[i % RING]
        if stage == 0:
            source = self.source.at[self.base + i]
        else:
            source = ring if stage == 1 else self.first.at[i]
        target = (self.first, self.second, self.first)[stage].at[i]
        device = (self.inside, self.across, self.outside)[stage]
        return pltpu.make_async_remote_copy(
            src_ref=source,
            dst_ref=target,
            send_sem=self.sends.at[stage, i],
            recv_sem=self.recvs.at[stage, i],
            device_id=(device, self.me),
            device_id_type=MESH,
        )

    def load(self, i):
        return pltpu.make_async_copy(
            self.source.at[self.base + i], self.held.at[i % 2], self.sems.at[self.count + i % 2]
        )

    def put(self, i):
        return pltpu.make_async_copy(self.first.at[i], self.out.at[i], self.sems.at[i])

    def loop(self, body, begin=0):
        def step(i, carry):
            body(i)
            return carry

        lax.fori_loop(begin, self.count, step, 0)

    def start(self, begin=0, end=None):
        end = self.count if end is None else end

        @pl.when(self.outer)
        def _():
            def step(i, carry):
                self.copy(0, i).start()
                return carry

            lax.fori_loop(begin, end, step, 0)

        if self.held is not None:

            @pl.when(self.inner)
            def _():
                self.load(0).start()

    def tick(self, j):
        full = jnp.float32
        low = jnp.bfloat16

        @pl.when(self.inner & (j >= 0) & (j < self.count))
        def _():
            if self.held is None:
                own = self.source[self.base + j]
            else:

                @pl.when(j + 1 < self.count)
                def _():
                    self.load(j + 1).start()

                self.load(j).wait()
                own = self.held[j % 2]
            self.copy(0, j).wait_recv()

            @pl.when(j >= RING)
            def _():
                self.copy(1, j - RING).wait_send()

            self.both[j % RING] = (own.astype(full) + self.first[j].astype(full)).astype(low)
            self.copy(1, j).start()

        i = j - LAG

        @pl.when(self.inner & (i >= 0) & (i < self.count))
        def _():
            self.copy(1, i).wait_recv()
            every = self.both[i % RING].astype(full) + self.second[i].astype(full)
            self.first[i] = every.astype(low)
            self.copy(2, i).start()
            if self.held is None:
                self.out[i] = every.astype(low)
            else:
                self.put(i).start()

    def ticks(self, begin, end):
        def step(j, carry):
            self.tick(j)
            return carry

        lax.fori_loop(begin, end, step, 0)

    def finish(self):
        @pl.when(self.outer)
        def _():
            def receive(i):
                self.copy(2, i).wait_recv()
                if self.held is None:
                    self.out[i] = self.first[i]
                else:
                    self.put(i).start()

            self.loop(receive)
            self.loop(lambda i: self.copy(0, i).wait_send())

        @pl.when(self.inner)
        def _():
            self.loop(lambda i: self.copy(1, i).wait_send(), self.count - RING)
            self.loop(lambda i: self.copy(2, i).wait_send())

        if self.held is not None:
            self.loop(lambda i: self.put(i).wait())


def line_scratch(shape, streamed=True):
    low = jnp.bfloat16
    dma = pltpu.SemaphoreType.DMA
    scratch = [
        pltpu.VMEM(shape, low),
        pltpu.VMEM(shape, low),
        pltpu.VMEM((RING,) + shape[1:], low),
        dma((3, shape[0])),
        dma((3, shape[0])),
    ]
    if streamed:
        scratch += [pltpu.VMEM((2,) + shape[1:], low), dma((shape[0] + 2,))]
    return scratch


def remote(source, target, sends, recvs, index, device):
    return pltpu.make_async_remote_copy(
        src_ref=source,
        dst_ref=target,
        send_sem=sends.at[index],
        recv_sem=recvs.at[index],
        device_id=device,
        device_id_type=MESH,
    )


class Gather:
    def __init__(self, count, rep, me, own, slot, sends, recvs):
        self.count, self.rep, self.me = count, rep, me
        self.own, self.slot, self.sends, self.recvs = own, slot, sends, recvs
        self.waiting = []

    def near(self, mask):
        return flip(self.me, mask, self.count)

    def send(self, source, owner, part, mask, index):
        remote(
            source,
            self.slot(owner, part),
            self.sends,
            self.recvs,
            index,
            (self.rep, self.near(mask)),
        ).start()
        self.waiting.append(index)

    def arrived(self, owner, part, index):
        remote(
            self.slot(owner, part),
            self.slot(owner, part),
            self.sends,
            self.recvs,
            index,
            (self.rep, self.me),
        ).wait_recv()

    def pass_on(self, mask, part, index, new, onward):
        owner = self.near(mask)
        if index is not None:
            self.arrived(owner, part, index)
        self.send(self.slot(owner, part), owner, part, onward, new)

    def start(self):
        if self.count == 8:
            plan = ((2, 0, 0), (4, 1, 1), (2, 1, 2), (4, 0, 3), (1, 0, 4), (1, 1, 5))
            for mask, part, index in plan:
                self.send(self.own(part), self.me, part, mask, index)
        else:
            for mask in [1] + list(range(2, self.count, 2)):
                for part in range(2):
                    self.send(self.own(part), self.me, part, mask, 2 * mask + part)

    def relay(self, stage):
        if self.count == 8:
            if stage == 0:
                self.pass_on(2, 0, 0, 6, 4)
                self.pass_on(4, 1, 1, 8, 2)
                self.pass_on(2, 0, None, 7, 1)
                self.pass_on(4, 1, None, 9, 1)
            elif stage == 1:
                self.pass_on(2, 1, 2, 10, 1)
                self.pass_on(4, 0, 3, 11, 1)
            else:
                self.pass_on(6, 0, 6, 12, 1)
                self.pass_on(6, 1, 8, 13, 1)
        elif stage == 2:
            for mask in range(2, self.count, 2):
                for part in range(2):
                    self.pass_on(mask, part, 2 * mask + part, 2 * mask + 2 + part, 1)

    def ready(self, masks):
        if self.count == 8:
            last = ((1, 0, 4), (1, 1, 5), (3, 0, 7), (5, 1, 9), (3, 1, 10), (5, 0, 11))
            last += ((7, 0, 12), (7, 1, 13))
        else:
            last = [(m, p, 2 * m + p) for m in range(1, self.count, 2) for p in range(2)]
        for mask, part, index in last:
            if mask in masks:
                self.arrived(self.near(mask), part, index)

    def finish(self, masks=None):
        self.ready(range(self.count) if masks is None else masks)
        for index in self.waiting:
            spot = self.slot(self.me, 0)
            remote(
                spot, spot, self.sends, self.recvs, index, (self.rep, self.me)
            ).wait_send()


PARTS = 8


def expert_kernel(count, reps, *refs):
    lined = reps == LINE
    (gate_ref, up_ref, down_ref), staging, refs = stage_in(refs, 3, 3)
    for copy in staging:
        copy.start()
    own_ref, slope_ref, mix_ref = refs[:3]
    refs = (None,) * 6 + refs[6:]
    hidden_out, grad_out, delta_out = refs[6:9]
    refs = refs[9:]
    if lined:
        line_out = refs[0]
        refs = refs[1:]
    (
        rows,
        slope_buf,
        hidden_buf,
        grad_buf,
        acc_both,
        acc_down,
        stage,
        send_sem,
        recv_sem,
        own_sem,
        slope_sem,
        hidden_sem,
        grad_sem,
        stage_sem,
    ) = refs[:14]
    rep = lax.axis_index("rep")
    me = lax.axis_index("shard")
    experts, width, hidden = gate_ref.shape
    tokens = own_ref.shape[0]
    half = tokens // 2
    low = jnp.bfloat16
    turns = experts * count
    swap = 2 + count

    def pair(t):
        late = jnp.where(t < swap, t - 2, t - count)
        return (
            jnp.where(t < 4, t // 2, late),
            jnp.where(t < 4, t % 2, jnp.where(t < swap, 0, 1)),
        )

    def pack_of(t):
        return flip(me, pair(t)[0], count)

    def slope_copy(t):
        return pltpu.make_async_copy(
            slope_ref.at[:, pack_of(t)], slope_buf.at[t % 2], slope_sem.at[t % 2]
        )

    def hidden_copy(t):
        spot = pl.ds(pl.multiple_of(pair(t)[1] * hidden, hidden), hidden)
        return pltpu.make_async_copy(
            hidden_buf.at[t % 2], hidden_out.at[pack_of(t), :, spot], hidden_sem.at[t % 2]
        )

    def grad_copy(t):
        spot = pl.ds(pl.multiple_of(pair(t)[1] * 2 * hidden, 2 * hidden), 2 * hidden)
        return pltpu.make_async_copy(
            grad_buf.at[t % 2], grad_out.at[pack_of(t), :, spot], grad_sem.at[t % 2]
        )

    def stage_copy(e):
        span = pl.ds(e * 3 * PARTS, 3 * PARTS)
        return pltpu.make_async_copy(stage.at[span], delta_out.at[span], stage_sem.at[e])

    slope_copy(0).start()
    own = pltpu.make_async_copy(own_ref, rows.at[me], own_sem)
    own.start()
    greet(me, rep, count, reps if lined else 1)
    gather = Gather(
        count,
        rep,
        me,
        lambda p: own_ref.at[pl.ds(p * half, half)],
        lambda owner, p: rows.at[owner, pl.ds(p * half, half)],
        send_sem,
        recv_sem,
    )
    gather.start()
    own.wait()
    for copy in staging:
        copy.wait()
    if lined:
        line = Line(rep, me, stage, line_out, *refs[14:], count=PARTS)

    def wrap_up(e):
        size = acc_down.shape[1] // PARTS
        side = acc_both.shape[1] // (2 * PARTS)
        base = e * 3 * PARTS
        for i in range(PARTS):
            down = base + (0 if e == 0 else 2 * PARTS) + i
            stage[down] = acc_down[e, i * size : (i + 1) * size, :].astype(low)
            for which in range(2):
                at = base + (PARTS if e == 0 else 0) + which * PARTS + i
                for piece in range(2):
                    span = slice((2 * i + piece) * side, (2 * i + piece + 1) * side)
                    stage[at, :, piece * hidden : (piece + 1) * hidden] = acc_both[
                        e, span, which * hidden : (which + 1) * hidden
                    ].astype(low)
        stage_copy(e).start()

    if count == 8:
        plan = {2: ((1,), 0), 4: ((), 1), 5: ((3,), None), 7: ((5,), 2), 9: ((7,), None)}
    else:
        plan = {2: ((1,), None), 4: ((), 2), 5: (tuple(range(3, count, 2)), None)}

    def step(t, carry):
        k, e = pair(t)
        pack = flip(me, k, count)
        for at, (masks, stage_at) in plan.items():

            @pl.when(t == at)
            def _():
                gather.ready(masks)
                if stage_at is not None:
                    gather.relay(stage_at)

        @pl.when(t + 1 < turns)
        def _():
            slope_copy(t + 1).start()

        if lined:
            line.ticks(2 * (t - swap - 1), 2 * (t - swap))
        slope_copy(t).wait()

        @pl.when(t >= 2)
        def _():
            hidden_copy(t - 2).wait()
            grad_copy(t - 2).wait()

        slot = t % 2
        x = rows[pack]
        dy = slope_buf[slot].reshape(tokens, width)
        mixes = jnp.transpose(mix_ref[pack])
        mix = jnp.where(e == 0, mixes[:, 0:1], mixes[:, 1:2])
        for part in range(hidden // TILE):
            span = pl.ds(part * TILE, TILE)
            ga = matmul(x, gate_ref[e, :, span], NN)
            ua = matmul(x, up_ref[e, :, span], NN)
            dh = matmul(dy, down_ref[e, span, :], NT) * mix
            sig = jax.nn.sigmoid(ga)
            act = ga * sig
            hidden_buf[slot, :, span] = (mix * (act * ua)).astype(low)
            grad_buf[slot, :, span] = (dh * ua * sig * (1.0 + ga * (1.0 - sig))).astype(low)
            grad_buf[slot, :, pl.ds(hidden + part * TILE, TILE)] = (dh * act).astype(low)
        hidden_copy(t).start()
        grad_copy(t).start()

        def add(acc, value):
            @pl.when(k == 0)
            def _():
                acc[e] = value

            @pl.when(k > 0)
            def _():
                acc[e] += value

        add(acc_both, matmul(x, grad_buf[slot], TN))
        add(acc_down, matmul(hidden_buf[slot], dy, TN))

        @pl.when(t == swap - 1)
        def _():
            wrap_up(0)
            if lined:
                line.start()

        return carry

    lax.fori_loop(0, turns, step, 0)
    wrap_up(1)
    if lined:
        line.ticks(2 * (turns - swap - 1), PARTS + LAG)
    for t in (turns - 2, turns - 1):
        hidden_copy(t).wait()
        grad_copy(t).wait()
    gather.finish(())
    stage_copy(0).wait()
    if lined:
        line.finish()
    stage_copy(1).wait()


def expert_pass(normed, all_slopes, mixing, gate_weight, up_weight, down_weight, count, reps):
    tokens, width = normed.shape
    experts, _, hidden = gate_weight.shape
    block = tokens // count
    low = jnp.bfloat16
    full = jnp.float32
    dma = pltpu.SemaphoreType.DMA
    vmem = pltpu.VMEM
    shape = jax.ShapeDtypeStruct
    anywhere = pl.BlockSpec(memory_space=pl.ANY)
    inside = pl.BlockSpec(memory_space=pltpu.VMEM)
    flops = 2 * count * tokens * width * hidden * experts * 6
    lined = reps == LINE
    segment = (hidden // PARTS, width)
    summed = (PARTS,) + segment
    return pl.pallas_call(
        functools.partial(expert_kernel, count, reps),
        name="expert_pass",
        out_shape=(
            shape((count, tokens, experts * hidden), low),
            shape((count, tokens, 2 * experts * hidden), low),
            shape((6 * PARTS,) + segment, low),
        )
        + ((shape(summed, low),) if lined else ()),
        in_specs=[anywhere, anywhere, inside, anywhere, anywhere, anywhere],
        out_specs=(anywhere,) * 3 + ((inside,) if lined else ()),
        scratch_shapes=[
            vmem((count, tokens, width), low),
            vmem((2, count, block, width), low),
            vmem((2, tokens, hidden), low),
            vmem((2, tokens, 2 * hidden), low),
            vmem((experts, width, 2 * hidden), full),
            vmem((experts, hidden, width), full),
            vmem((6 * PARTS,) + segment, low),
            dma((2 * count + 2,)),
            dma((2 * count + 2,)),
            dma,
            dma((2,)),
            dma((2,)),
            dma((2,)),
            dma((2,)),
        ]
        + (line_scratch(summed, False) if lined else [])
        + [vmem(w.shape, low) for w in (gate_weight, up_weight, down_weight)]
        + [dma((3,))],
        compiler_params=pltpu.CompilerParams(
            collective_id=1, has_side_effects=True, vmem_limit_bytes=VMEM_MOST
        ),
        cost_estimate=pl.CostEstimate(flops=flops, bytes_accessed=1 << 26, transcendentals=0),
    )(
        normed,
        all_slopes.reshape(count, count, block, width),
        mixing,
        gate_weight,
        up_weight,
        down_weight,
    )


def return_kernel(count, reps, *refs):
    (gate_ref, up_ref, down_ref, own_ref), staging, refs = stage_in(refs, 4, 2)
    for copy in staging:
        copy.start()
    grad_ref, hidden_ref = refs[:2]
    lined = reps == LINE
    refs = refs[6:]
    if lined:
        line_ref, back_ref, piece_out, line_out = refs[:4]
        refs = refs[4:]
    else:
        back_ref, piece_out = refs[:2]
        refs = refs[2:]
    (
        grad_buf,
        hidden_buf,
        pair_send,
        far_send,
        pair_recv,
        far_recv,
        total,
        piece,
        last_recv,
        relay_recv,
        load_sem,
        pair_send_sem,
        pair_recv_sem,
        far_send_sem,
        far_recv_sem,
        piece_sem,
        last_sem,
        relay_send_sem,
        relay_recv_sem,
    ) = refs[:19]
    rep = lax.axis_index("rep")
    me = lax.axis_index("shard")
    experts, width, hidden = gate_ref.shape
    tokens = own_ref.shape[0]
    block = tokens // count
    low = jnp.bfloat16
    full = jnp.float32
    pairs = count // 2
    partner = flip(me, 1, count)
    line = Line(rep, me, line_ref, line_out, *refs[19:], base=PARTS, count=2 * PARTS) if lined else None

    relayed = count == 8
    half = tokens // 2

    def mask_of(turn):
        return count - 2 - 2 * turn

    def target(item):
        return flip(me, mask_of(item // 2) + 1 - item % 2, count)

    def grad_load(item):
        return pltpu.make_async_copy(
            grad_ref.at[target(item)], grad_buf.at[item % 2], load_sem.at[item % 2]
        )

    def grad_part(slot, pack):
        value = None
        for e in range(experts):
            for at, weight in ((2 * e, gate_ref), (2 * e + 1, up_ref)):
                term = matmul(grad_buf[slot, :, pl.ds(at * hidden, hidden)], weight[e], NT)
                value = term if value is None else value + term
        total[...] = value

    def hidden_load(item):
        return pltpu.make_async_copy(
            hidden_ref.at[:, target(item)], hidden_buf.at[item % 2], load_sem.at[item % 2]
        )

    def hidden_part(slot, pack):
        value = None
        for e in range(experts):
            term = matmul(
                hidden_buf[slot, :, :, pl.ds(e * hidden, hidden)].reshape(tokens, hidden),
                down_ref[e],
                NN,
            )
            value = term if value is None else value + term
        total[...] = value
        mine = pl.ds(pl.multiple_of(me * block, block), block)
        theirs = pl.ds(pl.multiple_of(pack * block, block), block)
        total[mine, :] += own_ref[theirs, :].astype(full)

    def pair_copy(base, turn):
        return remote(
            pair_send.at[turn % 2],
            pair_recv.at[base + turn],
            pair_send_sem,
            pair_recv_sem,
            base + turn,
            (rep, partner),
        )

    def far_copy(turn, device):
        return remote(
            far_send.at[turn % 2], far_recv.at[turn], far_send_sem, far_recv_sem, turn, (rep, device)
        )

    def half_copy(side):
        span = pl.ds(side * half, half)
        return remote(
            far_send.at[1, span],
            far_recv.at[1, span],
            far_send_sem,
            far_recv_sem,
            side,
            (rep, flip(me, count - 4, count)),
        )

    def relay_copy(phase, side, source):
        return remote(
            source.at[pl.ds(side * half, half)],
            relay_recv.at[2 * phase + side],
            relay_send_sem,
            relay_recv_sem,
            2 * phase + side,
            (rep, flip(me, 2 + 2 * side, count)),
        )

    def last_copy(device):
        return pltpu.make_async_remote_copy(
            src_ref=piece.at[0],
            dst_ref=last_recv,
            send_sem=last_sem.at[0],
            recv_sem=last_sem.at[1],
            device_id=(rep, device),
            device_id_type=MESH,
        )

    def slot(turn):
        return jnp.where(turn == 0, 0, jnp.where(turn == pairs - 1, 3, 1 + turn % 2))

    def piece_copy(turn):
        return pltpu.make_async_copy(
            piece.at[slot(turn)], piece_out.at[turn], piece_sem.at[turn % 2]
        )

    def grad_combine(turn, mask):
        last = turn == pairs - 1
        total[...] += pair_recv[turn].astype(full)

        @pl.when(last)
        def _():
            back_ref[...] = total[...]

        if relayed:

            @pl.when(turn == 0)
            def _():
                far_send[0] = total[...].astype(low)
                for side in range(2):
                    relay_copy(0, side, far_send.at[0]).start()

            @pl.when(turn == 1)
            def _():
                far_send[1] = total[...].astype(low)
                half_copy(1).start()

            @pl.when(turn == 2)
            def _():
                early, later = pl.ds(0, half), pl.ds(half, half)
                for side in range(2):
                    relay_copy(0, side, far_send.at[0]).wait_recv()
                value = far_send[1, early, :].astype(full) + relay_recv[0].astype(full)
                far_send[1, early, :] = value.astype(low)
                half_copy(0).start()
                for side in range(2):
                    relay_copy(0, side, far_send.at[0]).wait_send()
                total[later, :] += relay_recv[1].astype(full)
                far_send[0] = total[...].astype(low)
                far_copy(2, flip(me, mask, count)).start()
        else:

            @pl.when(jnp.logical_not(last))
            def _():
                @pl.when(turn >= 2)
                def _():
                    far_copy(turn - 2, me).wait_send()

                far_send[turn % 2] = total[...].astype(low)
                far_copy(turn, flip(me, mask, count)).start()

    def hidden_combine(turn, mask):
        if not relayed:

            @pl.when((turn >= 3) & (turn < pairs - 1))
            def _():
                piece_copy(turn - 2).wait()

        piece[slot(turn)] = (total[...] + pair_recv[pairs + turn].astype(full)).astype(low)

        @pl.when(turn == 0)
        def _():
            if relayed:
                for side in range(2):
                    relay_copy(1, side, piece.at[0]).start()
            else:
                last_copy(flip(me, mask, count)).start()

        if not relayed:

            @pl.when((turn > 0) & (turn < pairs - 1))
            def _():
                piece_copy(turn).start()

    grad_load(0).start()
    greet(me, rep, count, reps if lined else 1)
    if lined:
        line.start()

    def sweep(base, load, part, combine, before):
        def item_step(item, carry):
            turn = item // 2
            mask = mask_of(turn)

            @pl.when(item + 1 < 2 * pairs)
            def _():
                load(item + 1).start()

            load(item).wait()
            part(item % 2, target(item))

            @pl.when(item % 2 == 0)
            def _():
                @pl.when(turn >= 2)
                def _():
                    pair_copy(base, turn - 2).wait_send()

                pair_send[turn % 2] = total[...].astype(low)
                pair_copy(base, turn).start()

            @pl.when(item % 2 == 1)
            def _():
                pair_copy(base, turn).wait_recv()
                combine(turn, mask)

            if lined:
                line.tick(before + item - 2)
            return carry

        lax.fori_loop(0, 2 * pairs, item_step, 0)
        for turn in range(max(0, pairs - 2), pairs):
            pair_copy(base, turn).wait_send()

    for copy in staging:
        copy.wait()
    sweep(0, grad_load, grad_part, grad_combine, 0)
    hidden_load(0).start()
    sweep(pairs, hidden_load, hidden_part, hidden_combine, 2 * pairs)
    if lined:
        line.ticks(4 * pairs - 2, 2 * PARTS - 1)
    if relayed:
        for side in range(2):
            half_copy(side).wait_recv()
        back_ref[...] += far_recv[1].astype(full)
        far_copy(2, me).wait_recv()
        back_ref[...] += far_recv[2].astype(full)
        for side in range(2):
            half_copy(side).wait_send()
        far_copy(2, me).wait_send()
    else:

        def add(turn, carry):
            far_copy(turn, me).wait_recv()
            back_ref[...] += far_recv[turn].astype(full)
            return carry

        lax.fori_loop(0, pairs - 1, add, 0)
        for turn in (pairs - 3, pairs - 2):
            far_copy(turn, me).wait_send()
    if lined:
        line.ticks(2 * PARTS - 1, 2 * PARTS + LAG)
    if relayed:
        for side in range(2):
            relay_copy(1, side, piece.at[0]).wait_recv()
            rows = pl.ds(side * half, half)
            spot = slot(1 + side)
            value = piece[spot, rows, :].astype(full) + relay_recv[2 + side].astype(full)
            piece[spot, rows, :] = value.astype(low)
            piece_copy(1 + side).start()
            relay_copy(1, side, piece.at[0]).wait_send()
    else:
        last_copy(me).wait_recv()
        value = piece[3].astype(full) + last_recv[...].astype(full)
        piece[3] = value.astype(low)
        last_copy(me).wait_send()
    for turn in (pairs - 3, pairs - 2):
        piece_copy(turn).wait()
    piece_copy(pairs - 1).start()
    if lined:
        line.finish()
    piece_copy(pairs - 1).wait()


def return_pass(grads, hiddens, gate_weight, up_weight, down_weight, own, deltas, count, reps):
    tokens, width = own.shape
    experts, _, hidden = gate_weight.shape
    block = tokens // count
    low = jnp.bfloat16
    full = jnp.float32
    pairs = count // 2
    dma = pltpu.SemaphoreType.DMA
    shape = jax.ShapeDtypeStruct
    anywhere = pl.BlockSpec(memory_space=pl.ANY)
    inside = pl.BlockSpec(memory_space=pltpu.VMEM)
    flops = 2 * count * tokens * width * hidden * experts * 3
    lined = reps == LINE
    extra = [deltas] if lined else []
    return pl.pallas_call(
        functools.partial(return_kernel, count, reps),
        name="return_pass",
        out_shape=(
            shape((tokens, width), full),
            shape((pairs, tokens, width), low),
        )
        + tuple(shape((2 * PARTS,) + d.shape[1:], low) for d in extra),
        in_specs=[anywhere] * (6 + len(extra)),
        out_specs=(inside, anywhere) + (anywhere,) * len(extra),
        scratch_shapes=[
            pltpu.VMEM((2, tokens, 2 * experts * hidden), low),
            pltpu.VMEM((2, count, block, experts * hidden), low),
            pltpu.VMEM((2, tokens, width), low),
            pltpu.VMEM((2, tokens, width), low),
            pltpu.VMEM((2 * pairs, tokens, width), low),
            pltpu.VMEM((pairs, tokens, width), low),
            pltpu.VMEM((tokens, width), full),
            pltpu.VMEM((4, tokens, width), low),
            pltpu.VMEM((8, 128) if count == 8 else (tokens, width), low),
            pltpu.VMEM((4, tokens // 2, width), low),
            dma((2,)),
            dma((2 * pairs,)),
            dma((2 * pairs,)),
            dma((pairs,)),
            dma((pairs,)),
            dma((2,)),
            dma((3,)),
            dma((4,)),
            dma((4,)),
        ]
        + (line_scratch((2 * PARTS,) + deltas.shape[1:]) if lined else [])
        + [pltpu.VMEM(a.shape, low) for a in (gate_weight, up_weight, down_weight, own)]
        + [dma((4,))],
        compiler_params=pltpu.CompilerParams(
            collective_id=2, has_side_effects=True, vmem_limit_bytes=VMEM_MOST
        ),
        cost_estimate=pl.CostEstimate(flops=flops, bytes_accessed=1 << 26, transcendentals=0),
    )(
        grads,
        hiddens.reshape(count, count, block, experts * hidden),
        gate_weight,
        up_weight,
        down_weight,
        own,
        *extra,
    )


def turn_pairs(rows, along, across, sign):
    lane = lax.broadcasted_iota(jnp.int32, (rows.shape[0], 128), 1)
    early = (lane % HEAD_SIZE) < HEAD_SIZE // 2
    pieces = []
    for at in range(0, rows.shape[1], 128):
        part = rows[:, at : at + 128]
        other = jnp.where(
            early,
            pltpu.roll(part, 128 - HEAD_SIZE // 2, 1),
            pltpu.roll(part, HEAD_SIZE // 2, 1),
        )
        pieces.append(part * along + sign * (other * across))
    return pieces[0] if len(pieces) == 1 else jnp.concatenate(pieces, axis=1)


def permutation(order_ref):
    tokens = order_ref.shape[1]
    rows = lax.broadcasted_iota(jnp.int32, (tokens, tokens), 0)
    return jnp.where(order_ref[...] == rows, 1.0, 0.0).astype(jnp.bfloat16)


def starts_of(position, length_ref):
    start = jnp.zeros_like(position)
    end = jnp.zeros((1, 1), jnp.int32)
    for k in range(length_ref.shape[1] - 1):
        end = end + length_ref[0:1, k : k + 1]
        start = jnp.where(position >= end, end, start)
    return start


def fill_bias(bias, length_ref):
    tokens = bias.shape[0]
    keys = lax.broadcasted_iota(jnp.int32, (tokens, tokens), 0)
    queries = lax.broadcasted_iota(jnp.int32, (tokens, tokens), 1)
    start = starts_of(lax.broadcasted_iota(jnp.int32, (1, tokens), 1), length_ref)
    bias[...] = jnp.where((keys >= start) & (keys <= queries), 0.0, -1e30)


def query_spans(tokens):
    half = tokens // 2
    return ((0, half, half), (half, half, tokens))


def first_kernel(
    count,
    token_ref,
    query_ref,
    key_ref,
    value_ref,
    output_ref,
    gain_ref,
    order_ref,
    id_ref,
    gate_ref,
    arrived_out,
    joined_out,
    gain_out,
    mix_out,
    mix_buf,
    gain_buf,
    token_send,
    token_recv,
    gain_send,
    gain_recv,
    mix_send,
    mix_recv,
    weight_send,
    weight_recv,
    local_sem,
):
    rep = lax.axis_index("rep")
    me = lax.axis_index("shard")
    full = jnp.float32
    low = jnp.bfloat16
    rows = query_ref.shape[0]
    experts = mix_out.shape[0] * 2
    mine = pl.multiple_of(me * rows, rows)
    locals_ = [pltpu.make_async_copy(token_ref.at[me], arrived_out.at[me], local_sem.at[0])]
    at = 0
    for i, ref in enumerate((query_ref, key_ref, value_ref, output_ref)):
        size = ref.shape[1]
        target = joined_out.at[pl.ds(mine, rows), pl.ds(at, size)]
        locals_.append(pltpu.make_async_copy(ref, target, local_sem.at[1 + i]))
        at += size
    for copy in locals_:
        copy.start()
    greet(me, rep, count)

    def token_copy(k):
        target = flip(me, k, count)
        return remote(
            token_ref.at[target], arrived_out.at[me], token_send, token_recv, k, (rep, target)
        )

    def gain_copy(k):
        return remote(
            gain_ref, gain_buf.at[me], gain_send, gain_recv, k, (rep, flip(me, k, count))
        )

    def mix_copy(k):
        target = flip(me, k, count)
        return remote(mix_buf.at[target], mix_out.at[me], mix_send, mix_recv, k, (rep, target))

    for k in range(count - 1, 0, -1):
        token_copy(k).start()
    for copy in locals_[1:]:
        copy.wait()
    half = rows // 2

    def block(owner, part):
        return joined_out.at[pl.ds(pl.multiple_of(owner * rows + part * half, half), half)]

    weights = Gather(count, rep, me, lambda p: block(me, p), block, weight_send, weight_recv)
    weights.start()
    for k in range(1, count):
        gain_copy(k).start()
    gain_buf[me] = gain_ref[...]
    tokens = order_ref.shape[0]
    lane = lax.broadcasted_iota(jnp.int32, (tokens, experts), 1)
    mixing = jnp.zeros((tokens, experts), full)
    for k in range(id_ref.shape[1]):
        mixing = mixing + jnp.where(id_ref[:, k : k + 1] == lane, gate_ref[:, k : k + 1], 0.0)
    place = permutation(order_ref)
    moved = jnp.zeros((experts, tokens), full)
    for _ in range(3):
        high = mixing.astype(low)
        moved = moved + matmul(high, place, TN)
        mixing = mixing - high.astype(full)
    for owner in range(count):
        mix_buf[owner, 0:2, :] = moved[2 * owner : 2 * owner + 2, :]
        mix_buf[owner, 2:8, :] = jnp.zeros((6, tokens), full)
    weights.relay(0)
    for k in range(1, count):
        mix_copy(k).start()
    mix_out[me] = mix_buf[me]
    weights.relay(1)
    weights.relay(2)
    locals_[0].wait()
    for k in range(1, count):
        gain_copy(k).wait_recv()
    for owner in range(count):
        gain_out[:, owner * rows : (owner + 1) * rows] = gain_buf[owner]
    for k in range(1, count):
        token_copy(k).wait_recv()
        mix_copy(k).wait_recv()
    weights.finish()
    for k in range(1, count):
        token_copy(k).wait_send()
        gain_copy(k).wait_send()
        mix_copy(k).wait_send()


def first_pass(tokens, weights, gains, order, expert_ids, gates, count):
    rows = weights[0].shape[0]
    number, width = tokens.shape
    block = number // count
    low = jnp.bfloat16
    full = jnp.float32
    dma = pltpu.SemaphoreType.DMA
    inside = pl.BlockSpec(memory_space=pltpu.VMEM)
    columns = sum(w.shape[1] for w in weights)
    shape = jax.ShapeDtypeStruct
    return pl.pallas_call(
        functools.partial(first_kernel, count),
        name="first_pass",
        out_shape=(
            shape((count, block, width), low),
            shape((rows * count, columns), low),
            shape((8, rows * count), full),
            shape((count, 8, number), full),
        ),
        in_specs=[inside] * 9,
        out_specs=(inside,) * 4,
        scratch_shapes=[
            pltpu.VMEM((count, 8, number), full),
            pltpu.VMEM((count, 8, rows), full),
            dma((count,)),
            dma((count,)),
            dma((count,)),
            dma((count,)),
            dma((count,)),
            dma((count,)),
            dma((2 * count + 2,)),
            dma((2 * count + 2,)),
            dma((5,)),
        ],
        compiler_params=pltpu.CompilerParams(
            collective_id=4, has_side_effects=True, vmem_limit_bytes=VMEM_MOST
        ),
        cost_estimate=pl.CostEstimate(flops=1 << 24, bytes_accessed=1 << 26, transcendentals=0),
    )(tokens.reshape(count, block, width), *weights, gains, order, expert_ids, gates)


def front_kernel(
    count,
    token_ref,
    query_ref,
    key_ref,
    value_ref,
    output_ref,
    first_ref,
    second_ref,
    order_ref,
    id_ref,
    gate_ref,
    length_ref,
    speed_ref,
    cotangent_ref,
    joined_out,
    gain_out,
    mix_out,
    along_out,
    across_out,
    input_out,
    query_out,
    key_out,
    value_out,
    mixed_out,
    logsum_out,
    hidden_out,
    normed_out,
    shared_out,
    slopes_out,
    arrived,
    joined,
    mix_buf,
    gain_src,
    gain_buf,
    place,
    bias,
    normed,
    inputs,
    projected,
    mixed,
    hidden,
    moved,
    shared,
    token_send,
    token_recv,
    gain_send,
    gain_recv,
    mix_send,
    mix_recv,
    weight_send,
    weight_recv,
    slope_send,
    slope_recv,
    local_sem,
    out_sem,
):
    rep = lax.axis_index("rep")
    me = lax.axis_index("shard")
    low = jnp.bfloat16
    full = jnp.float32
    rows = query_ref.shape[0]
    tokens, width = cotangent_ref.shape
    key_width = key_ref.shape[1]
    experts = mix_out.shape[0] * 2
    mine = pl.multiple_of(me * rows, rows)
    own = [pltpu.make_async_copy(token_ref.at[me], arrived.at[me], local_sem.at[0])]
    at = 0
    for i, ref in enumerate((query_ref, key_ref, value_ref, output_ref)):
        size = ref.shape[1]
        spot = joined.at[pl.ds(mine, rows), pl.ds(at, size)]
        own.append(pltpu.make_async_copy(ref, spot, local_sem.at[1 + i]))
        at += size
    own.append(pltpu.make_async_copy(cotangent_ref, slopes_out.at[me], local_sem.at[5]))
    for copy in own:
        copy.start()
    gain_src[...] = jnp.zeros(gain_src.shape, full)
    gain_src[0:1, :] = first_ref[...].astype(full)
    gain_src[1:2, :] = second_ref[...].astype(full)
    greet(me, rep, count)

    def token_copy(k):
        target = flip(me, k, count)
        return remote(
            token_ref.at[target], arrived.at[me], token_send, token_recv, k, (rep, target)
        )

    def gain_copy(k):
        return remote(
            gain_src, gain_buf.at[me], gain_send, gain_recv, k, (rep, flip(me, k, count))
        )

    def mix_copy(k):
        target = flip(me, k, count)
        return remote(mix_buf.at[target], mix_out.at[me], mix_send, mix_recv, k, (rep, target))

    for k in range(count - 1, 0, -1):
        token_copy(k).start()
    for copy in own[1:5]:
        copy.wait()
    half = rows // 2

    def block(owner, part):
        return joined.at[pl.ds(pl.multiple_of(owner * rows + part * half, half), half)]

    weights = Gather(count, rep, me, lambda p: block(me, p), block, weight_send, weight_recv)
    weights.start()
    for k in range(1, count):
        gain_copy(k).start()
    gain_buf[me] = gain_src[...]
    some = tokens // 2
    slopes = Gather(
        count,
        rep,
        me,
        lambda p: cotangent_ref.at[pl.ds(p * some, some)],
        lambda owner, p: slopes_out.at[owner, pl.ds(p * some, some)],
        slope_send,
        slope_recv,
    )
    kinds = lax.broadcasted_iota(jnp.int32, (experts, tokens), 0)
    mixing = jnp.zeros((experts, tokens), full)
    for k in range(id_ref.shape[0]):
        mixing = mixing + jnp.where(id_ref[k : k + 1, :] == kinds, gate_ref[k : k + 1, :], 0.0)
    place[...] = permutation(order_ref)
    dealt = jnp.zeros((experts, tokens), full)
    for _ in range(3):
        high = mixing.astype(low)
        dealt = dealt + matmul(high, place[...], NT)
        mixing = mixing - high.astype(full)
    for owner in range(count):
        mix_buf[owner, 0:2, :] = dealt[2 * owner : 2 * owner + 2, :]
        mix_buf[owner, 2:8, :] = jnp.zeros((6, tokens), full)
    weights.relay(0)
    for k in range(1, count):
        mix_copy(k).start()
    mix_out[me] = mix_buf[me]
    slopes.start()
    fill_bias(bias, length_ref)
    position = lax.broadcasted_iota(jnp.int32, along_out.shape, 0)
    angle = (position - starts_of(position, length_ref)).astype(full) * speed_ref[0:1, :]
    along_out[...] = jnp.cos(angle)
    across_out[...] = jnp.sin(angle) * speed_ref[1:2, :]
    own[0].wait()
    for k in range(1, count):
        token_copy(k).wait_recv()
        gain_copy(k).wait_recv()
    for owner in range(count):
        gain_out[:, owner * rows : (owner + 1) * rows] = gain_buf[owner]
    outs = (
        (inputs, input_out),
        (projected.at[:, pl.ds(0, width)], query_out),
        (projected.at[:, pl.ds(width, key_width)], key_out),
        (projected.at[:, pl.ds(width + key_width, key_width)], value_out),
        (mixed, mixed_out),
        (hidden, hidden_out),
        (moved, normed_out),
        (shared, shared_out),
        (joined, joined_out),
    )
    puts = [pltpu.make_async_copy(a, b, out_sem.at[k]) for k, (a, b) in enumerate(outs)]
    rows_in = matmul(place[...], arrived[...].reshape(tokens, width), TN)
    inputs[...] = rows_in.astype(low)
    scale = lax.rsqrt(jnp.mean(rows_in * rows_in, axis=1, keepdims=True) + EPS)
    normed[...] = (rows_in * scale * gain_out[0:1, :]).astype(low)
    puts[0].start()
    weights.relay(1)
    weights.relay(2)
    weights.ready(range(count))
    puts[8].start()
    along = along_out[...]
    across = across_out[...]

    def turned(at, carry):
        spot = pl.ds(pl.multiple_of(at * key_width, key_width), key_width)
        part = matmul(normed[...], joined[:, spot], NN)
        projected[:, spot] = turn_pairs(part, along, across, 1.0).astype(low)
        return carry

    lax.fori_loop(0, width // key_width + 1, turned, 0)
    part = matmul(normed[...], joined[:, width + key_width : width + 2 * key_width], NN)
    projected[:, width + key_width :] = part.astype(low)
    for copy in puts[1:4]:
        copy.start()

    def heads(g, carry):
        qs = pl.ds(pl.multiple_of(g * 256, 256), 256)
        kv = pl.ds(pl.multiple_of(width + g * 128, 128), 128)
        keys = projected[:, kv]
        kv = pl.ds(pl.multiple_of(width + key_width + g * 128, 128), 128)
        values = projected[:, kv]
        queries = projected[:, qs] * jnp.bfloat16(HEAD_SIZE**-0.5)
        for start, size, reach in query_spans(tokens):
            pieces = []
            for h in range(4):
                a = (h // 2) * HEAD_SIZE
                score = matmul(
                    keys[:reach, a : a + HEAD_SIZE],
                    queries[start : start + size, h * HEAD_SIZE : (h + 1) * HEAD_SIZE],
                    NT,
                )
                score = score + bias[:reach, start : start + size]
                largest = jnp.max(score, axis=0, keepdims=True)
                powers = jnp.exp(score - largest)
                totals = jnp.sum(powers, axis=0, keepdims=True)
                shares = (powers * (1.0 / totals)).astype(low)
                pieces.append(matmul(shares, values[:reach, a : a + HEAD_SIZE], TN))
                logsum_out[g, h : h + 1, start : start + size] = largest + jnp.log(totals)
            mixed[start : start + size, qs] = jnp.concatenate(pieces, axis=1).astype(low)

        @pl.when(g == 1)
        def _():
            slopes.relay(0)

        return carry

    lax.fori_loop(0, key_width // 128, heads, 0)
    puts[4].start()
    total = inputs[...].astype(full) + matmul(mixed[...], joined[:, width + 2 * key_width :], NN)
    hidden[...] = total
    scale = lax.rsqrt(jnp.mean(total * total, axis=1, keepdims=True) + EPS)
    normed[...] = (total * scale * gain_out[1:2, :]).astype(low)
    puts[5].start()
    moved[...] = matmul(place[...], normed[...], NN).astype(low)
    puts[6].start()
    shared[...] = matmul(place[...], hidden[...].astype(low), NN).astype(low)
    puts[7].start()
    slopes.relay(1)
    for k in range(1, count):
        mix_copy(k).wait_recv()
    for copy in puts:
        copy.wait()
    slopes.relay(2)
    own[5].wait()
    slopes.finish()
    weights.finish(())
    for k in range(1, count):
        token_copy(k).wait_send()
        gain_copy(k).wait_send()
        mix_copy(k).wait_send()


def front_pass(tokens, weights, gains, order, expert_ids, gates, lengths, cotangent, count):
    rows = weights[0].shape[0]
    number, width = tokens.shape
    key_width = weights[1].shape[1]
    block = number // count
    low = jnp.bfloat16
    full = jnp.float32
    dma = pltpu.SemaphoreType.DMA
    vmem = pltpu.VMEM
    anywhere = pl.BlockSpec(memory_space=pl.ANY)
    inside = pl.BlockSpec(memory_space=pltpu.VMEM)
    columns = sum(w.shape[1] for w in weights)
    shape = jax.ShapeDtypeStruct
    half = HEAD_SIZE // 2
    speed = np.tile(THETA ** (-2.0 * np.arange(half) / HEAD_SIZE), 128 // half)
    side = np.tile(np.repeat([-1.0, 1.0], half), 128 // HEAD_SIZE)
    speeds = jnp.asarray(np.stack([speed, side]).astype(np.float32))
    return pl.pallas_call(
        functools.partial(front_kernel, count),
        name="front_pass",
        out_shape=(
            shape((rows * count, columns), low),
            shape((8, rows * count), full),
            shape((count, 8, number), full),
            shape((number, 128), full),
            shape((number, 128), full),
            shape((number, width), low),
            shape((number, width), low),
            shape((number, key_width), low),
            shape((number, key_width), low),
            shape((number, width), low),
            shape((key_width // 128, 4, number), full),
            shape((number, width), full),
            shape((number, width), low),
            shape((number, width), low),
            shape((count, number, width), low),
        ),
        in_specs=[anywhere] * 5 + [inside] * 7 + [anywhere],
        out_specs=(anywhere,)
        + (inside,) * 4
        + (anywhere,) * 5
        + (inside,)
        + (anywhere,) * 4,
        scratch_shapes=[
            vmem((count, block, width), low),
            vmem((rows * count, columns), low),
            vmem((count, 8, number), full),
            vmem((8, rows), full),
            vmem((count, 8, rows), full),
            vmem((number, number), low),
            vmem((number, number), full),
            vmem((number, width), low),
            vmem((number, width), low),
            vmem((number, width + 2 * key_width), low),
            vmem((number, width), low),
            vmem((number, width), full),
            vmem((number, width), low),
            vmem((number, width), low),
            dma((count,)),
            dma((count,)),
            dma((count,)),
            dma((count,)),
            dma((count,)),
            dma((count,)),
            dma((2 * count + 2,)),
            dma((2 * count + 2,)),
            dma((2 * count + 2,)),
            dma((2 * count + 2,)),
            dma((6,)),
            dma((9,)),
        ],
        compiler_params=pltpu.CompilerParams(
            collective_id=4, has_side_effects=True, vmem_limit_bytes=VMEM_MOST
        ),
        cost_estimate=pl.CostEstimate(
            flops=12 << 30, bytes_accessed=1 << 26, transcendentals=1 << 22
        ),
    )(
        tokens.reshape(count, block, width),
        *weights,
        *(gain.reshape(1, rows) for gain in gains),
        order,
        expert_ids.T,
        gates.T,
        lengths,
        speeds,
        cotangent,
    )


def finish_kernel(count, reps, *refs):
    lined = reps == LINE
    (
        back_ref,
        slopes_ref,
        order_ref,
        length_ref,
        along_ref,
        across_ref,
        weight_ref,
        gain_ref,
        input_ref,
        query_ref,
        key_ref,
        value_ref,
        mixed_ref,
        logsum_ref,
        hidden_ref,
        piece_ref,
    ) = refs[:16]
    refs = refs[16:]
    staged = (
        back_ref,
        hidden_ref,
        mixed_ref,
        weight_ref,
        query_ref,
        key_ref,
        value_ref,
        input_ref,
    )
    held = refs[-len(staged) - 1 : -1]
    staging = [
        pltpu.make_async_copy(ref, buf, refs[-1].at[k])
        for k, (ref, buf) in enumerate(zip(staged, held, strict=True))
    ]
    refs = refs[: -len(staged) - 1]
    (
        back_ref,
        hidden_ref,
        mixed_ref,
        weight_ref,
        query_ref,
        key_ref,
        value_ref,
        input_ref,
    ) = held
    if lined:
        line_ref = refs[0]
        refs = refs[1:]
    delta_out, gain_out, slope_out, out_ref = refs[:4]
    refs = refs[4:]
    if lined:
        line_out = refs[0]
        refs = refs[1:]
    (
        place,
        bias,
        normed,
        steep,
        mixed_slope,
        backs,
        arrived,
        far_piece,
        far_piece_send,
        far_piece_recv,
        local_sem,
        delta,
        pair_recv,
        far_send,
        far_recv,
        pair_send_sem,
        pair_recv_sem,
        far_send_sem,
        far_recv_sem,
        slope_send_sem,
        slope_recv_sem,
        gain_buf,
        gain_recv,
        gain_sum,
        gain_line,
        gain_send_sem,
        gain_recv_sem,
        gain_line_send,
        gain_line_recv,
        owned,
    ) = refs[:30]
    refs = refs[30:]
    low = jnp.bfloat16
    full = jnp.float32
    rep = lax.axis_index("rep")
    me = lax.axis_index("shard")
    pairs = count // 2
    partner = flip(me, 1, count)
    tokens, width = back_ref.shape
    key_width = key_ref.shape[1]
    joined = width + 2 * key_width
    rows = width // count
    block = tokens // count
    own_slopes = pltpu.make_async_copy(
        slopes_ref.at[:, pl.ds(pl.multiple_of(me * block, block), block)],
        arrived,
        local_sem.at[0],
    )
    staging[0].start()
    own_slopes.start()
    for copy in staging[1:]:
        copy.start()
    own_piece = pltpu.make_async_copy(piece_ref.at[pairs - 1], mixed_slope, local_sem.at[1])
    greet(me, rep, count, reps)
    if lined:
        line = Line(rep, me, line_ref, line_out, *refs[:7], base=3 * PARTS, count=3 * PARTS)
        sums = Line(rep, me, owned, delta_out, *refs[7:12])
        line.start()
    else:
        spread, spread_send, spread_recv = refs

    def tick(begin, end):
        if lined:
            line.ticks(begin, end)

    def piece_copy(turn):
        return remote(
            piece_ref.at[turn],
            far_piece.at[turn - 1],
            far_piece_send,
            far_piece_recv,
            turn,
            (rep, flip(me, count - 2 - 2 * turn, count)),
        )

    def rows_of(owner):
        return pl.ds(pl.multiple_of(owner * rows, rows), rows)

    columns = (slice(joined, joined + width), slice(0, joined))

    def pair_copy(part, turn):
        return remote(
            delta.at[rows_of(flip(partner, 2 * turn, count)), columns[part]],
            pair_recv.at[turn, :, columns[part]],
            pair_send_sem,
            pair_recv_sem,
            part * pairs + turn,
            (rep, partner),
        )

    def far_copy(part, turn):
        return remote(
            far_send.at[turn - 1, :, columns[part]],
            far_recv.at[turn - 1, :, columns[part]],
            far_send_sem,
            far_recv_sem,
            part * pairs + turn,
            (rep, flip(me, 2 * turn, count)),
        )

    def exchange(part):
        for turn in range(pairs - 1, -1, -1):
            pair_copy(part, turn).start()

    def combine(part):
        def step(i, carry):
            turn = pairs - 1 - i
            pair_copy(part, turn).wait_recv()
            mine = delta[rows_of(flip(me, 2 * turn, count)), columns[part]].astype(full)
            far_send[turn - 1, :, columns[part]] = (
                mine + pair_recv[turn, :, columns[part]].astype(full)
            ).astype(low)
            far_copy(part, turn).start()
            return carry

        lax.fori_loop(0, pairs - 1, step, 0)

    def collect(part, first, number):
        pair_copy(part, 0).wait_recv()
        for turn in range(1, pairs):
            far_copy(part, turn).wait_recv()
        half = rows // 2

        def step(i, carry):
            at = pl.ds(
                pl.multiple_of(columns[part].start + (i // 2) * width, width), width
            )
            span = pl.ds(pl.multiple_of((i % 2) * half, half), half)
            mine = pl.ds(pl.multiple_of(me * rows + (i % 2) * half, half), half)
            value = delta[mine, at].astype(full) + pair_recv[0, span, at].astype(full)
            for turn in range(1, pairs):
                value = value + far_recv[turn - 1, span, at].astype(full)
            owned[first + i] = value.astype(low)
            return carry

        lax.fori_loop(0, number, step, 0)

    def slope_copy(k):
        target = flip(me, k, count)
        return remote(
            arrived.at[target],
            slope_out.at[me],
            slope_send_sem,
            slope_recv_sem,
            k,
            (rep, target),
        )

    def gain_copy(k):
        target = flip(me, k, count)
        return remote(
            gain_buf.at[target], gain_recv.at[k], gain_send_sem, gain_recv_sem, k, (rep, target)
        )

    def gain_line_copy(k):
        return remote(
            gain_sum,
            gain_line.at[rep],
            gain_line_send,
            gain_line_recv,
            k,
            (lax.rem(rep + k, reps), me),
        )

    for turn in range(1, pairs - 1):
        piece_copy(turn).start()
    place[...] = permutation(order_ref)
    fill_bias(bias, length_ref)
    own_slopes.wait()
    staging[0].wait()
    high = back_ref[...].astype(low)
    rest = (back_ref[...] - high.astype(full)).astype(low)
    slope = matmul(place[...], high, TN) + matmul(place[...], rest, TN)
    steep[...] = slope
    tick(0, 1)
    slope = steep[...]
    staging[1].wait()
    hidden = hidden_ref[...]
    scale = lax.rsqrt(jnp.mean(hidden * hidden, axis=1, keepdims=True) + EPS)
    scaled = slope * gain_ref[1:2, :]
    second = jnp.sum(slope * hidden * scale, axis=0, keepdims=True)
    for owner in range(count):
        gain_buf[owner, 1:2, :] = second[:, owner * rows : (owner + 1) * rows]
    tick(1, 2)
    steep[...] = (
        matmul(place[...], arrived[...].reshape(tokens, width), TN)
        + scale * scaled
        - hidden * (scale * scale * scale) * jnp.mean(hidden * scaled, axis=1, keepdims=True)
    )
    tick(2, 3)
    sharp = steep[...].astype(low)
    staging[2].wait()
    normed[...] = sharp

    def output_part(at, carry):
        spot = pl.ds(pl.multiple_of(at * 512, 512), 512)
        to = pl.ds(pl.multiple_of(joined + at * 512, 512), 512)
        delta[:, to] = matmul(mixed_ref[...], normed[:, spot], TN).astype(low)
        return carry

    lax.fori_loop(0, width // 512, output_part, 0)
    exchange(0)
    tick(3, 4)
    staging[3].wait()
    mixed_slope[...] = matmul(sharp, weight_ref[:, joined:], NT).astype(low)
    tick(4, 5)
    along = along_ref[...]
    across = across_ref[...]

    def heads(g, carry):
        kv = pl.ds(pl.multiple_of(g * 128, 128), 128)
        qs = pl.ds(pl.multiple_of(g * 256, 256), 256)
        keys = key_ref[:, kv]
        values = value_ref[:, kv]
        queries = query_ref[:, qs] * jnp.bfloat16(HEAD_SIZE**-0.5)
        slopes = mixed_slope[:, qs]
        key_parts = []
        value_parts = []
        query_parts = [[], []]
        for a in range(2):
            tick(5 + 2 * g + a, 6 + 2 * g + a)
            key_h = keys[:, a * HEAD_SIZE : (a + 1) * HEAD_SIZE]
            value_h = values[:, a * HEAD_SIZE : (a + 1) * HEAD_SIZE]
            key_slope = [None, None]
            value_slope = [None, None]
            for b in range(2):
                h = 2 * a + b
                spot = slice(h * HEAD_SIZE, (h + 1) * HEAD_SIZE)
                for i, (start, size, reach) in enumerate(query_spans(tokens)):
                    q = queries[start : start + size, spot]
                    d = slopes[start : start + size, spot]
                    score = matmul(key_h[:reach], q, NT) + bias[:reach, start : start + size]
                    probs = jnp.exp(score - logsum_ref[g, h : h + 1, start : start + size])
                    prob_slope = matmul(value_h[:reach], d, NT)
                    inner = jnp.sum(probs * prob_slope, axis=0, keepdims=True)
                    score_slope = (probs * (prob_slope - inner)).astype(low)
                    term = matmul(probs.astype(low), d, NN)
                    value_slope[i] = term if b == 0 else value_slope[i] + term
                    term = matmul(score_slope, q, NN)
                    key_slope[i] = term if b == 0 else key_slope[i] + term
                    query_parts[i].append(matmul(score_slope, key_h[:reach], TN))
            half = tokens // 2
            key_parts.append(
                jnp.concatenate([key_slope[0] + key_slope[1][:half], key_slope[1][half:]], axis=0)
            )
            value_parts.append(
                jnp.concatenate(
                    [value_slope[0] + value_slope[1][:half], value_slope[1][half:]], axis=0
                )
            )
        for i, (start, size, reach) in enumerate(query_spans(tokens)):
            span = slice(start, start + size)
            part = jnp.concatenate(query_parts[i], axis=1) * HEAD_SIZE**-0.5
            backs[span, qs] = turn_pairs(part, along[span], across[span], -1.0).astype(low)
        part = jnp.concatenate(key_parts, axis=1)
        spot = pl.ds(pl.multiple_of(width + g * 128, 128), 128)
        backs[:, spot] = turn_pairs(part, along, across, -1.0).astype(low)
        part = jnp.concatenate(value_parts, axis=1)
        spot = pl.ds(pl.multiple_of(width + key_width + g * 128, 128), 128)
        backs[:, spot] = part.astype(low)

        @pl.when(g == 1)
        def _():
            combine(0)

        return carry

    for copy in staging[4:]:
        copy.wait()
    loops = key_width // 128
    lax.fori_loop(0, loops, heads, 0)
    done = 5 + 2 * loops
    own_piece.start()
    inputs = input_ref[...].astype(full)
    scale = lax.rsqrt(jnp.mean(inputs * inputs, axis=1, keepdims=True) + EPS)
    normed[...] = (inputs * scale * gain_ref[0:1, :]).astype(low)

    def input_part(at, carry):
        spot = pl.ds(pl.multiple_of(at * 512, 512), 512)
        delta[:, spot] = matmul(normed[...], backs[:, spot], TN).astype(low)
        return carry

    lax.fori_loop(0, joined // 512, input_part, 0)
    exchange(1)
    tick(done, done + 1)
    slope = matmul(backs[...], weight_ref[:, :joined], NT)
    combine(1)
    tick(done + 1, done + 2)
    scaled = slope * gain_ref[0:1, :]
    first = jnp.sum(slope * inputs * scale, axis=0, keepdims=True)
    for owner in range(count):
        gain_buf[owner, 0:1, :] = first[:, owner * rows : (owner + 1) * rows]
        gain_buf[owner, 2:8, :] = jnp.zeros((6, rows), full)
    for k in range(1, count):
        gain_copy(k).start()
    result = (
        steep[...]
        + scale * scaled
        - inputs * (scale * scale * scale) * jnp.mean(inputs * scaled, axis=1, keepdims=True)
    )
    moved = matmul(place[...], result.astype(low), NN).astype(low)
    arrived[...] = moved.reshape(arrived.shape)
    for k in range(count - 1, 0, -1):
        slope_copy(k).start()
    slope_out[me] = arrived[me]
    tick(done + 2, done + 5)
    own_piece.wait()
    result = mixed_slope[...].astype(full)
    for turn in range(1, pairs - 1):
        piece_copy(turn).wait_recv()
        result = result + far_piece[turn - 1].astype(full)
    out_ref[...] = result.astype(low)
    collect(0, 0, 2)
    if lined:
        sums.start(0, 2)
    total = gain_buf[me]
    for k in range(1, count):
        gain_copy(k).wait_recv()
        total = total + gain_recv[k]
    gain_sum[...] = total
    gain_line[rep] = total
    for k in range(1, reps):
        gain_line_copy(k).start()
    tick(done + 5, done + 9)
    collect(1, 2, 4)
    if lined:
        sums.start(2, 6)
        tick(done + 9, 3 * PARTS + LAG)
        sums.ticks(0, 6 + LAG)
        sums.finish()
    else:

        def spread_copy(k):
            return remote(
                owned, spread.at[rep], spread_send, spread_recv, k, (lax.rem(rep + k, reps), me)
            )

        for k in range(1, reps):
            spread_copy(k).start()
        spread[rep] = owned[...]
        for k in range(1, reps):
            spread_copy(k).wait_recv()
        value = spread[0].astype(full)
        for k in range(1, reps):
            value = value + spread[k].astype(full)
        delta_out[...] = value.astype(low)
        for k in range(1, reps):
            spread_copy(k).wait_send()
    for k in range(1, reps):
        gain_line_copy(k).wait_recv()
    total = gain_line[0]
    for k in range(1, reps):
        total = total + gain_line[k]
    gain_out[...] = total
    for k in range(1, count):
        slope_copy(k).wait_recv()
    for k in range(1, count):
        slope_copy(k).wait_send()
        gain_copy(k).wait_send()
    for turn in range(1, pairs - 1):
        piece_copy(turn).wait_send()
    for part in range(2):
        for turn in range(pairs):
            pair_copy(part, turn).wait_send()
        for turn in range(1, pairs):
            far_copy(part, turn).wait_send()
    for k in range(1, reps):
        gain_line_copy(k).wait_send()
    if lined:
        line.finish()


def finish_pass(count, reps, back, slopes, *rest):
    *rest, pieces, extra = rest
    tokens, width = back.shape
    weights = rest[4]
    key_width = (weights.shape[1] - 2 * width) // 2
    pairs = count // 2
    rows = width // count
    block = tokens // count
    columns = weights.shape[1]
    low = jnp.bfloat16
    full = jnp.float32
    dma = pltpu.SemaphoreType.DMA
    vmem = pltpu.VMEM
    shape = jax.ShapeDtypeStruct
    lined = reps == LINE
    extra = [extra] if lined else []
    owned = (2 * columns // width, rows // 2, width)
    anywhere = pl.BlockSpec(memory_space=pl.ANY)
    inside = pl.BlockSpec(memory_space=pltpu.VMEM)
    if lined:
        last = line_scratch((3 * PARTS,) + extra[0].shape[1:]) + line_scratch(owned, False)
    else:
        last = [vmem((reps,) + owned, low), dma((reps,)), dma((reps,))]
    return pl.pallas_call(
        functools.partial(finish_kernel, count, reps),
        name="finish_pass",
        out_shape=(
            shape(owned, low),
            shape((8, rows), full),
            shape((count, block, width), low),
            shape((tokens, width), low),
        )
        + tuple(shape((3 * PARTS,) + d.shape[1:], low) for d in extra),
        in_specs=[anywhere, anywhere]
        + [inside] * 4
        + [anywhere, inside]
        + [anywhere] * 5
        + [inside]
        + [anywhere] * (2 + len(extra)),
        out_specs=(inside,) * 4 + (anywhere,) * len(extra),
        scratch_shapes=[
            vmem((tokens, tokens), low),
            vmem((tokens, tokens), full),
            vmem((tokens, width), low),
            vmem((tokens, width), full),
            vmem((tokens, width), low),
            vmem((tokens, width + 2 * key_width), low),
            vmem((count, block, width), low),
            vmem((pairs - 2, tokens, width), low),
            dma((pairs,)),
            dma((pairs,)),
            dma((2,)),
            vmem((width, columns), low),
            vmem((pairs, rows, columns), low),
            vmem((pairs - 1, rows, columns), low),
            vmem((pairs - 1, rows, columns), low),
            dma((2 * pairs,)),
            dma((2 * pairs,)),
            dma((2 * pairs,)),
            dma((2 * pairs,)),
            dma((count,)),
            dma((count,)),
            vmem((count, 8, rows), full),
            vmem((count, 8, rows), full),
            vmem((8, rows), full),
            vmem((reps, 8, rows), full),
            dma((count,)),
            dma((count,)),
            dma((reps,)),
            dma((reps,)),
            vmem(owned, low),
        ]
        + last
        + [
            vmem(a.shape, a.dtype)
            for a in (back, rest[12], rest[10], weights, rest[7], rest[8], rest[9], rest[6])
        ]
        + [dma((8,))],
        compiler_params=pltpu.CompilerParams(
            collective_id=6, has_side_effects=True, vmem_limit_bytes=VMEM_MOST
        ),
        cost_estimate=pl.CostEstimate(
            flops=24 << 30, bytes_accessed=1 << 24, transcendentals=1 << 22
        ),
    )(back, slopes, *rest, pieces, *extra)


def emit_kernel(
    tokens_ref,
    slopes_ref,
    gain_ref,
    delta_ref,
    early_ref,
    middle_ref,
    late_ref,
    tokens_out,
    slopes_out,
    first_out,
    query_out,
    key_out,
    value_out,
    output_out,
    second_out,
    gate_out,
    up_out,
    down_out,
):
    full = jnp.float32
    tokens_out[...] = tokens_ref[...]
    slopes_out[...] = slopes_ref[...]
    rows = early_ref.shape[1]
    hidden = gate_out.shape[3]
    for piece in range(2):
        to = slice(piece * rows, (piece + 1) * rows)
        spot = slice(piece * hidden, (piece + 1) * hidden)
        gate_out[0, :, to, :] = middle_ref[0, :, :, spot].astype(full)
        up_out[0, :, to, :] = middle_ref[1, :, :, spot].astype(full)
        gate_out[1, :, to, :] = late_ref[0, :, :, spot].astype(full)
        up_out[1, :, to, :] = late_ref[1, :, :, spot].astype(full)
    down_out[0] = early_ref[...].astype(full)
    down_out[1] = late_ref[2].astype(full)

    @pl.when(pl.program_id(0) == 0)
    def _():
        first_out[...] = gain_ref[0:1, :]
        second_out[...] = gain_ref[1:2, :]
        half = delta_ref.shape[1]
        key_width = key_out.shape[1]
        for i in range(2):
            span = slice(i * half, (i + 1) * half)
            output_out[span, :] = delta_ref[i].astype(full)
            query_out[span, :] = delta_ref[2 + i].astype(full)
            key_out[span, :] = delta_ref[4 + i, :, :key_width].astype(full)
            value_out[span, :] = delta_ref[4 + i, :, key_width:].astype(full)


def emit_pass(tokens, slopes, gains, deltas, early, middle, late):
    full = jnp.float32
    shape = jax.ShapeDtypeStruct
    number, width = tokens.shape
    rows = gains.shape[1]
    _, high, wide = early.shape
    hidden = high * PARTS
    steps = 4
    each = PARTS // steps

    def moving(*block):
        return pl.BlockSpec(block, lambda i: (i,) + (0,) * (len(block) - 1))

    def fixed(*block):
        return pl.BlockSpec(block, lambda i: (0,) * len(block))

    def inner(*block):
        return pl.BlockSpec(block, lambda i: (0, i, 0, 0))

    return pl.pallas_call(
        emit_kernel,
        name="emit_pass",
        grid=(steps,),
        out_shape=(
            shape(tokens.shape, tokens.dtype),
            shape(slopes.shape, slopes.dtype),
            shape((1, rows), full),
            shape((rows, width), full),
            shape((rows, width // 2), full),
            shape((rows, width // 2), full),
            shape((rows, width), full),
            shape((1, rows), full),
            shape((2, PARTS, 2 * high, hidden), full),
            shape((2, PARTS, 2 * high, hidden), full),
            shape((2, PARTS, high, wide), full),
        ),
        in_specs=[
            moving(number // steps, width),
            moving(number // steps, width),
            fixed(*gains.shape),
            fixed(*deltas.shape),
            moving(each, high, wide),
            inner(2, each, high, wide),
            inner(3, each, high, wide),
        ],
        out_specs=(
            moving(number // steps, width),
            moving(number // steps, width),
            fixed(1, rows),
            fixed(rows, width),
            fixed(rows, width // 2),
            fixed(rows, width // 2),
            fixed(rows, width),
            fixed(1, rows),
            inner(2, each, 2 * high, hidden),
            inner(2, each, 2 * high, hidden),
            inner(2, each, high, wide),
        ),
        compiler_params=pltpu.CompilerParams(vmem_limit_bytes=VMEM_MOST),
        cost_estimate=pl.CostEstimate(flops=1 << 20, bytes_accessed=1 << 24, transcendentals=0),
    )(
        tokens,
        slopes,
        gains,
        deltas,
        early,
        middle.reshape(2, PARTS, high, wide),
        late.reshape(3, PARTS, high, wide),
    )


def local(
    tokens,
    cotangent,
    seq_lengths,
    pack_order,
    unpack_order,
    expert_ids,
    gates,
    first_gain,
    query_weight,
    key_matrix,
    value_matrix,
    output_weight,
    second_gain,
    gate_weight,
    up_weight,
    down_weight,
):
    shards = lax.axis_size("shard")
    group_count, width = tokens.shape
    order = pack_order.reshape(1, group_count)
    (
        joined,
        gains,
        mixing,
        along,
        across,
        inputs,
        queries,
        keys,
        values,
        mixed,
        logsum,
        hidden,
        normed,
        shared,
        all_slopes,
    ) = front_pass(
        tokens,
        (query_weight, key_matrix, value_matrix, output_weight),
        (first_gain, second_gain),
        order,
        expert_ids,
        gates,
        seq_lengths,
        cotangent,
        shards,
    )
    tables = (order, seq_lengths, along, across, joined, gains)
    reps = lax.axis_size("rep")
    inner, row_slopes, partial, *early = expert_pass(
        normed, all_slopes, mixing, gate_weight, up_weight, down_weight, shards, reps
    )
    back, pieces, *middle = return_pass(
        row_slopes, inner, gate_weight, up_weight, down_weight, shared, partial, shards, reps
    )
    deltas, gain_deltas, delta_tokens, out_tokens, *late = finish_pass(
        shards,
        reps,
        back,
        all_slopes,
        *tables,
        inputs,
        queries,
        keys,
        values,
        mixed,
        logsum,
        hidden,
        pieces,
        partial,
    )
    if reps == LINE:
        early, middle, late = early[0], middle[0], late[0]
    else:
        summed = lax.psum(partial, "rep")
        early, middle, late = summed[:PARTS], summed[PARTS : 3 * PARTS], summed[3 * PARTS :]
    (
        out_tokens,
        delta_tokens,
        delta_first,
        delta_query,
        delta_key,
        delta_value,
        delta_output,
        delta_second,
        delta_gate,
        delta_up,
        delta_down,
    ) = emit_pass(
        out_tokens, delta_tokens.reshape(group_count, width), gain_deltas, deltas, early, middle, late
    )
    return (
        out_tokens,
        delta_tokens,
        delta_first.reshape(first_gain.shape),
        delta_query,
        delta_key,
        delta_value,
        delta_output,
        delta_second.reshape(second_gain.shape),
        delta_gate.reshape(gate_weight.shape),
        delta_up.reshape(up_weight.shape),
        delta_down.reshape(down_weight.shape),
    )


def solution(mesh):
    placed = (
        P(("rep", "shard"), None),
        P(("rep", "shard"), None),
        P(("rep", "shard"), None),
        P(("rep", "shard")),
        P(("rep", "shard")),
        P(("rep", "shard"), None),
        P(("rep", "shard"), None),
        P("shard"),
        P("shard", None),
        P("shard", None),
        P("shard", None),
        P("shard", None),
        P("shard"),
        P("shard", None, None),
        P("shard", None, None),
        P("shard", None, None),
    )
    return jax.shard_map(
        local,
        mesh=mesh,
        in_specs=placed,
        out_specs=(
            P(("rep", "shard"), None),
            P(("rep", "shard"), None),
            P("shard"),
            P("shard", None),
            P("shard", None),
            P("shard", None),
            P("shard", None),
            P("shard"),
            P("shard", None, None),
            P("shard", None, None),
            P("shard", None, None),
        ),
        check_vma=False,
    )
```

```python
import functools

import jax
import jax.numpy as jnp
import numpy as np
from jax import lax
from jax.experimental import pallas as pl
from jax.experimental.pallas import tpu as pltpu
from jax.sharding import PartitionSpec as P

QUERY_HEADS = 16
KEY_VALUE_HEADS = 8
HEAD_SIZE = 64


EPS = 1e-05
THETA = 10000.0


MESH = pl.DeviceIdType.MESH
NN = (((1,), (0,)), ((), ()))
NT = (((1,), (1,)), ((), ()))
TN = (((0,), (0,)), ((), ()))
TILE = 256
VMEM_MOST = 66_000_000


def matmul(left, right, dims):
    return lax.dot_general(left, right, dims, preferred_element_type=jnp.float32)


def stage_in(refs, count, start=0):
    held = refs[-count - 1 : -1]
    copies = [
        pltpu.make_async_copy(refs[start + k], held[k], refs[-1].at[k]) for k in range(count)
    ]
    return held, copies, refs[: -count - 1]


def flip(number, mask, count):
    out = 0
    bit = 1
    while bit < count:
        a = (number // bit) % 2
        b = (mask // bit) % 2
        out = out + (a + b - 2 * a * b) * bit
        bit *= 2
    return out


def greet(me, rep, count, reps=1):
    barrier = pltpu.get_barrier_semaphore()
    for k in range(1, count):
        pl.semaphore_signal(
            barrier, inc=1, device_id=(rep, lax.rem(me + k, count)), device_id_type=MESH
        )
    for k in range(1, reps):
        pl.semaphore_signal(
            barrier, inc=1, device_id=(lax.rem(rep + k, reps), me), device_id_type=MESH
        )
    pl.semaphore_wait(barrier, count + reps - 2)


LINE = 4
LAG = 2
RING = 4


class Line:
    def __init__(
        self,
        rep,
        me,
        source,
        out,
        first,
        second,
        both,
        sends,
        recvs,
        held=None,
        sems=None,
        base=0,
        count=None,
    ):
        self.rep, self.me = rep, me
        self.source, self.out = source, out
        self.first, self.second, self.both = first, second, both
        self.sends, self.recvs = sends, recvs
        self.held, self.sems = held, sems
        self.base = base
        self.count = source.shape[0] if count is None else count
        self.outer = (rep == 0) | (rep == LINE - 1)
        self.inner = jnp.logical_not(self.outer)
        self.inside = jnp.where(rep == 0, 1, 2)
        self.outside = jnp.where(rep == 1, 0, 3)
        self.across = LINE - 1 - rep

    def copy(self, stage, i):
        ring = self.both.at[i % RING]
        if stage == 0:
            source = self.source.at[self.base + i]
        else:
            source = ring if stage == 1 else self.first.at[i]
        target = (self.first, self.second, self.first)[stage].at[i]
        device = (self.inside, self.across, self.outside)[stage]
        return pltpu.make_async_remote_copy(
            src_ref=source,
            dst_ref=target,
            send_sem=self.sends.at[stage, i],
            recv_sem=self.recvs.at[stage, i],
            device_id=(device, self.me),
            device_id_type=MESH,
        )

    def load(self, i):
        return pltpu.make_async_copy(
            self.source.at[self.base + i], self.held.at[i % 2], self.sems.at[self.count + i % 2]
        )

    def put(self, i):
        return pltpu.make_async_copy(self.first.at[i], self.out.at[i], self.sems.at[i])

    def loop(self, body, begin=0):
        def step(i, carry):
            body(i)
            return carry

        lax.fori_loop(begin, self.count, step, 0)

    def start(self, begin=0, end=None):
        end = self.count if end is None else end

        @pl.when(self.outer)
        def _():
            def step(i, carry):
                self.copy(0, i).start()
                return carry

            lax.fori_loop(begin, end, step, 0)

        if self.held is not None:

            @pl.when(self.inner)
            def _():
                self.load(0).start()

    def tick(self, j):
        full = jnp.float32
        low = jnp.bfloat16

        @pl.when(self.inner & (j >= 0) & (j < self.count))
        def _():
            if self.held is None:
                own = self.source[self.base + j]
            else:

                @pl.when(j + 1 < self.count)
                def _():
                    self.load(j + 1).start()

                self.load(j).wait()
                own = self.held[j % 2]
            self.copy(0, j).wait_recv()

            @pl.when(j >= RING)
            def _():
                self.copy(1, j - RING).wait_send()

            self.both[j % RING] = (own.astype(full) + self.first[j].astype(full)).astype(low)
            self.copy(1, j).start()

        i = j - LAG

        @pl.when(self.inner & (i >= 0) & (i < self.count))
        def _():
            self.copy(1, i).wait_recv()
            every = self.both[i % RING].astype(full) + self.second[i].astype(full)
            self.first[i] = every.astype(low)
            self.copy(2, i).start()
            if self.held is None:
                self.out[i] = every.astype(low)
            else:
                self.put(i).start()

    def ticks(self, begin, end):
        def step(j, carry):
            self.tick(j)
            return carry

        lax.fori_loop(begin, end, step, 0)

    def receive(self):
        @pl.when(self.outer)
        def _():
            def step(i):
                self.copy(2, i).wait_recv()
                if self.held is None:
                    self.out[i] = self.first[i]
                else:
                    self.put(i).start()

            self.loop(step)

    def finish(self):
        @pl.when(self.outer)
        def _():
            self.loop(lambda i: self.copy(0, i).wait_send())

        @pl.when(self.inner)
        def _():
            self.loop(lambda i: self.copy(1, i).wait_send(), self.count - RING)
            self.loop(lambda i: self.copy(2, i).wait_send())

        if self.held is not None:
            self.loop(lambda i: self.put(i).wait())


def line_scratch(shape, streamed=True):
    low = jnp.bfloat16
    dma = pltpu.SemaphoreType.DMA
    scratch = [
        pltpu.VMEM(shape, low),
        pltpu.VMEM(shape, low),
        pltpu.VMEM((RING,) + shape[1:], low),
        dma((3, shape[0])),
        dma((3, shape[0])),
    ]
    if streamed:
        scratch += [pltpu.VMEM((2,) + shape[1:], low), dma((shape[0] + 2,))]
    return scratch


def remote(source, target, sends, recvs, index, device):
    return pltpu.make_async_remote_copy(
        src_ref=source,
        dst_ref=target,
        send_sem=sends.at[index],
        recv_sem=recvs.at[index],
        device_id=device,
        device_id_type=MESH,
    )


class Gather:
    def __init__(self, count, rep, me, own, slot, sends, recvs):
        self.count, self.rep, self.me = count, rep, me
        self.own, self.slot, self.sends, self.recvs = own, slot, sends, recvs
        self.waiting = []

    def near(self, mask):
        return flip(self.me, mask, self.count)

    def send(self, source, owner, part, mask, index):
        remote(
            source,
            self.slot(owner, part),
            self.sends,
            self.recvs,
            index,
            (self.rep, self.near(mask)),
        ).start()
        self.waiting.append(index)

    def arrived(self, owner, part, index):
        remote(
            self.slot(owner, part),
            self.slot(owner, part),
            self.sends,
            self.recvs,
            index,
            (self.rep, self.me),
        ).wait_recv()

    def pass_on(self, mask, part, index, new, onward):
        owner = self.near(mask)
        if index is not None:
            self.arrived(owner, part, index)
        self.send(self.slot(owner, part), owner, part, onward, new)

    def start(self):
        if self.count == 8:
            plan = ((2, 0, 0), (4, 1, 1), (2, 1, 2), (4, 0, 3), (1, 0, 4), (1, 1, 5))
            for mask, part, index in plan:
                self.send(self.own(part), self.me, part, mask, index)
        else:
            for mask in [1] + list(range(2, self.count, 2)):
                for part in range(2):
                    self.send(self.own(part), self.me, part, mask, 2 * mask + part)

    def relay(self, stage):
        if self.count == 8:
            if stage == 0:
                self.pass_on(2, 0, 0, 6, 4)
                self.pass_on(4, 1, 1, 8, 2)
                self.pass_on(2, 0, None, 7, 1)
                self.pass_on(4, 1, None, 9, 1)
            elif stage == 1:
                self.pass_on(2, 1, 2, 10, 1)
                self.pass_on(4, 0, 3, 11, 1)
            else:
                self.pass_on(6, 0, 6, 12, 1)
                self.pass_on(6, 1, 8, 13, 1)
        elif stage == 2:
            for mask in range(2, self.count, 2):
                for part in range(2):
                    self.pass_on(mask, part, 2 * mask + part, 2 * mask + 2 + part, 1)

    def ready(self, masks):
        if self.count == 8:
            last = ((1, 0, 4), (1, 1, 5), (3, 0, 7), (5, 1, 9), (3, 1, 10), (5, 0, 11))
            last += ((7, 0, 12), (7, 1, 13))
        else:
            last = [(m, p, 2 * m + p) for m in range(1, self.count, 2) for p in range(2)]
        for mask, part, index in last:
            if mask in masks:
                self.arrived(self.near(mask), part, index)

    def finish(self, masks=None):
        self.ready(range(self.count) if masks is None else masks)
        for index in self.waiting:
            spot = self.slot(self.me, 0)
            remote(
                spot, spot, self.sends, self.recvs, index, (self.rep, self.me)
            ).wait_send()


PARTS = 8


def expert_kernel(count, reps, *refs):
    lined = reps == LINE
    (gate_ref, up_ref, down_ref), staging, refs = stage_in(refs, 3, 3)
    for copy in staging:
        copy.start()
    own_ref, slope_ref, mix_ref = refs[:3]
    refs = (None,) * 6 + refs[6:]
    hidden_out, grad_out, delta_out = refs[6:9]
    refs = refs[9:]
    if lined:
        line_out = refs[0]
        refs = refs[1:]
    (
        rows,
        slope_buf,
        hidden_buf,
        grad_buf,
        acc_both,
        acc_down,
        stage,
        send_sem,
        recv_sem,
        own_sem,
        slope_sem,
        hidden_sem,
        grad_sem,
        stage_sem,
    ) = refs[:14]
    rep = lax.axis_index("rep")
    me = lax.axis_index("shard")
    experts, width, hidden = gate_ref.shape
    tokens = own_ref.shape[0]
    half = tokens // 2
    low = jnp.bfloat16
    turns = experts * count
    swap = 2 + count

    def pair(t):
        late = jnp.where(t < swap, t - 2, t - count)
        return (
            jnp.where(t < 4, t // 2, late),
            jnp.where(t < 4, t % 2, jnp.where(t < swap, 0, 1)),
        )

    def pack_of(t):
        return flip(me, pair(t)[0], count)

    def slope_copy(t):
        return pltpu.make_async_copy(
            slope_ref.at[:, pack_of(t)], slope_buf.at[t % 2], slope_sem.at[t % 2]
        )

    def hidden_copy(t):
        spot = pl.ds(pl.multiple_of(pair(t)[1] * hidden, hidden), hidden)
        return pltpu.make_async_copy(
            hidden_buf.at[t % 2], hidden_out.at[pack_of(t), :, spot], hidden_sem.at[t % 2]
        )

    def grad_copy(t):
        spot = pl.ds(pl.multiple_of(pair(t)[1] * 2 * hidden, 2 * hidden), 2 * hidden)
        return pltpu.make_async_copy(
            grad_buf.at[t % 2], grad_out.at[pack_of(t), :, spot], grad_sem.at[t % 2]
        )

    def stage_copy(e):
        span = pl.ds(e * 3 * PARTS, 3 * PARTS)
        return pltpu.make_async_copy(stage.at[span], delta_out.at[span], stage_sem.at[e])

    slope_copy(0).start()
    own = pltpu.make_async_copy(own_ref, rows.at[me], own_sem)
    own.start()
    greet(me, rep, count, reps if lined else 1)
    gather = Gather(
        count,
        rep,
        me,
        lambda p: own_ref.at[pl.ds(p * half, half)],
        lambda owner, p: rows.at[owner, pl.ds(p * half, half)],
        send_sem,
        recv_sem,
    )
    gather.start()
    own.wait()
    for copy in staging:
        copy.wait()
    if lined:
        line = Line(rep, me, stage, line_out, *refs[14:], count=PARTS)

    def spread(e, both, down):
        size = down.shape[0] // PARTS
        side = both.shape[0] // (2 * PARTS)
        base = e * 3 * PARTS
        for i in range(PARTS):
            at = base + (0 if e == 0 else 2 * PARTS) + i
            stage[at] = down[i * size : (i + 1) * size, :].astype(low)
            for which in range(2):
                at = base + (PARTS if e == 0 else 0) + which * PARTS + i
                for piece in range(2):
                    span = slice((2 * i + piece) * side, (2 * i + piece + 1) * side)
                    stage[at, :, piece * hidden : (piece + 1) * hidden] = both[
                        span, which * hidden : (which + 1) * hidden
                    ].astype(low)
        stage_copy(e).start()

    if count == 8:
        plan = {2: ((1,), 0), 4: ((), 1), 5: ((3,), None), 7: ((5,), 2), 9: ((7,), None)}
    else:
        plan = {2: ((1,), None), 4: ((), 2), 5: (tuple(range(3, count, 2)), None)}

    def step(t, carry):
        k, e = pair(t)
        pack = flip(me, k, count)
        for at, (masks, stage_at) in plan.items():

            @pl.when(t == at)
            def _():
                gather.ready(masks)
                if stage_at is not None:
                    gather.relay(stage_at)

        @pl.when(t + 1 < turns)
        def _():
            slope_copy(t + 1).start()

        if lined:
            line.tick(2 * (t - swap - 1))
        slope_copy(t).wait()

        @pl.when(t >= 2)
        def _():
            hidden_copy(t - 2).wait()
            grad_copy(t - 2).wait()

        slot = t % 2
        x = rows[pack]
        dy = slope_buf[slot].reshape(tokens, width)
        mixes = jnp.transpose(mix_ref[pack])
        mix = jnp.where(e == 0, mixes[:, 0:1], mixes[:, 1:2])
        for part in range(hidden // TILE):
            span = pl.ds(part * TILE, TILE)
            ga = matmul(x, gate_ref[e, :, span], NN)
            ua = matmul(x, up_ref[e, :, span], NN)
            dh = matmul(dy, down_ref[e, span, :], NT) * mix
            sig = jax.nn.sigmoid(ga)
            act = ga * sig
            hidden_buf[slot, :, span] = (mix * (act * ua)).astype(low)
            grad_buf[slot, :, span] = (dh * ua * sig * (1.0 + ga * (1.0 - sig))).astype(low)
            grad_buf[slot, :, pl.ds(hidden + part * TILE, TILE)] = (dh * act).astype(low)
        hidden_copy(t).start()
        grad_copy(t).start()
        if lined:
            line.tick(2 * (t - swap) - 1)

        both = matmul(x, grad_buf[slot], TN)
        down = matmul(hidden_buf[slot], dy, TN)

        @pl.when(k == 0)
        def _():
            acc_both[e] = both
            acc_down[e] = down

        @pl.when((k > 0) & (k < count - 1))
        def _():
            acc_both[e] += both
            acc_down[e] += down

        @pl.when(t == swap - 1)
        def _():
            spread(0, acc_both[0] + both, acc_down[0] + down)
            if lined:
                line.start()

        @pl.when(t == turns - 1)
        def _():
            spread(1, acc_both[1] + both, acc_down[1] + down)

        return carry

    lax.fori_loop(0, turns, step, 0)
    if lined:
        line.ticks(2 * (turns - swap - 1), PARTS + LAG)
    for t in (turns - 2, turns - 1):
        hidden_copy(t).wait()
        grad_copy(t).wait()
    gather.finish(())
    stage_copy(0).wait()
    if lined:
        line.receive()
        line.finish()
    stage_copy(1).wait()


def expert_pass(normed, all_slopes, mixing, gate_weight, up_weight, down_weight, count, reps):
    tokens, width = normed.shape
    experts, _, hidden = gate_weight.shape
    block = tokens // count
    low = jnp.bfloat16
    full = jnp.float32
    dma = pltpu.SemaphoreType.DMA
    vmem = pltpu.VMEM
    shape = jax.ShapeDtypeStruct
    anywhere = pl.BlockSpec(memory_space=pl.ANY)
    inside = pl.BlockSpec(memory_space=pltpu.VMEM)
    flops = 2 * count * tokens * width * hidden * experts * 6
    lined = reps == LINE
    segment = (hidden // PARTS, width)
    summed = (PARTS,) + segment
    return pl.pallas_call(
        functools.partial(expert_kernel, count, reps),
        name="expert_pass",
        out_shape=(
            shape((count, tokens, experts * hidden), low),
            shape((count, tokens, 2 * experts * hidden), low),
            shape((6 * PARTS,) + segment, low),
        )
        + ((shape(summed, low),) if lined else ()),
        in_specs=[anywhere, anywhere, inside, anywhere, anywhere, anywhere],
        out_specs=(anywhere,) * 3 + ((inside,) if lined else ()),
        scratch_shapes=[
            vmem((count, tokens, width), low),
            vmem((2, count, block, width), low),
            vmem((2, tokens, hidden), low),
            vmem((2, tokens, 2 * hidden), low),
            vmem((experts, width, 2 * hidden), full),
            vmem((experts, hidden, width), full),
            vmem((6 * PARTS,) + segment, low),
            dma((2 * count + 2,)),
            dma((2 * count + 2,)),
            dma,
            dma((2,)),
            dma((2,)),
            dma((2,)),
            dma((2,)),
        ]
        + (line_scratch(summed, False) if lined else [])
        + [vmem(w.shape, low) for w in (gate_weight, up_weight, down_weight)]
        + [dma((3,))],
        compiler_params=pltpu.CompilerParams(
            collective_id=1, has_side_effects=True, vmem_limit_bytes=VMEM_MOST
        ),
        cost_estimate=pl.CostEstimate(flops=flops, bytes_accessed=1 << 26, transcendentals=0),
    )(
        normed,
        all_slopes.reshape(count, count, block, width),
        mixing,
        gate_weight,
        up_weight,
        down_weight,
    )


def return_kernel(count, reps, *refs):
    (gate_ref, up_ref, down_ref, own_ref), staging, refs = stage_in(refs, 4, 2)
    for copy in staging:
        copy.start()
    grad_ref, hidden_ref = refs[:2]
    lined = reps == LINE
    refs = refs[6:]
    if lined:
        line_ref, back_ref, piece_out, line_out = refs[:4]
        refs = refs[4:]
    else:
        back_ref, piece_out = refs[:2]
        refs = refs[2:]
    (
        grad_buf,
        hidden_buf,
        pair_send,
        far_send,
        pair_recv,
        far_recv,
        total,
        piece,
        last_recv,
        relay_recv,
        load_sem,
        pair_send_sem,
        pair_recv_sem,
        far_send_sem,
        far_recv_sem,
        piece_sem,
        last_sem,
        relay_send_sem,
        relay_recv_sem,
    ) = refs[:19]
    rep = lax.axis_index("rep")
    me = lax.axis_index("shard")
    experts, width, hidden = gate_ref.shape
    tokens = own_ref.shape[0]
    block = tokens // count
    low = jnp.bfloat16
    full = jnp.float32
    pairs = count // 2
    partner = flip(me, 1, count)
    line = Line(rep, me, line_ref, line_out, *refs[19:], base=PARTS, count=2 * PARTS) if lined else None

    relayed = count == 8
    half = tokens // 2

    def mask_of(turn):
        return count - 2 - 2 * turn

    def target(item):
        return flip(me, mask_of(item // 2) + 1 - item % 2, count)

    def grad_load(item):
        return pltpu.make_async_copy(
            grad_ref.at[target(item)], grad_buf.at[item % 2], load_sem.at[item % 2]
        )

    def grad_part(slot, pack):
        value = None
        for e in range(experts):
            for at, weight in ((2 * e, gate_ref), (2 * e + 1, up_ref)):
                term = matmul(grad_buf[slot, :, pl.ds(at * hidden, hidden)], weight[e], NT)
                value = term if value is None else value + term
        total[...] = value

    def hidden_load(item):
        return pltpu.make_async_copy(
            hidden_ref.at[:, target(item)], hidden_buf.at[item % 2], load_sem.at[item % 2]
        )

    def hidden_part(slot, pack):
        value = None
        for e in range(experts):
            term = matmul(
                hidden_buf[slot, :, :, pl.ds(e * hidden, hidden)].reshape(tokens, hidden),
                down_ref[e],
                NN,
            )
            value = term if value is None else value + term
        total[...] = value
        mine = pl.ds(pl.multiple_of(me * block, block), block)
        theirs = pl.ds(pl.multiple_of(pack * block, block), block)
        total[mine, :] += own_ref[theirs, :].astype(full)

    def pair_copy(base, turn):
        return remote(
            pair_send.at[turn % 2],
            pair_recv.at[base + turn],
            pair_send_sem,
            pair_recv_sem,
            base + turn,
            (rep, partner),
        )

    def far_copy(turn, device):
        return remote(
            far_send.at[turn % 2], far_recv.at[turn], far_send_sem, far_recv_sem, turn, (rep, device)
        )

    def half_copy(side):
        span = pl.ds(side * half, half)
        return remote(
            far_send.at[1, span],
            far_recv.at[1, span],
            far_send_sem,
            far_recv_sem,
            side,
            (rep, flip(me, count - 4, count)),
        )

    def relay_copy(phase, side, source):
        return remote(
            source.at[pl.ds(side * half, half)],
            relay_recv.at[2 * phase + side],
            relay_send_sem,
            relay_recv_sem,
            2 * phase + side,
            (rep, flip(me, 2 + 2 * side, count)),
        )

    def last_copy(device):
        return pltpu.make_async_remote_copy(
            src_ref=piece.at[0],
            dst_ref=last_recv,
            send_sem=last_sem.at[0],
            recv_sem=last_sem.at[1],
            device_id=(rep, device),
            device_id_type=MESH,
        )

    def slot(turn):
        return jnp.where(turn == 0, 0, jnp.where(turn == pairs - 1, 3, 1 + turn % 2))

    def piece_copy(turn):
        return pltpu.make_async_copy(
            piece.at[slot(turn)], piece_out.at[turn], piece_sem.at[turn % 2]
        )

    def grad_combine(turn, mask):
        last = turn == pairs - 1
        total[...] += pair_recv[turn].astype(full)

        @pl.when(last)
        def _():
            back_ref[...] = total[...]

        if relayed:

            @pl.when(turn == 0)
            def _():
                far_send[0] = total[...].astype(low)
                for side in range(2):
                    relay_copy(0, side, far_send.at[0]).start()

            @pl.when(turn == 1)
            def _():
                far_send[1] = total[...].astype(low)
                half_copy(1).start()

            @pl.when(turn == 2)
            def _():
                early, later = pl.ds(0, half), pl.ds(half, half)
                for side in range(2):
                    relay_copy(0, side, far_send.at[0]).wait_recv()
                value = far_send[1, early, :].astype(full) + relay_recv[0].astype(full)
                far_send[1, early, :] = value.astype(low)
                half_copy(0).start()
                for side in range(2):
                    relay_copy(0, side, far_send.at[0]).wait_send()
                total[later, :] += relay_recv[1].astype(full)
                far_send[0] = total[...].astype(low)
                far_copy(2, flip(me, mask, count)).start()
        else:

            @pl.when(jnp.logical_not(last))
            def _():
                @pl.when(turn >= 2)
                def _():
                    far_copy(turn - 2, me).wait_send()

                far_send[turn % 2] = total[...].astype(low)
                far_copy(turn, flip(me, mask, count)).start()

    def hidden_combine(turn, mask):
        if not relayed:

            @pl.when((turn >= 3) & (turn < pairs - 1))
            def _():
                piece_copy(turn - 2).wait()

        piece[slot(turn)] = (total[...] + pair_recv[pairs + turn].astype(full)).astype(low)

        @pl.when(turn == 0)
        def _():
            if relayed:
                for side in range(2):
                    relay_copy(1, side, piece.at[0]).start()
            else:
                last_copy(flip(me, mask, count)).start()

        if not relayed:

            @pl.when((turn > 0) & (turn < pairs - 1))
            def _():
                piece_copy(turn).start()

    grad_load(0).start()
    greet(me, rep, count, reps if lined else 1)
    if lined:
        line.start()

    def sweep(base, load, part, combine, pace):
        def item_step(item, carry):
            turn = item // 2
            mask = mask_of(turn)

            @pl.when(item + 1 < 2 * pairs)
            def _():
                load(item + 1).start()

            load(item).wait()
            part(item % 2, target(item))

            @pl.when(item % 2 == 0)
            def _():
                @pl.when(turn >= 2)
                def _():
                    pair_copy(base, turn - 2).wait_send()

                pair_send[turn % 2] = total[...].astype(low)
                pair_copy(base, turn).start()

            @pl.when(item % 2 == 1)
            def _():
                pair_copy(base, turn).wait_recv()
                combine(turn, mask)

            if lined:
                line.ticks(pace(item) - 2, pace(item + 1) - 2)
            return carry

        lax.fori_loop(0, 2 * pairs, item_step, 0)
        for turn in range(max(0, pairs - 2), pairs):
            pair_copy(base, turn).wait_send()

    for copy in staging:
        copy.wait()
    sweep(0, grad_load, grad_part, grad_combine, lambda item: 3 * item // 2)
    hidden_load(0).start()
    sweep(pairs, hidden_load, hidden_part, hidden_combine, lambda item: 3 * pairs + item)
    if lined:
        line.ticks(5 * pairs - 2, 2 * PARTS + LAG)
    if relayed:
        for side in range(2):
            half_copy(side).wait_recv()
        back_ref[...] += far_recv[1].astype(full)
        far_copy(2, me).wait_recv()
        back_ref[...] += far_recv[2].astype(full)
        for side in range(2):
            half_copy(side).wait_send()
        far_copy(2, me).wait_send()
    else:

        def add(turn, carry):
            far_copy(turn, me).wait_recv()
            back_ref[...] += far_recv[turn].astype(full)
            return carry

        lax.fori_loop(0, pairs - 1, add, 0)
        for turn in (pairs - 3, pairs - 2):
            far_copy(turn, me).wait_send()
    if lined:
        line.receive()
    if relayed:
        for side in range(2):
            relay_copy(1, side, piece.at[0]).wait_recv()
            rows = pl.ds(side * half, half)
            spot = slot(1 + side)
            value = piece[spot, rows, :].astype(full) + relay_recv[2 + side].astype(full)
            piece[spot, rows, :] = value.astype(low)
            piece_copy(1 + side).start()
            relay_copy(1, side, piece.at[0]).wait_send()
    else:
        last_copy(me).wait_recv()
        value = piece[3].astype(full) + last_recv[...].astype(full)
        piece[3] = value.astype(low)
        last_copy(me).wait_send()
    for turn in (pairs - 3, pairs - 2):
        piece_copy(turn).wait()
    piece_copy(pairs - 1).start()
    if lined:
        line.finish()
    piece_copy(pairs - 1).wait()


def return_pass(grads, hiddens, gate_weight, up_weight, down_weight, own, deltas, count, reps):
    tokens, width = own.shape
    experts, _, hidden = gate_weight.shape
    block = tokens // count
    low = jnp.bfloat16
    full = jnp.float32
    pairs = count // 2
    dma = pltpu.SemaphoreType.DMA
    shape = jax.ShapeDtypeStruct
    anywhere = pl.BlockSpec(memory_space=pl.ANY)
    inside = pl.BlockSpec(memory_space=pltpu.VMEM)
    flops = 2 * count * tokens * width * hidden * experts * 3
    lined = reps == LINE
    extra = [deltas] if lined else []
    return pl.pallas_call(
        functools.partial(return_kernel, count, reps),
        name="return_pass",
        out_shape=(
            shape((tokens, width), full),
            shape((pairs, tokens, width), low),
        )
        + tuple(shape((2 * PARTS,) + d.shape[1:], low) for d in extra),
        in_specs=[anywhere] * (6 + len(extra)),
        out_specs=(inside, anywhere) + (anywhere,) * len(extra),
        scratch_shapes=[
            pltpu.VMEM((2, tokens, 2 * experts * hidden), low),
            pltpu.VMEM((2, count, block, experts * hidden), low),
            pltpu.VMEM((2, tokens, width), low),
            pltpu.VMEM((2, tokens, width), low),
            pltpu.VMEM((2 * pairs, tokens, width), low),
            pltpu.VMEM((pairs, tokens, width), low),
            pltpu.VMEM((tokens, width), full),
            pltpu.VMEM((4, tokens, width), low),
            pltpu.VMEM((8, 128) if count == 8 else (tokens, width), low),
            pltpu.VMEM((4, tokens // 2, width), low),
            dma((2,)),
            dma((2 * pairs,)),
            dma((2 * pairs,)),
            dma((pairs,)),
            dma((pairs,)),
            dma((2,)),
            dma((3,)),
            dma((4,)),
            dma((4,)),
        ]
        + (line_scratch((2 * PARTS,) + deltas.shape[1:]) if lined else [])
        + [pltpu.VMEM(a.shape, low) for a in (gate_weight, up_weight, down_weight, own)]
        + [dma((4,))],
        compiler_params=pltpu.CompilerParams(
            collective_id=2, has_side_effects=True, vmem_limit_bytes=VMEM_MOST
        ),
        cost_estimate=pl.CostEstimate(flops=flops, bytes_accessed=1 << 26, transcendentals=0),
    )(
        grads,
        hiddens.reshape(count, count, block, experts * hidden),
        gate_weight,
        up_weight,
        down_weight,
        own,
        *extra,
    )


def turn_pairs(rows, along, across, sign):
    lane = lax.broadcasted_iota(jnp.int32, (rows.shape[0], 128), 1)
    early = (lane % HEAD_SIZE) < HEAD_SIZE // 2
    pieces = []
    for at in range(0, rows.shape[1], 128):
        part = rows[:, at : at + 128]
        other = jnp.where(
            early,
            pltpu.roll(part, 128 - HEAD_SIZE // 2, 1),
            pltpu.roll(part, HEAD_SIZE // 2, 1),
        )
        pieces.append(part * along + sign * (other * across))
    return pieces[0] if len(pieces) == 1 else jnp.concatenate(pieces, axis=1)


def permutation(order_ref):
    tokens = order_ref.shape[1]
    rows = lax.broadcasted_iota(jnp.int32, (tokens, tokens), 0)
    return jnp.where(order_ref[...] == rows, 1.0, 0.0).astype(jnp.bfloat16)


def starts_of(position, length_ref):
    start = jnp.zeros_like(position)
    end = jnp.zeros((1, 1), jnp.int32)
    for k in range(length_ref.shape[1] - 1):
        end = end + length_ref[0:1, k : k + 1]
        start = jnp.where(position >= end, end, start)
    return start


def fill_bias(bias, length_ref):
    tokens = bias.shape[0]
    keys = lax.broadcasted_iota(jnp.int32, (tokens, tokens), 0)
    queries = lax.broadcasted_iota(jnp.int32, (tokens, tokens), 1)
    start = starts_of(lax.broadcasted_iota(jnp.int32, (1, tokens), 1), length_ref)
    bias[...] = jnp.where((keys >= start) & (keys <= queries), 0.0, -1e30)


def query_spans(tokens):
    half = tokens // 2
    return ((0, half, half), (half, half, tokens))


def first_kernel(
    count,
    token_ref,
    query_ref,
    key_ref,
    value_ref,
    output_ref,
    gain_ref,
    order_ref,
    id_ref,
    gate_ref,
    arrived_out,
    joined_out,
    gain_out,
    mix_out,
    mix_buf,
    gain_buf,
    token_send,
    token_recv,
    gain_send,
    gain_recv,
    mix_send,
    mix_recv,
    weight_send,
    weight_recv,
    local_sem,
):
    rep = lax.axis_index("rep")
    me = lax.axis_index("shard")
    full = jnp.float32
    low = jnp.bfloat16
    rows = query_ref.shape[0]
    experts = mix_out.shape[0] * 2
    mine = pl.multiple_of(me * rows, rows)
    locals_ = [pltpu.make_async_copy(token_ref.at[me], arrived_out.at[me], local_sem.at[0])]
    at = 0
    for i, ref in enumerate((query_ref, key_ref, value_ref, output_ref)):
        size = ref.shape[1]
        target = joined_out.at[pl.ds(mine, rows), pl.ds(at, size)]
        locals_.append(pltpu.make_async_copy(ref, target, local_sem.at[1 + i]))
        at += size
    for copy in locals_:
        copy.start()
    greet(me, rep, count)

    def token_copy(k):
        target = flip(me, k, count)
        return remote(
            token_ref.at[target], arrived_out.at[me], token_send, token_recv, k, (rep, target)
        )

    def gain_copy(k):
        return remote(
            gain_ref, gain_buf.at[me], gain_send, gain_recv, k, (rep, flip(me, k, count))
        )

    def mix_copy(k):
        target = flip(me, k, count)
        return remote(mix_buf.at[target], mix_out.at[me], mix_send, mix_recv, k, (rep, target))

    for k in range(count - 1, 0, -1):
        token_copy(k).start()
    for copy in locals_[1:]:
        copy.wait()
    half = rows // 2

    def block(owner, part):
        return joined_out.at[pl.ds(pl.multiple_of(owner * rows + part * half, half), half)]

    weights = Gather(count, rep, me, lambda p: block(me, p), block, weight_send, weight_recv)
    weights.start()
    for k in range(1, count):
        gain_copy(k).start()
    gain_buf[me] = gain_ref[...]
    tokens = order_ref.shape[0]
    lane = lax.broadcasted_iota(jnp.int32, (tokens, experts), 1)
    mixing = jnp.zeros((tokens, experts), full)
    for k in range(id_ref.shape[1]):
        mixing = mixing + jnp.where(id_ref[:, k : k + 1] == lane, gate_ref[:, k : k + 1], 0.0)
    place = permutation(order_ref)
    moved = jnp.zeros((experts, tokens), full)
    for _ in range(3):
        high = mixing.astype(low)
        moved = moved + matmul(high, place, TN)
        mixing = mixing - high.astype(full)
    for owner in range(count):
        mix_buf[owner, 0:2, :] = moved[2 * owner : 2 * owner + 2, :]
        mix_buf[owner, 2:8, :] = jnp.zeros((6, tokens), full)
    weights.relay(0)
    for k in range(1, count):
        mix_copy(k).start()
    mix_out[me] = mix_buf[me]
    weights.relay(1)
    weights.relay(2)
    locals_[0].wait()
    for k in range(1, count):
        gain_copy(k).wait_recv()
    for owner in range(count):
        gain_out[:, owner * rows : (owner + 1) * rows] = gain_buf[owner]
    for k in range(1, count):
        token_copy(k).wait_recv()
        mix_copy(k).wait_recv()
    weights.finish()
    for k in range(1, count):
        token_copy(k).wait_send()
        gain_copy(k).wait_send()
        mix_copy(k).wait_send()


def first_pass(tokens, weights, gains, order, expert_ids, gates, count):
    rows = weights[0].shape[0]
    number, width = tokens.shape
    block = number // count
    low = jnp.bfloat16
    full = jnp.float32
    dma = pltpu.SemaphoreType.DMA
    inside = pl.BlockSpec(memory_space=pltpu.VMEM)
    columns = sum(w.shape[1] for w in weights)
    shape = jax.ShapeDtypeStruct
    return pl.pallas_call(
        functools.partial(first_kernel, count),
        name="first_pass",
        out_shape=(
            shape((count, block, width), low),
            shape((rows * count, columns), low),
            shape((8, rows * count), full),
            shape((count, 8, number), full),
        ),
        in_specs=[inside] * 9,
        out_specs=(inside,) * 4,
        scratch_shapes=[
            pltpu.VMEM((count, 8, number), full),
            pltpu.VMEM((count, 8, rows), full),
            dma((count,)),
            dma((count,)),
            dma((count,)),
            dma((count,)),
            dma((count,)),
            dma((count,)),
            dma((2 * count + 2,)),
            dma((2 * count + 2,)),
            dma((5,)),
        ],
        compiler_params=pltpu.CompilerParams(
            collective_id=4, has_side_effects=True, vmem_limit_bytes=VMEM_MOST
        ),
        cost_estimate=pl.CostEstimate(flops=1 << 24, bytes_accessed=1 << 26, transcendentals=0),
    )(tokens.reshape(count, block, width), *weights, gains, order, expert_ids, gates)


def front_kernel(
    count,
    token_ref,
    query_ref,
    key_ref,
    value_ref,
    output_ref,
    first_ref,
    second_ref,
    order_ref,
    id_ref,
    gate_ref,
    length_ref,
    speed_ref,
    cotangent_ref,
    joined_out,
    gain_out,
    mix_out,
    along_out,
    across_out,
    input_out,
    query_out,
    key_out,
    value_out,
    mixed_out,
    logsum_out,
    hidden_out,
    normed_out,
    shared_out,
    slopes_out,
    arrived,
    joined,
    mix_buf,
    gain_src,
    gain_buf,
    place,
    bias,
    normed,
    inputs,
    projected,
    mixed,
    hidden,
    moved,
    shared,
    token_send,
    token_recv,
    gain_send,
    gain_recv,
    mix_send,
    mix_recv,
    weight_send,
    weight_recv,
    slope_send,
    slope_recv,
    local_sem,
    out_sem,
):
    rep = lax.axis_index("rep")
    me = lax.axis_index("shard")
    low = jnp.bfloat16
    full = jnp.float32
    rows = query_ref.shape[0]
    tokens, width = cotangent_ref.shape
    key_width = key_ref.shape[1]
    experts = mix_out.shape[0] * 2
    mine = pl.multiple_of(me * rows, rows)
    own = [pltpu.make_async_copy(token_ref.at[me], arrived.at[me], local_sem.at[0])]
    at = 0
    for i, ref in enumerate((query_ref, key_ref, value_ref, output_ref)):
        size = ref.shape[1]
        spot = joined.at[pl.ds(mine, rows), pl.ds(at, size)]
        own.append(pltpu.make_async_copy(ref, spot, local_sem.at[1 + i]))
        at += size
    own.append(pltpu.make_async_copy(cotangent_ref, slopes_out.at[me], local_sem.at[5]))
    for copy in own:
        copy.start()
    gain_src[...] = jnp.zeros(gain_src.shape, full)
    gain_src[0:1, :] = first_ref[...].astype(full)
    gain_src[1:2, :] = second_ref[...].astype(full)
    greet(me, rep, count)

    def token_copy(k):
        target = flip(me, k, count)
        return remote(
            token_ref.at[target], arrived.at[me], token_send, token_recv, k, (rep, target)
        )

    def gain_copy(k):
        return remote(
            gain_src, gain_buf.at[me], gain_send, gain_recv, k, (rep, flip(me, k, count))
        )

    def mix_copy(k):
        target = flip(me, k, count)
        return remote(mix_buf.at[target], mix_out.at[me], mix_send, mix_recv, k, (rep, target))

    for k in range(count - 1, 0, -1):
        token_copy(k).start()
    for copy in own[1:5]:
        copy.wait()
    half = rows // 2

    def block(owner, part):
        return joined.at[pl.ds(pl.multiple_of(owner * rows + part * half, half), half)]

    weights = Gather(count, rep, me, lambda p: block(me, p), block, weight_send, weight_recv)
    weights.start()
    for k in range(1, count):
        gain_copy(k).start()
    gain_buf[me] = gain_src[...]
    some = tokens // 2
    slopes = Gather(
        count,
        rep,
        me,
        lambda p: cotangent_ref.at[pl.ds(p * some, some)],
        lambda owner, p: slopes_out.at[owner, pl.ds(p * some, some)],
        slope_send,
        slope_recv,
    )
    kinds = lax.broadcasted_iota(jnp.int32, (experts, tokens), 0)
    mixing = jnp.zeros((experts, tokens), full)
    for k in range(id_ref.shape[0]):
        mixing = mixing + jnp.where(id_ref[k : k + 1, :] == kinds, gate_ref[k : k + 1, :], 0.0)
    place[...] = permutation(order_ref)
    dealt = jnp.zeros((experts, tokens), full)
    for _ in range(3):
        high = mixing.astype(low)
        dealt = dealt + matmul(high, place[...], NT)
        mixing = mixing - high.astype(full)
    for owner in range(count):
        mix_buf[owner, 0:2, :] = dealt[2 * owner : 2 * owner + 2, :]
        mix_buf[owner, 2:8, :] = jnp.zeros((6, tokens), full)
    weights.relay(0)
    for k in range(1, count):
        mix_copy(k).start()
    mix_out[me] = mix_buf[me]
    slopes.start()
    fill_bias(bias, length_ref)
    position = lax.broadcasted_iota(jnp.int32, along_out.shape, 0)
    angle = (position - starts_of(position, length_ref)).astype(full) * speed_ref[0:1, :]
    along_out[...] = jnp.cos(angle)
    across_out[...] = jnp.sin(angle) * speed_ref[1:2, :]
    own[0].wait()
    for k in range(1, count):
        token_copy(k).wait_recv()
        gain_copy(k).wait_recv()
    for owner in range(count):
        gain_out[:, owner * rows : (owner + 1) * rows] = gain_buf[owner]
    outs = (
        (inputs, input_out),
        (projected.at[:, pl.ds(0, width)], query_out),
        (projected.at[:, pl.ds(width, key_width)], key_out),
        (projected.at[:, pl.ds(width + key_width, key_width)], value_out),
        (mixed, mixed_out),
        (hidden, hidden_out),
        (moved, normed_out),
        (shared, shared_out),
        (joined, joined_out),
    )
    puts = [pltpu.make_async_copy(a, b, out_sem.at[k]) for k, (a, b) in enumerate(outs)]
    rows_in = matmul(place[...], arrived[...].reshape(tokens, width), TN)
    inputs[...] = rows_in.astype(low)
    scale = lax.rsqrt(jnp.mean(rows_in * rows_in, axis=1, keepdims=True) + EPS)
    normed[...] = (rows_in * scale * gain_out[0:1, :]).astype(low)
    puts[0].start()
    weights.relay(1)
    weights.relay(2)
    weights.ready(range(count))
    puts[8].start()
    along = along_out[...]
    across = across_out[...]

    def turned(at, carry):
        spot = pl.ds(pl.multiple_of(at * key_width, key_width), key_width)
        part = matmul(normed[...], joined[:, spot], NN)
        projected[:, spot] = turn_pairs(part, along, across, 1.0).astype(low)
        return carry

    lax.fori_loop(0, width // key_width + 1, turned, 0)
    part = matmul(normed[...], joined[:, width + key_width : width + 2 * key_width], NN)
    projected[:, width + key_width :] = part.astype(low)
    for copy in puts[1:4]:
        copy.start()

    def heads(g, carry):
        qs = pl.ds(pl.multiple_of(g * 256, 256), 256)
        kv = pl.ds(pl.multiple_of(width + g * 128, 128), 128)
        keys = projected[:, kv]
        kv = pl.ds(pl.multiple_of(width + key_width + g * 128, 128), 128)
        values = projected[:, kv]
        queries = projected[:, qs] * jnp.bfloat16(HEAD_SIZE**-0.5)
        for start, size, reach in query_spans(tokens):
            pieces = []
            for h in range(4):
                a = (h // 2) * HEAD_SIZE
                score = matmul(
                    keys[:reach, a : a + HEAD_SIZE],
                    queries[start : start + size, h * HEAD_SIZE : (h + 1) * HEAD_SIZE],
                    NT,
                )
                score = score + bias[:reach, start : start + size]
                largest = jnp.max(score, axis=0, keepdims=True)
                powers = jnp.exp(score - largest)
                totals = jnp.sum(powers, axis=0, keepdims=True)
                shares = (powers * (1.0 / totals)).astype(low)
                pieces.append(matmul(shares, values[:reach, a : a + HEAD_SIZE], TN))
                logsum_out[g, h : h + 1, start : start + size] = largest + jnp.log(totals)
            mixed[start : start + size, qs] = jnp.concatenate(pieces, axis=1).astype(low)

        @pl.when(g == 1)
        def _():
            slopes.relay(0)

        return carry

    lax.fori_loop(0, key_width // 128, heads, 0)
    puts[4].start()
    total = inputs[...].astype(full) + matmul(mixed[...], joined[:, width + 2 * key_width :], NN)
    hidden[...] = total
    scale = lax.rsqrt(jnp.mean(total * total, axis=1, keepdims=True) + EPS)
    normed[...] = (total * scale * gain_out[1:2, :]).astype(low)
    puts[5].start()
    moved[...] = matmul(place[...], normed[...], NN).astype(low)
    puts[6].start()
    shared[...] = matmul(place[...], hidden[...].astype(low), NN).astype(low)
    puts[7].start()
    slopes.relay(1)
    for k in range(1, count):
        mix_copy(k).wait_recv()
    for copy in puts:
        copy.wait()
    slopes.relay(2)
    own[5].wait()
    slopes.finish()
    weights.finish(())
    for k in range(1, count):
        token_copy(k).wait_send()
        gain_copy(k).wait_send()
        mix_copy(k).wait_send()


def front_pass(tokens, weights, gains, order, expert_ids, gates, lengths, cotangent, count):
    rows = weights[0].shape[0]
    number, width = tokens.shape
    key_width = weights[1].shape[1]
    block = number // count
    low = jnp.bfloat16
    full = jnp.float32
    dma = pltpu.SemaphoreType.DMA
    vmem = pltpu.VMEM
    anywhere = pl.BlockSpec(memory_space=pl.ANY)
    inside = pl.BlockSpec(memory_space=pltpu.VMEM)
    columns = sum(w.shape[1] for w in weights)
    shape = jax.ShapeDtypeStruct
    half = HEAD_SIZE // 2
    speed = np.tile(THETA ** (-2.0 * np.arange(half) / HEAD_SIZE), 128 // half)
    side = np.tile(np.repeat([-1.0, 1.0], half), 128 // HEAD_SIZE)
    speeds = jnp.asarray(np.stack([speed, side]).astype(np.float32))
    return pl.pallas_call(
        functools.partial(front_kernel, count),
        name="front_pass",
        out_shape=(
            shape((rows * count, columns), low),
            shape((8, rows * count), full),
            shape((count, 8, number), full),
            shape((number, 128), full),
            shape((number, 128), full),
            shape((number, width), low),
            shape((number, width), low),
            shape((number, key_width), low),
            shape((number, key_width), low),
            shape((number, width), low),
            shape((key_width // 128, 4, number), full),
            shape((number, width), full),
            shape((number, width), low),
            shape((number, width), low),
            shape((count, number, width), low),
        ),
        in_specs=[anywhere] * 5 + [inside] * 7 + [anywhere],
        out_specs=(anywhere,)
        + (inside,) * 4
        + (anywhere,) * 5
        + (inside,)
        + (anywhere,) * 4,
        scratch_shapes=[
            vmem((count, block, width), low),
            vmem((rows * count, columns), low),
            vmem((count, 8, number), full),
            vmem((8, rows), full),
            vmem((count, 8, rows), full),
            vmem((number, number), low),
            vmem((number, number), full),
            vmem((number, width), low),
            vmem((number, width), low),
            vmem((number, width + 2 * key_width), low),
            vmem((number, width), low),
            vmem((number, width), full),
            vmem((number, width), low),
            vmem((number, width), low),
            dma((count,)),
            dma((count,)),
            dma((count,)),
            dma((count,)),
            dma((count,)),
            dma((count,)),
            dma((2 * count + 2,)),
            dma((2 * count + 2,)),
            dma((2 * count + 2,)),
            dma((2 * count + 2,)),
            dma((6,)),
            dma((9,)),
        ],
        compiler_params=pltpu.CompilerParams(
            collective_id=4, has_side_effects=True, vmem_limit_bytes=VMEM_MOST
        ),
        cost_estimate=pl.CostEstimate(
            flops=12 << 30, bytes_accessed=1 << 26, transcendentals=1 << 22
        ),
    )(
        tokens.reshape(count, block, width),
        *weights,
        *(gain.reshape(1, rows) for gain in gains),
        order,
        expert_ids.T,
        gates.T,
        lengths,
        speeds,
        cotangent,
    )


def finish_kernel(count, reps, *refs):
    lined = reps == LINE
    (
        back_ref,
        slopes_ref,
        order_ref,
        length_ref,
        along_ref,
        across_ref,
        weight_ref,
        gain_ref,
        input_ref,
        query_ref,
        key_ref,
        value_ref,
        mixed_ref,
        logsum_ref,
        hidden_ref,
        piece_ref,
    ) = refs[:16]
    refs = refs[16:]
    staged = (
        back_ref,
        hidden_ref,
        mixed_ref,
        weight_ref,
        query_ref,
        key_ref,
        value_ref,
        input_ref,
    )
    held = refs[-len(staged) - 1 : -1]
    staging = [
        pltpu.make_async_copy(ref, buf, refs[-1].at[k])
        for k, (ref, buf) in enumerate(zip(staged, held, strict=True))
    ]
    refs = refs[: -len(staged) - 1]
    (
        back_ref,
        hidden_ref,
        mixed_ref,
        weight_ref,
        query_ref,
        key_ref,
        value_ref,
        input_ref,
    ) = held
    if lined:
        line_ref = refs[0]
        refs = refs[1:]
    delta_out, gain_out, slope_out, out_ref = refs[:4]
    refs = refs[4:]
    if lined:
        line_out = refs[0]
        refs = refs[1:]
    (
        place,
        bias,
        normed,
        steep,
        mixed_slope,
        backs,
        arrived,
        far_piece,
        far_piece_send,
        far_piece_recv,
        local_sem,
        delta,
        pair_recv,
        far_send,
        far_recv,
        pair_send_sem,
        pair_recv_sem,
        far_send_sem,
        far_recv_sem,
        slope_send_sem,
        slope_recv_sem,
        gain_buf,
        gain_recv,
        gain_sum,
        gain_line,
        gain_send_sem,
        gain_recv_sem,
        gain_line_send,
        gain_line_recv,
        owned,
    ) = refs[:30]
    refs = refs[30:]
    low = jnp.bfloat16
    full = jnp.float32
    rep = lax.axis_index("rep")
    me = lax.axis_index("shard")
    pairs = count // 2
    partner = flip(me, 1, count)
    tokens, width = back_ref.shape
    key_width = key_ref.shape[1]
    joined = width + 2 * key_width
    rows = width // count
    block = tokens // count
    own_slopes = pltpu.make_async_copy(
        slopes_ref.at[:, pl.ds(pl.multiple_of(me * block, block), block)],
        arrived,
        local_sem.at[0],
    )
    staging[0].start()
    own_slopes.start()
    for copy in staging[1:]:
        copy.start()
    own_piece = pltpu.make_async_copy(piece_ref.at[pairs - 1], mixed_slope, local_sem.at[1])
    greet(me, rep, count, reps)
    if lined:
        line = Line(rep, me, line_ref, line_out, *refs[:7], base=3 * PARTS, count=3 * PARTS)
        sums = Line(rep, me, owned, delta_out, *refs[7:12])
        line.start()
    else:
        spread, spread_send, spread_recv = refs

    def tick(begin, end):
        if lined:
            line.ticks(begin, end)

    def piece_copy(turn):
        return remote(
            piece_ref.at[turn],
            far_piece.at[turn - 1],
            far_piece_send,
            far_piece_recv,
            turn,
            (rep, flip(me, count - 2 - 2 * turn, count)),
        )

    def rows_of(owner):
        return pl.ds(pl.multiple_of(owner * rows, rows), rows)

    columns = (slice(joined, joined + width), slice(0, joined))

    def pair_copy(part, turn):
        return remote(
            delta.at[rows_of(flip(partner, 2 * turn, count)), columns[part]],
            pair_recv.at[turn, :, columns[part]],
            pair_send_sem,
            pair_recv_sem,
            part * pairs + turn,
            (rep, partner),
        )

    def far_copy(part, turn):
        return remote(
            far_send.at[turn - 1, :, columns[part]],
            far_recv.at[turn - 1, :, columns[part]],
            far_send_sem,
            far_recv_sem,
            part * pairs + turn,
            (rep, flip(me, 2 * turn, count)),
        )

    def exchange(part):
        for turn in range(pairs - 1, -1, -1):
            pair_copy(part, turn).start()

    def combine(part):
        def step(i, carry):
            turn = pairs - 1 - i
            pair_copy(part, turn).wait_recv()
            mine = delta[rows_of(flip(me, 2 * turn, count)), columns[part]].astype(full)
            far_send[turn - 1, :, columns[part]] = (
                mine + pair_recv[turn, :, columns[part]].astype(full)
            ).astype(low)
            far_copy(part, turn).start()
            return carry

        lax.fori_loop(0, pairs - 1, step, 0)

    def collect(part, first, number):
        pair_copy(part, 0).wait_recv()
        for turn in range(1, pairs):
            far_copy(part, turn).wait_recv()
        half = rows // 2

        def step(i, carry):
            at = pl.ds(
                pl.multiple_of(columns[part].start + (i // 2) * width, width), width
            )
            span = pl.ds(pl.multiple_of((i % 2) * half, half), half)
            mine = pl.ds(pl.multiple_of(me * rows + (i % 2) * half, half), half)
            value = delta[mine, at].astype(full) + pair_recv[0, span, at].astype(full)
            for turn in range(1, pairs):
                value = value + far_recv[turn - 1, span, at].astype(full)
            owned[first + i] = value.astype(low)
            return carry

        lax.fori_loop(0, number, step, 0)

    def slope_copy(k):
        target = flip(me, k, count)
        return remote(
            arrived.at[target],
            slope_out.at[me],
            slope_send_sem,
            slope_recv_sem,
            k,
            (rep, target),
        )

    def gain_copy(k):
        target = flip(me, k, count)
        return remote(
            gain_buf.at[target], gain_recv.at[k], gain_send_sem, gain_recv_sem, k, (rep, target)
        )

    def gain_line_copy(k):
        return remote(
            gain_sum,
            gain_line.at[rep],
            gain_line_send,
            gain_line_recv,
            k,
            (lax.rem(rep + k, reps), me),
        )

    for turn in range(1, pairs - 1):
        piece_copy(turn).start()
    place[...] = permutation(order_ref)
    fill_bias(bias, length_ref)
    own_slopes.wait()
    staging[0].wait()
    high = back_ref[...].astype(low)
    rest = (back_ref[...] - high.astype(full)).astype(low)
    slope = matmul(place[...], high, TN) + matmul(place[...], rest, TN)
    steep[...] = slope
    tick(0, 1)
    slope = steep[...]
    staging[1].wait()
    hidden = hidden_ref[...]
    scale = lax.rsqrt(jnp.mean(hidden * hidden, axis=1, keepdims=True) + EPS)
    scaled = slope * gain_ref[1:2, :]
    second = jnp.sum(slope * hidden * scale, axis=0, keepdims=True)
    for owner in range(count):
        gain_buf[owner, 1:2, :] = second[:, owner * rows : (owner + 1) * rows]
    tick(1, 2)
    steep[...] = (
        matmul(place[...], arrived[...].reshape(tokens, width), TN)
        + scale * scaled
        - hidden * (scale * scale * scale) * jnp.mean(hidden * scaled, axis=1, keepdims=True)
    )
    tick(2, 3)
    sharp = steep[...].astype(low)
    staging[2].wait()
    normed[...] = sharp

    def output_part(at, carry):
        spot = pl.ds(pl.multiple_of(at * 512, 512), 512)
        to = pl.ds(pl.multiple_of(joined + at * 512, 512), 512)
        delta[:, to] = matmul(mixed_ref[...], normed[:, spot], TN).astype(low)
        return carry

    lax.fori_loop(0, width // 512, output_part, 0)
    exchange(0)
    tick(3, 4)
    staging[3].wait()
    mixed_slope[...] = matmul(sharp, weight_ref[:, joined:], NT).astype(low)
    tick(4, 5)
    along = along_ref[...]
    across = across_ref[...]

    def heads(g, carry):
        kv = pl.ds(pl.multiple_of(g * 128, 128), 128)
        qs = pl.ds(pl.multiple_of(g * 256, 256), 256)
        keys = key_ref[:, kv]
        values = value_ref[:, kv]
        queries = query_ref[:, qs] * jnp.bfloat16(HEAD_SIZE**-0.5)
        slopes = mixed_slope[:, qs]
        key_parts = []
        value_parts = []
        query_parts = [[], []]
        for a in range(2):
            tick(5 + 3 * (2 * g + a) // 2, 5 + 3 * (2 * g + a + 1) // 2)
            key_h = keys[:, a * HEAD_SIZE : (a + 1) * HEAD_SIZE]
            value_h = values[:, a * HEAD_SIZE : (a + 1) * HEAD_SIZE]
            key_slope = [None, None]
            value_slope = [None, None]
            for b in range(2):
                h = 2 * a + b
                spot = slice(h * HEAD_SIZE, (h + 1) * HEAD_SIZE)
                for i, (start, size, reach) in enumerate(query_spans(tokens)):
                    q = queries[start : start + size, spot]
                    d = slopes[start : start + size, spot]
                    score = matmul(key_h[:reach], q, NT) + bias[:reach, start : start + size]
                    probs = jnp.exp(score - logsum_ref[g, h : h + 1, start : start + size])
                    prob_slope = matmul(value_h[:reach], d, NT)
                    inner = jnp.sum(probs * prob_slope, axis=0, keepdims=True)
                    score_slope = (probs * (prob_slope - inner)).astype(low)
                    term = matmul(probs.astype(low), d, NN)
                    value_slope[i] = term if b == 0 else value_slope[i] + term
                    term = matmul(score_slope, q, NN)
                    key_slope[i] = term if b == 0 else key_slope[i] + term
                    query_parts[i].append(matmul(score_slope, key_h[:reach], TN))
            half = tokens // 2
            key_parts.append(
                jnp.concatenate([key_slope[0] + key_slope[1][:half], key_slope[1][half:]], axis=0)
            )
            value_parts.append(
                jnp.concatenate(
                    [value_slope[0] + value_slope[1][:half], value_slope[1][half:]], axis=0
                )
            )
        for i, (start, size, reach) in enumerate(query_spans(tokens)):
            span = slice(start, start + size)
            part = jnp.concatenate(query_parts[i], axis=1) * HEAD_SIZE**-0.5
            backs[span, qs] = turn_pairs(part, along[span], across[span], -1.0).astype(low)
        part = jnp.concatenate(key_parts, axis=1)
        spot = pl.ds(pl.multiple_of(width + g * 128, 128), 128)
        backs[:, spot] = turn_pairs(part, along, across, -1.0).astype(low)
        part = jnp.concatenate(value_parts, axis=1)
        spot = pl.ds(pl.multiple_of(width + key_width + g * 128, 128), 128)
        backs[:, spot] = part.astype(low)

        @pl.when(g == 1)
        def _():
            combine(0)

        return carry

    for copy in staging[4:]:
        copy.wait()
    loops = key_width // 128
    lax.fori_loop(0, loops, heads, 0)
    done = 5 + 3 * loops
    own_piece.start()
    inputs = input_ref[...].astype(full)
    scale = lax.rsqrt(jnp.mean(inputs * inputs, axis=1, keepdims=True) + EPS)
    normed[...] = (inputs * scale * gain_ref[0:1, :]).astype(low)
    tick(done, done + 1)

    def input_part(at, carry):
        tick(done + 1 + at // 2, done + 1 + at // 2 + at % 2)
        spot = pl.ds(pl.multiple_of(at * 512, 512), 512)
        delta[:, spot] = matmul(normed[...], backs[:, spot], TN).astype(low)
        return carry

    lax.fori_loop(0, joined // 512, input_part, 0)
    exchange(1)
    slope = matmul(backs[...], weight_ref[:, :joined], NT)
    tick(done + 3, done + 4)
    combine(1)
    tick(done + 4, done + 5)
    scaled = slope * gain_ref[0:1, :]
    first = jnp.sum(slope * inputs * scale, axis=0, keepdims=True)
    for owner in range(count):
        gain_buf[owner, 0:1, :] = first[:, owner * rows : (owner + 1) * rows]
        gain_buf[owner, 2:8, :] = jnp.zeros((6, rows), full)
    for k in range(1, count):
        gain_copy(k).start()
    tick(done + 5, done + 6)
    result = (
        steep[...]
        + scale * scaled
        - inputs * (scale * scale * scale) * jnp.mean(inputs * scaled, axis=1, keepdims=True)
    )
    moved = matmul(place[...], result.astype(low), NN).astype(low)
    arrived[...] = moved.reshape(arrived.shape)
    for k in range(count - 1, 0, -1):
        slope_copy(k).start()
    slope_out[me] = arrived[me]
    tick(done + 6, done + 7)
    own_piece.wait()
    result = mixed_slope[...].astype(full)
    for turn in range(1, pairs - 1):
        piece_copy(turn).wait_recv()
        result = result + far_piece[turn - 1].astype(full)
    out_ref[...] = result.astype(low)
    collect(0, 0, 2)
    if lined:
        sums.start(0, 2)
    total = gain_buf[me]
    for k in range(1, count):
        gain_copy(k).wait_recv()
        total = total + gain_recv[k]
    gain_sum[...] = total
    gain_line[rep] = total
    for k in range(1, reps):
        gain_line_copy(k).start()
    tick(done + 7, 3 * PARTS + LAG - 1)
    collect(1, 2, 4)
    if lined:
        sums.start(2, 6)
        tick(3 * PARTS + LAG - 1, 3 * PARTS + LAG)
        line.receive()
        sums.ticks(0, 6 + LAG)
        sums.receive()
        sums.finish()
    else:

        def spread_copy(k):
            return remote(
                owned, spread.at[rep], spread_send, spread_recv, k, (lax.rem(rep + k, reps), me)
            )

        for k in range(1, reps):
            spread_copy(k).start()
        spread[rep] = owned[...]
        for k in range(1, reps):
            spread_copy(k).wait_recv()
        value = spread[0].astype(full)
        for k in range(1, reps):
            value = value + spread[k].astype(full)
        delta_out[...] = value.astype(low)
        for k in range(1, reps):
            spread_copy(k).wait_send()
    for k in range(1, reps):
        gain_line_copy(k).wait_recv()
    total = gain_line[0]
    for k in range(1, reps):
        total = total + gain_line[k]
    gain_out[...] = total
    for k in range(1, count):
        slope_copy(k).wait_recv()
    for k in range(1, count):
        slope_copy(k).wait_send()
        gain_copy(k).wait_send()
    for turn in range(1, pairs - 1):
        piece_copy(turn).wait_send()
    for part in range(2):
        for turn in range(pairs):
            pair_copy(part, turn).wait_send()
        for turn in range(1, pairs):
            far_copy(part, turn).wait_send()
    for k in range(1, reps):
        gain_line_copy(k).wait_send()
    if lined:
        line.finish()


def finish_pass(count, reps, back, slopes, *rest):
    *rest, pieces, extra = rest
    tokens, width = back.shape
    weights = rest[4]
    key_width = (weights.shape[1] - 2 * width) // 2
    pairs = count // 2
    rows = width // count
    block = tokens // count
    columns = weights.shape[1]
    low = jnp.bfloat16
    full = jnp.float32
    dma = pltpu.SemaphoreType.DMA
    vmem = pltpu.VMEM
    shape = jax.ShapeDtypeStruct
    lined = reps == LINE
    extra = [extra] if lined else []
    owned = (2 * columns // width, rows // 2, width)
    anywhere = pl.BlockSpec(memory_space=pl.ANY)
    inside = pl.BlockSpec(memory_space=pltpu.VMEM)
    if lined:
        last = line_scratch((3 * PARTS,) + extra[0].shape[1:]) + line_scratch(owned, False)
    else:
        last = [vmem((reps,) + owned, low), dma((reps,)), dma((reps,))]
    return pl.pallas_call(
        functools.partial(finish_kernel, count, reps),
        name="finish_pass",
        out_shape=(
            shape(owned, low),
            shape((8, rows), full),
            shape((count, block, width), low),
            shape((tokens, width), low),
        )
        + tuple(shape((3 * PARTS,) + d.shape[1:], low) for d in extra),
        in_specs=[anywhere, anywhere]
        + [inside] * 4
        + [anywhere, inside]
        + [anywhere] * 5
        + [inside]
        + [anywhere] * (2 + len(extra)),
        out_specs=(inside,) * 4 + (anywhere,) * len(extra),
        scratch_shapes=[
            vmem((tokens, tokens), low),
            vmem((tokens, tokens), full),
            vmem((tokens, width), low),
            vmem((tokens, width), full),
            vmem((tokens, width), low),
            vmem((tokens, width + 2 * key_width), low),
            vmem((count, block, width), low),
            vmem((pairs - 2, tokens, width), low),
            dma((pairs,)),
            dma((pairs,)),
            dma((2,)),
            vmem((width, columns), low),
            vmem((pairs, rows, columns), low),
            vmem((pairs - 1, rows, columns), low),
            vmem((pairs - 1, rows, columns), low),
            dma((2 * pairs,)),
            dma((2 * pairs,)),
            dma((2 * pairs,)),
            dma((2 * pairs,)),
            dma((count,)),
            dma((count,)),
            vmem((count, 8, rows), full),
            vmem((count, 8, rows), full),
            vmem((8, rows), full),
            vmem((reps, 8, rows), full),
            dma((count,)),
            dma((count,)),
            dma((reps,)),
            dma((reps,)),
            vmem(owned, low),
        ]
        + last
        + [
            vmem(a.shape, a.dtype)
            for a in (back, rest[12], rest[10], weights, rest[7], rest[8], rest[9], rest[6])
        ]
        + [dma((8,))],
        compiler_params=pltpu.CompilerParams(
            collective_id=6, has_side_effects=True, vmem_limit_bytes=VMEM_MOST
        ),
        cost_estimate=pl.CostEstimate(
            flops=24 << 30, bytes_accessed=1 << 24, transcendentals=1 << 22
        ),
    )(back, slopes, *rest, pieces, *extra)


def emit_kernel(
    tokens_ref,
    slopes_ref,
    gain_ref,
    delta_ref,
    early_ref,
    middle_ref,
    late_ref,
    tokens_out,
    slopes_out,
    first_out,
    query_out,
    key_out,
    value_out,
    output_out,
    second_out,
    gate_out,
    up_out,
    down_out,
):
    full = jnp.float32
    tokens_out[...] = tokens_ref[...]
    slopes_out[...] = slopes_ref[...]
    rows = early_ref.shape[1]
    hidden = gate_out.shape[3]
    for piece in range(2):
        to = slice(piece * rows, (piece + 1) * rows)
        spot = slice(piece * hidden, (piece + 1) * hidden)
        gate_out[0, :, to, :] = middle_ref[0, :, :, spot].astype(full)
        up_out[0, :, to, :] = middle_ref[1, :, :, spot].astype(full)
        gate_out[1, :, to, :] = late_ref[0, :, :, spot].astype(full)
        up_out[1, :, to, :] = late_ref[1, :, :, spot].astype(full)
    down_out[0] = early_ref[...].astype(full)
    down_out[1] = late_ref[2].astype(full)

    @pl.when(pl.program_id(0) == 0)
    def _():
        first_out[...] = gain_ref[0:1, :]
        second_out[...] = gain_ref[1:2, :]
        half = delta_ref.shape[1]
        key_width = key_out.shape[1]
        for i in range(2):
            span = slice(i * half, (i + 1) * half)
            output_out[span, :] = delta_ref[i].astype(full)
            query_out[span, :] = delta_ref[2 + i].astype(full)
            key_out[span, :] = delta_ref[4 + i, :, :key_width].astype(full)
            value_out[span, :] = delta_ref[4 + i, :, key_width:].astype(full)


def emit_pass(tokens, slopes, gains, deltas, early, middle, late):
    full = jnp.float32
    shape = jax.ShapeDtypeStruct
    number, width = tokens.shape
    rows = gains.shape[1]
    _, high, wide = early.shape
    hidden = high * PARTS
    steps = 4
    each = PARTS // steps

    def moving(*block):
        return pl.BlockSpec(block, lambda i: (i,) + (0,) * (len(block) - 1))

    def fixed(*block):
        return pl.BlockSpec(block, lambda i: (0,) * len(block))

    def inner(*block):
        return pl.BlockSpec(block, lambda i: (0, i, 0, 0))

    return pl.pallas_call(
        emit_kernel,
        name="emit_pass",
        grid=(steps,),
        out_shape=(
            shape(tokens.shape, tokens.dtype),
            shape(slopes.shape, slopes.dtype),
            shape((1, rows), full),
            shape((rows, width), full),
            shape((rows, width // 2), full),
            shape((rows, width // 2), full),
            shape((rows, width), full),
            shape((1, rows), full),
            shape((2, PARTS, 2 * high, hidden), full),
            shape((2, PARTS, 2 * high, hidden), full),
            shape((2, PARTS, high, wide), full),
        ),
        in_specs=[
            moving(number // steps, width),
            moving(number // steps, width),
            fixed(*gains.shape),
            fixed(*deltas.shape),
            moving(each, high, wide),
            inner(2, each, high, wide),
            inner(3, each, high, wide),
        ],
        out_specs=(
            moving(number // steps, width),
            moving(number // steps, width),
            fixed(1, rows),
            fixed(rows, width),
            fixed(rows, width // 2),
            fixed(rows, width // 2),
            fixed(rows, width),
            fixed(1, rows),
            inner(2, each, 2 * high, hidden),
            inner(2, each, 2 * high, hidden),
            inner(2, each, high, wide),
        ),
        compiler_params=pltpu.CompilerParams(vmem_limit_bytes=VMEM_MOST),
        cost_estimate=pl.CostEstimate(flops=1 << 20, bytes_accessed=1 << 24, transcendentals=0),
    )(
        tokens,
        slopes,
        gains,
        deltas,
        early,
        middle.reshape(2, PARTS, high, wide),
        late.reshape(3, PARTS, high, wide),
    )


def local(
    tokens,
    cotangent,
    seq_lengths,
    pack_order,
    unpack_order,
    expert_ids,
    gates,
    first_gain,
    query_weight,
    key_matrix,
    value_matrix,
    output_weight,
    second_gain,
    gate_weight,
    up_weight,
    down_weight,
):
    shards = lax.axis_size("shard")
    group_count, width = tokens.shape
    order = pack_order.reshape(1, group_count)
    (
        joined,
        gains,
        mixing,
        along,
        across,
        inputs,
        queries,
        keys,
        values,
        mixed,
        logsum,
        hidden,
        normed,
        shared,
        all_slopes,
    ) = front_pass(
        tokens,
        (query_weight, key_matrix, value_matrix, output_weight),
        (first_gain, second_gain),
        order,
        expert_ids,
        gates,
        seq_lengths,
        cotangent,
        shards,
    )
    tables = (order, seq_lengths, along, across, joined, gains)
    reps = lax.axis_size("rep")
    inner, row_slopes, partial, *early = expert_pass(
        normed, all_slopes, mixing, gate_weight, up_weight, down_weight, shards, reps
    )
    back, pieces, *middle = return_pass(
        row_slopes, inner, gate_weight, up_weight, down_weight, shared, partial, shards, reps
    )
    deltas, gain_deltas, delta_tokens, out_tokens, *late = finish_pass(
        shards,
        reps,
        back,
        all_slopes,
        *tables,
        inputs,
        queries,
        keys,
        values,
        mixed,
        logsum,
        hidden,
        pieces,
        partial,
    )
    if reps == LINE:
        early, middle, late = early[0], middle[0], late[0]
    else:
        summed = lax.psum(partial, "rep")
        early, middle, late = summed[:PARTS], summed[PARTS : 3 * PARTS], summed[3 * PARTS :]
    (
        out_tokens,
        delta_tokens,
        delta_first,
        delta_query,
        delta_key,
        delta_value,
        delta_output,
        delta_second,
        delta_gate,
        delta_up,
        delta_down,
    ) = emit_pass(
        out_tokens, delta_tokens.reshape(group_count, width), gain_deltas, deltas, early, middle, late
    )
    return (
        out_tokens,
        delta_tokens,
        delta_first.reshape(first_gain.shape),
        delta_query,
        delta_key,
        delta_value,
        delta_output,
        delta_second.reshape(second_gain.shape),
        delta_gate.reshape(gate_weight.shape),
        delta_up.reshape(up_weight.shape),
        delta_down.reshape(down_weight.shape),
    )


def solution(mesh):
    placed = (
        P(("rep", "shard"), None),
        P(("rep", "shard"), None),
        P(("rep", "shard"), None),
        P(("rep", "shard")),
        P(("rep", "shard")),
        P(("rep", "shard"), None),
        P(("rep", "shard"), None),
        P("shard"),
        P("shard", None),
        P("shard", None),
        P("shard", None),
        P("shard", None),
        P("shard"),
        P("shard", None, None),
        P("shard", None, None),
        P("shard", None, None),
    )
    return jax.shard_map(
        local,
        mesh=mesh,
        in_specs=placed,
        out_specs=(
            P(("rep", "shard"), None),
            P(("rep", "shard"), None),
            P("shard"),
            P("shard", None),
            P("shard", None),
            P("shard", None),
            P("shard", None),
            P("shard"),
            P("shard", None, None),
            P("shard", None, None),
            P("shard", None, None),
        ),
        check_vma=False,
    )
```

```python
import functools

import jax
import jax.numpy as jnp
import numpy as np
from jax import lax
from jax.experimental import pallas as pl
from jax.experimental.pallas import tpu as pltpu
from jax.sharding import PartitionSpec as P

QUERY_HEADS = 16
KEY_VALUE_HEADS = 8
HEAD_SIZE = 64


EPS = 1e-05
THETA = 10000.0


MESH = pl.DeviceIdType.MESH
NN = (((1,), (0,)), ((), ()))
NT = (((1,), (1,)), ((), ()))
TN = (((0,), (0,)), ((), ()))
TILE = 256
VMEM_MOST = 66_000_000


def matmul(left, right, dims):
    return lax.dot_general(left, right, dims, preferred_element_type=jnp.float32)


def stage_in(refs, count, start=0):
    held = refs[-count - 1 : -1]
    copies = [
        pltpu.make_async_copy(refs[start + k], held[k], refs[-1].at[k]) for k in range(count)
    ]
    return held, copies, refs[: -count - 1]


def flip(number, mask, count):
    out = 0
    bit = 1
    while bit < count:
        a = (number // bit) % 2
        b = (mask // bit) % 2
        out = out + (a + b - 2 * a * b) * bit
        bit *= 2
    return out


def greet(me, rep, count, reps=1):
    barrier = pltpu.get_barrier_semaphore()
    for k in range(1, count):
        pl.semaphore_signal(
            barrier, inc=1, device_id=(rep, lax.rem(me + k, count)), device_id_type=MESH
        )
    for k in range(1, reps):
        pl.semaphore_signal(
            barrier, inc=1, device_id=(lax.rem(rep + k, reps), me), device_id_type=MESH
        )
    pl.semaphore_wait(barrier, count + reps - 2)


LINE = 4
LAG = 2
RING = 4


class Line:
    def __init__(
        self,
        rep,
        me,
        source,
        out,
        first,
        second,
        both,
        sends,
        recvs,
        held=None,
        sems=None,
        base=0,
        count=None,
    ):
        self.rep, self.me = rep, me
        self.source, self.out = source, out
        self.first, self.second, self.both = first, second, both
        self.sends, self.recvs = sends, recvs
        self.held, self.sems = held, sems
        self.base = base
        self.count = source.shape[0] if count is None else count
        self.outer = (rep == 0) | (rep == LINE - 1)
        self.inner = jnp.logical_not(self.outer)
        self.inside = jnp.where(rep == 0, 1, 2)
        self.outside = jnp.where(rep == 1, 0, 3)
        self.across = LINE - 1 - rep

    def copy(self, stage, i):
        ring = self.both.at[i % RING]
        if stage == 0:
            source = self.source.at[self.base + i]
        else:
            source = ring if stage == 1 else self.first.at[i]
        target = (self.first, self.second, self.first)[stage].at[i]
        device = (self.inside, self.across, self.outside)[stage]
        return pltpu.make_async_remote_copy(
            src_ref=source,
            dst_ref=target,
            send_sem=self.sends.at[stage, i],
            recv_sem=self.recvs.at[stage, i],
            device_id=(device, self.me),
            device_id_type=MESH,
        )

    def load(self, i):
        return pltpu.make_async_copy(
            self.source.at[self.base + i], self.held.at[i % 2], self.sems.at[self.count + i % 2]
        )

    def put(self, i):
        return pltpu.make_async_copy(self.first.at[i], self.out.at[i], self.sems.at[i])

    def loop(self, body, begin=0):
        def step(i, carry):
            body(i)
            return carry

        lax.fori_loop(begin, self.count, step, 0)

    def start(self, begin=0, end=None):
        end = self.count if end is None else end

        @pl.when(self.outer)
        def _():
            def step(i, carry):
                self.copy(0, i).start()
                return carry

            lax.fori_loop(begin, end, step, 0)

        if self.held is not None:

            @pl.when(self.inner)
            def _():
                self.load(0).start()

    def tick(self, j):
        full = jnp.float32
        low = jnp.bfloat16

        @pl.when(self.inner & (j >= 0) & (j < self.count))
        def _():
            if self.held is None:
                own = self.source[self.base + j]
            else:

                @pl.when(j + 1 < self.count)
                def _():
                    self.load(j + 1).start()

                self.load(j).wait()
                own = self.held[j % 2]
            self.copy(0, j).wait_recv()

            @pl.when(j >= RING)
            def _():
                self.copy(1, j - RING).wait_send()

            self.both[j % RING] = (own.astype(full) + self.first[j].astype(full)).astype(low)
            self.copy(1, j).start()

        i = j - LAG

        @pl.when(self.inner & (i >= 0) & (i < self.count))
        def _():
            self.copy(1, i).wait_recv()
            every = self.both[i % RING].astype(full) + self.second[i].astype(full)
            self.first[i] = every.astype(low)
            self.copy(2, i).start()
            if self.held is None:
                self.out[i] = every.astype(low)
            else:
                self.put(i).start()

    def ticks(self, begin, end):
        def step(j, carry):
            self.tick(j)
            return carry

        lax.fori_loop(begin, end, step, 0)

    def receive(self):
        @pl.when(self.outer)
        def _():
            def step(i):
                self.copy(2, i).wait_recv()
                if self.held is None:
                    self.out[i] = self.first[i]
                else:
                    self.put(i).start()

            self.loop(step)

    def finish(self):
        @pl.when(self.outer)
        def _():
            self.loop(lambda i: self.copy(0, i).wait_send())

        @pl.when(self.inner)
        def _():
            self.loop(lambda i: self.copy(1, i).wait_send(), self.count - RING)
            self.loop(lambda i: self.copy(2, i).wait_send())

        if self.held is not None:
            self.loop(lambda i: self.put(i).wait())


def line_scratch(shape, streamed=True):
    low = jnp.bfloat16
    dma = pltpu.SemaphoreType.DMA
    scratch = [
        pltpu.VMEM(shape, low),
        pltpu.VMEM(shape, low),
        pltpu.VMEM((RING,) + shape[1:], low),
        dma((3, shape[0])),
        dma((3, shape[0])),
    ]
    if streamed:
        scratch += [pltpu.VMEM((2,) + shape[1:], low), dma((shape[0] + 2,))]
    return scratch


def remote(source, target, sends, recvs, index, device):
    return pltpu.make_async_remote_copy(
        src_ref=source,
        dst_ref=target,
        send_sem=sends.at[index],
        recv_sem=recvs.at[index],
        device_id=device,
        device_id_type=MESH,
    )


class Gather:
    def __init__(self, count, rep, me, own, slot, sends, recvs):
        self.count, self.rep, self.me = count, rep, me
        self.own, self.slot, self.sends, self.recvs = own, slot, sends, recvs
        self.waiting = []

    def near(self, mask):
        return flip(self.me, mask, self.count)

    def send(self, source, owner, part, mask, index):
        remote(
            source,
            self.slot(owner, part),
            self.sends,
            self.recvs,
            index,
            (self.rep, self.near(mask)),
        ).start()
        self.waiting.append(index)

    def arrived(self, owner, part, index):
        remote(
            self.slot(owner, part),
            self.slot(owner, part),
            self.sends,
            self.recvs,
            index,
            (self.rep, self.me),
        ).wait_recv()

    def pass_on(self, mask, part, index, new, onward):
        owner = self.near(mask)
        if index is not None:
            self.arrived(owner, part, index)
        self.send(self.slot(owner, part), owner, part, onward, new)

    def start(self):
        if self.count == 8:
            plan = ((2, 0, 0), (4, 1, 1), (2, 1, 2), (4, 0, 3), (1, 0, 4), (1, 1, 5))
            for mask, part, index in plan:
                self.send(self.own(part), self.me, part, mask, index)
        else:
            for mask in [1] + list(range(2, self.count, 2)):
                for part in range(2):
                    self.send(self.own(part), self.me, part, mask, 2 * mask + part)

    def relay(self, stage):
        if self.count == 8:
            if stage == 0:
                self.pass_on(2, 0, 0, 6, 4)
                self.pass_on(4, 1, 1, 8, 2)
                self.pass_on(2, 0, None, 7, 1)
                self.pass_on(4, 1, None, 9, 1)
            elif stage == 1:
                self.pass_on(2, 1, 2, 10, 1)
                self.pass_on(4, 0, 3, 11, 1)
            else:
                self.pass_on(6, 0, 6, 12, 1)
                self.pass_on(6, 1, 8, 13, 1)
        elif stage == 2:
            for mask in range(2, self.count, 2):
                for part in range(2):
                    self.pass_on(mask, part, 2 * mask + part, 2 * mask + 2 + part, 1)

    def ready(self, masks):
        if self.count == 8:
            last = ((1, 0, 4), (1, 1, 5), (3, 0, 7), (5, 1, 9), (3, 1, 10), (5, 0, 11))
            last += ((7, 0, 12), (7, 1, 13))
        else:
            last = [(m, p, 2 * m + p) for m in range(1, self.count, 2) for p in range(2)]
        for mask, part, index in last:
            if mask in masks:
                self.arrived(self.near(mask), part, index)

    def finish(self, masks=None):
        self.ready(range(self.count) if masks is None else masks)
        for index in self.waiting:
            spot = self.slot(self.me, 0)
            remote(
                spot, spot, self.sends, self.recvs, index, (self.rep, self.me)
            ).wait_send()


PARTS = 8


def expert_kernel(count, reps, *refs):
    lined = reps == LINE
    (gate_ref, up_ref, down_ref), staging, refs = stage_in(refs, 3, 3)
    for copy in staging:
        copy.start()
    own_ref, slope_ref, mix_ref = refs[:3]
    refs = (None,) * 6 + refs[6:]
    hidden_out, grad_out, delta_out = refs[6:9]
    refs = refs[9:]
    if lined:
        line_out = refs[0]
        refs = refs[1:]
    (
        rows,
        slope_buf,
        hidden_buf,
        grad_buf,
        acc_both,
        acc_down,
        stage,
        send_sem,
        recv_sem,
        own_sem,
        slope_sem,
        hidden_sem,
        grad_sem,
        stage_sem,
    ) = refs[:14]
    rep = lax.axis_index("rep")
    me = lax.axis_index("shard")
    experts, width, hidden = gate_ref.shape
    tokens = own_ref.shape[0]
    half = tokens // 2
    low = jnp.bfloat16
    turns = experts * count
    swap = 2 + count

    def pair(t):
        late = jnp.where(t < swap, t - 2, t - count)
        return (
            jnp.where(t < 4, t // 2, late),
            jnp.where(t < 4, t % 2, jnp.where(t < swap, 0, 1)),
        )

    def pack_of(t):
        return flip(me, pair(t)[0], count)

    def slope_copy(t):
        return pltpu.make_async_copy(
            slope_ref.at[:, pack_of(t)], slope_buf.at[t % 2], slope_sem.at[t % 2]
        )

    def hidden_copy(t):
        spot = pl.ds(pl.multiple_of(pair(t)[1] * hidden, hidden), hidden)
        return pltpu.make_async_copy(
            hidden_buf.at[t % 2], hidden_out.at[pack_of(t), :, spot], hidden_sem.at[t % 2]
        )

    def grad_copy(t):
        spot = pl.ds(pl.multiple_of(pair(t)[1] * 2 * hidden, 2 * hidden), 2 * hidden)
        return pltpu.make_async_copy(
            grad_buf.at[t % 2], grad_out.at[pack_of(t), :, spot], grad_sem.at[t % 2]
        )

    def stage_copy(e):
        span = pl.ds(e * 3 * PARTS, 3 * PARTS)
        return pltpu.make_async_copy(stage.at[span], delta_out.at[span], stage_sem.at[e])

    slope_copy(0).start()
    own = pltpu.make_async_copy(own_ref, rows.at[me], own_sem)
    own.start()
    greet(me, rep, count, reps if lined else 1)
    gather = Gather(
        count,
        rep,
        me,
        lambda p: own_ref.at[pl.ds(p * half, half)],
        lambda owner, p: rows.at[owner, pl.ds(p * half, half)],
        send_sem,
        recv_sem,
    )
    gather.start()
    own.wait()
    for copy in staging:
        copy.wait()
    if lined:
        line = Line(rep, me, stage, line_out, *refs[14:], count=PARTS)

    def spread(e, both, down):
        size = down.shape[0] // PARTS
        side = both.shape[0] // (2 * PARTS)
        base = e * 3 * PARTS
        for i in range(PARTS):
            at = base + 2 * PARTS * e + i
            stage[at] = down[i * size : (i + 1) * size, :].astype(low)
            for which in range(2):
                at = base + PARTS * (1 - e) + which * PARTS + i
                for piece in range(2):
                    span = slice((2 * i + piece) * side, (2 * i + piece + 1) * side)
                    stage[at, :, piece * hidden : (piece + 1) * hidden] = both[
                        span, which * hidden : (which + 1) * hidden
                    ].astype(low)
        stage_copy(e).start()

    if count == 8:
        plan = {2: ((1,), 0), 4: ((), 1), 5: ((3,), None), 7: ((5,), 2), 9: ((7,), None)}
    else:
        plan = {2: ((1,), None), 4: ((), 2), 5: (tuple(range(3, count, 2)), None)}

    def step(t, carry):
        k, e = pair(t)
        pack = flip(me, k, count)
        for at, (masks, stage_at) in plan.items():

            @pl.when(t == at)
            def _():
                gather.ready(masks)
                if stage_at is not None:
                    gather.relay(stage_at)

        @pl.when(t + 1 < turns)
        def _():
            slope_copy(t + 1).start()

        if lined:
            line.tick(2 * (t - swap - 1))
        slope_copy(t).wait()

        @pl.when(t >= 2)
        def _():
            hidden_copy(t - 2).wait()
            grad_copy(t - 2).wait()

        slot = t % 2
        x = rows[pack]
        dy = slope_buf[slot].reshape(tokens, width)
        mixes = jnp.transpose(mix_ref[pack])
        mix = jnp.where(e == 0, mixes[:, 0:1], mixes[:, 1:2])
        for part in range(hidden // TILE):
            span = pl.ds(part * TILE, TILE)
            ga = matmul(x, gate_ref[e, :, span], NN)
            ua = matmul(x, up_ref[e, :, span], NN)
            dh = matmul(dy, down_ref[e, span, :], NT) * mix
            sig = jax.nn.sigmoid(ga)
            act = ga * sig
            hidden_buf[slot, :, span] = (mix * (act * ua)).astype(low)
            grad_buf[slot, :, span] = (dh * ua * sig * (1.0 + ga * (1.0 - sig))).astype(low)
            grad_buf[slot, :, pl.ds(hidden + part * TILE, TILE)] = (dh * act).astype(low)
        hidden_copy(t).start()
        grad_copy(t).start()
        if lined:
            line.tick(2 * (t - swap) - 1)

        both = matmul(x, grad_buf[slot], TN)
        down = matmul(hidden_buf[slot], dy, TN)

        @pl.when(k == 0)
        def _():
            acc_both[e] = both
            acc_down[e] = down

        @pl.when((k > 0) & (k < count - 1))
        def _():
            acc_both[e] += both
            acc_down[e] += down

        @pl.when((t == swap - 1) | (t == turns - 1))
        def _():
            spread(e, acc_both[e] + both, acc_down[e] + down)

        if lined:

            @pl.when(t == swap - 1)
            def _():
                line.start()

        return carry

    lax.fori_loop(0, turns, step, 0)
    if lined:
        line.ticks(2 * (turns - swap - 1), PARTS + LAG)
    for t in (turns - 2, turns - 1):
        hidden_copy(t).wait()
        grad_copy(t).wait()
    gather.finish(())
    stage_copy(0).wait()
    if lined:
        line.receive()
        line.finish()
    stage_copy(1).wait()


def expert_pass(normed, all_slopes, mixing, gate_weight, up_weight, down_weight, count, reps):
    tokens, width = normed.shape
    experts, _, hidden = gate_weight.shape
    block = tokens // count
    low = jnp.bfloat16
    full = jnp.float32
    dma = pltpu.SemaphoreType.DMA
    vmem = pltpu.VMEM
    shape = jax.ShapeDtypeStruct
    anywhere = pl.BlockSpec(memory_space=pl.ANY)
    inside = pl.BlockSpec(memory_space=pltpu.VMEM)
    flops = 2 * count * tokens * width * hidden * experts * 6
    lined = reps == LINE
    segment = (hidden // PARTS, width)
    summed = (PARTS,) + segment
    return pl.pallas_call(
        functools.partial(expert_kernel, count, reps),
        name="expert_pass",
        out_shape=(
            shape((count, tokens, experts * hidden), low),
            shape((count, tokens, 2 * experts * hidden), low),
            shape((6 * PARTS,) + segment, low),
        )
        + ((shape(summed, low),) if lined else ()),
        in_specs=[anywhere, anywhere, inside, anywhere, anywhere, anywhere],
        out_specs=(anywhere,) * 3 + ((inside,) if lined else ()),
        scratch_shapes=[
            vmem((count, tokens, width), low),
            vmem((2, count, block, width), low),
            vmem((2, tokens, hidden), low),
            vmem((2, tokens, 2 * hidden), low),
            vmem((experts, width, 2 * hidden), full),
            vmem((experts, hidden, width), full),
            vmem((6 * PARTS,) + segment, low),
            dma((2 * count + 2,)),
            dma((2 * count + 2,)),
            dma,
            dma((2,)),
            dma((2,)),
            dma((2,)),
            dma((2,)),
        ]
        + (line_scratch(summed, False) if lined else [])
        + [vmem(w.shape, low) for w in (gate_weight, up_weight, down_weight)]
        + [dma((3,))],
        compiler_params=pltpu.CompilerParams(
            collective_id=1, has_side_effects=True, vmem_limit_bytes=VMEM_MOST
        ),
        cost_estimate=pl.CostEstimate(flops=flops, bytes_accessed=1 << 26, transcendentals=0),
    )(
        normed,
        all_slopes.reshape(count, count, block, width),
        mixing,
        gate_weight,
        up_weight,
        down_weight,
    )


def return_kernel(count, reps, *refs):
    (gate_ref, up_ref, down_ref, own_ref), staging, refs = stage_in(refs, 4, 2)
    for copy in staging:
        copy.start()
    grad_ref, hidden_ref = refs[:2]
    lined = reps == LINE
    refs = refs[6:]
    if lined:
        line_ref, back_ref, piece_out, line_out = refs[:4]
        refs = refs[4:]
    else:
        back_ref, piece_out = refs[:2]
        refs = refs[2:]
    (
        grad_buf,
        hidden_buf,
        pair_send,
        far_send,
        pair_recv,
        far_recv,
        total,
        piece,
        last_recv,
        relay_recv,
        load_sem,
        pair_send_sem,
        pair_recv_sem,
        far_send_sem,
        far_recv_sem,
        piece_sem,
        last_sem,
        relay_send_sem,
        relay_recv_sem,
    ) = refs[:19]
    rep = lax.axis_index("rep")
    me = lax.axis_index("shard")
    experts, width, hidden = gate_ref.shape
    tokens = own_ref.shape[0]
    block = tokens // count
    low = jnp.bfloat16
    full = jnp.float32
    pairs = count // 2
    partner = flip(me, 1, count)
    line = Line(rep, me, line_ref, line_out, *refs[19:], base=PARTS, count=2 * PARTS) if lined else None

    relayed = count == 8
    half = tokens // 2

    def mask_of(turn):
        return count - 2 - 2 * turn

    def target(item):
        return flip(me, mask_of(item // 2) + 1 - item % 2, count)

    def grad_load(item):
        return pltpu.make_async_copy(
            grad_ref.at[target(item)], grad_buf.at[item % 2], load_sem.at[item % 2]
        )

    def grad_part(slot, pack):
        value = None
        for e in range(experts):
            for at, weight in ((2 * e, gate_ref), (2 * e + 1, up_ref)):
                term = matmul(grad_buf[slot, :, pl.ds(at * hidden, hidden)], weight[e], NT)
                value = term if value is None else value + term
        total[...] = value

    def hidden_load(item):
        return pltpu.make_async_copy(
            hidden_ref.at[:, target(item)], hidden_buf.at[item % 2], load_sem.at[item % 2]
        )

    def hidden_part(slot, pack):
        value = None
        for e in range(experts):
            term = matmul(
                hidden_buf[slot, :, :, pl.ds(e * hidden, hidden)].reshape(tokens, hidden),
                down_ref[e],
                NN,
            )
            value = term if value is None else value + term
        total[...] = value
        mine = pl.ds(pl.multiple_of(me * block, block), block)
        theirs = pl.ds(pl.multiple_of(pack * block, block), block)
        total[mine, :] += own_ref[theirs, :].astype(full)

    def pair_copy(base, turn):
        return remote(
            pair_send.at[turn % 2],
            pair_recv.at[base + turn],
            pair_send_sem,
            pair_recv_sem,
            base + turn,
            (rep, partner),
        )

    def far_copy(turn, device):
        return remote(
            far_send.at[turn % 2], far_recv.at[turn], far_send_sem, far_recv_sem, turn, (rep, device)
        )

    def half_copy(side):
        span = pl.ds(side * half, half)
        return remote(
            far_send.at[1, span],
            far_recv.at[1, span],
            far_send_sem,
            far_recv_sem,
            side,
            (rep, flip(me, count - 4, count)),
        )

    def relay_copy(phase, side, source):
        return remote(
            source.at[pl.ds(side * half, half)],
            relay_recv.at[2 * phase + side],
            relay_send_sem,
            relay_recv_sem,
            2 * phase + side,
            (rep, flip(me, 2 + 2 * side, count)),
        )

    def last_copy(device):
        return pltpu.make_async_remote_copy(
            src_ref=piece.at[0],
            dst_ref=last_recv,
            send_sem=last_sem.at[0],
            recv_sem=last_sem.at[1],
            device_id=(rep, device),
            device_id_type=MESH,
        )

    def slot(turn):
        return jnp.where(turn == 0, 0, jnp.where(turn == pairs - 1, 3, 1 + turn % 2))

    def piece_copy(turn):
        return pltpu.make_async_copy(
            piece.at[slot(turn)], piece_out.at[turn], piece_sem.at[turn % 2]
        )

    def grad_combine(turn, mask):
        last = turn == pairs - 1
        total[...] += pair_recv[turn].astype(full)

        @pl.when(last)
        def _():
            back_ref[...] = total[...]

        if relayed:

            @pl.when(turn == 0)
            def _():
                far_send[0] = total[...].astype(low)
                for side in range(2):
                    relay_copy(0, side, far_send.at[0]).start()

            @pl.when(turn == 1)
            def _():
                far_send[1] = total[...].astype(low)
                half_copy(1).start()

            @pl.when(turn == 2)
            def _():
                early, later = pl.ds(0, half), pl.ds(half, half)
                for side in range(2):
                    relay_copy(0, side, far_send.at[0]).wait_recv()
                value = far_send[1, early, :].astype(full) + relay_recv[0].astype(full)
                far_send[1, early, :] = value.astype(low)
                half_copy(0).start()
                for side in range(2):
                    relay_copy(0, side, far_send.at[0]).wait_send()
                total[later, :] += relay_recv[1].astype(full)
                far_send[0] = total[...].astype(low)
                far_copy(2, flip(me, mask, count)).start()
        else:

            @pl.when(jnp.logical_not(last))
            def _():
                @pl.when(turn >= 2)
                def _():
                    far_copy(turn - 2, me).wait_send()

                far_send[turn % 2] = total[...].astype(low)
                far_copy(turn, flip(me, mask, count)).start()

    def hidden_combine(turn, mask):
        if not relayed:

            @pl.when((turn >= 3) & (turn < pairs - 1))
            def _():
                piece_copy(turn - 2).wait()

        piece[slot(turn)] = (total[...] + pair_recv[pairs + turn].astype(full)).astype(low)

        @pl.when(turn == 0)
        def _():
            if relayed:
                for side in range(2):
                    relay_copy(1, side, piece.at[0]).start()
            else:
                last_copy(flip(me, mask, count)).start()

        if not relayed:

            @pl.when((turn > 0) & (turn < pairs - 1))
            def _():
                piece_copy(turn).start()

    grad_load(0).start()
    greet(me, rep, count, reps if lined else 1)
    if lined:
        line.start()

    def sweep(base, load, part, combine, pace):
        def item_step(item, carry):
            turn = item // 2
            mask = mask_of(turn)

            @pl.when(item + 1 < 2 * pairs)
            def _():
                load(item + 1).start()

            load(item).wait()
            part(item % 2, target(item))

            @pl.when(item % 2 == 0)
            def _():
                @pl.when(turn >= 2)
                def _():
                    pair_copy(base, turn - 2).wait_send()

                pair_send[turn % 2] = total[...].astype(low)
                pair_copy(base, turn).start()

            @pl.when(item % 2 == 1)
            def _():
                pair_copy(base, turn).wait_recv()
                combine(turn, mask)

            if lined:
                line.ticks(pace(item) - 2, pace(item + 1) - 2)
            return carry

        lax.fori_loop(0, 2 * pairs, item_step, 0)
        for turn in range(max(0, pairs - 2), pairs):
            pair_copy(base, turn).wait_send()

    for copy in staging:
        copy.wait()
    sweep(0, grad_load, grad_part, grad_combine, lambda item: 3 * item // 2)
    hidden_load(0).start()
    sweep(pairs, hidden_load, hidden_part, hidden_combine, lambda item: 3 * pairs + item)
    if lined:
        line.ticks(5 * pairs - 2, 2 * PARTS + LAG)
    if relayed:
        for side in range(2):
            half_copy(side).wait_recv()
        back_ref[...] += far_recv[1].astype(full)
        far_copy(2, me).wait_recv()
        back_ref[...] += far_recv[2].astype(full)
        for side in range(2):
            half_copy(side).wait_send()
        far_copy(2, me).wait_send()
    else:

        def add(turn, carry):
            far_copy(turn, me).wait_recv()
            back_ref[...] += far_recv[turn].astype(full)
            return carry

        lax.fori_loop(0, pairs - 1, add, 0)
        for turn in (pairs - 3, pairs - 2):
            far_copy(turn, me).wait_send()
    if lined:
        line.receive()
    if relayed:
        for side in range(2):
            relay_copy(1, side, piece.at[0]).wait_recv()
            rows = pl.ds(side * half, half)
            spot = slot(1 + side)
            value = piece[spot, rows, :].astype(full) + relay_recv[2 + side].astype(full)
            piece[spot, rows, :] = value.astype(low)
            piece_copy(1 + side).start()
            relay_copy(1, side, piece.at[0]).wait_send()
    else:
        last_copy(me).wait_recv()
        value = piece[3].astype(full) + last_recv[...].astype(full)
        piece[3] = value.astype(low)
        last_copy(me).wait_send()
    for turn in (pairs - 3, pairs - 2):
        piece_copy(turn).wait()
    piece_copy(pairs - 1).start()
    if lined:
        line.finish()
    piece_copy(pairs - 1).wait()


def return_pass(grads, hiddens, gate_weight, up_weight, down_weight, own, deltas, count, reps):
    tokens, width = own.shape
    experts, _, hidden = gate_weight.shape
    block = tokens // count
    low = jnp.bfloat16
    full = jnp.float32
    pairs = count // 2
    dma = pltpu.SemaphoreType.DMA
    shape = jax.ShapeDtypeStruct
    anywhere = pl.BlockSpec(memory_space=pl.ANY)
    inside = pl.BlockSpec(memory_space=pltpu.VMEM)
    flops = 2 * count * tokens * width * hidden * experts * 3
    lined = reps == LINE
    extra = [deltas] if lined else []
    return pl.pallas_call(
        functools.partial(return_kernel, count, reps),
        name="return_pass",
        out_shape=(
            shape((tokens, width), full),
            shape((pairs, tokens, width), low),
        )
        + tuple(shape((2 * PARTS,) + d.shape[1:], low) for d in extra),
        in_specs=[anywhere] * (6 + len(extra)),
        out_specs=(inside, anywhere) + (anywhere,) * len(extra),
        scratch_shapes=[
            pltpu.VMEM((2, tokens, 2 * experts * hidden), low),
            pltpu.VMEM((2, count, block, experts * hidden), low),
            pltpu.VMEM((2, tokens, width), low),
            pltpu.VMEM((2, tokens, width), low),
            pltpu.VMEM((2 * pairs, tokens, width), low),
            pltpu.VMEM((pairs, tokens, width), low),
            pltpu.VMEM((tokens, width), full),
            pltpu.VMEM((4, tokens, width), low),
            pltpu.VMEM((8, 128) if count == 8 else (tokens, width), low),
            pltpu.VMEM((4, tokens // 2, width), low),
            dma((2,)),
            dma((2 * pairs,)),
            dma((2 * pairs,)),
            dma((pairs,)),
            dma((pairs,)),
            dma((2,)),
            dma((3,)),
            dma((4,)),
            dma((4,)),
        ]
        + (line_scratch((2 * PARTS,) + deltas.shape[1:]) if lined else [])
        + [pltpu.VMEM(a.shape, low) for a in (gate_weight, up_weight, down_weight, own)]
        + [dma((4,))],
        compiler_params=pltpu.CompilerParams(
            collective_id=2, has_side_effects=True, vmem_limit_bytes=VMEM_MOST
        ),
        cost_estimate=pl.CostEstimate(flops=flops, bytes_accessed=1 << 26, transcendentals=0),
    )(
        grads,
        hiddens.reshape(count, count, block, experts * hidden),
        gate_weight,
        up_weight,
        down_weight,
        own,
        *extra,
    )


def turn_pairs(rows, along, across, sign):
    lane = lax.broadcasted_iota(jnp.int32, (rows.shape[0], 128), 1)
    early = (lane % HEAD_SIZE) < HEAD_SIZE // 2
    pieces = []
    for at in range(0, rows.shape[1], 128):
        part = rows[:, at : at + 128]
        other = jnp.where(
            early,
            pltpu.roll(part, 128 - HEAD_SIZE // 2, 1),
            pltpu.roll(part, HEAD_SIZE // 2, 1),
        )
        pieces.append(part * along + sign * (other * across))
    return pieces[0] if len(pieces) == 1 else jnp.concatenate(pieces, axis=1)


def permutation(order_ref):
    tokens = order_ref.shape[1]
    rows = lax.broadcasted_iota(jnp.int32, (tokens, tokens), 0)
    return jnp.where(order_ref[...] == rows, 1.0, 0.0).astype(jnp.bfloat16)


def starts_of(position, length_ref):
    start = jnp.zeros_like(position)
    end = jnp.zeros((1, 1), jnp.int32)
    for k in range(length_ref.shape[1] - 1):
        end = end + length_ref[0:1, k : k + 1]
        start = jnp.where(position >= end, end, start)
    return start


def fill_bias(bias, length_ref):
    tokens = bias.shape[0]
    keys = lax.broadcasted_iota(jnp.int32, (tokens, tokens), 0)
    queries = lax.broadcasted_iota(jnp.int32, (tokens, tokens), 1)
    start = starts_of(lax.broadcasted_iota(jnp.int32, (1, tokens), 1), length_ref)
    bias[...] = jnp.where((keys >= start) & (keys <= queries), 0.0, -1e30)


def query_spans(tokens):
    half = tokens // 2
    return ((0, half, half), (half, half, tokens))


def first_kernel(
    count,
    token_ref,
    query_ref,
    key_ref,
    value_ref,
    output_ref,
    gain_ref,
    order_ref,
    id_ref,
    gate_ref,
    arrived_out,
    joined_out,
    gain_out,
    mix_out,
    mix_buf,
    gain_buf,
    token_send,
    token_recv,
    gain_send,
    gain_recv,
    mix_send,
    mix_recv,
    weight_send,
    weight_recv,
    local_sem,
):
    rep = lax.axis_index("rep")
    me = lax.axis_index("shard")
    full = jnp.float32
    low = jnp.bfloat16
    rows = query_ref.shape[0]
    experts = mix_out.shape[0] * 2
    mine = pl.multiple_of(me * rows, rows)
    locals_ = [pltpu.make_async_copy(token_ref.at[me], arrived_out.at[me], local_sem.at[0])]
    at = 0
    for i, ref in enumerate((query_ref, key_ref, value_ref, output_ref)):
        size = ref.shape[1]
        target = joined_out.at[pl.ds(mine, rows), pl.ds(at, size)]
        locals_.append(pltpu.make_async_copy(ref, target, local_sem.at[1 + i]))
        at += size
    for copy in locals_:
        copy.start()
    greet(me, rep, count)

    def token_copy(k):
        target = flip(me, k, count)
        return remote(
            token_ref.at[target], arrived_out.at[me], token_send, token_recv, k, (rep, target)
        )

    def gain_copy(k):
        return remote(
            gain_ref, gain_buf.at[me], gain_send, gain_recv, k, (rep, flip(me, k, count))
        )

    def mix_copy(k):
        target = flip(me, k, count)
        return remote(mix_buf.at[target], mix_out.at[me], mix_send, mix_recv, k, (rep, target))

    for k in range(count - 1, 0, -1):
        token_copy(k).start()
    for copy in locals_[1:]:
        copy.wait()
    half = rows // 2

    def block(owner, part):
        return joined_out.at[pl.ds(pl.multiple_of(owner * rows + part * half, half), half)]

    weights = Gather(count, rep, me, lambda p: block(me, p), block, weight_send, weight_recv)
    weights.start()
    for k in range(1, count):
        gain_copy(k).start()
    gain_buf[me] = gain_ref[...]
    tokens = order_ref.shape[0]
    lane = lax.broadcasted_iota(jnp.int32, (tokens, experts), 1)
    mixing = jnp.zeros((tokens, experts), full)
    for k in range(id_ref.shape[1]):
        mixing = mixing + jnp.where(id_ref[:, k : k + 1] == lane, gate_ref[:, k : k + 1], 0.0)
    place = permutation(order_ref)
    moved = jnp.zeros((experts, tokens), full)
    for _ in range(3):
        high = mixing.astype(low)
        moved = moved + matmul(high, place, TN)
        mixing = mixing - high.astype(full)
    for owner in range(count):
        mix_buf[owner, 0:2, :] = moved[2 * owner : 2 * owner + 2, :]
        mix_buf[owner, 2:8, :] = jnp.zeros((6, tokens), full)
    weights.relay(0)
    for k in range(1, count):
        mix_copy(k).start()
    mix_out[me] = mix_buf[me]
    weights.relay(1)
    weights.relay(2)
    locals_[0].wait()
    for k in range(1, count):
        gain_copy(k).wait_recv()
    for owner in range(count):
        gain_out[:, owner * rows : (owner + 1) * rows] = gain_buf[owner]
    for k in range(1, count):
        token_copy(k).wait_recv()
        mix_copy(k).wait_recv()
    weights.finish()
    for k in range(1, count):
        token_copy(k).wait_send()
        gain_copy(k).wait_send()
        mix_copy(k).wait_send()


def first_pass(tokens, weights, gains, order, expert_ids, gates, count):
    rows = weights[0].shape[0]
    number, width = tokens.shape
    block = number // count
    low = jnp.bfloat16
    full = jnp.float32
    dma = pltpu.SemaphoreType.DMA
    inside = pl.BlockSpec(memory_space=pltpu.VMEM)
    columns = sum(w.shape[1] for w in weights)
    shape = jax.ShapeDtypeStruct
    return pl.pallas_call(
        functools.partial(first_kernel, count),
        name="first_pass",
        out_shape=(
            shape((count, block, width), low),
            shape((rows * count, columns), low),
            shape((8, rows * count), full),
            shape((count, 8, number), full),
        ),
        in_specs=[inside] * 9,
        out_specs=(inside,) * 4,
        scratch_shapes=[
            pltpu.VMEM((count, 8, number), full),
            pltpu.VMEM((count, 8, rows), full),
            dma((count,)),
            dma((count,)),
            dma((count,)),
            dma((count,)),
            dma((count,)),
            dma((count,)),
            dma((2 * count + 2,)),
            dma((2 * count + 2,)),
            dma((5,)),
        ],
        compiler_params=pltpu.CompilerParams(
            collective_id=4, has_side_effects=True, vmem_limit_bytes=VMEM_MOST
        ),
        cost_estimate=pl.CostEstimate(flops=1 << 24, bytes_accessed=1 << 26, transcendentals=0),
    )(tokens.reshape(count, block, width), *weights, gains, order, expert_ids, gates)


def front_kernel(
    count,
    token_ref,
    query_ref,
    key_ref,
    value_ref,
    output_ref,
    first_ref,
    second_ref,
    order_ref,
    id_ref,
    gate_ref,
    length_ref,
    speed_ref,
    cotangent_ref,
    joined_out,
    gain_out,
    mix_out,
    along_out,
    across_out,
    input_out,
    query_out,
    key_out,
    value_out,
    mixed_out,
    logsum_out,
    hidden_out,
    normed_out,
    shared_out,
    slopes_out,
    arrived,
    joined,
    mix_buf,
    gain_src,
    gain_buf,
    place,
    bias,
    normed,
    inputs,
    projected,
    mixed,
    hidden,
    moved,
    shared,
    token_send,
    token_recv,
    gain_send,
    gain_recv,
    mix_send,
    mix_recv,
    weight_send,
    weight_recv,
    slope_send,
    slope_recv,
    local_sem,
    out_sem,
):
    rep = lax.axis_index("rep")
    me = lax.axis_index("shard")
    low = jnp.bfloat16
    full = jnp.float32
    rows = query_ref.shape[0]
    tokens, width = cotangent_ref.shape
    key_width = key_ref.shape[1]
    experts = mix_out.shape[0] * 2
    mine = pl.multiple_of(me * rows, rows)
    own = [pltpu.make_async_copy(token_ref.at[me], arrived.at[me], local_sem.at[0])]
    at = 0
    for i, ref in enumerate((query_ref, key_ref, value_ref, output_ref)):
        size = ref.shape[1]
        spot = joined.at[pl.ds(mine, rows), pl.ds(at, size)]
        own.append(pltpu.make_async_copy(ref, spot, local_sem.at[1 + i]))
        at += size
    own.append(pltpu.make_async_copy(cotangent_ref, slopes_out.at[me], local_sem.at[5]))
    for copy in own:
        copy.start()
    gain_src[...] = jnp.zeros(gain_src.shape, full)
    gain_src[0:1, :] = first_ref[...].astype(full)
    gain_src[1:2, :] = second_ref[...].astype(full)
    greet(me, rep, count)

    def token_copy(k):
        target = flip(me, k, count)
        return remote(
            token_ref.at[target], arrived.at[me], token_send, token_recv, k, (rep, target)
        )

    def gain_copy(k):
        return remote(
            gain_src, gain_buf.at[me], gain_send, gain_recv, k, (rep, flip(me, k, count))
        )

    def mix_copy(k):
        target = flip(me, k, count)
        return remote(mix_buf.at[target], mix_out.at[me], mix_send, mix_recv, k, (rep, target))

    for k in range(count - 1, 0, -1):
        token_copy(k).start()
    for copy in own[1:5]:
        copy.wait()
    half = rows // 2

    def block(owner, part):
        return joined.at[pl.ds(pl.multiple_of(owner * rows + part * half, half), half)]

    weights = Gather(count, rep, me, lambda p: block(me, p), block, weight_send, weight_recv)
    weights.start()
    for k in range(1, count):
        gain_copy(k).start()
    gain_buf[me] = gain_src[...]
    some = tokens // 2
    slopes = Gather(
        count,
        rep,
        me,
        lambda p: cotangent_ref.at[pl.ds(p * some, some)],
        lambda owner, p: slopes_out.at[owner, pl.ds(p * some, some)],
        slope_send,
        slope_recv,
    )
    kinds = lax.broadcasted_iota(jnp.int32, (experts, tokens), 0)
    mixing = jnp.zeros((experts, tokens), full)
    for k in range(id_ref.shape[0]):
        mixing = mixing + jnp.where(id_ref[k : k + 1, :] == kinds, gate_ref[k : k + 1, :], 0.0)
    place[...] = permutation(order_ref)
    dealt = jnp.zeros((experts, tokens), full)
    for _ in range(3):
        high = mixing.astype(low)
        dealt = dealt + matmul(high, place[...], NT)
        mixing = mixing - high.astype(full)
    for owner in range(count):
        mix_buf[owner, 0:2, :] = dealt[2 * owner : 2 * owner + 2, :]
        mix_buf[owner, 2:8, :] = jnp.zeros((6, tokens), full)
    weights.relay(0)
    for k in range(1, count):
        mix_copy(k).start()
    mix_out[me] = mix_buf[me]
    slopes.start()
    fill_bias(bias, length_ref)
    position = lax.broadcasted_iota(jnp.int32, along_out.shape, 0)
    angle = (position - starts_of(position, length_ref)).astype(full) * speed_ref[0:1, :]
    along_out[...] = jnp.cos(angle)
    across_out[...] = jnp.sin(angle) * speed_ref[1:2, :]
    own[0].wait()
    for k in range(1, count):
        token_copy(k).wait_recv()
        gain_copy(k).wait_recv()
    for owner in range(count):
        gain_out[:, owner * rows : (owner + 1) * rows] = gain_buf[owner]
    outs = (
        (inputs, input_out),
        (projected.at[:, pl.ds(0, width)], query_out),
        (projected.at[:, pl.ds(width, key_width)], key_out),
        (projected.at[:, pl.ds(width + key_width, key_width)], value_out),
        (mixed, mixed_out),
        (hidden, hidden_out),
        (moved, normed_out),
        (shared, shared_out),
        (joined, joined_out),
    )
    puts = [pltpu.make_async_copy(a, b, out_sem.at[k]) for k, (a, b) in enumerate(outs)]
    rows_in = matmul(place[...], arrived[...].reshape(tokens, width), TN)
    inputs[...] = rows_in.astype(low)
    scale = lax.rsqrt(jnp.mean(rows_in * rows_in, axis=1, keepdims=True) + EPS)
    normed[...] = (rows_in * scale * gain_out[0:1, :]).astype(low)
    puts[0].start()
    weights.relay(1)
    weights.relay(2)
    weights.ready(range(count))
    puts[8].start()
    along = along_out[...]
    across = across_out[...]

    def turned(at, carry):
        spot = pl.ds(pl.multiple_of(at * key_width, key_width), key_width)
        part = matmul(normed[...], joined[:, spot], NN)
        projected[:, spot] = turn_pairs(part, along, across, 1.0).astype(low)
        return carry

    lax.fori_loop(0, width // key_width + 1, turned, 0)
    part = matmul(normed[...], joined[:, width + key_width : width + 2 * key_width], NN)
    projected[:, width + key_width :] = part.astype(low)
    for copy in puts[1:4]:
        copy.start()

    def heads(g, carry):
        qs = pl.ds(pl.multiple_of(g * 256, 256), 256)
        kv = pl.ds(pl.multiple_of(width + g * 128, 128), 128)
        keys = projected[:, kv]
        kv = pl.ds(pl.multiple_of(width + key_width + g * 128, 128), 128)
        values = projected[:, kv]
        queries = projected[:, qs] * jnp.bfloat16(HEAD_SIZE**-0.5)
        for start, size, reach in query_spans(tokens):
            pieces = []
            for h in range(4):
                a = (h // 2) * HEAD_SIZE
                score = matmul(
                    keys[:reach, a : a + HEAD_SIZE],
                    queries[start : start + size, h * HEAD_SIZE : (h + 1) * HEAD_SIZE],
                    NT,
                )
                score = score + bias[:reach, start : start + size]
                largest = jnp.max(score, axis=0, keepdims=True)
                powers = jnp.exp(score - largest)
                totals = jnp.sum(powers, axis=0, keepdims=True)
                shares = (powers * (1.0 / totals)).astype(low)
                pieces.append(matmul(shares, values[:reach, a : a + HEAD_SIZE], TN))
                logsum_out[g, h : h + 1, start : start + size] = largest + jnp.log(totals)
            mixed[start : start + size, qs] = jnp.concatenate(pieces, axis=1).astype(low)

        @pl.when(g == 1)
        def _():
            slopes.relay(0)

        return carry

    lax.fori_loop(0, key_width // 128, heads, 0)
    puts[4].start()
    total = inputs[...].astype(full) + matmul(mixed[...], joined[:, width + 2 * key_width :], NN)
    hidden[...] = total
    scale = lax.rsqrt(jnp.mean(total * total, axis=1, keepdims=True) + EPS)
    normed[...] = (total * scale * gain_out[1:2, :]).astype(low)
    puts[5].start()
    moved[...] = matmul(place[...], normed[...], NN).astype(low)
    puts[6].start()
    shared[...] = matmul(place[...], hidden[...].astype(low), NN).astype(low)
    puts[7].start()
    slopes.relay(1)
    for k in range(1, count):
        mix_copy(k).wait_recv()
    for copy in puts:
        copy.wait()
    slopes.relay(2)
    own[5].wait()
    slopes.finish()
    weights.finish(())
    for k in range(1, count):
        token_copy(k).wait_send()
        gain_copy(k).wait_send()
        mix_copy(k).wait_send()


def front_pass(tokens, weights, gains, order, expert_ids, gates, lengths, cotangent, count):
    rows = weights[0].shape[0]
    number, width = tokens.shape
    key_width = weights[1].shape[1]
    block = number // count
    low = jnp.bfloat16
    full = jnp.float32
    dma = pltpu.SemaphoreType.DMA
    vmem = pltpu.VMEM
    anywhere = pl.BlockSpec(memory_space=pl.ANY)
    inside = pl.BlockSpec(memory_space=pltpu.VMEM)
    columns = sum(w.shape[1] for w in weights)
    shape = jax.ShapeDtypeStruct
    half = HEAD_SIZE // 2
    speed = np.tile(THETA ** (-2.0 * np.arange(half) / HEAD_SIZE), 128 // half)
    side = np.tile(np.repeat([-1.0, 1.0], half), 128 // HEAD_SIZE)
    speeds = jnp.asarray(np.stack([speed, side]).astype(np.float32))
    return pl.pallas_call(
        functools.partial(front_kernel, count),
        name="front_pass",
        out_shape=(
            shape((rows * count, columns), low),
            shape((8, rows * count), full),
            shape((count, 8, number), full),
            shape((number, 128), full),
            shape((number, 128), full),
            shape((number, width), low),
            shape((number, width), low),
            shape((number, key_width), low),
            shape((number, key_width), low),
            shape((number, width), low),
            shape((key_width // 128, 4, number), full),
            shape((number, width), full),
            shape((number, width), low),
            shape((number, width), low),
            shape((count, number, width), low),
        ),
        in_specs=[anywhere] * 5 + [inside] * 7 + [anywhere],
        out_specs=(anywhere,)
        + (inside,) * 4
        + (anywhere,) * 5
        + (inside,)
        + (anywhere,) * 4,
        scratch_shapes=[
            vmem((count, block, width), low),
            vmem((rows * count, columns), low),
            vmem((count, 8, number), full),
            vmem((8, rows), full),
            vmem((count, 8, rows), full),
            vmem((number, number), low),
            vmem((number, number), full),
            vmem((number, width), low),
            vmem((number, width), low),
            vmem((number, width + 2 * key_width), low),
            vmem((number, width), low),
            vmem((number, width), full),
            vmem((number, width), low),
            vmem((number, width), low),
            dma((count,)),
            dma((count,)),
            dma((count,)),
            dma((count,)),
            dma((count,)),
            dma((count,)),
            dma((2 * count + 2,)),
            dma((2 * count + 2,)),
            dma((2 * count + 2,)),
            dma((2 * count + 2,)),
            dma((6,)),
            dma((9,)),
        ],
        compiler_params=pltpu.CompilerParams(
            collective_id=4, has_side_effects=True, vmem_limit_bytes=VMEM_MOST
        ),
        cost_estimate=pl.CostEstimate(
            flops=12 << 30, bytes_accessed=1 << 26, transcendentals=1 << 22
        ),
    )(
        tokens.reshape(count, block, width),
        *weights,
        *(gain.reshape(1, rows) for gain in gains),
        order,
        expert_ids.T,
        gates.T,
        lengths,
        speeds,
        cotangent,
    )


def finish_kernel(count, reps, *refs):
    lined = reps == LINE
    (
        back_ref,
        slopes_ref,
        order_ref,
        length_ref,
        along_ref,
        across_ref,
        weight_ref,
        gain_ref,
        input_ref,
        query_ref,
        key_ref,
        value_ref,
        mixed_ref,
        logsum_ref,
        hidden_ref,
        piece_ref,
    ) = refs[:16]
    refs = refs[16:]
    staged = (
        back_ref,
        hidden_ref,
        mixed_ref,
        weight_ref,
        query_ref,
        key_ref,
        value_ref,
        input_ref,
    )
    held = refs[-len(staged) - 1 : -1]
    staging = [
        pltpu.make_async_copy(ref, buf, refs[-1].at[k])
        for k, (ref, buf) in enumerate(zip(staged, held, strict=True))
    ]
    refs = refs[: -len(staged) - 1]
    (
        back_ref,
        hidden_ref,
        mixed_ref,
        weight_ref,
        query_ref,
        key_ref,
        value_ref,
        input_ref,
    ) = held
    if lined:
        line_ref = refs[0]
        refs = refs[1:]
    delta_out, gain_out, slope_out, out_ref = refs[:4]
    refs = refs[4:]
    if lined:
        line_out = refs[0]
        refs = refs[1:]
    (
        place,
        bias,
        normed,
        steep,
        mixed_slope,
        backs,
        arrived,
        far_piece,
        far_piece_send,
        far_piece_recv,
        local_sem,
        delta,
        pair_recv,
        far_send,
        far_recv,
        pair_send_sem,
        pair_recv_sem,
        far_send_sem,
        far_recv_sem,
        slope_send_sem,
        slope_recv_sem,
        gain_buf,
        gain_recv,
        gain_sum,
        gain_line,
        gain_send_sem,
        gain_recv_sem,
        gain_line_send,
        gain_line_recv,
        owned,
    ) = refs[:30]
    refs = refs[30:]
    low = jnp.bfloat16
    full = jnp.float32
    rep = lax.axis_index("rep")
    me = lax.axis_index("shard")
    pairs = count // 2
    partner = flip(me, 1, count)
    tokens, width = back_ref.shape
    key_width = key_ref.shape[1]
    joined = width + 2 * key_width
    rows = width // count
    block = tokens // count
    own_slopes = pltpu.make_async_copy(
        slopes_ref.at[:, pl.ds(pl.multiple_of(me * block, block), block)],
        arrived,
        local_sem.at[0],
    )
    staging[0].start()
    own_slopes.start()
    for copy in staging[1:]:
        copy.start()
    own_piece = pltpu.make_async_copy(piece_ref.at[pairs - 1], mixed_slope, local_sem.at[1])
    greet(me, rep, count, reps)
    if lined:
        line = Line(rep, me, line_ref, line_out, *refs[:7], base=3 * PARTS, count=3 * PARTS)
        sums = Line(rep, me, owned, delta_out, *refs[7:12])
        line.start()
    else:
        spread, spread_send, spread_recv = refs

    def tick(begin, end):
        if lined:
            line.ticks(begin, end)

    def piece_copy(turn):
        return remote(
            piece_ref.at[turn],
            far_piece.at[turn - 1],
            far_piece_send,
            far_piece_recv,
            turn,
            (rep, flip(me, count - 2 - 2 * turn, count)),
        )

    def rows_of(owner):
        return pl.ds(pl.multiple_of(owner * rows, rows), rows)

    columns = (slice(joined, joined + width), slice(0, joined))

    def pair_copy(part, turn):
        return remote(
            delta.at[rows_of(flip(partner, 2 * turn, count)), columns[part]],
            pair_recv.at[turn, :, columns[part]],
            pair_send_sem,
            pair_recv_sem,
            part * pairs + turn,
            (rep, partner),
        )

    def far_copy(part, turn):
        return remote(
            far_send.at[turn - 1, :, columns[part]],
            far_recv.at[turn - 1, :, columns[part]],
            far_send_sem,
            far_recv_sem,
            part * pairs + turn,
            (rep, flip(me, 2 * turn, count)),
        )

    def exchange(part):
        for turn in range(pairs - 1, -1, -1):
            pair_copy(part, turn).start()

    def combine(part):
        def step(i, carry):
            turn = pairs - 1 - i
            pair_copy(part, turn).wait_recv()
            mine = delta[rows_of(flip(me, 2 * turn, count)), columns[part]].astype(full)
            far_send[turn - 1, :, columns[part]] = (
                mine + pair_recv[turn, :, columns[part]].astype(full)
            ).astype(low)
            far_copy(part, turn).start()
            return carry

        lax.fori_loop(0, pairs - 1, step, 0)

    def collect(part, first, number):
        pair_copy(part, 0).wait_recv()
        for turn in range(1, pairs):
            far_copy(part, turn).wait_recv()
        half = rows // 2

        def step(i, carry):
            at = pl.ds(
                pl.multiple_of(columns[part].start + (i // 2) * width, width), width
            )
            span = pl.ds(pl.multiple_of((i % 2) * half, half), half)
            mine = pl.ds(pl.multiple_of(me * rows + (i % 2) * half, half), half)
            value = delta[mine, at].astype(full) + pair_recv[0, span, at].astype(full)
            for turn in range(1, pairs):
                value = value + far_recv[turn - 1, span, at].astype(full)
            owned[first + i] = value.astype(low)
            return carry

        lax.fori_loop(0, number, step, 0)

    def slope_copy(k):
        target = flip(me, k, count)
        return remote(
            arrived.at[target],
            slope_out.at[me],
            slope_send_sem,
            slope_recv_sem,
            k,
            (rep, target),
        )

    def gain_copy(k):
        target = flip(me, k, count)
        return remote(
            gain_buf.at[target], gain_recv.at[k], gain_send_sem, gain_recv_sem, k, (rep, target)
        )

    def gain_line_copy(k):
        return remote(
            gain_sum,
            gain_line.at[rep],
            gain_line_send,
            gain_line_recv,
            k,
            (lax.rem(rep + k, reps), me),
        )

    for turn in range(1, pairs - 1):
        piece_copy(turn).start()
    place[...] = permutation(order_ref)
    fill_bias(bias, length_ref)
    own_slopes.wait()
    staging[0].wait()
    high = back_ref[...].astype(low)
    rest = (back_ref[...] - high.astype(full)).astype(low)
    slope = matmul(place[...], high, TN) + matmul(place[...], rest, TN)
    steep[...] = slope
    tick(0, 1)
    slope = steep[...]
    staging[1].wait()
    hidden = hidden_ref[...]
    scale = lax.rsqrt(jnp.mean(hidden * hidden, axis=1, keepdims=True) + EPS)
    scaled = slope * gain_ref[1:2, :]
    second = jnp.sum(slope * hidden * scale, axis=0, keepdims=True)
    for owner in range(count):
        gain_buf[owner, 1:2, :] = second[:, owner * rows : (owner + 1) * rows]
    tick(1, 2)
    steep[...] = (
        matmul(place[...], arrived[...].reshape(tokens, width), TN)
        + scale * scaled
        - hidden * (scale * scale * scale) * jnp.mean(hidden * scaled, axis=1, keepdims=True)
    )
    tick(2, 3)
    sharp = steep[...].astype(low)
    staging[2].wait()
    normed[...] = sharp

    def output_part(at, carry):
        spot = pl.ds(pl.multiple_of(at * 512, 512), 512)
        to = pl.ds(pl.multiple_of(joined + at * 512, 512), 512)
        delta[:, to] = matmul(mixed_ref[...], normed[:, spot], TN).astype(low)
        return carry

    lax.fori_loop(0, width // 512, output_part, 0)
    exchange(0)
    tick(3, 4)
    staging[3].wait()
    mixed_slope[...] = matmul(sharp, weight_ref[:, joined:], NT).astype(low)
    tick(4, 5)
    along = along_ref[...]
    across = across_ref[...]

    def heads(g, carry):
        kv = pl.ds(pl.multiple_of(g * 128, 128), 128)
        qs = pl.ds(pl.multiple_of(g * 256, 256), 256)
        keys = key_ref[:, kv]
        values = value_ref[:, kv]
        queries = query_ref[:, qs] * jnp.bfloat16(HEAD_SIZE**-0.5)
        slopes = mixed_slope[:, qs]
        key_parts = []
        value_parts = []
        query_parts = [[], []]
        for a in range(2):
            tick(5 + 3 * (2 * g + a) // 2, 5 + 3 * (2 * g + a + 1) // 2)
            key_h = keys[:, a * HEAD_SIZE : (a + 1) * HEAD_SIZE]
            value_h = values[:, a * HEAD_SIZE : (a + 1) * HEAD_SIZE]
            key_slope = [None, None]
            value_slope = [None, None]
            for b in range(2):
                h = 2 * a + b
                spot = slice(h * HEAD_SIZE, (h + 1) * HEAD_SIZE)
                for i, (start, size, reach) in enumerate(query_spans(tokens)):
                    q = queries[start : start + size, spot]
                    d = slopes[start : start + size, spot]
                    score = matmul(key_h[:reach], q, NT) + bias[:reach, start : start + size]
                    probs = jnp.exp(score - logsum_ref[g, h : h + 1, start : start + size])
                    prob_slope = matmul(value_h[:reach], d, NT)
                    inner = jnp.sum(probs * prob_slope, axis=0, keepdims=True)
                    score_slope = (probs * (prob_slope - inner)).astype(low)
                    term = matmul(probs.astype(low), d, NN)
                    value_slope[i] = term if b == 0 else value_slope[i] + term
                    term = matmul(score_slope, q, NN)
                    key_slope[i] = term if b == 0 else key_slope[i] + term
                    query_parts[i].append(matmul(score_slope, key_h[:reach], TN))
            half = tokens // 2
            key_parts.append(
                jnp.concatenate([key_slope[0] + key_slope[1][:half], key_slope[1][half:]], axis=0)
            )
            value_parts.append(
                jnp.concatenate(
                    [value_slope[0] + value_slope[1][:half], value_slope[1][half:]], axis=0
                )
            )
        for i, (start, size, reach) in enumerate(query_spans(tokens)):
            span = slice(start, start + size)
            part = jnp.concatenate(query_parts[i], axis=1) * HEAD_SIZE**-0.5
            backs[span, qs] = turn_pairs(part, along[span], across[span], -1.0).astype(low)
        part = jnp.concatenate(key_parts, axis=1)
        spot = pl.ds(pl.multiple_of(width + g * 128, 128), 128)
        backs[:, spot] = turn_pairs(part, along, across, -1.0).astype(low)
        part = jnp.concatenate(value_parts, axis=1)
        spot = pl.ds(pl.multiple_of(width + key_width + g * 128, 128), 128)
        backs[:, spot] = part.astype(low)

        @pl.when(g == 1)
        def _():
            combine(0)

        return carry

    for copy in staging[4:]:
        copy.wait()
    loops = key_width // 128
    lax.fori_loop(0, loops, heads, 0)
    done = 5 + 3 * loops
    own_piece.start()
    inputs = input_ref[...].astype(full)
    scale = lax.rsqrt(jnp.mean(inputs * inputs, axis=1, keepdims=True) + EPS)
    normed[...] = (inputs * scale * gain_ref[0:1, :]).astype(low)
    tick(done, done + 1)

    def input_part(at, carry):
        tick(done + 1 + at // 2, done + 1 + at // 2 + at % 2)
        spot = pl.ds(pl.multiple_of(at * 512, 512), 512)
        delta[:, spot] = matmul(normed[...], backs[:, spot], TN).astype(low)
        return carry

    lax.fori_loop(0, joined // 512, input_part, 0)
    exchange(1)
    slope = matmul(backs[...], weight_ref[:, :joined], NT)
    tick(done + 3, done + 4)
    combine(1)
    tick(done + 4, done + 5)
    scaled = slope * gain_ref[0:1, :]
    first = jnp.sum(slope * inputs * scale, axis=0, keepdims=True)
    for owner in range(count):
        gain_buf[owner, 0:1, :] = first[:, owner * rows : (owner + 1) * rows]
        gain_buf[owner, 2:8, :] = jnp.zeros((6, rows), full)
    for k in range(1, count):
        gain_copy(k).start()
    tick(done + 5, done + 6)
    result = (
        steep[...]
        + scale * scaled
        - inputs * (scale * scale * scale) * jnp.mean(inputs * scaled, axis=1, keepdims=True)
    )
    moved = matmul(place[...], result.astype(low), NN).astype(low)
    arrived[...] = moved.reshape(arrived.shape)
    for k in range(count - 1, 0, -1):
        slope_copy(k).start()
    slope_out[me] = arrived[me]
    tick(done + 6, done + 7)
    own_piece.wait()
    result = mixed_slope[...].astype(full)
    for turn in range(1, pairs - 1):
        piece_copy(turn).wait_recv()
        result = result + far_piece[turn - 1].astype(full)
    out_ref[...] = result.astype(low)
    collect(0, 0, 2)
    if lined:
        sums.start(0, 2)
    total = gain_buf[me]
    for k in range(1, count):
        gain_copy(k).wait_recv()
        total = total + gain_recv[k]
    gain_sum[...] = total
    gain_line[rep] = total
    for k in range(1, reps):
        gain_line_copy(k).start()
    tick(done + 7, 3 * PARTS + LAG - 1)
    collect(1, 2, 4)
    if lined:
        sums.start(2, 6)
        tick(3 * PARTS + LAG - 1, 3 * PARTS + LAG)
        line.receive()
        sums.ticks(0, 6 + LAG)
        sums.receive()
        sums.finish()
    else:

        def spread_copy(k):
            return remote(
                owned, spread.at[rep], spread_send, spread_recv, k, (lax.rem(rep + k, reps), me)
            )

        for k in range(1, reps):
            spread_copy(k).start()
        spread[rep] = owned[...]
        for k in range(1, reps):
            spread_copy(k).wait_recv()
        value = spread[0].astype(full)
        for k in range(1, reps):
            value = value + spread[k].astype(full)
        delta_out[...] = value.astype(low)
        for k in range(1, reps):
            spread_copy(k).wait_send()
    for k in range(1, reps):
        gain_line_copy(k).wait_recv()
    total = gain_line[0]
    for k in range(1, reps):
        total = total + gain_line[k]
    gain_out[...] = total
    for k in range(1, count):
        slope_copy(k).wait_recv()
    for k in range(1, count):
        slope_copy(k).wait_send()
        gain_copy(k).wait_send()
    for turn in range(1, pairs - 1):
        piece_copy(turn).wait_send()
    for part in range(2):
        for turn in range(pairs):
            pair_copy(part, turn).wait_send()
        for turn in range(1, pairs):
            far_copy(part, turn).wait_send()
    for k in range(1, reps):
        gain_line_copy(k).wait_send()
    if lined:
        line.finish()


def finish_pass(count, reps, back, slopes, *rest):
    *rest, pieces, extra = rest
    tokens, width = back.shape
    weights = rest[4]
    key_width = (weights.shape[1] - 2 * width) // 2
    pairs = count // 2
    rows = width // count
    block = tokens // count
    columns = weights.shape[1]
    low = jnp.bfloat16
    full = jnp.float32
    dma = pltpu.SemaphoreType.DMA
    vmem = pltpu.VMEM
    shape = jax.ShapeDtypeStruct
    lined = reps == LINE
    extra = [extra] if lined else []
    owned = (2 * columns // width, rows // 2, width)
    anywhere = pl.BlockSpec(memory_space=pl.ANY)
    inside = pl.BlockSpec(memory_space=pltpu.VMEM)
    if lined:
        last = line_scratch((3 * PARTS,) + extra[0].shape[1:]) + line_scratch(owned, False)
    else:
        last = [vmem((reps,) + owned, low), dma((reps,)), dma((reps,))]
    return pl.pallas_call(
        functools.partial(finish_kernel, count, reps),
        name="finish_pass",
        out_shape=(
            shape(owned, low),
            shape((8, rows), full),
            shape((count, block, width), low),
            shape((tokens, width), low),
        )
        + tuple(shape((3 * PARTS,) + d.shape[1:], low) for d in extra),
        in_specs=[anywhere, anywhere]
        + [inside] * 4
        + [anywhere, inside]
        + [anywhere] * 5
        + [inside]
        + [anywhere] * (2 + len(extra)),
        out_specs=(inside,) * 4 + (anywhere,) * len(extra),
        scratch_shapes=[
            vmem((tokens, tokens), low),
            vmem((tokens, tokens), full),
            vmem((tokens, width), low),
            vmem((tokens, width), full),
            vmem((tokens, width), low),
            vmem((tokens, width + 2 * key_width), low),
            vmem((count, block, width), low),
            vmem((pairs - 2, tokens, width), low),
            dma((pairs,)),
            dma((pairs,)),
            dma((2,)),
            vmem((width, columns), low),
            vmem((pairs, rows, columns), low),
            vmem((pairs - 1, rows, columns), low),
            vmem((pairs - 1, rows, columns), low),
            dma((2 * pairs,)),
            dma((2 * pairs,)),
            dma((2 * pairs,)),
            dma((2 * pairs,)),
            dma((count,)),
            dma((count,)),
            vmem((count, 8, rows), full),
            vmem((count, 8, rows), full),
            vmem((8, rows), full),
            vmem((reps, 8, rows), full),
            dma((count,)),
            dma((count,)),
            dma((reps,)),
            dma((reps,)),
            vmem(owned, low),
        ]
        + last
        + [
            vmem(a.shape, a.dtype)
            for a in (back, rest[12], rest[10], weights, rest[7], rest[8], rest[9], rest[6])
        ]
        + [dma((8,))],
        compiler_params=pltpu.CompilerParams(
            collective_id=6, has_side_effects=True, vmem_limit_bytes=VMEM_MOST
        ),
        cost_estimate=pl.CostEstimate(
            flops=24 << 30, bytes_accessed=1 << 24, transcendentals=1 << 22
        ),
    )(back, slopes, *rest, pieces, *extra)


def emit_kernel(
    tokens_ref,
    slopes_ref,
    gain_ref,
    delta_ref,
    early_ref,
    middle_ref,
    late_ref,
    tokens_out,
    slopes_out,
    first_out,
    query_out,
    key_out,
    value_out,
    output_out,
    second_out,
    gate_out,
    up_out,
    down_out,
):
    full = jnp.float32
    tokens_out[...] = tokens_ref[...]
    slopes_out[...] = slopes_ref[...]
    rows = early_ref.shape[1]
    hidden = gate_out.shape[3]
    for piece in range(2):
        to = slice(piece * rows, (piece + 1) * rows)
        spot = slice(piece * hidden, (piece + 1) * hidden)
        gate_out[0, :, to, :] = middle_ref[0, :, :, spot].astype(full)
        up_out[0, :, to, :] = middle_ref[1, :, :, spot].astype(full)
        gate_out[1, :, to, :] = late_ref[0, :, :, spot].astype(full)
        up_out[1, :, to, :] = late_ref[1, :, :, spot].astype(full)
    down_out[0] = early_ref[...].astype(full)
    down_out[1] = late_ref[2].astype(full)

    @pl.when(pl.program_id(0) == 0)
    def _():
        first_out[...] = gain_ref[0:1, :]
        second_out[...] = gain_ref[1:2, :]
        half = delta_ref.shape[1]
        key_width = key_out.shape[1]
        for i in range(2):
            span = slice(i * half, (i + 1) * half)
            output_out[span, :] = delta_ref[i].astype(full)
            query_out[span, :] = delta_ref[2 + i].astype(full)
            key_out[span, :] = delta_ref[4 + i, :, :key_width].astype(full)
            value_out[span, :] = delta_ref[4 + i, :, key_width:].astype(full)


def emit_pass(tokens, slopes, gains, deltas, early, middle, late):
    full = jnp.float32
    shape = jax.ShapeDtypeStruct
    number, width = tokens.shape
    rows = gains.shape[1]
    _, high, wide = early.shape
    hidden = high * PARTS
    steps = 4
    each = PARTS // steps

    def moving(*block):
        return pl.BlockSpec(block, lambda i: (i,) + (0,) * (len(block) - 1))

    def fixed(*block):
        return pl.BlockSpec(block, lambda i: (0,) * len(block))

    def inner(*block):
        return pl.BlockSpec(block, lambda i: (0, i, 0, 0))

    return pl.pallas_call(
        emit_kernel,
        name="emit_pass",
        grid=(steps,),
        out_shape=(
            shape(tokens.shape, tokens.dtype),
            shape(slopes.shape, slopes.dtype),
            shape((1, rows), full),
            shape((rows, width), full),
            shape((rows, width // 2), full),
            shape((rows, width // 2), full),
            shape((rows, width), full),
            shape((1, rows), full),
            shape((2, PARTS, 2 * high, hidden), full),
            shape((2, PARTS, 2 * high, hidden), full),
            shape((2, PARTS, high, wide), full),
        ),
        in_specs=[
            moving(number // steps, width),
            moving(number // steps, width),
            fixed(*gains.shape),
            fixed(*deltas.shape),
            moving(each, high, wide),
            inner(2, each, high, wide),
            inner(3, each, high, wide),
        ],
        out_specs=(
            moving(number // steps, width),
            moving(number // steps, width),
            fixed(1, rows),
            fixed(rows, width),
            fixed(rows, width // 2),
            fixed(rows, width // 2),
            fixed(rows, width),
            fixed(1, rows),
            inner(2, each, 2 * high, hidden),
            inner(2, each, 2 * high, hidden),
            inner(2, each, high, wide),
        ),
        compiler_params=pltpu.CompilerParams(vmem_limit_bytes=VMEM_MOST),
        cost_estimate=pl.CostEstimate(flops=1 << 20, bytes_accessed=1 << 24, transcendentals=0),
    )(
        tokens,
        slopes,
        gains,
        deltas,
        early,
        middle.reshape(2, PARTS, high, wide),
        late.reshape(3, PARTS, high, wide),
    )


def local(
    tokens,
    cotangent,
    seq_lengths,
    pack_order,
    unpack_order,
    expert_ids,
    gates,
    first_gain,
    query_weight,
    key_matrix,
    value_matrix,
    output_weight,
    second_gain,
    gate_weight,
    up_weight,
    down_weight,
):
    shards = lax.axis_size("shard")
    group_count, width = tokens.shape
    order = pack_order.reshape(1, group_count)
    (
        joined,
        gains,
        mixing,
        along,
        across,
        inputs,
        queries,
        keys,
        values,
        mixed,
        logsum,
        hidden,
        normed,
        shared,
        all_slopes,
    ) = front_pass(
        tokens,
        (query_weight, key_matrix, value_matrix, output_weight),
        (first_gain, second_gain),
        order,
        expert_ids,
        gates,
        seq_lengths,
        cotangent,
        shards,
    )
    tables = (order, seq_lengths, along, across, joined, gains)
    reps = lax.axis_size("rep")
    inner, row_slopes, partial, *early = expert_pass(
        normed, all_slopes, mixing, gate_weight, up_weight, down_weight, shards, reps
    )
    back, pieces, *middle = return_pass(
        row_slopes, inner, gate_weight, up_weight, down_weight, shared, partial, shards, reps
    )
    deltas, gain_deltas, delta_tokens, out_tokens, *late = finish_pass(
        shards,
        reps,
        back,
        all_slopes,
        *tables,
        inputs,
        queries,
        keys,
        values,
        mixed,
        logsum,
        hidden,
        pieces,
        partial,
    )
    if reps == LINE:
        early, middle, late = early[0], middle[0], late[0]
    else:
        summed = lax.psum(partial, "rep")
        early, middle, late = summed[:PARTS], summed[PARTS : 3 * PARTS], summed[3 * PARTS :]
    (
        out_tokens,
        delta_tokens,
        delta_first,
        delta_query,
        delta_key,
        delta_value,
        delta_output,
        delta_second,
        delta_gate,
        delta_up,
        delta_down,
    ) = emit_pass(
        out_tokens, delta_tokens.reshape(group_count, width), gain_deltas, deltas, early, middle, late
    )
    return (
        out_tokens,
        delta_tokens,
        delta_first.reshape(first_gain.shape),
        delta_query,
        delta_key,
        delta_value,
        delta_output,
        delta_second.reshape(second_gain.shape),
        delta_gate.reshape(gate_weight.shape),
        delta_up.reshape(up_weight.shape),
        delta_down.reshape(down_weight.shape),
    )


def solution(mesh):
    placed = (
        P(("rep", "shard"), None),
        P(("rep", "shard"), None),
        P(("rep", "shard"), None),
        P(("rep", "shard")),
        P(("rep", "shard")),
        P(("rep", "shard"), None),
        P(("rep", "shard"), None),
        P("shard"),
        P("shard", None),
        P("shard", None),
        P("shard", None),
        P("shard", None),
        P("shard"),
        P("shard", None, None),
        P("shard", None, None),
        P("shard", None, None),
    )
    return jax.shard_map(
        local,
        mesh=mesh,
        in_specs=placed,
        out_specs=(
            P(("rep", "shard"), None),
            P(("rep", "shard"), None),
            P("shard"),
            P("shard", None),
            P("shard", None),
            P("shard", None),
            P("shard", None),
            P("shard"),
            P("shard", None, None),
            P("shard", None, None),
            P("shard", None, None),
        ),
        check_vma=False,
    )
```

```python
import functools

import jax
import jax.numpy as jnp
import numpy as np
from jax import lax
from jax.experimental import pallas as pl
from jax.experimental.pallas import tpu as pltpu
from jax.sharding import PartitionSpec as P

QUERY_HEADS = 16
KEY_VALUE_HEADS = 8
HEAD_SIZE = 64


EPS = 1e-05
THETA = 10000.0


MESH = pl.DeviceIdType.MESH
NN = (((1,), (0,)), ((), ()))
NT = (((1,), (1,)), ((), ()))
TN = (((0,), (0,)), ((), ()))
TILE = 256
VMEM_MOST = 66_000_000


def matmul(left, right, dims):
    return lax.dot_general(left, right, dims, preferred_element_type=jnp.float32)


def stage_in(refs, count, start=0):
    held = refs[-count - 1 : -1]
    copies = [
        pltpu.make_async_copy(refs[start + k], held[k], refs[-1].at[k]) for k in range(count)
    ]
    return held, copies, refs[: -count - 1]


def flip(number, mask, count):
    out = 0
    bit = 1
    while bit < count:
        a = (number // bit) % 2
        b = (mask // bit) % 2
        out = out + (a + b - 2 * a * b) * bit
        bit *= 2
    return out


def greet(me, rep, count, reps=1):
    barrier = pltpu.get_barrier_semaphore()
    for k in range(1, count):
        pl.semaphore_signal(
            barrier, inc=1, device_id=(rep, lax.rem(me + k, count)), device_id_type=MESH
        )
    for k in range(1, reps):
        pl.semaphore_signal(
            barrier, inc=1, device_id=(lax.rem(rep + k, reps), me), device_id_type=MESH
        )
    pl.semaphore_wait(barrier, count + reps - 2)


LINE = 4
LAG = 2
RING = 4


class Line:
    def __init__(
        self,
        rep,
        me,
        source,
        out,
        first,
        second,
        both,
        sends,
        recvs,
        held=None,
        sems=None,
        base=0,
        count=None,
    ):
        self.rep, self.me = rep, me
        self.source, self.out = source, out
        self.first, self.second, self.both = first, second, both
        self.sends, self.recvs = sends, recvs
        self.held, self.sems = held, sems
        self.base = base
        self.count = source.shape[0] if count is None else count
        self.outer = (rep == 0) | (rep == LINE - 1)
        self.inner = jnp.logical_not(self.outer)
        self.inside = jnp.where(rep == 0, 1, 2)
        self.outside = jnp.where(rep == 1, 0, 3)
        self.across = LINE - 1 - rep

    def copy(self, stage, i):
        ring = self.both.at[i % RING]
        if stage == 0:
            source = self.source.at[self.base + i]
        else:
            source = ring if stage == 1 else self.first.at[i]
        target = (self.first, self.second, self.first)[stage].at[i]
        device = (self.inside, self.across, self.outside)[stage]
        return pltpu.make_async_remote_copy(
            src_ref=source,
            dst_ref=target,
            send_sem=self.sends.at[stage, i],
            recv_sem=self.recvs.at[stage, i],
            device_id=(device, self.me),
            device_id_type=MESH,
        )

    def load(self, i):
        return pltpu.make_async_copy(
            self.source.at[self.base + i], self.held.at[i % 2], self.sems.at[self.count + i % 2]
        )

    def put(self, i):
        return pltpu.make_async_copy(self.first.at[i], self.out.at[i], self.sems.at[i])

    def loop(self, body, begin=0):
        def step(i, carry):
            body(i)
            return carry

        lax.fori_loop(begin, self.count, step, 0)

    def start(self, begin=0, end=None):
        end = self.count if end is None else end

        @pl.when(self.outer)
        def _():
            def step(i, carry):
                self.copy(0, i).start()
                return carry

            lax.fori_loop(begin, end, step, 0)

        if self.held is not None:

            @pl.when(self.inner)
            def _():
                self.load(0).start()

    def tick(self, j):
        full = jnp.float32
        low = jnp.bfloat16

        @pl.when(self.inner & (j >= 0) & (j < self.count))
        def _():
            if self.held is None:
                own = self.source[self.base + j]
            else:

                @pl.when(j + 1 < self.count)
                def _():
                    self.load(j + 1).start()

                self.load(j).wait()
                own = self.held[j % 2]
            self.copy(0, j).wait_recv()

            @pl.when(j >= RING)
            def _():
                self.copy(1, j - RING).wait_send()

            self.both[j % RING] = (own.astype(full) + self.first[j].astype(full)).astype(low)
            self.copy(1, j).start()

        i = j - LAG

        @pl.when(self.inner & (i >= 0) & (i < self.count))
        def _():
            self.copy(1, i).wait_recv()
            every = self.both[i % RING].astype(full) + self.second[i].astype(full)
            self.first[i] = every.astype(low)
            self.copy(2, i).start()
            if self.held is None:
                self.out[i] = every.astype(low)
            else:
                self.put(i).start()

    def ticks(self, begin, end):
        def step(j, carry):
            self.tick(j)
            return carry

        lax.fori_loop(begin, end, step, 0)

    def receive(self):
        @pl.when(self.outer)
        def _():
            def step(i):
                self.copy(2, i).wait_recv()
                if self.held is None:
                    self.out[i] = self.first[i]
                else:
                    self.put(i).start()

            self.loop(step)

    def finish(self):
        @pl.when(self.outer)
        def _():
            self.loop(lambda i: self.copy(0, i).wait_send())

        @pl.when(self.inner)
        def _():
            self.loop(lambda i: self.copy(1, i).wait_send(), self.count - RING)
            self.loop(lambda i: self.copy(2, i).wait_send())

        if self.held is not None:
            self.loop(lambda i: self.put(i).wait())


def line_scratch(shape, streamed=True):
    low = jnp.bfloat16
    dma = pltpu.SemaphoreType.DMA
    scratch = [
        pltpu.VMEM(shape, low),
        pltpu.VMEM(shape, low),
        pltpu.VMEM((RING,) + shape[1:], low),
        dma((3, shape[0])),
        dma((3, shape[0])),
    ]
    if streamed:
        scratch += [pltpu.VMEM((2,) + shape[1:], low), dma((shape[0] + 2,))]
    return scratch


def remote(source, target, sends, recvs, index, device):
    return pltpu.make_async_remote_copy(
        src_ref=source,
        dst_ref=target,
        send_sem=sends.at[index],
        recv_sem=recvs.at[index],
        device_id=device,
        device_id_type=MESH,
    )


class Gather:
    def __init__(self, count, rep, me, own, slot, sends, recvs):
        self.count, self.rep, self.me = count, rep, me
        self.own, self.slot, self.sends, self.recvs = own, slot, sends, recvs
        self.waiting = []

    def near(self, mask):
        return flip(self.me, mask, self.count)

    def send(self, source, owner, part, mask, index):
        remote(
            source,
            self.slot(owner, part),
            self.sends,
            self.recvs,
            index,
            (self.rep, self.near(mask)),
        ).start()
        self.waiting.append(index)

    def arrived(self, owner, part, index):
        remote(
            self.slot(owner, part),
            self.slot(owner, part),
            self.sends,
            self.recvs,
            index,
            (self.rep, self.me),
        ).wait_recv()

    def pass_on(self, mask, part, index, new, onward):
        owner = self.near(mask)
        if index is not None:
            self.arrived(owner, part, index)
        self.send(self.slot(owner, part), owner, part, onward, new)

    def start(self):
        if self.count == 8:
            plan = ((2, 0, 0), (4, 1, 1), (2, 1, 2), (4, 0, 3), (1, 0, 4), (1, 1, 5))
            for mask, part, index in plan:
                self.send(self.own(part), self.me, part, mask, index)
        else:
            for mask in [1] + list(range(2, self.count, 2)):
                for part in range(2):
                    self.send(self.own(part), self.me, part, mask, 2 * mask + part)

    def relay(self, stage):
        if self.count == 8:
            if stage == 0:
                self.pass_on(2, 0, 0, 6, 4)
                self.pass_on(4, 1, 1, 8, 2)
                self.pass_on(2, 0, None, 7, 1)
                self.pass_on(4, 1, None, 9, 1)
            elif stage == 1:
                self.pass_on(2, 1, 2, 10, 1)
                self.pass_on(4, 0, 3, 11, 1)
            else:
                self.pass_on(6, 0, 6, 12, 1)
                self.pass_on(6, 1, 8, 13, 1)
        elif stage == 2:
            for mask in range(2, self.count, 2):
                for part in range(2):
                    self.pass_on(mask, part, 2 * mask + part, 2 * mask + 2 + part, 1)

    def ready(self, masks):
        if self.count == 8:
            last = ((1, 0, 4), (1, 1, 5), (3, 0, 7), (5, 1, 9), (3, 1, 10), (5, 0, 11))
            last += ((7, 0, 12), (7, 1, 13))
        else:
            last = [(m, p, 2 * m + p) for m in range(1, self.count, 2) for p in range(2)]
        for mask, part, index in last:
            if mask in masks:
                self.arrived(self.near(mask), part, index)

    def finish(self, masks=None):
        self.ready(range(self.count) if masks is None else masks)
        for index in self.waiting:
            spot = self.slot(self.me, 0)
            remote(
                spot, spot, self.sends, self.recvs, index, (self.rep, self.me)
            ).wait_send()


PARTS = 8


def expert_kernel(count, reps, *refs):
    lined = reps == LINE
    (gate_ref, up_ref, down_ref), staging, refs = stage_in(refs, 3, 3)
    for copy in staging:
        copy.start()
    own_ref, slope_ref, mix_ref = refs[:3]
    refs = (None,) * 6 + refs[6:]
    hidden_out, grad_out, delta_out = refs[6:9]
    refs = refs[9:]
    if lined:
        line_out = refs[0]
        refs = refs[1:]
    (
        rows,
        slope_buf,
        hidden_buf,
        grad_buf,
        acc_both,
        acc_down,
        stage,
        send_sem,
        recv_sem,
        own_sem,
        slope_sem,
        hidden_sem,
        grad_sem,
        stage_sem,
    ) = refs[:14]
    rep = lax.axis_index("rep")
    me = lax.axis_index("shard")
    experts, width, hidden = gate_ref.shape
    tokens = own_ref.shape[0]
    half = tokens // 2
    low = jnp.bfloat16
    turns = experts * count
    swap = 2 + count

    def pair(t):
        late = jnp.where(t < swap, t - 2, t - count)
        return (
            jnp.where(t < 4, t // 2, late),
            jnp.where(t < 4, t % 2, jnp.where(t < swap, 0, 1)),
        )

    def pack_of(t):
        return flip(me, pair(t)[0], count)

    def slope_copy(t):
        return pltpu.make_async_copy(
            slope_ref.at[:, pack_of(t)], slope_buf.at[t % 2], slope_sem.at[t % 2]
        )

    def hidden_copy(t):
        spot = pl.ds(pl.multiple_of(pair(t)[1] * hidden, hidden), hidden)
        return pltpu.make_async_copy(
            hidden_buf.at[t % 2], hidden_out.at[pack_of(t), :, spot], hidden_sem.at[t % 2]
        )

    def grad_copy(t):
        spot = pl.ds(pl.multiple_of(pair(t)[1] * 2 * hidden, 2 * hidden), 2 * hidden)
        return pltpu.make_async_copy(
            grad_buf.at[t % 2], grad_out.at[pack_of(t), :, spot], grad_sem.at[t % 2]
        )

    def stage_copy(e):
        span = pl.ds(e * 3 * PARTS, 3 * PARTS)
        return pltpu.make_async_copy(stage.at[span], delta_out.at[span], stage_sem.at[e])

    slope_copy(0).start()
    own = pltpu.make_async_copy(own_ref, rows.at[me], own_sem)
    own.start()
    greet(me, rep, count, reps if lined else 1)
    gather = Gather(
        count,
        rep,
        me,
        lambda p: own_ref.at[pl.ds(p * half, half)],
        lambda owner, p: rows.at[owner, pl.ds(p * half, half)],
        send_sem,
        recv_sem,
    )
    gather.start()
    own.wait()
    for copy in staging:
        copy.wait()
    if lined:
        line = Line(rep, me, stage, line_out, *refs[14:], count=PARTS)

    def spread(e, both, down):
        size = down.shape[0] // PARTS
        side = both.shape[0] // (2 * PARTS)
        base = e * 3 * PARTS
        for i in range(PARTS):
            at = base + 2 * PARTS * e + i
            stage[at] = down[i * size : (i + 1) * size, :].astype(low)
            for which in range(2):
                at = base + PARTS * (1 - e) + which * PARTS + i
                for piece in range(2):
                    span = slice((2 * i + piece) * side, (2 * i + piece + 1) * side)
                    stage[at, :, piece * hidden : (piece + 1) * hidden] = both[
                        span, which * hidden : (which + 1) * hidden
                    ].astype(low)
        stage_copy(e).start()

    if count == 8:
        plan = {2: ((1,), 0), 4: ((), 1), 5: ((3,), None), 7: ((5,), 2), 9: ((7,), None)}
    else:
        plan = {2: ((1,), None), 4: ((), 2), 5: (tuple(range(3, count, 2)), None)}

    def step(t, carry):
        k, e = pair(t)
        pack = flip(me, k, count)
        for at, (masks, stage_at) in plan.items():

            @pl.when(t == at)
            def _():
                gather.ready(masks)
                if stage_at is not None:
                    gather.relay(stage_at)

        @pl.when(t + 1 < turns)
        def _():
            slope_copy(t + 1).start()

        if lined:
            line.tick(2 * (t - swap - 1))
        slope_copy(t).wait()

        @pl.when(t >= 2)
        def _():
            hidden_copy(t - 2).wait()
            grad_copy(t - 2).wait()

        slot = t % 2
        x = rows[pack]
        dy = slope_buf[slot].reshape(tokens, width)
        mixes = jnp.transpose(mix_ref[pack])
        mix = jnp.where(e == 0, mixes[:, 0:1], mixes[:, 1:2])
        for part in range(hidden // TILE):
            span = pl.ds(part * TILE, TILE)
            ga = matmul(x, gate_ref[e, :, span], NN)
            ua = matmul(x, up_ref[e, :, span], NN)
            dh = matmul(dy, down_ref[e, span, :], NT) * mix
            sig = jax.nn.sigmoid(ga)
            act = ga * sig
            hidden_buf[slot, :, span] = (mix * (act * ua)).astype(low)
            grad_buf[slot, :, span] = (dh * ua * sig * (1.0 + ga * (1.0 - sig))).astype(low)
            grad_buf[slot, :, pl.ds(hidden + part * TILE, TILE)] = (dh * act).astype(low)
        hidden_copy(t).start()
        grad_copy(t).start()
        if lined:
            line.tick(2 * (t - swap) - 1)

        both = matmul(x, grad_buf[slot], TN)
        down = matmul(hidden_buf[slot], dy, TN)

        @pl.when(k == 0)
        def _():
            acc_both[e] = both
            acc_down[e] = down

        @pl.when((k > 0) & (k < count - 1))
        def _():
            acc_both[e] += both
            acc_down[e] += down

        @pl.when((t == swap - 1) | (t == turns - 1))
        def _():
            spread(e, acc_both[e] + both, acc_down[e] + down)

        if lined:

            @pl.when(t == swap - 1)
            def _():
                line.start()

        return carry

    lax.fori_loop(0, turns, step, 0)
    if lined:
        line.ticks(2 * (turns - swap - 1), PARTS + LAG)
    for t in (turns - 2, turns - 1):
        hidden_copy(t).wait()
        grad_copy(t).wait()
    gather.finish(())
    stage_copy(0).wait()
    if lined:
        line.receive()
        line.finish()
    stage_copy(1).wait()


def expert_pass(normed, all_slopes, mixing, gate_weight, up_weight, down_weight, count, reps):
    tokens, width = normed.shape
    experts, _, hidden = gate_weight.shape
    block = tokens // count
    low = jnp.bfloat16
    full = jnp.float32
    dma = pltpu.SemaphoreType.DMA
    vmem = pltpu.VMEM
    shape = jax.ShapeDtypeStruct
    anywhere = pl.BlockSpec(memory_space=pl.ANY)
    inside = pl.BlockSpec(memory_space=pltpu.VMEM)
    flops = 2 * count * tokens * width * hidden * experts * 6
    lined = reps == LINE
    segment = (hidden // PARTS, width)
    summed = (PARTS,) + segment
    return pl.pallas_call(
        functools.partial(expert_kernel, count, reps),
        name="expert_pass",
        out_shape=(
            shape((count, tokens, experts * hidden), low),
            shape((count, tokens, 2 * experts * hidden), low),
            shape((6 * PARTS,) + segment, low),
        )
        + ((shape(summed, low),) if lined else ()),
        in_specs=[anywhere, anywhere, inside, anywhere, anywhere, anywhere],
        out_specs=(anywhere,) * 3 + ((inside,) if lined else ()),
        scratch_shapes=[
            vmem((count, tokens, width), low),
            vmem((2, count, block, width), low),
            vmem((2, tokens, hidden), low),
            vmem((2, tokens, 2 * hidden), low),
            vmem((experts, width, 2 * hidden), full),
            vmem((experts, hidden, width), full),
            vmem((6 * PARTS,) + segment, low),
            dma((2 * count + 2,)),
            dma((2 * count + 2,)),
            dma,
            dma((2,)),
            dma((2,)),
            dma((2,)),
            dma((2,)),
        ]
        + (line_scratch(summed, False) if lined else [])
        + [vmem(w.shape, low) for w in (gate_weight, up_weight, down_weight)]
        + [dma((3,))],
        compiler_params=pltpu.CompilerParams(
            collective_id=1, has_side_effects=True, vmem_limit_bytes=VMEM_MOST
        ),
        cost_estimate=pl.CostEstimate(flops=flops, bytes_accessed=1 << 26, transcendentals=0),
    )(
        normed,
        all_slopes.reshape(count, count, block, width),
        mixing,
        gate_weight,
        up_weight,
        down_weight,
    )


def return_kernel(count, reps, *refs):
    (gate_ref, up_ref, down_ref, own_ref), staging, refs = stage_in(refs, 4, 2)
    for copy in staging:
        copy.start()
    grad_ref, hidden_ref = refs[:2]
    lined = reps == LINE
    refs = refs[6:]
    if lined:
        line_ref, back_ref, piece_out, line_out = refs[:4]
        refs = refs[4:]
    else:
        back_ref, piece_out = refs[:2]
        refs = refs[2:]
    (
        grad_buf,
        hidden_buf,
        pair_send,
        far_send,
        pair_recv,
        far_recv,
        total,
        piece,
        last_recv,
        relay_recv,
        load_sem,
        pair_send_sem,
        pair_recv_sem,
        far_send_sem,
        far_recv_sem,
        piece_sem,
        last_sem,
        relay_send_sem,
        relay_recv_sem,
    ) = refs[:19]
    rep = lax.axis_index("rep")
    me = lax.axis_index("shard")
    experts, width, hidden = gate_ref.shape
    tokens = own_ref.shape[0]
    block = tokens // count
    low = jnp.bfloat16
    full = jnp.float32
    pairs = count // 2
    partner = flip(me, 1, count)
    line = Line(rep, me, line_ref, line_out, *refs[19:], base=PARTS, count=2 * PARTS) if lined else None

    relayed = count == 8
    half = tokens // 2

    def mask_of(turn):
        return count - 2 - 2 * turn

    def target(item):
        return flip(me, mask_of(item // 2) + 1 - item % 2, count)

    def grad_load(item):
        return pltpu.make_async_copy(
            grad_ref.at[target(item)], grad_buf.at[item % 2], load_sem.at[item % 2]
        )

    def grad_part(slot, pack):
        value = None
        for e in range(experts):
            for at, weight in ((2 * e, gate_ref), (2 * e + 1, up_ref)):
                term = matmul(grad_buf[slot, :, pl.ds(at * hidden, hidden)], weight[e], NT)
                value = term if value is None else value + term
        total[...] = value

    def hidden_load(item):
        return pltpu.make_async_copy(
            hidden_ref.at[:, target(item)], hidden_buf.at[item % 2], load_sem.at[item % 2]
        )

    def hidden_part(slot, pack):
        value = None
        for e in range(experts):
            term = matmul(
                hidden_buf[slot, :, :, pl.ds(e * hidden, hidden)].reshape(tokens, hidden),
                down_ref[e],
                NN,
            )
            value = term if value is None else value + term
        total[...] = value
        mine = pl.ds(pl.multiple_of(me * block, block), block)
        theirs = pl.ds(pl.multiple_of(pack * block, block), block)
        total[mine, :] += own_ref[theirs, :].astype(full)

    def pair_copy(base, turn):
        return remote(
            pair_send.at[turn % 2],
            pair_recv.at[base + turn],
            pair_send_sem,
            pair_recv_sem,
            base + turn,
            (rep, partner),
        )

    def far_copy(turn, device):
        return remote(
            far_send.at[turn % 2], far_recv.at[turn], far_send_sem, far_recv_sem, turn, (rep, device)
        )

    def half_copy(side):
        span = pl.ds(side * half, half)
        return remote(
            far_send.at[1, span],
            far_recv.at[1, span],
            far_send_sem,
            far_recv_sem,
            side,
            (rep, flip(me, count - 4, count)),
        )

    def relay_copy(phase, side, source):
        return remote(
            source.at[pl.ds(side * half, half)],
            relay_recv.at[2 * phase + side],
            relay_send_sem,
            relay_recv_sem,
            2 * phase + side,
            (rep, flip(me, 2 + 2 * side, count)),
        )

    def last_copy(device):
        return pltpu.make_async_remote_copy(
            src_ref=piece.at[0],
            dst_ref=last_recv,
            send_sem=last_sem.at[0],
            recv_sem=last_sem.at[1],
            device_id=(rep, device),
            device_id_type=MESH,
        )

    def slot(turn):
        return jnp.where(turn == 0, 0, jnp.where(turn == pairs - 1, 3, 1 + turn % 2))

    def piece_copy(turn):
        return pltpu.make_async_copy(
            piece.at[slot(turn)], piece_out.at[turn], piece_sem.at[turn % 2]
        )

    def grad_combine(turn, mask):
        last = turn == pairs - 1
        total[...] += pair_recv[turn].astype(full)

        @pl.when(last)
        def _():
            back_ref[...] = total[...]

        if relayed:

            @pl.when(turn == 0)
            def _():
                far_send[0] = total[...].astype(low)
                for side in range(2):
                    relay_copy(0, side, far_send.at[0]).start()

            @pl.when(turn == 1)
            def _():
                far_send[1] = total[...].astype(low)
                half_copy(1).start()

            @pl.when(turn == 2)
            def _():
                early, later = pl.ds(0, half), pl.ds(half, half)
                for side in range(2):
                    relay_copy(0, side, far_send.at[0]).wait_recv()
                value = far_send[1, early, :].astype(full) + relay_recv[0].astype(full)
                far_send[1, early, :] = value.astype(low)
                half_copy(0).start()
                for side in range(2):
                    relay_copy(0, side, far_send.at[0]).wait_send()
                total[later, :] += relay_recv[1].astype(full)
                far_send[0] = total[...].astype(low)
                far_copy(2, flip(me, mask, count)).start()
        else:

            @pl.when(jnp.logical_not(last))
            def _():
                @pl.when(turn >= 2)
                def _():
                    far_copy(turn - 2, me).wait_send()

                far_send[turn % 2] = total[...].astype(low)
                far_copy(turn, flip(me, mask, count)).start()

    def hidden_combine(turn, mask):
        if not relayed:

            @pl.when((turn >= 3) & (turn < pairs - 1))
            def _():
                piece_copy(turn - 2).wait()

        piece[slot(turn)] = (total[...] + pair_recv[pairs + turn].astype(full)).astype(low)

        @pl.when(turn == 0)
        def _():
            if relayed:
                for side in range(2):
                    relay_copy(1, side, piece.at[0]).start()
            else:
                last_copy(flip(me, mask, count)).start()

        if not relayed:

            @pl.when((turn > 0) & (turn < pairs - 1))
            def _():
                piece_copy(turn).start()

    grad_load(0).start()
    greet(me, rep, count, reps if lined else 1)
    if lined:
        line.start()

    def sweep(base, load, part, combine, pace):
        def item_step(item, carry):
            turn = item // 2
            mask = mask_of(turn)

            @pl.when(item + 1 < 2 * pairs)
            def _():
                load(item + 1).start()

            load(item).wait()
            part(item % 2, target(item))

            @pl.when(item % 2 == 0)
            def _():
                @pl.when(turn >= 2)
                def _():
                    pair_copy(base, turn - 2).wait_send()

                pair_send[turn % 2] = total[...].astype(low)
                pair_copy(base, turn).start()

            @pl.when(item % 2 == 1)
            def _():
                pair_copy(base, turn).wait_recv()
                combine(turn, mask)

            if lined:
                line.ticks(pace(item) - 2, pace(item + 1) - 2)
            return carry

        lax.fori_loop(0, 2 * pairs, item_step, 0)
        for turn in range(max(0, pairs - 2), pairs):
            pair_copy(base, turn).wait_send()

    for copy in staging:
        copy.wait()
    sweep(0, grad_load, grad_part, grad_combine, lambda item: 3 * item // 2)
    hidden_load(0).start()
    sweep(pairs, hidden_load, hidden_part, hidden_combine, lambda item: 3 * pairs + item)
    if lined:
        line.ticks(5 * pairs - 2, 2 * PARTS + LAG)
    if relayed:
        for side in range(2):
            half_copy(side).wait_recv()
        back_ref[...] += far_recv[1].astype(full)
        far_copy(2, me).wait_recv()
        back_ref[...] += far_recv[2].astype(full)
        for side in range(2):
            half_copy(side).wait_send()
        far_copy(2, me).wait_send()
    else:

        def add(turn, carry):
            far_copy(turn, me).wait_recv()
            back_ref[...] += far_recv[turn].astype(full)
            return carry

        lax.fori_loop(0, pairs - 1, add, 0)
        for turn in (pairs - 3, pairs - 2):
            far_copy(turn, me).wait_send()
    if lined:
        line.receive()
    if relayed:
        for side in range(2):
            relay_copy(1, side, piece.at[0]).wait_recv()
            rows = pl.ds(side * half, half)
            spot = slot(1 + side)
            value = piece[spot, rows, :].astype(full) + relay_recv[2 + side].astype(full)
            piece[spot, rows, :] = value.astype(low)
            piece_copy(1 + side).start()
            relay_copy(1, side, piece.at[0]).wait_send()
    else:
        last_copy(me).wait_recv()
        value = piece[3].astype(full) + last_recv[...].astype(full)
        piece[3] = value.astype(low)
        last_copy(me).wait_send()
    for turn in (pairs - 3, pairs - 2):
        piece_copy(turn).wait()
    piece_copy(pairs - 1).start()
    if lined:
        line.finish()
    piece_copy(pairs - 1).wait()


def return_pass(grads, hiddens, gate_weight, up_weight, down_weight, own, deltas, count, reps):
    tokens, width = own.shape
    experts, _, hidden = gate_weight.shape
    block = tokens // count
    low = jnp.bfloat16
    full = jnp.float32
    pairs = count // 2
    dma = pltpu.SemaphoreType.DMA
    shape = jax.ShapeDtypeStruct
    anywhere = pl.BlockSpec(memory_space=pl.ANY)
    inside = pl.BlockSpec(memory_space=pltpu.VMEM)
    flops = 2 * count * tokens * width * hidden * experts * 3
    lined = reps == LINE
    extra = [deltas] if lined else []
    return pl.pallas_call(
        functools.partial(return_kernel, count, reps),
        name="return_pass",
        out_shape=(
            shape((tokens, width), full),
            shape((pairs, tokens, width), low),
        )
        + tuple(shape((2 * PARTS,) + d.shape[1:], low) for d in extra),
        in_specs=[anywhere] * (6 + len(extra)),
        out_specs=(inside, anywhere) + (anywhere,) * len(extra),
        scratch_shapes=[
            pltpu.VMEM((2, tokens, 2 * experts * hidden), low),
            pltpu.VMEM((2, count, block, experts * hidden), low),
            pltpu.VMEM((2, tokens, width), low),
            pltpu.VMEM((2, tokens, width), low),
            pltpu.VMEM((2 * pairs, tokens, width), low),
            pltpu.VMEM((pairs, tokens, width), low),
            pltpu.VMEM((tokens, width), full),
            pltpu.VMEM((4, tokens, width), low),
            pltpu.VMEM((8, 128) if count == 8 else (tokens, width), low),
            pltpu.VMEM((4, tokens // 2, width), low),
            dma((2,)),
            dma((2 * pairs,)),
            dma((2 * pairs,)),
            dma((pairs,)),
            dma((pairs,)),
            dma((2,)),
            dma((3,)),
            dma((4,)),
            dma((4,)),
        ]
        + (line_scratch((2 * PARTS,) + deltas.shape[1:]) if lined else [])
        + [pltpu.VMEM(a.shape, low) for a in (gate_weight, up_weight, down_weight, own)]
        + [dma((4,))],
        compiler_params=pltpu.CompilerParams(
            collective_id=2, has_side_effects=True, vmem_limit_bytes=VMEM_MOST
        ),
        cost_estimate=pl.CostEstimate(flops=flops, bytes_accessed=1 << 26, transcendentals=0),
    )(
        grads,
        hiddens.reshape(count, count, block, experts * hidden),
        gate_weight,
        up_weight,
        down_weight,
        own,
        *extra,
    )


def turn_pairs(rows, along, across, sign):
    lane = lax.broadcasted_iota(jnp.int32, (rows.shape[0], 128), 1)
    early = (lane % HEAD_SIZE) < HEAD_SIZE // 2
    pieces = []
    for at in range(0, rows.shape[1], 128):
        part = rows[:, at : at + 128]
        other = jnp.where(
            early,
            pltpu.roll(part, 128 - HEAD_SIZE // 2, 1),
            pltpu.roll(part, HEAD_SIZE // 2, 1),
        )
        pieces.append(part * along + sign * (other * across))
    return pieces[0] if len(pieces) == 1 else jnp.concatenate(pieces, axis=1)


def permutation(order_ref):
    tokens = order_ref.shape[1]
    rows = lax.broadcasted_iota(jnp.int32, (tokens, tokens), 0)
    return jnp.where(order_ref[...] == rows, 1.0, 0.0).astype(jnp.bfloat16)


def starts_of(position, length_ref):
    start = jnp.zeros_like(position)
    end = jnp.zeros((1, 1), jnp.int32)
    for k in range(length_ref.shape[1] - 1):
        end = end + length_ref[0:1, k : k + 1]
        start = jnp.where(position >= end, end, start)
    return start


def fill_bias(bias, length_ref):
    tokens = bias.shape[0]
    keys = lax.broadcasted_iota(jnp.int32, (tokens, tokens), 0)
    queries = lax.broadcasted_iota(jnp.int32, (tokens, tokens), 1)
    start = starts_of(lax.broadcasted_iota(jnp.int32, (1, tokens), 1), length_ref)
    bias[...] = jnp.where((keys >= start) & (keys <= queries), 0.0, -1e30)


def query_spans(tokens):
    half = tokens // 2
    return ((0, half, half), (half, half, tokens))


def first_kernel(
    count,
    token_ref,
    query_ref,
    key_ref,
    value_ref,
    output_ref,
    gain_ref,
    order_ref,
    id_ref,
    gate_ref,
    arrived_out,
    joined_out,
    gain_out,
    mix_out,
    mix_buf,
    gain_buf,
    token_send,
    token_recv,
    gain_send,
    gain_recv,
    mix_send,
    mix_recv,
    weight_send,
    weight_recv,
    local_sem,
):
    rep = lax.axis_index("rep")
    me = lax.axis_index("shard")
    full = jnp.float32
    low = jnp.bfloat16
    rows = query_ref.shape[0]
    experts = mix_out.shape[0] * 2
    mine = pl.multiple_of(me * rows, rows)
    locals_ = [pltpu.make_async_copy(token_ref.at[me], arrived_out.at[me], local_sem.at[0])]
    at = 0
    for i, ref in enumerate((query_ref, key_ref, value_ref, output_ref)):
        size = ref.shape[1]
        target = joined_out.at[pl.ds(mine, rows), pl.ds(at, size)]
        locals_.append(pltpu.make_async_copy(ref, target, local_sem.at[1 + i]))
        at += size
    for copy in locals_:
        copy.start()
    greet(me, rep, count)

    def token_copy(k):
        target = flip(me, k, count)
        return remote(
            token_ref.at[target], arrived_out.at[me], token_send, token_recv, k, (rep, target)
        )

    def gain_copy(k):
        return remote(
            gain_ref, gain_buf.at[me], gain_send, gain_recv, k, (rep, flip(me, k, count))
        )

    def mix_copy(k):
        target = flip(me, k, count)
        return remote(mix_buf.at[target], mix_out.at[me], mix_send, mix_recv, k, (rep, target))

    for k in range(count - 1, 0, -1):
        token_copy(k).start()
    for copy in locals_[1:]:
        copy.wait()
    half = rows // 2

    def block(owner, part):
        return joined_out.at[pl.ds(pl.multiple_of(owner * rows + part * half, half), half)]

    weights = Gather(count, rep, me, lambda p: block(me, p), block, weight_send, weight_recv)
    weights.start()
    for k in range(1, count):
        gain_copy(k).start()
    gain_buf[me] = gain_ref[...]
    tokens = order_ref.shape[0]
    lane = lax.broadcasted_iota(jnp.int32, (tokens, experts), 1)
    mixing = jnp.zeros((tokens, experts), full)
    for k in range(id_ref.shape[1]):
        mixing = mixing + jnp.where(id_ref[:, k : k + 1] == lane, gate_ref[:, k : k + 1], 0.0)
    place = permutation(order_ref)
    moved = jnp.zeros((experts, tokens), full)
    for _ in range(3):
        high = mixing.astype(low)
        moved = moved + matmul(high, place, TN)
        mixing = mixing - high.astype(full)
    for owner in range(count):
        mix_buf[owner, 0:2, :] = moved[2 * owner : 2 * owner + 2, :]
        mix_buf[owner, 2:8, :] = jnp.zeros((6, tokens), full)
    weights.relay(0)
    for k in range(1, count):
        mix_copy(k).start()
    mix_out[me] = mix_buf[me]
    weights.relay(1)
    weights.relay(2)
    locals_[0].wait()
    for k in range(1, count):
        gain_copy(k).wait_recv()
    for owner in range(count):
        gain_out[:, owner * rows : (owner + 1) * rows] = gain_buf[owner]
    for k in range(1, count):
        token_copy(k).wait_recv()
        mix_copy(k).wait_recv()
    weights.finish()
    for k in range(1, count):
        token_copy(k).wait_send()
        gain_copy(k).wait_send()
        mix_copy(k).wait_send()


def first_pass(tokens, weights, gains, order, expert_ids, gates, count):
    rows = weights[0].shape[0]
    number, width = tokens.shape
    block = number // count
    low = jnp.bfloat16
    full = jnp.float32
    dma = pltpu.SemaphoreType.DMA
    inside = pl.BlockSpec(memory_space=pltpu.VMEM)
    columns = sum(w.shape[1] for w in weights)
    shape = jax.ShapeDtypeStruct
    return pl.pallas_call(
        functools.partial(first_kernel, count),
        name="first_pass",
        out_shape=(
            shape((count, block, width), low),
            shape((rows * count, columns), low),
            shape((8, rows * count), full),
            shape((count, 8, number), full),
        ),
        in_specs=[inside] * 9,
        out_specs=(inside,) * 4,
        scratch_shapes=[
            pltpu.VMEM((count, 8, number), full),
            pltpu.VMEM((count, 8, rows), full),
            dma((count,)),
            dma((count,)),
            dma((count,)),
            dma((count,)),
            dma((count,)),
            dma((count,)),
            dma((2 * count + 2,)),
            dma((2 * count + 2,)),
            dma((5,)),
        ],
        compiler_params=pltpu.CompilerParams(
            collective_id=4, has_side_effects=True, vmem_limit_bytes=VMEM_MOST
        ),
        cost_estimate=pl.CostEstimate(flops=1 << 24, bytes_accessed=1 << 26, transcendentals=0),
    )(tokens.reshape(count, block, width), *weights, gains, order, expert_ids, gates)


def front_kernel(
    count,
    token_ref,
    query_ref,
    key_ref,
    value_ref,
    output_ref,
    first_ref,
    second_ref,
    order_ref,
    id_ref,
    gate_ref,
    length_ref,
    speed_ref,
    cotangent_ref,
    joined_out,
    gain_out,
    mix_out,
    along_out,
    across_out,
    input_out,
    query_out,
    key_out,
    value_out,
    mixed_out,
    logsum_out,
    hidden_out,
    normed_out,
    shared_out,
    slopes_out,
    arrived,
    joined,
    mix_buf,
    gain_src,
    gain_buf,
    place,
    bias,
    normed,
    inputs,
    projected,
    mixed,
    hidden,
    moved,
    shared,
    token_send,
    token_recv,
    gain_send,
    gain_recv,
    mix_send,
    mix_recv,
    weight_send,
    weight_recv,
    slope_send,
    slope_recv,
    local_sem,
    out_sem,
):
    rep = lax.axis_index("rep")
    me = lax.axis_index("shard")
    low = jnp.bfloat16
    full = jnp.float32
    rows = query_ref.shape[0]
    tokens, width = cotangent_ref.shape
    key_width = key_ref.shape[1]
    experts = mix_out.shape[0] * 2
    mine = pl.multiple_of(me * rows, rows)
    own = [pltpu.make_async_copy(token_ref.at[me], arrived.at[me], local_sem.at[0])]
    at = 0
    for i, ref in enumerate((query_ref, key_ref, value_ref, output_ref)):
        size = ref.shape[1]
        spot = joined.at[pl.ds(mine, rows), pl.ds(at, size)]
        own.append(pltpu.make_async_copy(ref, spot, local_sem.at[1 + i]))
        at += size
    own.append(pltpu.make_async_copy(cotangent_ref, slopes_out.at[me], local_sem.at[5]))
    for copy in own:
        copy.start()
    gain_src[...] = jnp.zeros(gain_src.shape, full)
    gain_src[0:1, :] = first_ref[...].astype(full)
    gain_src[1:2, :] = second_ref[...].astype(full)
    greet(me, rep, count)

    def token_copy(k):
        target = flip(me, k, count)
        return remote(
            token_ref.at[target], arrived.at[me], token_send, token_recv, k, (rep, target)
        )

    def gain_copy(k):
        return remote(
            gain_src, gain_buf.at[me], gain_send, gain_recv, k, (rep, flip(me, k, count))
        )

    def mix_copy(k):
        target = flip(me, k, count)
        return remote(mix_buf.at[target], mix_out.at[me], mix_send, mix_recv, k, (rep, target))

    for k in range(count - 1, 0, -1):
        token_copy(k).start()
    for copy in own[1:5]:
        copy.wait()
    half = rows // 2

    def block(owner, part):
        return joined.at[pl.ds(pl.multiple_of(owner * rows + part * half, half), half)]

    weights = Gather(count, rep, me, lambda p: block(me, p), block, weight_send, weight_recv)
    weights.start()
    for k in range(1, count):
        gain_copy(k).start()
    gain_buf[me] = gain_src[...]
    some = tokens // 2
    slopes = Gather(
        count,
        rep,
        me,
        lambda p: cotangent_ref.at[pl.ds(p * some, some)],
        lambda owner, p: slopes_out.at[owner, pl.ds(p * some, some)],
        slope_send,
        slope_recv,
    )
    kinds = lax.broadcasted_iota(jnp.int32, (experts, tokens), 0)
    mixing = jnp.zeros((experts, tokens), full)
    for k in range(id_ref.shape[0]):
        mixing = mixing + jnp.where(id_ref[k : k + 1, :] == kinds, gate_ref[k : k + 1, :], 0.0)
    place[...] = permutation(order_ref)
    dealt = jnp.zeros((experts, tokens), full)
    for _ in range(3):
        high = mixing.astype(low)
        dealt = dealt + matmul(high, place[...], NT)
        mixing = mixing - high.astype(full)
    for owner in range(count):
        mix_buf[owner, 0:2, :] = dealt[2 * owner : 2 * owner + 2, :]
        mix_buf[owner, 2:8, :] = jnp.zeros((6, tokens), full)
    weights.relay(0)
    for k in range(1, count):
        mix_copy(k).start()
    mix_out[me] = mix_buf[me]
    slopes.start()
    fill_bias(bias, length_ref)
    position = lax.broadcasted_iota(jnp.int32, along_out.shape, 0)
    angle = (position - starts_of(position, length_ref)).astype(full) * speed_ref[0:1, :]
    along_out[...] = jnp.cos(angle)
    across_out[...] = jnp.sin(angle) * speed_ref[1:2, :]
    own[0].wait()
    for k in range(1, count):
        token_copy(k).wait_recv()
        gain_copy(k).wait_recv()
    for owner in range(count):
        gain_out[:, owner * rows : (owner + 1) * rows] = gain_buf[owner]
    outs = (
        (inputs, input_out),
        (projected.at[:, pl.ds(0, width)], query_out),
        (projected.at[:, pl.ds(width, key_width)], key_out),
        (projected.at[:, pl.ds(width + key_width, key_width)], value_out),
        (mixed, mixed_out),
        (hidden, hidden_out),
        (moved, normed_out),
        (shared, shared_out),
        (joined, joined_out),
    )
    puts = [pltpu.make_async_copy(a, b, out_sem.at[k]) for k, (a, b) in enumerate(outs)]
    rows_in = matmul(place[...], arrived[...].reshape(tokens, width), TN)
    inputs[...] = rows_in.astype(low)
    scale = lax.rsqrt(jnp.mean(rows_in * rows_in, axis=1, keepdims=True) + EPS)
    normed[...] = (rows_in * scale * gain_out[0:1, :]).astype(low)
    puts[0].start()
    weights.relay(1)
    weights.relay(2)
    weights.ready(range(count))
    puts[8].start()
    along = along_out[...]
    across = across_out[...]

    def turned(at, carry):
        spot = pl.ds(pl.multiple_of(at * key_width, key_width), key_width)
        part = matmul(normed[...], joined[:, spot], NN)
        projected[:, spot] = turn_pairs(part, along, across, 1.0).astype(low)
        return carry

    lax.fori_loop(0, width // key_width + 1, turned, 0)
    part = matmul(normed[...], joined[:, width + key_width : width + 2 * key_width], NN)
    projected[:, width + key_width :] = part.astype(low)
    for copy in puts[1:4]:
        copy.start()

    def heads(g, carry):
        qs = pl.ds(pl.multiple_of(g * 256, 256), 256)
        kv = pl.ds(pl.multiple_of(width + g * 128, 128), 128)
        keys = projected[:, kv]
        kv = pl.ds(pl.multiple_of(width + key_width + g * 128, 128), 128)
        values = projected[:, kv]
        queries = projected[:, qs] * jnp.bfloat16(HEAD_SIZE**-0.5)
        for start, size, reach in query_spans(tokens):
            pieces = []
            for h in range(4):
                a = (h // 2) * HEAD_SIZE
                score = matmul(
                    keys[:reach, a : a + HEAD_SIZE],
                    queries[start : start + size, h * HEAD_SIZE : (h + 1) * HEAD_SIZE],
                    NT,
                )
                score = score + bias[:reach, start : start + size]
                largest = jnp.max(score, axis=0, keepdims=True)
                powers = jnp.exp(score - largest)
                totals = jnp.sum(powers, axis=0, keepdims=True)
                shares = (powers * (1.0 / totals)).astype(low)
                pieces.append(matmul(shares, values[:reach, a : a + HEAD_SIZE], TN))
                logsum_out[g, h : h + 1, start : start + size] = largest + jnp.log(totals)
            mixed[start : start + size, qs] = jnp.concatenate(pieces, axis=1).astype(low)

        @pl.when(g == 1)
        def _():
            slopes.relay(0)

        return carry

    lax.fori_loop(0, key_width // 128, heads, 0)
    puts[4].start()
    total = inputs[...].astype(full) + matmul(mixed[...], joined[:, width + 2 * key_width :], NN)
    hidden[...] = total
    scale = lax.rsqrt(jnp.mean(total * total, axis=1, keepdims=True) + EPS)
    normed[...] = (total * scale * gain_out[1:2, :]).astype(low)
    puts[5].start()
    moved[...] = matmul(place[...], normed[...], NN).astype(low)
    puts[6].start()
    shared[...] = matmul(place[...], hidden[...].astype(low), NN).astype(low)
    puts[7].start()
    slopes.relay(1)
    for k in range(1, count):
        mix_copy(k).wait_recv()
    for copy in puts:
        copy.wait()
    slopes.relay(2)
    own[5].wait()
    slopes.finish()
    weights.finish(())
    for k in range(1, count):
        token_copy(k).wait_send()
        gain_copy(k).wait_send()
        mix_copy(k).wait_send()


def front_pass(tokens, weights, gains, order, expert_ids, gates, lengths, cotangent, count):
    rows = weights[0].shape[0]
    number, width = tokens.shape
    key_width = weights[1].shape[1]
    block = number // count
    low = jnp.bfloat16
    full = jnp.float32
    dma = pltpu.SemaphoreType.DMA
    vmem = pltpu.VMEM
    anywhere = pl.BlockSpec(memory_space=pl.ANY)
    inside = pl.BlockSpec(memory_space=pltpu.VMEM)
    columns = sum(w.shape[1] for w in weights)
    shape = jax.ShapeDtypeStruct
    half = HEAD_SIZE // 2
    speed = np.tile(THETA ** (-2.0 * np.arange(half) / HEAD_SIZE), 128 // half)
    side = np.tile(np.repeat([-1.0, 1.0], half), 128 // HEAD_SIZE)
    speeds = jnp.asarray(np.stack([speed, side]).astype(np.float32))
    return pl.pallas_call(
        functools.partial(front_kernel, count),
        name="front_pass",
        out_shape=(
            shape((rows * count, columns), low),
            shape((8, rows * count), full),
            shape((count, 8, number), full),
            shape((number, 128), full),
            shape((number, 128), full),
            shape((number, width), low),
            shape((number, width), low),
            shape((number, key_width), low),
            shape((number, key_width), low),
            shape((number, width), low),
            shape((key_width // 128, 4, number), full),
            shape((number, width), full),
            shape((number, width), low),
            shape((number, width), low),
            shape((count, number, width), low),
        ),
        in_specs=[anywhere] * 5 + [inside] * 7 + [anywhere],
        out_specs=(anywhere,)
        + (inside,) * 4
        + (anywhere,) * 5
        + (inside,)
        + (anywhere,) * 4,
        scratch_shapes=[
            vmem((count, block, width), low),
            vmem((rows * count, columns), low),
            vmem((count, 8, number), full),
            vmem((8, rows), full),
            vmem((count, 8, rows), full),
            vmem((number, number), low),
            vmem((number, number), full),
            vmem((number, width), low),
            vmem((number, width), low),
            vmem((number, width + 2 * key_width), low),
            vmem((number, width), low),
            vmem((number, width), full),
            vmem((number, width), low),
            vmem((number, width), low),
            dma((count,)),
            dma((count,)),
            dma((count,)),
            dma((count,)),
            dma((count,)),
            dma((count,)),
            dma((2 * count + 2,)),
            dma((2 * count + 2,)),
            dma((2 * count + 2,)),
            dma((2 * count + 2,)),
            dma((6,)),
            dma((9,)),
        ],
        compiler_params=pltpu.CompilerParams(
            collective_id=4, has_side_effects=True, vmem_limit_bytes=VMEM_MOST
        ),
        cost_estimate=pl.CostEstimate(
            flops=12 << 30, bytes_accessed=1 << 26, transcendentals=1 << 22
        ),
    )(
        tokens.reshape(count, block, width),
        *weights,
        *(gain.reshape(1, rows) for gain in gains),
        order,
        expert_ids.T,
        gates.T,
        lengths,
        speeds,
        cotangent,
    )


def finish_kernel(count, reps, *refs):
    lined = reps == LINE
    (
        back_ref,
        slopes_ref,
        order_ref,
        length_ref,
        along_ref,
        across_ref,
        weight_ref,
        gain_ref,
        input_ref,
        query_ref,
        key_ref,
        value_ref,
        mixed_ref,
        logsum_ref,
        hidden_ref,
        piece_ref,
    ) = refs[:16]
    refs = refs[16:]
    staged = (
        back_ref,
        hidden_ref,
        mixed_ref,
        weight_ref,
        query_ref,
        key_ref,
        value_ref,
        input_ref,
    )
    held = refs[-len(staged) - 1 : -1]
    staging = [
        pltpu.make_async_copy(ref, buf, refs[-1].at[k])
        for k, (ref, buf) in enumerate(zip(staged, held, strict=True))
    ]
    refs = refs[: -len(staged) - 1]
    (
        back_ref,
        hidden_ref,
        mixed_ref,
        weight_ref,
        query_ref,
        key_ref,
        value_ref,
        input_ref,
    ) = held
    if lined:
        line_ref = refs[0]
        refs = refs[1:]
    delta_out, gain_out, slope_out, out_ref = refs[:4]
    refs = refs[4:]
    if lined:
        line_out = refs[0]
        refs = refs[1:]
    (
        place,
        bias,
        normed,
        steep,
        mixed_slope,
        backs,
        arrived,
        far_piece,
        far_piece_send,
        far_piece_recv,
        local_sem,
        delta,
        pair_recv,
        far_send,
        far_recv,
        pair_send_sem,
        pair_recv_sem,
        far_send_sem,
        far_recv_sem,
        slope_send_sem,
        slope_recv_sem,
        gain_buf,
        gain_recv,
        gain_sum,
        gain_line,
        gain_send_sem,
        gain_recv_sem,
        gain_line_send,
        gain_line_recv,
        owned,
    ) = refs[:30]
    refs = refs[30:]
    low = jnp.bfloat16
    full = jnp.float32
    rep = lax.axis_index("rep")
    me = lax.axis_index("shard")
    pairs = count // 2
    partner = flip(me, 1, count)
    tokens, width = back_ref.shape
    key_width = key_ref.shape[1]
    joined = width + 2 * key_width
    rows = width // count
    block = tokens // count
    own_slopes = pltpu.make_async_copy(
        slopes_ref.at[:, pl.ds(pl.multiple_of(me * block, block), block)],
        arrived,
        local_sem.at[0],
    )
    staging[0].start()
    own_slopes.start()
    for copy in staging[1:]:
        copy.start()
    own_piece = pltpu.make_async_copy(piece_ref.at[pairs - 1], mixed_slope, local_sem.at[1])
    greet(me, rep, count, reps)
    if lined:
        line = Line(rep, me, line_ref, line_out, *refs[:7], base=3 * PARTS, count=3 * PARTS)
        sums = Line(rep, me, owned, delta_out, *refs[7:12])
        line.start()
    else:
        spread, spread_send, spread_recv = refs

    def tick(begin, end):
        if lined:
            line.ticks(begin, end)

    def piece_copy(turn):
        return remote(
            piece_ref.at[turn],
            far_piece.at[turn - 1],
            far_piece_send,
            far_piece_recv,
            turn,
            (rep, flip(me, count - 2 - 2 * turn, count)),
        )

    def rows_of(owner):
        return pl.ds(pl.multiple_of(owner * rows, rows), rows)

    columns = (slice(joined, joined + width), slice(0, joined))

    def pair_copy(part, turn):
        return remote(
            delta.at[rows_of(flip(partner, 2 * turn, count)), columns[part]],
            pair_recv.at[turn, :, columns[part]],
            pair_send_sem,
            pair_recv_sem,
            part * pairs + turn,
            (rep, partner),
        )

    def far_copy(part, turn):
        return remote(
            far_send.at[turn - 1, :, columns[part]],
            far_recv.at[turn - 1, :, columns[part]],
            far_send_sem,
            far_recv_sem,
            part * pairs + turn,
            (rep, flip(me, 2 * turn, count)),
        )

    def exchange(part):
        for turn in range(pairs - 1, -1, -1):
            pair_copy(part, turn).start()

    def combine(part):
        def step(i, carry):
            turn = pairs - 1 - i
            pair_copy(part, turn).wait_recv()
            mine = delta[rows_of(flip(me, 2 * turn, count)), columns[part]].astype(full)
            far_send[turn - 1, :, columns[part]] = (
                mine + pair_recv[turn, :, columns[part]].astype(full)
            ).astype(low)
            far_copy(part, turn).start()
            return carry

        lax.fori_loop(0, pairs - 1, step, 0)

    def collect(part, first, number):
        pair_copy(part, 0).wait_recv()
        for turn in range(1, pairs):
            far_copy(part, turn).wait_recv()
        half = rows // 2

        def step(i, carry):
            at = pl.ds(
                pl.multiple_of(columns[part].start + (i // 2) * width, width), width
            )
            span = pl.ds(pl.multiple_of((i % 2) * half, half), half)
            mine = pl.ds(pl.multiple_of(me * rows + (i % 2) * half, half), half)
            value = delta[mine, at].astype(full) + pair_recv[0, span, at].astype(full)
            for turn in range(1, pairs):
                value = value + far_recv[turn - 1, span, at].astype(full)
            owned[first + i] = value.astype(low)
            return carry

        lax.fori_loop(0, number, step, 0)

    def slope_copy(k):
        target = flip(me, k, count)
        return remote(
            arrived.at[target],
            slope_out.at[me],
            slope_send_sem,
            slope_recv_sem,
            k,
            (rep, target),
        )

    def gain_copy(k):
        target = flip(me, k, count)
        return remote(
            gain_buf.at[target], gain_recv.at[k], gain_send_sem, gain_recv_sem, k, (rep, target)
        )

    def gain_line_copy(k):
        return remote(
            gain_sum,
            gain_line.at[rep],
            gain_line_send,
            gain_line_recv,
            k,
            (lax.rem(rep + k, reps), me),
        )

    for turn in range(1, pairs - 1):
        piece_copy(turn).start()
    place[...] = permutation(order_ref)
    fill_bias(bias, length_ref)
    own_slopes.wait()
    staging[0].wait()
    high = back_ref[...].astype(low)
    rest = (back_ref[...] - high.astype(full)).astype(low)
    slope = matmul(place[...], high, TN) + matmul(place[...], rest, TN)
    steep[...] = slope
    tick(0, 1)
    slope = steep[...]
    staging[1].wait()
    hidden = hidden_ref[...]
    scale = lax.rsqrt(jnp.mean(hidden * hidden, axis=1, keepdims=True) + EPS)
    scaled = slope * gain_ref[1:2, :]
    second = jnp.sum(slope * hidden * scale, axis=0, keepdims=True)
    for owner in range(count):
        gain_buf[owner, 1:2, :] = second[:, owner * rows : (owner + 1) * rows]
    tick(1, 2)
    steep[...] = (
        matmul(place[...], arrived[...].reshape(tokens, width), TN)
        + scale * scaled
        - hidden * (scale * scale * scale) * jnp.mean(hidden * scaled, axis=1, keepdims=True)
    )
    tick(2, 3)
    sharp = steep[...].astype(low)
    staging[2].wait()
    normed[...] = sharp

    def output_part(at, carry):
        spot = pl.ds(pl.multiple_of(at * 512, 512), 512)
        to = pl.ds(pl.multiple_of(joined + at * 512, 512), 512)
        delta[:, to] = matmul(mixed_ref[...], normed[:, spot], TN).astype(low)
        return carry

    lax.fori_loop(0, width // 512, output_part, 0)
    exchange(0)
    tick(3, 4)
    staging[3].wait()
    mixed_slope[...] = matmul(sharp, weight_ref[:, joined:], NT).astype(low)
    tick(4, 5)
    along = along_ref[...]
    across = across_ref[...]

    def heads(g, carry):
        kv = pl.ds(pl.multiple_of(g * 128, 128), 128)
        qs = pl.ds(pl.multiple_of(g * 256, 256), 256)
        keys = key_ref[:, kv]
        values = value_ref[:, kv]
        queries = query_ref[:, qs] * jnp.bfloat16(HEAD_SIZE**-0.5)
        slopes = mixed_slope[:, qs]
        key_parts = []
        value_parts = []
        query_parts = [[], []]
        for a in range(2):
            tick(5 + 3 * (2 * g + a) // 2, 5 + 3 * (2 * g + a + 1) // 2)
            key_h = keys[:, a * HEAD_SIZE : (a + 1) * HEAD_SIZE]
            value_h = values[:, a * HEAD_SIZE : (a + 1) * HEAD_SIZE]
            key_slope = [None, None]
            value_slope = [None, None]
            for b in range(2):
                h = 2 * a + b
                spot = slice(h * HEAD_SIZE, (h + 1) * HEAD_SIZE)
                for i, (start, size, reach) in enumerate(query_spans(tokens)):
                    q = queries[start : start + size, spot]
                    d = slopes[start : start + size, spot]
                    score = matmul(key_h[:reach], q, NT) + bias[:reach, start : start + size]
                    probs = jnp.exp(score - logsum_ref[g, h : h + 1, start : start + size])
                    prob_slope = matmul(value_h[:reach], d, NT)
                    inner = jnp.sum(probs * prob_slope, axis=0, keepdims=True)
                    score_slope = (probs * (prob_slope - inner)).astype(low)
                    term = matmul(probs.astype(low), d, NN)
                    value_slope[i] = term if b == 0 else value_slope[i] + term
                    term = matmul(score_slope, q, NN)
                    key_slope[i] = term if b == 0 else key_slope[i] + term
                    query_parts[i].append(matmul(score_slope, key_h[:reach], TN))
            half = tokens // 2
            key_parts.append(
                jnp.concatenate([key_slope[0] + key_slope[1][:half], key_slope[1][half:]], axis=0)
            )
            value_parts.append(
                jnp.concatenate(
                    [value_slope[0] + value_slope[1][:half], value_slope[1][half:]], axis=0
                )
            )
        for i, (start, size, reach) in enumerate(query_spans(tokens)):
            span = slice(start, start + size)
            part = jnp.concatenate(query_parts[i], axis=1) * HEAD_SIZE**-0.5
            backs[span, qs] = turn_pairs(part, along[span], across[span], -1.0).astype(low)
        part = jnp.concatenate(key_parts, axis=1)
        spot = pl.ds(pl.multiple_of(width + g * 128, 128), 128)
        backs[:, spot] = turn_pairs(part, along, across, -1.0).astype(low)
        part = jnp.concatenate(value_parts, axis=1)
        spot = pl.ds(pl.multiple_of(width + key_width + g * 128, 128), 128)
        backs[:, spot] = part.astype(low)

        @pl.when(g == 1)
        def _():
            combine(0)

        return carry

    for copy in staging[4:]:
        copy.wait()
    loops = key_width // 128
    lax.fori_loop(0, loops, heads, 0)
    done = 5 + 3 * loops
    own_piece.start()
    inputs = input_ref[...].astype(full)
    scale = lax.rsqrt(jnp.mean(inputs * inputs, axis=1, keepdims=True) + EPS)
    normed[...] = (inputs * scale * gain_ref[0:1, :]).astype(low)
    tick(done, done + 1)

    def input_part(at, carry):
        tick(done + 1 + at // 2, done + 1 + at // 2 + at % 2)
        spot = pl.ds(pl.multiple_of(at * 512, 512), 512)
        delta[:, spot] = matmul(normed[...], backs[:, spot], TN).astype(low)
        return carry

    lax.fori_loop(0, joined // 512, input_part, 0)
    exchange(1)
    slope = matmul(backs[...], weight_ref[:, :joined], NT)
    tick(done + 3, done + 4)
    combine(1)
    tick(done + 4, done + 5)
    scaled = slope * gain_ref[0:1, :]
    first = jnp.sum(slope * inputs * scale, axis=0, keepdims=True)
    for owner in range(count):
        gain_buf[owner, 0:1, :] = first[:, owner * rows : (owner + 1) * rows]
        gain_buf[owner, 2:8, :] = jnp.zeros((6, rows), full)
    for k in range(1, count):
        gain_copy(k).start()
    tick(done + 5, done + 6)
    result = (
        steep[...]
        + scale * scaled
        - inputs * (scale * scale * scale) * jnp.mean(inputs * scaled, axis=1, keepdims=True)
    )
    moved = matmul(place[...], result.astype(low), NN).astype(low)
    arrived[...] = moved.reshape(arrived.shape)
    for k in range(count - 1, 0, -1):
        slope_copy(k).start()
    slope_out[me] = arrived[me]
    tick(done + 6, done + 7)
    own_piece.wait()
    result = mixed_slope[...].astype(full)
    for turn in range(1, pairs - 1):
        piece_copy(turn).wait_recv()
        result = result + far_piece[turn - 1].astype(full)
    out_ref[...] = result.astype(low)
    collect(0, 0, 2)
    if lined:
        sums.start(0, 2)
    total = gain_buf[me]
    for k in range(1, count):
        gain_copy(k).wait_recv()
        total = total + gain_recv[k]
    gain_sum[...] = total
    gain_line[rep] = total
    for k in range(1, reps):
        gain_line_copy(k).start()
    tick(done + 7, 3 * PARTS + LAG - 1)
    collect(1, 2, 4)
    if lined:
        sums.start(2, 6)
        tick(3 * PARTS + LAG - 1, 3 * PARTS + LAG)
        line.receive()
        sums.ticks(0, 6 + LAG)
        sums.receive()
        sums.finish()
    else:

        def spread_copy(k):
            return remote(
                owned, spread.at[rep], spread_send, spread_recv, k, (lax.rem(rep + k, reps), me)
            )

        for k in range(1, reps):
            spread_copy(k).start()
        spread[rep] = owned[...]
        for k in range(1, reps):
            spread_copy(k).wait_recv()
        value = spread[0].astype(full)
        for k in range(1, reps):
            value = value + spread[k].astype(full)
        delta_out[...] = value.astype(low)
        for k in range(1, reps):
            spread_copy(k).wait_send()
    for k in range(1, reps):
        gain_line_copy(k).wait_recv()
    total = gain_line[0]
    for k in range(1, reps):
        total = total + gain_line[k]
    gain_out[...] = total
    for k in range(1, count):
        slope_copy(k).wait_recv()
    for k in range(1, count):
        slope_copy(k).wait_send()
        gain_copy(k).wait_send()
    for turn in range(1, pairs - 1):
        piece_copy(turn).wait_send()
    for part in range(2):
        for turn in range(pairs):
            pair_copy(part, turn).wait_send()
        for turn in range(1, pairs):
            far_copy(part, turn).wait_send()
    for k in range(1, reps):
        gain_line_copy(k).wait_send()
    if lined:
        line.finish()


def finish_pass(count, reps, back, slopes, *rest):
    *rest, pieces, extra = rest
    tokens, width = back.shape
    weights = rest[4]
    key_width = (weights.shape[1] - 2 * width) // 2
    pairs = count // 2
    rows = width // count
    block = tokens // count
    columns = weights.shape[1]
    low = jnp.bfloat16
    full = jnp.float32
    dma = pltpu.SemaphoreType.DMA
    vmem = pltpu.VMEM
    shape = jax.ShapeDtypeStruct
    lined = reps == LINE
    extra = [extra] if lined else []
    owned = (2 * columns // width, rows // 2, width)
    anywhere = pl.BlockSpec(memory_space=pl.ANY)
    inside = pl.BlockSpec(memory_space=pltpu.VMEM)
    if lined:
        last = line_scratch((3 * PARTS,) + extra[0].shape[1:]) + line_scratch(owned, False)
    else:
        last = [vmem((reps,) + owned, low), dma((reps,)), dma((reps,))]
    return pl.pallas_call(
        functools.partial(finish_kernel, count, reps),
        name="finish_pass",
        out_shape=(
            shape(owned, low),
            shape((8, rows), full),
            shape((count, block, width), low),
            shape((tokens, width), low),
        )
        + tuple(shape((3 * PARTS,) + d.shape[1:], low) for d in extra),
        in_specs=[anywhere, anywhere]
        + [inside] * 4
        + [anywhere, inside]
        + [anywhere] * 5
        + [inside]
        + [anywhere] * (2 + len(extra)),
        out_specs=(inside,) * 4 + (anywhere,) * len(extra),
        scratch_shapes=[
            vmem((tokens, tokens), low),
            vmem((tokens, tokens), full),
            vmem((tokens, width), low),
            vmem((tokens, width), full),
            vmem((tokens, width), low),
            vmem((tokens, width + 2 * key_width), low),
            vmem((count, block, width), low),
            vmem((pairs - 2, tokens, width), low),
            dma((pairs,)),
            dma((pairs,)),
            dma((2,)),
            vmem((width, columns), low),
            vmem((pairs, rows, columns), low),
            vmem((pairs - 1, rows, columns), low),
            vmem((pairs - 1, rows, columns), low),
            dma((2 * pairs,)),
            dma((2 * pairs,)),
            dma((2 * pairs,)),
            dma((2 * pairs,)),
            dma((count,)),
            dma((count,)),
            vmem((count, 8, rows), full),
            vmem((count, 8, rows), full),
            vmem((8, rows), full),
            vmem((reps, 8, rows), full),
            dma((count,)),
            dma((count,)),
            dma((reps,)),
            dma((reps,)),
            vmem(owned, low),
        ]
        + last
        + [
            vmem(a.shape, a.dtype)
            for a in (back, rest[12], rest[10], weights, rest[7], rest[8], rest[9], rest[6])
        ]
        + [dma((8,))],
        compiler_params=pltpu.CompilerParams(
            collective_id=6, has_side_effects=True, vmem_limit_bytes=VMEM_MOST
        ),
        cost_estimate=pl.CostEstimate(
            flops=24 << 30, bytes_accessed=1 << 24, transcendentals=1 << 22
        ),
    )(back, slopes, *rest, pieces, *extra)


def emit_kernel(
    tokens_ref,
    slopes_ref,
    gain_ref,
    delta_ref,
    early_ref,
    middle_ref,
    late_ref,
    tokens_out,
    slopes_out,
    first_out,
    query_out,
    key_out,
    value_out,
    output_out,
    second_out,
    gate_out,
    up_out,
    down_out,
):
    full = jnp.float32
    tokens_out[...] = tokens_ref[...]
    slopes_out[...] = slopes_ref[...]
    rows = early_ref.shape[1]
    hidden = gate_out.shape[3]
    for piece in range(2):
        to = slice(piece * rows, (piece + 1) * rows)
        spot = slice(piece * hidden, (piece + 1) * hidden)
        gate_out[0, :, to, :] = middle_ref[0, :, :, spot].astype(full)
        up_out[0, :, to, :] = middle_ref[1, :, :, spot].astype(full)
        gate_out[1, :, to, :] = late_ref[0, :, :, spot].astype(full)
        up_out[1, :, to, :] = late_ref[1, :, :, spot].astype(full)
    down_out[0] = early_ref[...].astype(full)
    down_out[1] = late_ref[2].astype(full)

    @pl.when(pl.program_id(0) == 0)
    def _():
        first_out[...] = gain_ref[0:1, :]
        second_out[...] = gain_ref[1:2, :]
        half = delta_ref.shape[1]
        key_width = key_out.shape[1]
        for i in range(2):
            span = slice(i * half, (i + 1) * half)
            output_out[span, :] = delta_ref[i].astype(full)
            query_out[span, :] = delta_ref[2 + i].astype(full)
            key_out[span, :] = delta_ref[4 + i, :, :key_width].astype(full)
            value_out[span, :] = delta_ref[4 + i, :, key_width:].astype(full)


def emit_pass(tokens, slopes, gains, deltas, early, middle, late):
    full = jnp.float32
    shape = jax.ShapeDtypeStruct
    number, width = tokens.shape
    rows = gains.shape[1]
    _, high, wide = early.shape
    hidden = high * PARTS
    steps = 2
    each = PARTS // steps

    def moving(*block):
        return pl.BlockSpec(block, lambda i: (i,) + (0,) * (len(block) - 1))

    def fixed(*block):
        return pl.BlockSpec(block, lambda i: (0,) * len(block))

    def inner(*block):
        return pl.BlockSpec(block, lambda i: (0, i, 0, 0))

    return pl.pallas_call(
        emit_kernel,
        name="emit_pass",
        grid=(steps,),
        out_shape=(
            shape(tokens.shape, tokens.dtype),
            shape(slopes.shape, slopes.dtype),
            shape((1, rows), full),
            shape((rows, width), full),
            shape((rows, width // 2), full),
            shape((rows, width // 2), full),
            shape((rows, width), full),
            shape((1, rows), full),
            shape((2, PARTS, 2 * high, hidden), full),
            shape((2, PARTS, 2 * high, hidden), full),
            shape((2, PARTS, high, wide), full),
        ),
        in_specs=[
            moving(number // steps, width),
            moving(number // steps, width),
            fixed(*gains.shape),
            fixed(*deltas.shape),
            moving(each, high, wide),
            inner(2, each, high, wide),
            inner(3, each, high, wide),
        ],
        out_specs=(
            moving(number // steps, width),
            moving(number // steps, width),
            fixed(1, rows),
            fixed(rows, width),
            fixed(rows, width // 2),
            fixed(rows, width // 2),
            fixed(rows, width),
            fixed(1, rows),
            inner(2, each, 2 * high, hidden),
            inner(2, each, 2 * high, hidden),
            inner(2, each, high, wide),
        ),
        compiler_params=pltpu.CompilerParams(vmem_limit_bytes=VMEM_MOST),
        cost_estimate=pl.CostEstimate(flops=1 << 20, bytes_accessed=1 << 24, transcendentals=0),
    )(
        tokens,
        slopes,
        gains,
        deltas,
        early,
        middle.reshape(2, PARTS, high, wide),
        late.reshape(3, PARTS, high, wide),
    )


def local(
    tokens,
    cotangent,
    seq_lengths,
    pack_order,
    unpack_order,
    expert_ids,
    gates,
    first_gain,
    query_weight,
    key_matrix,
    value_matrix,
    output_weight,
    second_gain,
    gate_weight,
    up_weight,
    down_weight,
):
    shards = lax.axis_size("shard")
    group_count, width = tokens.shape
    order = pack_order.reshape(1, group_count)
    (
        joined,
        gains,
        mixing,
        along,
        across,
        inputs,
        queries,
        keys,
        values,
        mixed,
        logsum,
        hidden,
        normed,
        shared,
        all_slopes,
    ) = front_pass(
        tokens,
        (query_weight, key_matrix, value_matrix, output_weight),
        (first_gain, second_gain),
        order,
        expert_ids,
        gates,
        seq_lengths,
        cotangent,
        shards,
    )
    tables = (order, seq_lengths, along, across, joined, gains)
    reps = lax.axis_size("rep")
    inner, row_slopes, partial, *early = expert_pass(
        normed, all_slopes, mixing, gate_weight, up_weight, down_weight, shards, reps
    )
    back, pieces, *middle = return_pass(
        row_slopes, inner, gate_weight, up_weight, down_weight, shared, partial, shards, reps
    )
    deltas, gain_deltas, delta_tokens, out_tokens, *late = finish_pass(
        shards,
        reps,
        back,
        all_slopes,
        *tables,
        inputs,
        queries,
        keys,
        values,
        mixed,
        logsum,
        hidden,
        pieces,
        partial,
    )
    if reps == LINE:
        early, middle, late = early[0], middle[0], late[0]
    else:
        summed = lax.psum(partial, "rep")
        early, middle, late = summed[:PARTS], summed[PARTS : 3 * PARTS], summed[3 * PARTS :]
    (
        out_tokens,
        delta_tokens,
        delta_first,
        delta_query,
        delta_key,
        delta_value,
        delta_output,
        delta_second,
        delta_gate,
        delta_up,
        delta_down,
    ) = emit_pass(
        out_tokens, delta_tokens.reshape(group_count, width), gain_deltas, deltas, early, middle, late
    )
    return (
        out_tokens,
        delta_tokens,
        delta_first.reshape(first_gain.shape),
        delta_query,
        delta_key,
        delta_value,
        delta_output,
        delta_second.reshape(second_gain.shape),
        delta_gate.reshape(gate_weight.shape),
        delta_up.reshape(up_weight.shape),
        delta_down.reshape(down_weight.shape),
    )


def solution(mesh):
    placed = (
        P(("rep", "shard"), None),
        P(("rep", "shard"), None),
        P(("rep", "shard"), None),
        P(("rep", "shard")),
        P(("rep", "shard")),
        P(("rep", "shard"), None),
        P(("rep", "shard"), None),
        P("shard"),
        P("shard", None),
        P("shard", None),
        P("shard", None),
        P("shard", None),
        P("shard"),
        P("shard", None, None),
        P("shard", None, None),
        P("shard", None, None),
    )
    return jax.shard_map(
        local,
        mesh=mesh,
        in_specs=placed,
        out_specs=(
            P(("rep", "shard"), None),
            P(("rep", "shard"), None),
            P("shard"),
            P("shard", None),
            P("shard", None),
            P("shard", None),
            P("shard", None),
            P("shard"),
            P("shard", None, None),
            P("shard", None, None),
            P("shard", None, None),
        ),
        check_vma=False,
    )
```
